32 devices in a mesh: dp: 8 (over y, x, core), tensor: 4 (over z).
Axes of the slice: x: 2, y: 2, z: 4, core: 2. Of those that a mesh axis runs over, the one named last changes fastest.
Arguments:
- inputs: bfloat16 [16384, 512], P(('dp', 'tensor')), may hold values from -6 to 6
- teacher: bfloat16 [16384, 512], P(('dp', 'tensor')), may hold values from -6 to 6
- lengths: int32 [8], replicated, may hold values from 512 to 2048, as said below
- positions: bfloat16 [2048, 512], replicated, may hold values from -3 to 3
- qkv_weight: bfloat16 [512, 3, 512], P(None, None, 'tensor'), may hold values from -0.25 to 0.25
- query_value_bias: bfloat16 [2, 512], P(None, 'tensor'), may hold values from -1.796875 to 1.796875
- output_weight: bfloat16 [512, 512], P('tensor'), may hold values from -2 to 2
- output_bias: bfloat16 [512], replicated, may hold values from -1.796875 to 1.796875
- first_gain: bfloat16 [512], replicated, may hold values from 0.5 to 1.5
- first_shift: bfloat16 [512], replicated, may hold values from -1.796875 to 1.796875
- inner_weight: bfloat16 [512, 2048], P(None, 'tensor'), may hold values from -0.25 to 0.25
- inner_bias: bfloat16 [2048], P('tensor'), may hold values from -1.796875 to 1.796875
- outer_weight: bfloat16 [2048, 512], P('tensor'), may hold values from -0.25 to 0.25
- outer_bias: bfloat16 [512], replicated, may hold values from -1.796875 to 1.796875
- second_gain: bfloat16 [512], replicated, may hold values from 0.5 to 1.5
- second_shift: bfloat16 [512], replicated, may hold values from -1.796875 to 1.796875
Outputs:
- output: bfloat16 [16384, 512], P(('dp', 'tensor'))
- input_grad: bfloat16 [16384, 512], P(('dp', 'tensor'))
- position_grad: float32 [2048, 512], P(('dp', 'tensor'))
- qkv_grad: float32 [512, 3, 512], P(None, None, 'tensor')
- query_value_bias_grad: float32 [2, 512], P(None, 'tensor')
- output_weight_grad: float32 [512, 512], P('tensor')
- output_bias_grad: float32 [512], replicated
- first_gain_grad: float32 [512], replicated
- first_shift_grad: float32 [512], replicated
- inner_weight_grad: float32 [512, 2048], P(None, 'tensor')
- inner_bias_grad: float32 [2048], P('tensor')
- outer_weight_grad: float32 [2048, 512], P('tensor')
- outer_bias_grad: float32 [512], replicated
- second_gain_grad: float32 [512], replicated
- second_shift_grad: float32 [512], replicated
The draws below stay inside these ranges and needn't reach their ends.
Inputs may be any that keep to these rules, and one draw needn't show every extreme that they name: `lengths`: every draw has at least one slot of length 2048.
All inputs are finite; a program needn't handle non-finite values.
Results may differ from the reference program's by a relative error of at most 0.035.
The reference program's roundings to bfloat16 on the way count: a program that leaves them out, or rounds other values in their place, can miss the bound.
Values may be sent and summed in bfloat16 or wider, within the bound.
A program may use at most 128 MiB of HBM per device.

```python
import math
import jax
import jax.numpy as jnp
from jax import lax

D = 512
HEADS = 8
HD = 64
FF = 2048
LEN = 2048
SLOTS = 8
TOKENS = 16384


def draw_lengths(key, part):
    first_key, second_key = jax.random.split(key, 2)
    slot_ids = jnp.arange(SLOTS, dtype=jnp.int32)
    baseline = LEN // 4 + 5 * LEN // 8 * slot_ids // (SLOTS - 1)
    jitter = jax.random.randint(first_key, (SLOTS,), 0, LEN // 8 + 1, dtype=jnp.int32)
    chosen = jax.random.randint(second_key, (), 0, SLOTS, dtype=jnp.int32)
    drawn = jnp.minimum(baseline + jitter, LEN)
    return jnp.where(slot_ids == chosen, LEN, drawn).astype(jnp.int32)


def shard_levels(stream_key, shape, shards, least, largest):
    level = 1.0
    for dim, shards_of in shards:
        heights = jax.random.uniform(jax.random.fold_in(jax.random.fold_in(stream_key, 6), dim), (shards_of,), jnp.float32, least / len(shards), largest / len(shards))
        level = level * jnp.repeat(jnp.exp(heights), shape[dim] // shards_of).reshape((-1,) + (1,) * (len(shape) - 1 - dim))
    return level


def bell_draw(rng, dims, scale, limit, cuts=(), held_as=jnp.bfloat16):
    level = shard_levels(rng, dims, cuts, -0.22, 0.18) if cuts else 1.0
    array = jax.random.normal(rng, dims, jnp.float32) * scale * level
    return jnp.minimum(jnp.maximum(array, -limit), limit).astype(held_as)


def setup_inputs(seed: int = 0) -> dict:
    streams_of = jax.random.split(jax.random.key(seed), 17)
    inputs = bell_draw(streams_of[0], (TOKENS, D), 1.0, 6.0, ((0, 32),))
    teacher = bell_draw(streams_of[1], (TOKENS, D), 1.0, 6.0, ((0, 32),))
    lengths = draw_lengths(jax.random.fold_in(streams_of[16], 71), 0)
    positions = bell_draw(streams_of[3], (LEN, D), 0.5, 3.0)
    qkv_weight = bell_draw(streams_of[4], (D, 3, D), D ** -0.5, 0.25, ((2, 4),))
    query_value_bias = bell_draw(streams_of[5], (2, D), 0.3, 1.796875, ((1, 4),))
    output_weight = bell_draw(streams_of[6], (D, D), 8 ** -0.5, 2.0, ((0, 4),))
    output_bias = bell_draw(streams_of[7], (D,), 0.3, 1.796875)
    first_gain = jnp.clip(1.0 + 0.1 * jax.random.normal(streams_of[8], (D,), jnp.float32), 0.5, 1.5).astype(jnp.bfloat16)
    first_shift = bell_draw(streams_of[9], (D,), 0.3, 1.796875)
    inner_weight = bell_draw(streams_of[10], (D, FF), D ** -0.5, 0.25, ((1, 4),))
    inner_bias = bell_draw(streams_of[11], (FF,), 0.3, 1.796875, ((0, 4),))
    outer_weight = bell_draw(streams_of[12], (FF, D), (FF // 4) ** -0.5, 0.25, ((0, 4),))
    outer_bias = bell_draw(streams_of[13], (D,), 0.3, 1.796875)
    second_gain = jnp.clip(1.0 + 0.1 * jax.random.normal(streams_of[14], (D,), jnp.float32), 0.5, 1.5).astype(jnp.bfloat16)
    second_shift = bell_draw(streams_of[15], (D,), 0.3, 1.796875)
    return {"inputs": inputs, "teacher": teacher, "lengths": lengths, "positions": positions, "qkv_weight": qkv_weight, "query_value_bias": query_value_bias, "output_weight": output_weight, "output_bias": output_bias, "first_gain": first_gain, "first_shift": first_shift, "inner_weight": inner_weight, "inner_bias": inner_bias, "outer_weight": outer_weight, "outer_bias": outer_bias, "second_gain": second_gain, "second_shift": second_shift}


precise = lax.Precision.HIGHEST
norm_eps = 1e-05
masked_fill = -1e+30

@jax.custom_vjp
def low(v):
    return lax.optimization_barrier(v.astype(jnp.bfloat16)).astype(jnp.float32)

@jax.custom_vjp
def low_back(v):
    return v

def low_keep(v):
    return (low(v), None)

def low_pass(kept, grad):
    return (grad,)

def back_keep(v):
    return (v, None)

def back_low(kept, grad):
    return (low(grad),)
low.defvjp(low_keep, low_pass)
low_back.defvjp(back_keep, back_low)

def layer_norm(value, gain, shift):
    centre = lax.optimization_barrier(jnp.mean(value, axis=-1, keepdims=True))
    centred = value - centre
    spread = lax.optimization_barrier(jnp.mean(centred * centred, axis=-1, keepdims=True))
    return centred * lax.rsqrt(spread + norm_eps) * gain + shift

def attend_one(queries, key_rows, value_rows, length):
    seq_length = queries.shape[0]
    block_size = min(512, seq_length)
    places = jnp.arange(seq_length, dtype=jnp.int32)
    score_scale = 1.0 / math.sqrt(HD)

    def one_block(offset):
        query_block = lax.dynamic_slice_in_dim(queries, offset, block_size, 0)
        query_places = offset + jnp.arange(block_size, dtype=jnp.int32)
        scores = jnp.einsum('qhd,khd->hqk', query_block, key_rows, precision=precise) * score_scale
        scores = low_back(scores)
        allowed = (places[None, :] <= query_places[:, None]) & (places[None, :] < length)
        scores = jnp.where(allowed[None], scores, masked_fill)
        probs = low(jax.nn.softmax(scores, axis=-1))
        return jnp.einsum('hqk,khd->qhd', probs, value_rows, precision=precise)
    offsets = jnp.arange(seq_length // block_size, dtype=jnp.int32) * block_size
    blocks = lax.map(jax.checkpoint(one_block), offsets)
    return blocks.reshape(seq_length, queries.shape[1], queries.shape[2])

def forward(parameters, embedded_in, teacher_rows, slot_lengths, loss_scale):
    positions, qkv_weight, query_value_bias, output_weight, output_bias, first_gain, first_shift, inner_weight, inner_bias, outer_weight, outer_bias, second_gain, second_shift = parameters
    slot_count = slot_lengths.shape[0]
    total_rows = embedded_in.shape[0]
    embedded = embedded_in + jnp.tile(positions, (slot_count, 1))
    embedded_low = low(embedded)
    zero_row = jnp.zeros_like(query_value_bias[0])
    biases = jnp.stack([query_value_bias[0], zero_row, query_value_bias[1]])
    projected = jnp.einsum('nd,dpe->npe', embedded_low, qkv_weight, precision=precise) + biases
    projected = low(low_back(projected))
    shaped = projected.reshape(slot_count, LEN, 3, HEADS, HD)
    attended = jax.vmap(attend_one)(shaped[:, :, 0], shaped[:, :, 1], shaped[:, :, 2], slot_lengths)
    mixed = low(low_back(attended.reshape(total_rows, D)))
    branch = low_back(jnp.dot(mixed, output_weight, precision=precise))
    first = layer_norm(embedded + branch + output_bias, first_gain, first_shift)
    pre = low_back(jnp.dot(low(first), inner_weight, precision=precise) + inner_bias)
    hidden = low(jax.nn.relu(pre))
    feed = low_back(jnp.dot(hidden, outer_weight, precision=precise))
    result = layer_norm(first + feed + outer_bias, second_gain, second_shift)
    places = jnp.arange(LEN, dtype=jnp.int32)
    valid = (places[None, :] < slot_lengths[:, None]).reshape(total_rows, 1).astype(jnp.float32)
    error = (result - teacher_rows) * valid
    loss_value = 0.5 * loss_scale * jnp.sum(error * error)
    return (loss_value, result)

def reference(inputs, teacher, lengths, positions, qkv_weight, query_value_bias, output_weight, output_bias, first_gain, first_shift, inner_weight, inner_bias, outer_weight, outer_bias, second_gain, second_shift):
    parameters = tuple((array_in.astype(jnp.float32) for array_in in (positions, qkv_weight, query_value_bias, output_weight, output_bias, first_gain, first_shift, inner_weight, inner_bias, outer_weight, outer_bias, second_gain, second_shift)))
    token_count = jnp.sum(lengths).astype(jnp.float32)
    loss_scale = jnp.float32(SLOTS * LEN) / token_count
    pair_count = SLOTS // 2
    input_pairs = inputs.astype(jnp.float32).reshape(pair_count, 2 * LEN, D)
    teacher_pairs = teacher.astype(jnp.float32).reshape(pair_count, 2 * LEN, D)
    length_pairs = lengths.reshape(pair_count, 2)

    def one_pair(carry, packed):
        input_pair, teacher_pair, length_pair = packed

        def loss_of(weights, embedded_in):
            return forward(weights, embedded_in, teacher_pair, length_pair, loss_scale)
        loss_value, pull_back, result = jax.vjp(loss_of, parameters, input_pair, has_aux=True)
        weight_grads, input_grads = pull_back(jnp.ones_like(loss_value))
        carry = jax.tree.map(lambda summed, added: summed + added, carry, weight_grads)
        return (carry, (result.astype(jnp.bfloat16), input_grads.astype(jnp.bfloat16)))
    start_grads = jax.tree.map(jnp.zeros_like, parameters)
    weight_sums, (results, input_grads) = lax.scan(one_pair, start_grads, (input_pairs, teacher_pairs, length_pairs))
    return (results.reshape(TOKENS, D), input_grads.reshape(TOKENS, D), weight_sums[0], weight_sums[1], weight_sums[2], weight_sums[3], weight_sums[4], weight_sums[5], weight_sums[6], weight_sums[7], weight_sums[8], weight_sums[9], weight_sums[10], weight_sums[11], weight_sums[12])
```

```python
import functools
import math

import jax
import jax.numpy as jnp
from jax import lax
from jax.experimental import pallas as pl
from jax.experimental.pallas import tpu as pltpu
from jax.sharding import PartitionSpec as P

HD = 64
EPS = 1e-05
NEG = -1e30
BF = jnp.bfloat16
F32 = jnp.float32
MESH = pl.DeviceIdType.MESH
VM = pl.BlockSpec(memory_space=pltpu.VMEM)
SM = pl.BlockSpec(memory_space=pltpu.SMEM)


class Geo:
    def __init__(self, mesh, slots, seq, width, hidden):
        self.T = mesh.shape["tensor"]
        self.DP = mesh.shape["dp"]
        self.H = self.T // 2
        self.NC = self.DP // 2
        self.nbits = self.NC.bit_length() - 1
        self.slots = slots
        self.L = seq
        self.D = width
        self.FF = hidden
        self.R = seq // self.T
        self.W = width // self.T
        self.WP = max(self.W, 128)
        self.NH = self.W // HD
        self.F = hidden // self.T
        self.PR = seq // (self.DP * self.T)


class Co:
    def __init__(self, G):
        self.dp = lax.axis_index("dp")
        self.z = lax.axis_index("tensor")
        self.c = self.dp % 2
        self.col = self.dp // 2
        self.g = self.z // G.H
        self.zz = self.z - self.g * G.H
        self.other = (self.z + G.H) % G.T
        self.native = self.c == self.g
        self.swapped = self.c != self.g
        self.hb = (self.z + self.c * G.H) % G.T
        self.ob = self.own_block(G, self.z, self.c)
        self.slot = 2 * self.col + self.g
        self.mate = self.dp + 1 - 2 * self.c
        b0 = self.col % 2
        b1 = (self.col // 2) % 2
        self.bf = b0 + self.c * (b1 - b0)
        self.bs = b1 + self.c * (b0 - b1)
        wf = 1 + self.c
        ws = 2 - self.c
        self.dpf = self.dp + 2 * wf * (1 - 2 * self.bf)
        self.dps = self.dp + 2 * ws * (1 - 2 * self.bs)

    @staticmethod
    def own_block(G, z, c):
        d = c - z // G.H
        return (z + d * d * G.H) % G.T

    def extra(self, G, bit):
        b = (self.col // (1 << bit)) % 2
        return self.dp + (2 << bit) * (1 - 2 * b)

    def piece(self):
        return self.c * 4 + self.bs * 2 + self.bf


def rcopy(src, dst, ss, rs, dev):
    return pltpu.make_async_remote_copy(
        src_ref=src, dst_ref=dst, send_sem=ss, recv_sem=rs, device_id=dev, device_id_type=MESH
    )


def greet(partners):
    bar = pltpu.get_barrier_semaphore()
    for dev in partners:
        pl.semaphore_signal(bar, inc=1, device_id=dev, device_id_type=MESH)
    pl.semaphore_wait(bar, len(partners))


class Sems:
    def __init__(self, ref):
        self.ref = ref
        self.n = 0

    def take(self, n=1):
        base = self.n
        self.n += n
        return lambda i=0: self.ref.at[base + i]


class Pending:
    def __init__(self):
        self.items = []

    def send(self, copy, cond=None):
        if cond is None:
            copy.start()
        else:
            pl.when(cond)(copy.start)
        self.items.append((cond, copy.wait_send))
        return copy

    def local(self, copy, cond=None):
        if cond is None:
            copy.start()
        else:
            pl.when(cond)(copy.start)
        self.items.append((cond, copy.wait))
        return copy

    def drain(self):
        for cond, wait in self.items:
            if cond is None:
                wait()
            else:
                pl.when(cond)(wait)
        self.items = []


def column_partners(G, co):
    out = [(co.mate, co.z), (co.dpf, co.z), (co.dps, co.z), (co.mate, co.other)]
    out += [(co.dp, (co.z + k) % G.T) for k in range(1, G.T)]
    return out


def gather_rows(G, co, S, pend, x, xall, chunks=2):
    T, H, R = G.T, G.H, G.R
    n = R // chunks
    rs = S.take(T * chunks)
    ss = S.take(T * chunks * 4)
    used = [0]

    def nexts():
        used[0] += 1
        return ss(used[0] - 1)

    def rows(r, ch):
        return xall.at[pl.ds(r * R + ch * n, n)]

    def arrive(r, ch):
        rcopy(rows(r, ch), rows(r, ch), ss(0), rs(r * chunks + ch), (co.mate, co.z)).wait_recv()

    z = co.z
    zb = H - 1 + co.c
    for ch in range(chunks):
        mine = x.at[pl.ds(ch * n, n)]
        arrives = rs(z * chunks + ch)
        pend.send(rcopy(mine, rows(z, ch), nexts(), arrives, (co.dp, zb)), co.swapped)
        for j in range(1, H):
            dest = co.g * H + (co.zz + j) % H
            pend.send(rcopy(mine, rows(z, ch), nexts(), arrives, (co.dp, dest)), co.native)
        pend.send(rcopy(mine, rows(z, ch), nexts(), arrives, (co.mate, z)), co.native)
        pend.local(pltpu.make_async_copy(mine, rows(z, ch), nexts()), co.native)

    edge = jnp.logical_and(co.native, z == H - 1 + co.g)
    order = []
    for ch in range(chunks):
        for j in range(1, H):
            order.append((co.g * H + (co.zz + j) % H, ch, False))
    for ch in range(chunks):
        for k in range(H):
            order.append(((H - 1 - k) + (1 - co.g) * (2 * k + 1), ch, True))

    for r, ch, outside in order:

        @pl.when(co.native)
        def _():
            arrive(r, ch)

        if outside:
            for j in range(1, H):
                dest = co.g * H + (co.zz + j) % H
                pend.send(
                    rcopy(rows(r, ch), rows(r, ch), nexts(), rs(r * chunks + ch), (co.dp, dest)),
                    edge,
                )
        pend.send(
            rcopy(rows(r, ch), rows(r, ch), nexts(), rs(r * chunks + ch), (co.mate, z)), co.native
        )

    def finish():
        @pl.when(co.swapped)
        def _():
            for ch in range(chunks):
                for r in range(T):
                    arrive(r, ch)

    return finish


def gather_weights(G, co, S, pend, wq, wqo, pairs):
    T, H = G.T, G.H
    z = co.z
    items = [(wq, wqo, None, H)]
    for k in range(1, T):
        for src, dst in pairs:
            items.append((src, dst, (z - k) % T, k))
    n = len(items)
    ss = S.take(4 * n)
    rs = S.take(4 * n)
    p = co.piece()

    def view(dst, slab, first, count, size):
        rows = pl.ds(first * size, count * size)
        return dst.at[rows] if slab is None else dst.at[slab, rows]

    for i, (src, dst, slab, k) in enumerate(items):
        size = src.shape[0] // 8
        target = view(dst, None if slab is None else z, p, 1, size)
        mine = view(src, None, p, 1, size)
        pend.send(rcopy(mine, target, ss(i), rs(i), (co.dp, (z + k) % T)))

    stages = [(p, 1, co.dpf), (p // 2 * 2, 2, co.dps), (co.c * 4, 4, co.mate)]
    before = (p, 1)

    def steps():
        first, count = before
        for s, (nf, nc, dest) in enumerate(stages):
            for i, (src, dst, slab, k) in enumerate(items):
                size = src.shape[0] // 8
                got = view(dst, slab, first, count, size)
                rcopy(got, got, ss(0), rs(s * n + i), (co.mate, z)).wait_recv()
                out = view(dst, slab, nf, nc, size)
                pend.send(rcopy(out, out, ss((s + 1) * n + i), rs((s + 1) * n + i), (dest, z)))
            first, count = nf, nc
        for i, (src, dst, slab, k) in enumerate(items):
            size = src.shape[0] // 8
            got = view(dst, slab, first, count, size)
            rcopy(got, got, ss(0), rs(3 * n + i), (co.mate, z)).wait_recv()

    return steps


def gather_kernel(G, x, te, wq, wi, wo, wp, sm, xall, teach, wqo, wif, wof, wpf, smalls, sem):
    co = Co(G)
    S = Sems(sem)
    pend = Pending()
    greet(column_partners(G, co))
    loc = S.take(5)
    tsem = S.take(2)
    bs, br = S.take(G.T), S.take(G.T)
    pend.local(pltpu.make_async_copy(sm, smalls.at[co.z], bs(0)))
    small = [
        pend.send(rcopy(sm, smalls.at[co.z], bs(k), br(k), (co.dp, (co.z + k) % G.T)))
        for k in range(1, G.T)
    ]
    for i, (src, dst) in enumerate(((wi, wif), (wo, wof), (wp, wpf))):
        pend.local(pltpu.make_async_copy(src, dst.at[co.z], loc(i)))
    wsteps = gather_weights(G, co, S, pend, wq, wqo, ((wi, wif), (wo, wof), (wp, wpf)))
    xfinish = gather_rows(G, co, S, pend, x, xall)
    pend.local(pltpu.make_async_copy(te, teach, loc(3)), co.native)
    swap = pend.send(rcopy(te, teach, tsem(0), tsem(1), (co.mate, co.other)), co.swapped)
    xfinish()
    wsteps()
    for cp in small:
        cp.wait_recv()
    pl.when(co.swapped)(swap.wait_recv)
    pend.drain()


def lanes(shape):
    return lax.broadcasted_iota(jnp.int32, shape, len(shape) - 1)


def aug_base(h):
    return HD if h == 0 else 0


def dot(a, b):
    return lax.dot_general(a, b, (((1,), (0,)), ((), ())), preferred_element_type=F32)


def dot_nt(a, b):
    return lax.dot_general(a, b, (((1,), (1,)), ((), ())), preferred_element_type=F32)


def dot_tn(a, b):
    return lax.dot_general(a, b, (((0,), (0,)), ((), ())), preferred_element_type=F32)


def parts3(v):
    hi = v.astype(BF).astype(F32)
    mid = (v - hi).astype(BF).astype(F32)
    return hi, mid, v - hi - mid


def place3(base, lane, first, v):
    hi, mid, lo = parts3(v)
    base = jnp.where(lane == first, hi, base)
    base = jnp.where(lane == first + 1, mid, base)
    return jnp.where(lane == first + 2, lo, base)


def project(G, co, lengths, xall, pos, wqh, bias, emb, qa, ka, va):
    CH = 256
    WP = G.WP
    length = lengths[co.slot]

    def step(i, carry):
        rows = pl.ds(pl.multiple_of(i * CH, CH), CH)
        low = (xall[rows, :].astype(F32) + pos[rows, :].astype(F32)).astype(BF)
        emb[rows, :] = low
        pr = dot(low, wqh[...])
        q = (pr[:, :WP] + bias[0]).astype(BF).astype(F32) * (1.0 / math.sqrt(HD))
        k = pr[:, WP : 2 * WP].astype(BF).astype(F32)
        v = (pr[:, 2 * WP :] + bias[1]).astype(BF).astype(F32)
        lane = lanes((CH, WP))
        place = lax.broadcasted_iota(jnp.int32, (CH, WP), 0) + i * CH
        limit = jnp.where(place < length, 0.0, NEG)
        for h in range(G.NH):
            a0 = aug_base(h)
            data = lane // HD == h
            ones = jnp.where((lane >= a0) & (lane < a0 + 4), 1.0, 0.0)
            qa[h, rows, :] = jnp.where(data, q, jnp.where(lane == a0, 1.0, 0.0)).astype(BF)
            ka[h, rows, :] = jnp.where(data, k, jnp.where(lane == a0, limit, ones)).astype(BF)
            va[h, rows, :] = jnp.where(data, v, ones).astype(BF)
        return carry

    lax.fori_loop(0, G.L // CH, step, 0)


def attend_forward(G, qa, ka, va, mixed, acc, top, BQ):
    WP = G.WP
    nq = G.L // BQ

    def tile(i, j, masked):
        qrows = pl.ds(pl.multiple_of(i * BQ, BQ), BQ)
        krows = pl.ds(pl.multiple_of(j * BQ, BQ), BQ)
        for h in range(G.NH):
            s = dot_nt(qa[h, qrows, :], ka[h, krows, :])
            if masked:
                below = lax.broadcasted_iota(jnp.int32, (BQ, BQ), 0) >= lanes((BQ, BQ))
                s = jnp.where(below, s, NEG)
            old = top[h, :, :1]
            new = jnp.maximum(old, jnp.max(s, axis=-1, keepdims=True))
            p = jnp.exp(s - new).astype(BF)
            acc[h] = acc[h] * jnp.exp(old - new) + dot(p, va[h, krows, :])
            top[h] = jnp.broadcast_to(new, (BQ, WP))

    def block(i, carry):
        for h in range(G.NH):
            acc[h] = jnp.zeros((BQ, WP), F32)
            top[h] = jnp.full((BQ, WP), NEG, F32)

        def inner(j, c2):
            tile(i, j, False)
            return c2

        lax.fori_loop(0, i, inner, 0)
        tile(i, i, True)
        rows = pl.ds(pl.multiple_of(i * BQ, BQ), BQ)
        lane = lanes((BQ, WP))
        out = jnp.zeros((BQ, WP), F32)
        for h in range(G.NH):
            a0 = aug_base(h)
            total = acc[h, :, a0 : a0 + 1]
            out = jnp.where(lane // HD == h, acc[h] / total, out)
            lse = top[h, :, :1] + jnp.log(total)
            q = qa[h, rows, :].astype(F32)
            qa[h, rows, :] = place3(q, lane, a0 + 1, -lse).astype(BF)
        mixed[rows, :] = out.astype(BF)
        return carry

    lax.fori_loop(0, nq, block, 0)


def forward_kernel(G, BQ, lengths, xall, pos, wq, wqo, smalls, mixed, emb, qa, ka, va, wqh, acc, top):
    co = Co(G)

    @pl.when(co.c == 0)
    def _():
        wqh[...] = wq[...]

    @pl.when(co.c != 0)
    def _():
        wqh[...] = wqo[...]

    qb, vb = smalls[co.hb, 0:1, : G.WP], smalls[co.hb, 1:2, : G.WP]
    project(G, co, lengths, xall, pos, wqh, (qb, vb), emb, qa, ka, va)
    attend_forward(G, qa, ka, va, mixed, acc, top, BQ)


def members(G, co):
    me = co.zz * 2 + co.c
    for k in range(1, G.T):
        m = (me + k) % G.T
        yield k, m % 2, co.g * G.H + m // 2


def exchange(G, co, S, pend, source, target, mine):
    ss, rs = S.take(G.T), S.take(G.T)
    waits = []
    for k, c2, z2 in members(G, co):
        dev = (2 * co.col + c2, z2)
        waits.append(pend.send(rcopy(source(z2, c2), target, ss(k), rs(k), dev)))
    pend.local(pltpu.make_async_copy(mine, target, ss(0)))
    return waits


def mixed_kernel(G, mixed, mixr, sem):
    co = Co(G)
    S, pend = Sems(sem), Pending()
    greet([(2 * co.col + c2, z2) for _, c2, z2 in members(G, co)])

    def block(z2, c2):
        return mixed.at[pl.ds(co.own_block(G, z2, c2) * G.R, G.R)]

    waits = exchange(G, co, S, pend, block, mixr.at[co.hb], block(co.z, co.c))
    for w in waits:
        w.wait_recv()
    pend.drain()


def grad_mixed_kernel(G, gm, gmall, sem):
    co = Co(G)
    S, pend = Sems(sem), Pending()
    greet([(2 * co.col + c2, z2) for _, c2, z2 in members(G, co)])

    def block(z2, c2):
        return gm.at[(z2 + c2 * G.H) % G.T]

    target = gmall.at[pl.ds(co.ob * G.R, G.R)]
    waits = exchange(G, co, S, pend, block, target, block(co.z, co.c))
    for w in waits:
        w.wait_recv()
    pend.drain()


def norm(v):
    centre = jnp.mean(v, axis=-1, keepdims=True)
    v = v - centre
    inv = lax.rsqrt(jnp.mean(v * v, axis=-1, keepdims=True) + EPS)
    return v * inv, inv


def norm_back(e, normal, inv):
    a = jnp.mean(e, axis=-1, keepdims=True)
    b = jnp.mean(e * normal, axis=-1, keepdims=True)
    return inv * (e - a - normal * b)


def colsum(v):
    return jnp.sum(v, axis=0, keepdims=True)


def feed_kernel(
    G, lengths, mixr, xall, pos, teach, wif, wof, wpf, vecs, smalls,
    out, gmid, gm, dwi, dwo, dwp, vsum, ibsum,
    flow, hid, gpre, gfeed, gbr,
):
    co = Co(G)
    T, R = G.T, G.R
    CR = min(256, R)
    length = lengths[co.slot]
    count = lengths[0]
    for i in range(1, G.slots):
        count = count + lengths[i]
    scale = (G.slots * G.L) / jnp.full((1, 1), count, jnp.int32).astype(F32)
    vsum[...] = jnp.zeros(vsum.shape, F32)
    ibsum[...] = jnp.zeros(ibsum.shape, F32)
    output_bias, g1, s1 = vecs[0:1], vecs[1:2], vecs[2:3]
    outer_bias, g2, s2 = vecs[3:4], vecs[4:5], vecs[5:6]

    def step(i, carry):
        off = pl.multiple_of(i * CR, CR)
        rows = pl.ds(off, CR)
        grows = pl.ds(pl.multiple_of(co.ob * R + off, CR), CR)
        branch = lax.fori_loop(
            0, T, lambda t, a: a + dot(mixr[t, rows, :], wpf[t]), jnp.zeros((CR, G.D), F32)
        )
        e = xall[grows, :].astype(F32) + pos[grows, :].astype(F32)
        n1, inv1 = norm(e + branch + output_bias)
        first = n1 * g1 + s1
        low = first.astype(BF)
        flow[rows, :] = low

        def up(t, a):
            pre = dot(low, wif[t]) + smalls[t, 2:3, : G.F]
            h = jnp.maximum(pre, 0.0).astype(BF)
            hid[t, rows, :] = h
            return a + dot(h, wof[t])

        feed = lax.fori_loop(0, T, up, jnp.zeros((CR, G.D), F32))
        n2, inv2 = norm(first + feed + outer_bias)
        result = n2 * g2 + s2
        out[rows, :] = result.astype(BF)
        place = lax.broadcasted_iota(jnp.int32, (CR, 1), 0) + (co.ob * R + off)
        valid = jnp.where(place < length, scale, 0.0)
        gr = valid * (result - teach[rows, :].astype(F32))
        gs = norm_back(gr * g2, n2, inv2)
        gf = gs.astype(BF)
        gfeed[rows, :] = gf

        def down(t, a):
            gh = dot_nt(gf, wof[t])
            gp = jnp.where(hid[t, rows, :].astype(F32) > 0, gh, 0.0).astype(BF)
            gpre[t, rows, :] = gp
            ibsum[t] += colsum(gp.astype(F32))
            return a + dot_nt(gp, wif[t])

        g_first = lax.fori_loop(0, T, down, gs)
        gv = norm_back(g_first * g1, n1, inv1)
        gmid[rows, :] = gv
        gb = gv.astype(BF)
        gbr[rows, :] = gb

        def mix(t, a):
            gm[t, rows, :] = dot_nt(gb, wpf[t]).astype(BF)
            return a

        lax.fori_loop(0, T, mix, 0)
        vsum[0:1] += colsum(gv)
        vsum[1:2] += colsum(g_first * n1)
        vsum[2:3] += colsum(g_first)
        vsum[3:4] += colsum(gs)
        vsum[4:5] += colsum(gr * n2)
        vsum[5:6] += colsum(gr)
        return carry

    lax.fori_loop(0, R // CR, step, 0)

    def grads(t, carry):
        dwo[t] = dot_tn(hid[t], gfeed[...]).astype(BF)
        dwi[t] = dot_tn(flow[...], gpre[t]).astype(BF)
        dwp[t] = dot_tn(mixr[t], gbr[...]).astype(BF)
        return carry

    lax.fori_loop(0, T, grads, 0)


def backward_kernel(
    G, BQ, gm, mixed, emb, qa, ka, va, wq, wqo,
    ge, dwq, qvb,
    da, kt, dq, dk, dv, gp, wqh,
):
    co = Co(G)
    WP, L, NH = G.WP, G.L, G.NH
    CH = 256

    @pl.when(co.c == 0)
    def _():
        wqh[...] = wq[...]

    @pl.when(co.c != 0)
    def _():
        wqh[...] = wqo[...]

    def prepare(i, carry):
        rows = pl.ds(pl.multiple_of(i * CH, CH), CH)
        g = gm[rows, :].astype(F32)
        prod = g * mixed[rows, :].astype(F32)
        lane = lanes((CH, WP))
        k = jnp.zeros((CH, WP), F32)
        for h in range(NH):
            a0 = aug_base(h)
            data = lane // HD == h
            delta = jnp.sum(jnp.where(data, prod, 0.0), axis=-1, keepdims=True)
            base = place3(jnp.zeros((CH, WP), F32), lane, a0 + 1, -delta)
            da[h, rows, :] = jnp.where(data, g, base).astype(BF)
            k = jnp.where(data, ka[h, rows, :].astype(F32), k)
        kt[:, rows] = k.T.astype(BF)
        zero = jnp.zeros((CH, WP), F32)
        dk[rows, :] = zero
        dv[rows, :] = zero
        dq[:, rows] = zero.T
        return carry

    lax.fori_loop(0, L // CH, prepare, 0)

    def tile(i, j, masked):
        qrows = pl.ds(pl.multiple_of(i * BQ, BQ), BQ)
        krows = pl.ds(pl.multiple_of(j * BQ, BQ), BQ)
        lane = lanes((BQ, WP))
        sub = lax.broadcasted_iota(jnp.int32, (WP, BQ), 0)
        dks, dvs, dqs = [], [], []
        for h in range(NH):
            q, d = qa[h, qrows, :], da[h, qrows, :]
            p = jnp.exp(dot_nt(ka[h, krows, :], q))
            if masked:
                above = lax.broadcasted_iota(jnp.int32, (BQ, BQ), 0) <= lanes((BQ, BQ))
                p = jnp.where(above, p, 0.0)
            ds = (p * dot_nt(va[h, krows, :], d)).astype(BF)
            dvs.append(dot(p.astype(BF), d))
            dks.append(dot(ds, q))
            dqs.append(dot(kt[:, krows], ds))
        if NH == 1:
            dk[krows, :] += dks[0]
            dv[krows, :] += dvs[0]
            dq[:, qrows] += dqs[0]
        else:
            dk[krows, :] += jnp.where(lane < HD, dks[0], dks[1])
            dv[krows, :] += jnp.where(lane < HD, dvs[0], dvs[1])
            dq[:, qrows] += jnp.where(sub < HD, dqs[0], dqs[1])

    qvb[...] = jnp.zeros(qvb.shape, F32)
    dwq[...] = jnp.zeros(dwq.shape, F32)

    def block(s, carry):
        b = L // BQ - 1 - s

        def inner(j, c2):
            tile(b, j, False)
            return c2

        tile(b, b, True)
        lax.fori_loop(0, b, inner, 0)
        rows = pl.ds(pl.multiple_of(b * BQ, BQ), BQ)
        keep = lanes((BQ, WP)) < G.W
        q = dq[:, rows].T * (1.0 / math.sqrt(HD))
        for n, part in enumerate((q, dk[rows, :], dv[rows, :])):
            part = jnp.where(keep, part, 0.0).astype(BF)
            gp[rows, n * WP : (n + 1) * WP] = part
            if n != 1:
                qvb[n // 2 : n // 2 + 1, :] += colsum(part.astype(F32))
        g = gp[rows, :]
        ge[rows, :] = dot_nt(g, wqh[...]).astype(BF)
        dwq[...] += dot_tn(emb[rows, :], g)
        return carry

    lax.fori_loop(0, L // BQ, block, 0)


def finish_kernel(
    G, out_in, gmid, ge, dwi, dwo, dwp, dwq, vsum, ibsum, qvb,
    out, igrad, pgrad, qg, qvg, og, ig, ug, vout, ibout,
    nat, s0i, s0o, s0p, s0q, r0i, r0o, r0p, r0q, r1i, r1o, r1p, r1q, r2i, r2o, r2p, r2q,
    r3i, r3o, r3p, r3q, gi, go, gp, gq, esum, er0, er1, p0, p1, p2, pr0, pr1, pr2, pr3,
    va, vr, sem,
):
    co = Co(G)
    S, pend = Sems(sem), Pending()
    T, H, R, L = G.T, G.H, G.R, G.L
    z, c = co.z, co.c
    pp = c * (G.DP // 2) + co.bf * (G.DP // 4) + co.bs * (G.DP // 8)
    for bit in range(2, G.nbits):
        pp = pp + ((co.col // (1 << bit)) % 2) * (G.DP // (4 << bit))
    flat = z * G.DP + pp
    pdp, pz = flat // T, flat % T
    away = jnp.logical_or(pdp != co.dp, pz != z)
    mine = co.dp * T + z
    fz, fp = mine // G.DP, mine % G.DP
    fc = fp // (G.DP // 2)
    f1 = (fp // (G.DP // 4)) % 2
    f2 = (fp // (G.DP // 8)) % 2
    fcol = (f1 + fc * (f2 - f1)) + 2 * (f2 + fc * (f1 - f2))
    for bit in range(2, G.nbits):
        fcol = fcol + ((fp // (G.DP // (4 << bit))) % 2) * (1 << bit)
    bar = pltpu.get_barrier_semaphore()
    partners = column_partners(G, co) + [(co.extra(G, b), z) for b in range(2, G.nbits)]
    for dev in partners:
        pl.semaphore_signal(bar, inc=1, device_id=dev, device_id_type=MESH)

    @pl.when(away)
    def _():
        pl.semaphore_signal(bar, inc=1, device_id=(2 * fcol + fc, fz), device_id_type=MESH)

    pl.semaphore_wait(bar, len(partners) + away.astype(jnp.int32))

    mate = (co.mate, z)
    step1 = (co.dpf, z)
    step2 = (co.dps, z)

    def go_send(src, dst, dev, cond=None):
        s, r = S.take(), S.take()
        return pend.send(rcopy(src, dst, s(), r(), dev), cond)

    def go_now(src, dst, dev):
        s, r = S.take(), S.take()
        cp = rcopy(src, dst, s(), r(), dev)
        cp.start()
        return cp

    pend.local(pltpu.make_async_copy(out_in, out, S.take()()), co.native)
    swap = go_send(out_in, out, (co.mate, co.other), co.swapped)

    ecopies = []
    for j in range(H):
        blk = co.own_block(G, co.g * H + (co.zz + j) % H, 1 - c)
        ecopies.append(go_send(ge.at[pl.ds(blk * R, R)], er0.at[j], mate))

    big = ((dwi, s0i, r0i, r1i, r2i, r3i, gi), (dwo, s0o, r0o, r1o, r2o, r3o, go),
           (dwp, s0p, r0p, r1p, r2p, r3p, gp))
    first = []
    for X, s0, r0, *_ in big:
        hr = X.shape[1] // 2
        first.append(go_send(X.at[:, pl.ds((1 - c) * hr, hr)], r0, mate))
    hq = dwq.shape[0] // 2
    first.append(go_send(dwq.at[pl.ds((1 - c) * hq, hq)], r0q.at[c], mate))

    va[...] = jnp.zeros(va.shape, F32)
    va[0:6, :] = vsum[0:6, :]
    for t in range(T):
        va[8 + t : 9 + t, : G.F] = ibsum[t]
    row = lax.broadcasted_iota(jnp.int32, (2 * T, G.WP), 0)
    spread = jnp.where(row % 2 == 0, qvb[0:1, :], qvb[1:2, :])
    va[16 : 16 + 2 * T, : G.WP] = jnp.where(row // 2 == co.hb, spread, 0.0)

    def vec_stage(i, dev):
        return go_now(va, vr.at[i], dev)

    vs = vec_stage(0, mate)

    for cp in ecopies:
        cp.wait_recv()

    ew = []
    for j in range(1, H):
        z2 = co.g * H + (co.zz + j) % H
        blk = co.own_block(G, z2, c)
        total = ge[pl.ds(pl.multiple_of(blk * R, R), R), :].astype(F32) + er0[j].astype(F32)
        esum[j - 1] = total.astype(BF)
        ew.append(go_send(esum.at[j - 1], er1.at[j - 1], (co.dp, z2)))

    vs.wait_recv()
    vs.wait_send()
    va[...] += vr[0]
    vs = vec_stage(1, step1)

    for (X, s0, r0, *_), cp in zip(big, first):
        hr = X.shape[1] // 2
        cp.wait_recv()

        def add0(t, carry, X=X, s0=s0, r0=r0, hr=hr):
            own = X[t, pl.ds(pl.multiple_of(c * hr, hr), hr), :]
            s0[t] = (own.astype(F32) + r0[t].astype(F32)).astype(BF)
            return carry

        lax.fori_loop(0, T, add0, 0)
    s0q[c] = dwq[pl.ds(pl.multiple_of(c * hq, hq), hq), :]
    first[3].wait_recv()
    s0q[1 - c] = r0q[1 - c]

    def halves(s0, r1, bit, dev):
        q = s0.shape[1] // 2
        return go_send(s0.at[:, pl.ds((1 - bit) * q, q)], r1, dev)

    def fold(s0, r1, bit, n):
        q = r1.shape[1]

        def add(t, carry):
            own = s0[t, pl.ds(pl.multiple_of(bit * q, q), q), :]
            r1[t] = (own.astype(F32) + r1[t].astype(F32)).astype(BF)
            return carry

        lax.fori_loop(0, n, add, 0)

    arrays = [(s0i, r1i, r2i, T), (s0o, r1o, r2o, T), (s0p, r1p, r2p, T), (s0q, r1q, r2q, 2)]
    w1 = [halves(s0, r1, co.bf, step1) for s0, r1, r2, n in arrays]

    blk = co.ob
    total = gmid[...] + ge[pl.ds(pl.multiple_of(blk * R, R), R), :].astype(F32) + er0[0].astype(F32)
    for j in range(1, H):
        ew[j - 1].wait_recv()
        total = total + er1[j - 1].astype(F32)
    nat_mine = total.astype(BF)
    esum[H - 1] = nat_mine

    swap2 = go_send(esum.at[H - 1], nat, (co.mate, co.other), co.swapped)

    @pl.when(co.native)
    def _():
        nat[...] = nat_mine

    pl.when(co.swapped)(swap2.wait_recv)
    igrad[...] = nat[...]

    half = R // 2
    p0[...] = nat[...].astype(F32)
    pw = go_send(p0.at[pl.ds((1 - c) * half, half)], pr0, mate)

    vs.wait_recv()
    vs.wait_send()
    va[...] += vr[1]
    vs = vec_stage(2, step2)

    w2 = []
    for (s0, r1, r2, n), cp in zip(arrays, w1):
        cp.wait_recv()
        fold(s0, r1, co.bf, n)
        w2.append(halves(r1, r2, co.bs, step2))

    pw.wait_recv()
    pr0[...] += p0[pl.ds(pl.multiple_of(c * half, half), half), :]
    q1 = half // 2
    pw = go_send(pr0.at[pl.ds((1 - co.bf) * q1, q1)], pr1, step1)

    vs.wait_recv()
    vs.wait_send()
    va[...] += vr[2]
    slot = 3
    for bit in range(2, G.nbits):
        vs = vec_stage(slot, (co.extra(G, bit), z))
        vs.wait()
        va[...] += vr[slot]
        slot += 1
    zs = [vec_stage(slot + k - 1, (co.dp, (z + k) % T)) for k in range(1, T)]

    pw.wait_recv()
    pr1[...] += pr0[pl.ds(pl.multiple_of(co.bf * q1, q1), q1), :]
    q2 = q1 // 2
    pw = go_send(pr1.at[pl.ds((1 - co.bs) * q2, q2)], pr2, step2)

    w3 = []
    for i, ((s0, r1, r2, n), cp) in enumerate(zip(arrays, w2)):
        cp.wait_recv()
        fold(r1, r2, co.bs, n)
        for bit in range(2, G.nbits):
            tmp = (s0i, s0o, s0p, s0q)[i].at[pl.ds(0, n), pl.ds(0, r2.shape[1])]
            cp = go_now(r2, tmp, (co.extra(G, bit), z))
            cp.wait()

            def add(t, carry, r2=r2, s=(s0i, s0o, s0p, s0q)[i]):
                r2[t] = (r2[t].astype(F32) + s[t, : r2.shape[1], :].astype(F32)).astype(BF)
                return carry

            lax.fori_loop(0, n, add, 0)

    for i, (X, s0, r0, r1, r2, r3, gx) in enumerate(big):
        for k in range(1, T):
            z2 = (z + k) % T
            w3.append(go_send(r2.at[z2], r3.at[k - 1], (co.dp, z2)))
    w3.append(go_send(r2q.at[1], r3q, (co.dp, co.other)))

    pw.wait_recv()
    pr2[...] += pr1[pl.ds(pl.multiple_of(co.bs * q2, q2), q2), :]
    psrc = pr2
    size = q2
    tmps = []
    for n, bit in enumerate(range(2, G.nbits)):
        b = (co.col // (1 << bit)) % 2
        size = size // 2
        land = p1.at[pl.ds(0, size)] if n % 2 == 0 else p2.at[pl.ds(0, size)]
        cp = go_now(psrc.at[pl.ds((1 - b) * size, size)], land, (co.extra(G, bit), z))
        cp.wait()
        kept = psrc[pl.ds(pl.multiple_of(b * size, 8), size), :]
        dst = p1 if n % 2 == 0 else p2
        dst[0:size, :] += kept
        psrc = dst
    pw = go_send(psrc.at[pl.ds(0, size)], pr3, (pdp, pz), away)

    def piece_rows(gx, n, width):
        e = gx.shape[0] // 8
        first_row = c * 4 * e + (co.bf * 2 * e if n < 2 else 0) + (co.bs * e if n < 1 else 0)
        return gx.at[pl.ds(pl.multiple_of(first_row, 8), width * e)]

    idx = 0
    w4 = []
    gs = (gi, go, gp, gq)
    for i, (X, s0, r0, r1, r2, r3, gx) in enumerate(big):
        tot = r2[z].astype(F32)
        for k in range(1, T):
            w3[idx].wait_recv()
            idx += 1
            tot = tot + r3[k - 1].astype(F32)
        ref = piece_rows(gx, 0, 1)
        ref[...] = tot.astype(BF)
        w4.append(go_send(ref, ref, step2))
    w3[idx].wait_recv()
    ref = piece_rows(gq, 0, 1)
    ref[...] = (r2q[0].astype(F32) + r3q[...].astype(F32)).astype(BF)
    w4.append(go_send(ref, ref, step2))

    slot0 = slot
    for k in range(1, T):
        zs[k - 1].wait()
    for k in range(1, T):
        va[...] += vr[slot0 + k - 1]
    vout[...] = va[0:8, :]
    vrow = lax.broadcasted_iota(jnp.int32, va.shape, 0)
    ibout[...] = colsum(jnp.where(vrow == 8 + z, va[...], 0.0))
    for n in range(2):
        qvg[n : n + 1, :] = colsum(jnp.where(vrow == 16 + 2 * z + n, va[...], 0.0))

    w5 = []
    for gx, cp in zip(gs, w4):
        cp.wait_recv()
        ref = piece_rows(gx, 1, 2)
        w5.append(go_send(ref, ref, step1))
    w6 = []
    for gx, cp in zip(gs, w5):
        cp.wait_recv()
        ref = piece_rows(gx, 2, 4)
        w6.append(go_send(ref, ref, mate))
    for gx, cp, dst in zip(gs, w6, (ig, ug, og, qg)):
        cp.wait_recv()
        dst[...] = gx[...].astype(F32)

    pl.when(away)(pw.wait_recv)

    @pl.when(jnp.logical_not(away))
    def _():
        pr3[...] = psrc[0 : G.PR, :]

    pgrad[...] = pr3[...]
    pl.when(co.swapped)(swap.wait_recv)
    pend.drain()


def call(kernel, name, outs, scratch, cid=None, smem_first=False):
    params = dict(vmem_limit_bytes=60 << 20)
    if cid is not None:
        params.update(collective_id=cid, has_side_effects=True)

    def run(*args):
        specs = [VM] * len(args)
        if smem_first:
            specs[0] = SM
        return pl.pallas_call(
            kernel,
            out_shape=tuple(jax.ShapeDtypeStruct(s, d) for s, d in outs),
            in_specs=specs,
            out_specs=tuple([VM] * len(outs)),
            scratch_shapes=scratch,
            compiler_params=pltpu.CompilerParams(**params),
            name=name,
        )(*args)

    return run


def on_device(G, *args):
    (inputs, teacher, lengths, positions, qkv_weight, query_value_bias, output_weight, output_bias,
     first_gain, first_shift, inner_weight, inner_bias, outer_weight, outer_bias, second_gain,
     second_shift) = args
    T, R, D, L, W, WP, NH, F = G.T, G.R, G.D, G.L, G.W, G.WP, G.NH, G.F
    part = functools.partial
    dma = lambda n: pltpu.SemaphoreType.DMA((n,))
    vm = pltpu.VMEM
    wide = ((0, 0), (0, 0), (0, WP - W))
    wq = jnp.pad(qkv_weight, wide).reshape(D, 3 * WP)
    wp = jnp.pad(output_weight, ((0, WP - W), (0, 0)))
    lane_pad = lambda v: jnp.pad(v, ((0, 0), (0, D - v.shape[1])))
    small = jnp.concatenate(
        [lane_pad(query_value_bias), lane_pad(inner_bias[None]), jnp.zeros((5, D), BF)]
    ).astype(F32)
    vecs = jnp.stack(
        [output_bias, first_gain, first_shift, outer_bias, second_gain, second_shift]
    ).astype(F32)

    xall, teach, wqo, wif, wof, wpf, smalls = call(
        part(gather_kernel, G), "gather",
        [((L, D), BF), ((R, D), BF), ((D, 3 * WP), BF), ((T, D, F), BF), ((T, F, D), BF),
         ((T, WP, D), BF), ((T, 8, D), F32)],
        [dma(200)], cid=0,
    )(inputs, teacher, wq, inner_weight, outer_weight, wp, small)

    BQ = min(512, L)
    mixed, emb, qa, ka, va = call(
        part(forward_kernel, G, BQ), "attend_fwd",
        [((L, WP), BF), ((L, D), BF)] + [((NH, L, WP), BF)] * 3,
        [vm((D, 3 * WP), BF), vm((NH, BQ, WP), F32), vm((NH, BQ, WP), F32)], smem_first=True,
    )(lengths, xall, positions, wq, wqo, smalls)

    (mixr,) = call(part(mixed_kernel, G), "mixed_exchange", [((T, R, WP), BF)], [dma(2 * T)], cid=1)(mixed)

    out, gmid, gm, dwi, dwo, dwp, vsum, ibsum = call(
        part(feed_kernel, G), "feed",
        [((R, D), BF), ((R, D), F32), ((T, R, WP), BF), ((T, D, F), BF), ((T, F, D), BF),
         ((T, WP, D), BF), ((8, D), F32), ((T, 1, F), F32)],
        [vm((R, D), BF), vm((T, R, F), BF), vm((T, R, F), BF), vm((R, D), BF), vm((R, D), BF)],
        smem_first=True,
    )(lengths, mixr, xall, positions, teach, wif, wof, wpf, vecs, smalls)

    (gmall,) = call(part(grad_mixed_kernel, G), "grad_exchange", [((L, WP), BF)], [dma(2 * T)], cid=2)(gm)

    ge, dwq, qvb = call(
        part(backward_kernel, G, BQ), "attend_bwd",
        [((L, D), BF), ((D, 3 * WP), F32), ((2, WP), F32)],
        [vm((NH, L, WP), BF), vm((WP, L), BF), vm((WP, L), F32), vm((L, WP), F32),
         vm((L, WP), F32), vm((L, 3 * WP), BF), vm((D, 3 * WP), BF)],
    )(gmall, mixed, emb, qa, ka, va, wq, wqo)
    dwq = dwq.astype(BF)

    def shapes(rows, width, n):
        return [(n, rows >> k, width) for k in range(1, 4)] + [(rows >> 3, width), (rows, width)]

    geo = [(D, F, T), (F, D, T), (WP, D, T), (D, 3 * WP, 2)]
    s0 = [vm((n, r // 2, w), BF) for r, w, n in geo]
    r0 = s0
    r1 = [vm((n, r // 4, w), BF) for r, w, n in geo]
    r2 = [vm((n, r // 8, w), BF) for r, w, n in geo]
    r3 = [vm((T - 1, r // 8, w), BF) for r, w, n in geo[:3]] + [vm((D // 8, 3 * WP), BF)]
    gx = [vm((r, w), BF) for r, w, n in geo]
    nv = 3 + (G.nbits - 2) + T - 1
    V = 16 + 2 * T
    V = (V + 7) // 8 * 8
    scratch = (
        [vm((R, D), BF)] + s0 + r0 + r1 + r2 + r3 + gx
        + [vm((G.H, R, D), BF), vm((G.H, R, D), BF), vm((max(G.H - 1, 1), R, D), BF)]
        + [vm((R, D), F32), vm((max(R // 8, 8), D), F32), vm((max(R // 8, 8), D), F32)]
        + [vm((R // 2, D), F32), vm((R // 4, D), F32), vm((R // 8, D), F32), vm((G.PR, D), F32)]
        + [vm((V, D), F32), vm((nv, V, D), F32), dma(160)]
    )
    (out, igrad, pgrad, qg, qvg, og, ig, ug, vout, ibout) = call(
        part(finish_kernel, G), "finish",
        [((R, D), BF), ((R, D), BF), ((G.PR, D), F32), ((D, 3 * WP), F32), ((2, D), F32),
         ((WP, D), F32), ((D, F), F32), ((F, D), F32), ((8, D), F32), ((1, D), F32)],
        scratch, cid=3,
    )(out, gmid, ge, dwi, dwo, dwp, dwq, vsum, ibsum, qvb)
    qg = qg.reshape(D, 3, WP)[:, :, :W]
    return (
        out, igrad, pgrad, qg, qvg[:, :W], og[:W], vout[0], vout[1], vout[2],
        ig, ibout[0, :F], ug, vout[3], vout[4], vout[5],
    )


def solution(mesh):
    rows = P(("dp", "tensor"), None)
    specs = (
        rows, rows, P(), P(), P(None, None, "tensor"), P(None, "tensor"), P("tensor", None), P(),
        P(), P(), P(None, "tensor"), P("tensor"), P("tensor", None), P(), P(), P(),
    )
    outs = (
        rows, rows, rows, P(None, None, "tensor"), P(None, "tensor"), P("tensor", None), P(), P(),
        P(), P(None, "tensor"), P("tensor"), P("tensor", None), P(), P(), P(),
    )

    def step(*args):
        G = Geo(mesh, args[2].shape[0], args[3].shape[0], args[0].shape[1], args[11].shape[0])
        body = jax.shard_map(
            functools.partial(on_device, G), mesh=mesh, in_specs=specs, out_specs=outs,
            check_vma=False,
        )
        return body(*args)

    return step
```

```python
import functools
import math

import jax
import jax.numpy as jnp
from jax import lax
from jax.experimental import pallas as pl
from jax.experimental.pallas import tpu as pltpu
from jax.sharding import PartitionSpec as P

HD = 64
EPS = 1e-05
NSEM = 480
NEG = -1e30
BF = jnp.bfloat16
F32 = jnp.float32
MESH = pl.DeviceIdType.MESH
VM = pl.BlockSpec(memory_space=pltpu.VMEM)
SM = pl.BlockSpec(memory_space=pltpu.SMEM)


class Geo:
    def __init__(self, mesh, slots, seq, width, hidden):
        self.T = mesh.shape["tensor"]
        self.DP = mesh.shape["dp"]
        self.H = self.T // 2
        self.NC = self.DP // 2
        self.nbits = self.NC.bit_length() - 1
        self.slots = slots
        self.L = seq
        self.D = width
        self.FF = hidden
        self.R = seq // self.T
        self.W = width // self.T
        self.WP = max(self.W, 128)
        self.NH = self.W // HD
        self.F = hidden // self.T
        self.PR = seq // (self.DP * self.T)


class Co:
    def __init__(self, G):
        self.dp = lax.axis_index("dp")
        self.z = lax.axis_index("tensor")
        self.c = self.dp % 2
        self.col = self.dp // 2
        self.g = self.z // G.H
        self.zz = self.z - self.g * G.H
        self.other = (self.z + G.H) % G.T
        self.native = self.c == self.g
        self.swapped = self.c != self.g
        self.hb = (self.z + self.c * G.H) % G.T
        self.ob = self.own_block(G, self.z, self.c)
        self.slot = 2 * self.col + self.g
        self.mate = self.dp + 1 - 2 * self.c
        b0 = self.col % 2
        b1 = (self.col // 2) % 2
        self.bf = b0 + self.c * (b1 - b0)
        self.bs = b1 + self.c * (b0 - b1)
        wf = 1 + self.c
        ws = 2 - self.c
        self.dpf = self.dp + 2 * wf * (1 - 2 * self.bf)
        self.dps = self.dp + 2 * ws * (1 - 2 * self.bs)

    @staticmethod
    def own_block(G, z, c):
        d = c - z // G.H
        return (z + d * d * G.H) % G.T

    def extra(self, G, bit):
        b = (self.col // (1 << bit)) % 2
        return self.dp + (2 << bit) * (1 - 2 * b)

    def piece(self):
        return self.c * 4 + self.bs * 2 + self.bf


def owner(G, co, b):
    out = (b // G.H - co.g) * (b // G.H - co.g)
    return co.g + out * (1 - 2 * co.g), (b + out * G.H) % G.T


class Net:
    def __init__(self, ref):
        self.ref = ref
        self.n = 0
        self.items = []

    def take(self, n=1):
        base = self.n
        self.n += n
        return base

    def sem(self, i):
        return self.ref.at[i]

    def remote(self, src, dst, dev, cond=None, ss=None, rs=None):
        ss = self.take() if ss is None else ss
        rs = self.take() if rs is None else rs
        return Copy(self, src, dst, dev, ss, rs, cond)

    def local(self, src, dst, cond=None):
        return Copy(self, src, dst, None, self.take(), None, cond)

    def drain(self):
        for copy in self.items:
            copy.guard(copy.wait_sent)
        self.items = []


class Copy:
    def __init__(self, net, src, dst, dev, ss, rs, cond):
        self.net, self.src, self.dst, self.dev = net, src, dst, dev
        self.ss, self.rs, self.cond = ss, rs, cond

    def make(self):
        net = self.net
        if self.dev is None:
            return pltpu.make_async_copy(self.src(), self.dst(), net.sem(self.ss))
        return pltpu.make_async_remote_copy(
            src_ref=self.src(), dst_ref=self.dst(), send_sem=net.sem(self.ss),
            recv_sem=net.sem(self.rs), device_id=self.dev, device_id_type=MESH,
        )

    def guard(self, fn):
        if self.cond is None:
            fn()
        else:
            pl.when(self.cond)(fn)

    def start(self, hold=True):
        self.guard(lambda: self.make().start())
        if hold:
            self.net.items.append(self)
        return self

    def wait_sent(self):
        if self.dev is None:
            self.make().wait()
        else:
            self.make().wait_send()

    def got(self):
        self.make().wait_recv()


def column_partners(G, co):
    out = [(co.mate, co.z), (co.dpf, co.z), (co.dps, co.z), (co.mate, co.other)]
    out += [(co.dp, (co.z + k) % G.T) for k in range(1, G.T)]
    out += [(co.mate, (co.z + k) % G.T) for k in range(1, G.T) if k != G.H]
    out += [(co.extra(G, b), co.z) for b in range(2, G.nbits)]
    return out


def lanes(shape):
    return lax.broadcasted_iota(jnp.int32, shape, len(shape) - 1)


def aug_base(h):
    return HD if h == 0 else 0


def dot(a, b):
    return lax.dot_general(a, b, (((1,), (0,)), ((), ())), preferred_element_type=F32)


def dot_nt(a, b):
    return lax.dot_general(a, b, (((1,), (1,)), ((), ())), preferred_element_type=F32)


def dot_tn(a, b):
    return lax.dot_general(a, b, (((0,), (0,)), ((), ())), preferred_element_type=F32)


def parts3(v):
    hi = v.astype(BF).astype(F32)
    mid = (v - hi).astype(BF).astype(F32)
    return hi, mid, v - hi - mid


def place3(base, lane, first, v):
    hi, mid, lo = parts3(v)
    base = jnp.where(lane == first, hi, base)
    base = jnp.where(lane == first + 1, mid, base)
    return jnp.where(lane == first + 2, lo, base)


def norm(v):
    centre = jnp.mean(v, axis=-1, keepdims=True)
    v = v - centre
    inv = lax.rsqrt(jnp.mean(v * v, axis=-1, keepdims=True) + EPS)
    return v * inv, inv


def norm_back(e, normal, inv):
    a = jnp.mean(e, axis=-1, keepdims=True)
    b = jnp.mean(e * normal, axis=-1, keepdims=True)
    return inv * (e - a - normal * b)


def colsum(v):
    return jnp.sum(v, axis=0, keepdims=True)


def al(v, n):
    return pl.multiple_of(v, n)


def layer_kernel(
    G, lengths, x, te, wq, wi, wo, wp, sm, pos_in, vecs,
    out, igrad, pgrad, qg, qvg, og, ig, ug, vout, ibout,
    xall, pos, emb, qa, ka, va, da, kt, acc, top, mixed, mixr,
    wqo, wqh, wif, wof, wpf, smalls, teach,
    flow, hid, gpre, gfeed, gbr, gmid, osrc, gm, gmall, vsum, ibsum,
    dwi, dwo, dwp, dq, gp, dwq, dwqb,
    s0i, s0o, s0p, s0q, r0i, r0o, r0p, r0q, r1i, r1o, r1p, r1q, r2i, r2o, r2p, r2q,
    r3i, r3o, r3p, r3q, rxi, rxo, rxp, rxq, gi, go, gpp, gq,
    er0, esum, er1, gtot, nat, nsrc, p0, p1, p2, pr0, pr1, pr2, pr3, vb, vr, qb, qr,
    sem,
):
    co = Co(G)
    net = Net(sem)
    T, H, R, L, WP, NH, D, F = G.T, G.H, G.R, G.L, G.WP, G.NH, G.D, G.F
    z, c, g = co.z, co.c, co.g
    mate, step1, step2 = (co.mate, z), (co.dpf, z), (co.dps, z)
    length = lengths[co.slot]
    ge, dk, dv = xall, acc.at[0], acc.at[1]

    def rows(b, n=R):
        return pl.ds(al(b * R, R), n)

    pp = c * (G.DP // 2) + co.bf * (G.DP // 4) + co.bs * (G.DP // 8)
    for bit in range(2, G.nbits):
        pp = pp + ((co.col // (1 << bit)) % 2) * (G.DP // (4 << bit))
    flat = z * G.DP + pp
    pdp, pz = flat // T, flat % T
    away = jnp.logical_or(pdp != co.dp, pz != z)
    mine = co.dp * T + z
    fz, fp = mine // G.DP, mine % G.DP
    fc = fp // (G.DP // 2)
    f1 = (fp // (G.DP // 4)) % 2
    f2 = (fp // (G.DP // 8)) % 2
    fcol = (f1 + fc * (f2 - f1)) + 2 * (f2 + fc * (f1 - f2))
    for bit in range(2, G.nbits):
        fcol = fcol + ((fp // (G.DP // (4 << bit))) % 2) * (1 << bit)
    poscopy = net.local(lambda: pos_in, lambda: pos).start()
    bar = pltpu.get_barrier_semaphore()
    partners = column_partners(G, co)
    for dev in partners:
        pl.semaphore_signal(bar, inc=1, device_id=dev, device_id_type=MESH)

    @pl.when(away)
    def _():
        pl.semaphore_signal(bar, inc=1, device_id=(2 * fcol + fc, fz), device_id_type=MESH)

    pl.semaphore_wait(bar, len(partners) + away.astype(jnp.int32))

    chunks = 2
    n = R // chunks
    xr = net.take(T * chunks)

    def order(r):
        if r == 0:
            return z
        if r < H:
            return g * H + (co.zz + r) % H
        k = r - H
        return (H - 1 - k) + (1 - g) * (2 * k + 1)

    blocks = [order(r) for r in range(T)]
    zb = H - 1 + c
    edge = jnp.logical_and(co.native, z == H - 1 + g)

    def xrow(b, ch):
        return lambda: xall.at[pl.ds(al(b * R + ch * n, n), n)]

    def xmine(ch):
        return lambda: x.at[pl.ds(ch * n, n)]

    def xsend(src, b, ch, dev, cond):
        return net.remote(src, xrow(b, ch), dev, cond, rs=xr + b * chunks + ch)

    def send_swapped(k):
        dist = (z - zb) * (1 - 2 * c)
        for ch in range(chunks):
            xsend(xmine(ch), z, ch, (co.dp, zb), jnp.logical_and(co.swapped, dist == k + 1)).start()

    own_x = []
    for ch in range(chunks):
        for j in range(1, H):
            xsend(xmine(ch), z, ch, (co.dp, g * H + (co.zz + j) % H), co.native).start()
        xsend(xmine(ch), z, ch, mate, co.native).start()
        own_x.append(net.local(xmine(ch), xrow(z, ch), co.native).start(hold=False))
    send_swapped(0)

    bs, br = net.take(T), net.take(T)
    small_own = net.local(lambda: sm, lambda: smalls.at[z]).start(hold=False)
    small = [
        net.remote(lambda: sm, lambda: smalls.at[z], (co.dp, (z + k) % T)).start()
        for k in range(1, T)
    ]
    p = co.piece()

    def weight_chain(src, dst, slab, k):
        size = src.shape[0] // 8

        def view(ref, s, first, count):
            where = pl.ds(al(first * size, size), count * size)
            return ref.at[where] if s is None else ref.at[s, where]

        to = None if slab is None else z
        cps = [net.remote(lambda: view(src, None, p, 1), lambda: view(dst, to, p, 1), (co.dp, (z + k) % T))]
        at = [(p, 1)]
        for first, count, dev in ((p, 1, step1), (p // 2 * 2, 2, step2), (c * 4, 4, mate)):
            ref = lambda first=first, count=count: view(dst, slab, first, count)
            cps.append(net.remote(ref, ref, dev))
        return cps

    qchain = weight_chain(wq, wqo, None, H)
    wchains = []
    for src, dst in ((wp, wpf), (wi, wif), (wo, wof)):
        net.local(lambda src=src: src, lambda dst=dst: dst.at[z]).start()
        for k in range(1, T):
            wchains.append(weight_chain(src, dst, (z - k) % T, k))

    tlocal = net.local(lambda: te, lambda: teach, co.native)
    tswap = net.remote(lambda: te, lambda: teach, (co.mate, co.other), co.swapped)

    qchain[0].start()
    for s in range(3):
        qchain[s].got()
        qchain[s + 1].start()
    qchain[3].got()

    @pl.when(c == 0)
    def _():
        pltpu.sync_copy(wq, wqh)

    @pl.when(c != 0)
    def _():
        wqh[...] = wqo[...]

    small_own.wait_sent()
    for cp in small:
        cp.got()

    def project(b):
        CH = min(256, R)
        qb_, vb_ = smalls[co.hb, 0:1, :WP], smalls[co.hb, 1:2, :WP]

        def step(i, carry):
            first = b * R + i * CH
            rr = pl.ds(al(first, CH), CH)
            low = (xall[rr, :].astype(F32) + pos[rr, :].astype(F32)).astype(BF)
            emb[rr, :] = low
            pr = dot(low, wqh[...])
            q = (pr[:, :WP] + qb_).astype(BF).astype(F32) * (1.0 / math.sqrt(HD))
            k = pr[:, WP : 2 * WP].astype(BF).astype(F32)
            v = (pr[:, 2 * WP :] + vb_).astype(BF).astype(F32)
            lane = lanes((CH, WP))
            place = lax.broadcasted_iota(jnp.int32, (CH, WP), 0) + first
            limit = jnp.where(place < length, 0.0, NEG)
            for h in range(NH):
                a0 = aug_base(h)
                data = lane // HD == h
                ones = jnp.where((lane >= a0) & (lane < a0 + 4), 1.0, 0.0)
                qa[h, rr, :] = jnp.where(data, q, jnp.where(lane == a0, 1.0, 0.0)).astype(BF)
                ka[h, rr, :] = jnp.where(data, k, jnp.where(lane == a0, limit, ones)).astype(BF)
                va[h, rr, :] = jnp.where(data, v, ones).astype(BF)
                acc[h, rr, :] = jnp.zeros((CH, WP), F32)
                top[h, rr, :] = jnp.full((CH, WP), NEG, F32)
            return carry

        lax.fori_loop(0, R // CH, step, 0)

    def ftile(i, j, masked):
        qr, kr = rows(i), rows(j)
        for h in range(NH):
            s = dot_nt(qa[h, qr, :], ka[h, kr, :])
            if masked:
                below = lax.broadcasted_iota(jnp.int32, (R, R), 0) >= lanes((R, R))
                s = jnp.where(below, s, NEG)
            old = top[h, qr, :1]
            new = jnp.maximum(old, jnp.max(s, axis=-1, keepdims=True))
            e = jnp.exp(s - new).astype(BF)
            acc[h, qr, :] = acc[h, qr, :] * jnp.exp(old - new) + dot(e, va[h, kr, :])
            top[h, qr, :] = jnp.broadcast_to(new, (R, WP))

    def finalize(b):
        rr = rows(b)
        lane = lanes((R, WP))
        o = jnp.zeros((R, WP), F32)
        for h in range(NH):
            a0 = aug_base(h)
            total = acc[h, rr, a0 : a0 + 1]
            o = jnp.where(lane // HD == h, acc[h, rr, :] / total, o)
            lse = top[h, rr, :1] + jnp.log(total)
            q = qa[h, rr, :].astype(F32)
            qa[h, rr, :] = place3(q, lane, a0 + 1, -lse).astype(BF)
        mixed[rr, :] = o.astype(BF)

    def arrive(r, cond, pass_on):
        b = blocks[r]
        for ch in range(chunks):
            pl.when(cond)(xsend(xrow(b, ch), b, ch, mate, None).got)
            if pass_on:
                for j in range(1, H):
                    xsend(xrow(b, ch), b, ch, (co.dp, g * H + (co.zz + j) % H), cond).start()
            xsend(xrow(b, ch), b, ch, mate, cond).start()

    def mate_arrive(r):
        @pl.when(co.swapped)
        def _():
            for ch in range(chunks):
                xsend(xrow(blocks[r], ch), blocks[r], ch, mate, None).got()

    mr = net.take(T)

    def send_mixed(r):
        b = blocks[r]
        oc, oz = owner(G, co, b)
        me = jnp.logical_and(oc == c, oz == z)
        src = lambda: mixed.at[rows(b)]
        dst = lambda: mixr.at[co.hb]
        net.remote(src, dst, (2 * co.col + oc, oz), jnp.logical_not(me), rs=mr + co.hb).start()
        net.local(src, dst, me).start()

    inner = jnp.logical_and(co.native, jnp.logical_not(edge))

    def fstage(r):
        project(blocks[r])
        last = r == T - 1
        for q in range(r):
            a, b = blocks[r], blocks[q]
            ftile(jnp.maximum(a, b), jnp.minimum(a, b), False)
            if last:
                finalize(b)
                send_mixed(q)
        ftile(blocks[r], blocks[r], True)
        if last:
            finalize(blocks[r])
            send_mixed(r)

    poscopy.wait_sent()
    net.items.remove(poscopy)
    for cp in own_x:
        cp.guard(cp.wait_sent)
    mate_arrive(0)
    fstage(0)
    for r in range(1, T):
        if r < H:
            arrive(r, co.native, False)
        else:
            arrive(r, inner, False)
        mate_arrive(r)
        if r < H:
            send_swapped(r)
        if r + 1 >= H and r + 1 < T:
            arrive(r + 1, edge, True)
        if r == T - 2:
            for ch in wchains:
                ch[0].start()
            tlocal.start()
            tswap.start()
        fstage(r)

    for hop in range(3):
        for ch in wchains:
            ch[hop].got()
            ch[hop + 1].start()
    for ch in wchains:
        ch[3].got()
    pl.when(co.swapped)(tswap.got)
    tlocal.guard(tlocal.wait_sent)
    net.items.remove(tlocal)
    for cp in net.items:
        if cp.dev is None:
            cp.guard(cp.wait_sent)
    net.items = [cp for cp in net.items if cp.dev is not None]
    for k in range(1, T):
        hb = (co.hb + k) % T
        net.remote(lambda: mixed.at[rows(0)], lambda hb=hb: mixr.at[hb], mate, rs=mr + hb).got()

    count = lengths[0]
    for i in range(1, G.slots):
        count = count + lengths[i]
    scale = (G.slots * L) / jnp.full((1, 1), count, jnp.int32).astype(F32)
    vsum[...] = jnp.zeros(vsum.shape, F32)
    ibsum[...] = jnp.zeros(ibsum.shape, F32)
    output_bias, g1, s1 = vecs[0:1], vecs[1:2], vecs[2:3]
    outer_bias, g2, s2 = vecs[3:4], vecs[4:5], vecs[5:6]
    CR = min(256, R)

    def ffn(off):
        rr = pl.ds(off, CR)
        base = co.ob * R + off
        grows = pl.ds(al(base, CR), CR)
        branch = lax.fori_loop(
            0, T, lambda t, a: a + dot(mixr[t, rr, :], wpf[t]), jnp.zeros((CR, D), F32)
        )
        e = xall[grows, :].astype(F32) + pos[grows, :].astype(F32)
        n1, inv1 = norm(e + branch + output_bias)
        first = n1 * g1 + s1
        low = first.astype(BF)
        flow[rr, :] = low

        def up(t, a):
            pre = dot(low, wif[t]) + smalls[t, 2:3, :F]
            h = jnp.maximum(pre, 0.0).astype(BF)
            hid[t, rr, :] = h
            return a + dot(h, wof[t])

        feed = lax.fori_loop(0, T, up, jnp.zeros((CR, D), F32))
        n2, inv2 = norm(first + feed + outer_bias)
        result = n2 * g2 + s2
        osrc[rr, :] = result.astype(BF)
        place = lax.broadcasted_iota(jnp.int32, (CR, 1), 0) + base
        valid = jnp.where(place < length, scale, 0.0)
        gr = valid * (result - teach[rr, :].astype(F32))
        gs = norm_back(gr * g2, n2, inv2)
        gf = gs.astype(BF)
        gfeed[rr, :] = gf

        def down(t, a):
            gh = dot_nt(gf, wof[t])
            gpt = jnp.where(hid[t, rr, :].astype(F32) > 0, gh, 0.0).astype(BF)
            gpre[t, rr, :] = gpt
            ibsum[t] += colsum(gpt.astype(F32))
            return a + dot_nt(gpt, wif[t])

        g_first = lax.fori_loop(0, T, down, gs)
        gv = norm_back(g_first * g1, n1, inv1)
        gmid[rr, :] = gv
        gb = gv.astype(BF)
        gbr[rr, :] = gb

        def mix(t, a):
            gm[t, rr, :] = dot_nt(gb, wpf[t]).astype(BF)
            return a

        lax.fori_loop(0, T, mix, 0)
        vsum[0:1] += colsum(gv)
        vsum[1:2] += colsum(g_first * n1)
        vsum[2:3] += colsum(g_first)
        vsum[3:4] += colsum(gs)
        vsum[4:5] += colsum(gr * n2)
        vsum[5:6] += colsum(gr)

    gmr = net.take(T * (R // CR))
    gm_in = []
    gm_own = []
    for i in range(R // CR):
        ffn(i * CR)
        if i == 0:
            net.drain()
        for k in range(T):
            m = (co.zz * 2 + c + k) % T
            c2, z2 = m % 2, g * H + m // 2
            hb2 = (z2 + c2 * H) % T
            src = lambda hb2=hb2, i=i: gm.at[hb2, pl.ds(i * CR, CR)]
            dst = lambda i=i: gmall.at[pl.ds(al(co.ob * R + i * CR, CR), CR)]
            if k == 0:
                gm_own.append(net.local(src, dst).start(hold=False))
                continue
            net.remote(src, dst, (2 * co.col + c2, z2), rs=gmr + k * (R // CR) + i).start()
            gm_in.append((k, i))

    olocal = net.local(lambda: osrc, lambda: out, co.native).start()
    oswap = net.remote(lambda: osrc, lambda: out, (co.mate, co.other), co.swapped).start()

    def grads(t, carry):
        dwo[t] = dot_tn(hid[t], gfeed[...]).astype(BF)
        dwi[t] = dot_tn(flow[...], gpre[t]).astype(BF)
        dwp[t] = dot_tn(mixr[t], gbr[...]).astype(BF)
        return carry

    lax.fori_loop(0, T, grads, 0)

    def now(src, dst, dev):
        return net.remote(src, dst, dev)

    def wgrad_chain(s0, r0, r1, r2, r3, rx, gx, start, add0, n):
        q1, q2 = r1.shape[1], r2.shape[1]
        send1 = now(lambda: s0.at[:, pl.ds(al((1 - co.bf) * q1, q1), q1)], lambda: r1, step1)
        send2 = now(lambda: r1.at[:, pl.ds(al((1 - co.bs) * q2, q2), q2)], lambda: r2, step2)
        if n == T:
            over = [
                now(lambda k=k: r2.at[(z + k) % T], lambda k=k: r3.at[k - 1], (co.dp, (z + k) % T))
                for k in range(1, T)
            ]
        else:
            over = [now(lambda: r2.at[1], lambda: r3.at[0], (co.dp, co.other))]
        extra = [
            now(lambda: r2, lambda b=b: rx.at[b - 2], (co.extra(G, b), z))
            for b in range(2, G.nbits)
        ]

        def place(width, first):
            return lambda: gx.at[pl.ds(al(first * q2, q2), width * q2)]

        own = c * 4 + co.bf * 2 + co.bs
        back = []
        for width, first, dev in ((1, own, step2), (2, own // 2 * 2, step1), (4, c * 4, mate)):
            back.append(now(place(width, first), place(width, first), dev))

        def fold(r, rn, bit, q):
            def add(t, carry):
                kept = r[t, pl.ds(al(bit * q, q), q), :]
                rn[t] = (kept.astype(F32) + rn[t].astype(F32)).astype(BF)
                return carry

            lax.fori_loop(0, n, add, 0)

        def a0():
            start.got()
            add0()
            send1.start()

        def a1():
            send1.got()
            fold(s0, r1, co.bf, q1)
            send2.start()

        def a2():
            send2.got()
            fold(r1, r2, co.bs, q2)
            for m, cp in enumerate(extra):
                cp.start(hold=False)
                cp.got()
                cp.wait_sent()

                def add(t, carry, m=m):
                    r2[t] = (r2[t].astype(F32) + rx[m, t].astype(F32)).astype(BF)
                    return carry

                lax.fori_loop(0, n, add, 0)
            for cp in over:
                cp.start()

        def a3():
            tot = (r2[z] if n == T else r2[0]).astype(F32)
            for k, cp in enumerate(over):
                cp.got()
                tot = tot + r3[k].astype(F32)
            place(1, own)()[...] = tot.astype(BF)
            back[0].start()

        def a4():
            back[0].got()
            back[1].start()

        def a5():
            back[1].got()
            back[2].start()

        def a6():
            back[2].got()

        return [a0, a1, a2, a3, a4, a5, a6, send1]

    def big_chain(X, s0, r0, r1, r2, r3, rx, gx):
        hr = X.shape[1] // 2
        start = now(lambda: X.at[:, pl.ds(al((1 - c) * hr, hr), hr)], lambda: r0, mate).start()

        def add0():
            def add(t, carry):
                kept = X[t, pl.ds(al(c * hr, hr), hr), :]
                s0[t] = (kept.astype(F32) + r0[t].astype(F32)).astype(BF)
                return carry

            lax.fori_loop(0, T, add, 0)

        return wgrad_chain(s0, r0, r1, r2, r3, rx, gx, start, add0, T)

    cho = big_chain(dwo, s0o, r0o, r1o, r2o, r3o, rxo, go)
    chi = big_chain(dwi, s0i, r0i, r1i, r2i, r3i, rxi, gi)
    chp = big_chain(dwp, s0p, r0p, r1p, r2p, r3p, rxp, gpp)

    vb[...] = jnp.zeros(vb.shape, F32)
    vb[0:6, :] = vsum[0:6, :]
    for t in range(T):
        vb[8 + t : 9 + t, :F] = ibsum[t]

    def sum_chain(v, r, devs):
        cps = [now(lambda: v, lambda i=i: r.at[i], dev) for i, dev in enumerate(devs)]

        def step(i):
            def act():
                cps[i].got()
                cps[i].wait_sent()
                v[...] += r[i]
                if i + 1 < len(cps):
                    cps[i + 1].start(hold=False)

            return act

        return cps[0], [step(i) for i in range(len(cps))]

    plane = [step1, step2] + [(co.extra(G, b), z) for b in range(2, G.nbits)]
    vstart, vchain = sum_chain(vb, vr, [mate] + plane)
    vstart.start(hold=False)
    nv = len(vchain)
    vover = [
        now(lambda: vb, lambda k=k: vr.at[nv + k - 1], (co.dp, (z + k) % T))
        for k in range(1, T)
    ]

    def vz():
        for cp in vover:
            cp.start(hold=False)

    def vdone():
        for cp in vover:
            cp.got()
            cp.wait_sent()
        for k in range(1, T):
            vb[...] += vr[nv + k - 1]
        vout[...] = vb[0:8, :]
        vrow = lax.broadcasted_iota(jnp.int32, vb.shape, 0)
        ibout[...] = colsum(jnp.where(vrow == 8 + z, vb[...], 0.0))

    vchain = vchain + [vz, vdone]

    for k, i in gm_in:
        net.remote(
            lambda: gm.at[0, pl.ds(0, CR)], lambda: gmall.at[pl.ds(0, CR)], mate,
            rs=gmr + k * (R // CR) + i,
        ).got()
    for cp in gm_own:
        cp.wait_sent()

    def prepare(i, carry):
        CH = min(256, R)
        rr = pl.ds(al(i * CH, CH), CH)
        gg = gmall[rr, :].astype(F32)
        prod = gg * mixed[rr, :].astype(F32)
        lane = lanes((CH, WP))
        k = jnp.zeros((CH, WP), F32)
        for h in range(NH):
            a0 = aug_base(h)
            data = lane // HD == h
            delta = jnp.sum(jnp.where(data, prod, 0.0), axis=-1, keepdims=True)
            base = place3(jnp.zeros((CH, WP), F32), lane, a0 + 1, -delta)
            da[h, rr, :] = jnp.where(data, gg, base).astype(BF)
            k = jnp.where(data, ka[h, rr, :].astype(F32), k)
        kt[:, rr] = k.T.astype(BF)
        zero = jnp.zeros((CH, WP), F32)
        dk[rr, :] = zero
        dv[rr, :] = zero
        dq[:, rr] = zero.T
        return carry

    lax.fori_loop(0, L // min(256, R), prepare, 0)

    def btile(i, j, masked):
        qr, kr = rows(i), rows(j)
        lane = lanes((R, WP))
        sub = lax.broadcasted_iota(jnp.int32, (WP, R), 0)
        dks, dvs, dqs = [], [], []
        for h in range(NH):
            q, d = qa[h, qr, :], da[h, qr, :]
            pm = jnp.exp(dot_nt(ka[h, kr, :], q))
            if masked:
                above = lax.broadcasted_iota(jnp.int32, (R, R), 0) <= lanes((R, R))
                pm = jnp.where(above, pm, 0.0)
            ds = (pm * dot_nt(va[h, kr, :], d)).astype(BF)
            dvs.append(dot(pm.astype(BF), d))
            dks.append(dot(ds, q))
            dqs.append(dot(kt[:, kr], ds))
        if NH == 1:
            dk[kr, :] += dks[0]
            dv[kr, :] += dvs[0]
            dq[:, qr] += dqs[0]
        else:
            dk[kr, :] += jnp.where(lane < HD, dks[0], dks[1])
            dv[kr, :] += jnp.where(lane < HD, dvs[0], dvs[1])
            dq[:, qr] += jnp.where(sub < HD, dqs[0], dqs[1])

    dwq[...] = jnp.zeros(dwq.shape, F32)
    qsum = jnp.zeros((1, 3 * WP), F32)

    def complete(b):
        rr = rows(b)
        keep = lanes((R, WP)) < G.W
        q = dq[:, rr].T * (1.0 / math.sqrt(HD))
        sums = []
        for n_, part in enumerate((q, dk[rr, :], dv[rr, :])):
            part = jnp.where(keep, part, 0.0).astype(BF)
            gp[rr, n_ * WP : (n_ + 1) * WP] = part
            sums.append(colsum(part.astype(F32)))
        gg = gp[rr, :]
        ge[rr, :] = dot_nt(gg, wqh[...]).astype(BF)
        dwq[...] += dot_tn(emb[rr, :], gg)
        return jnp.concatenate(sums, axis=1)

    nlocal = net.local(lambda: nsrc, lambda: nat, co.native)
    nswap = net.remote(lambda: nsrc, lambda: nat, (co.mate, co.other), co.swapped)
    order_b = [(T - 1 - s_) + g * (2 * s_ - T + 1) for s_ in range(T)]
    er1s = net.take(T * max(H - 1, 1))
    echain = []
    for s_ in range(T):
        b = order_b[s_]
        oc, oz = owner(G, co, b)
        give = oc != c
        keep_c = oc == c
        here = jnp.logical_and(keep_c, oz == z)
        there = jnp.logical_and(keep_c, oz != z)
        up = net.remote(lambda b=b: ge.at[rows(b)], lambda s_=s_: er0.at[s_], mate, give)
        dist = (co.zz - (oz - g * H) + H - 1) % H
        over = net.remote(
            lambda s_=s_: esum.at[s_], lambda dist=dist: er1.at[dist], (co.dp, oz), there,
            rs=er1s + s_ * max(H - 1, 1) + dist,
        )

        def e0(up=up):
            up.start()

        def e1(up=up, over=over, b=b, keep_c=keep_c, here=here, there=there, s_=s_):
            pl.when(keep_c)(up.got)

            @pl.when(there)
            def _():
                esum[s_] = (ge[rows(b), :].astype(F32) + er0[s_].astype(F32)).astype(BF)

            @pl.when(here)
            def _():
                gtot[...] = gmid[...] + ge[rows(b), :].astype(F32) + er0[s_].astype(F32)

            over.start()

        def e2(here=here, s_=s_):
            @pl.when(here)
            def _():
                total = gtot[...]
                for j in range(H - 1):
                    net.remote(
                        lambda s_=s_: esum.at[s_], lambda j=j: er1.at[j], mate,
                        rs=er1s + s_ * max(H - 1, 1) + j, ss=er1s,
                    ).got()
                    total = total + er1[j].astype(F32)
                nsrc[...] = total.astype(BF)
                nlocal.guard(lambda: nlocal.make().start())
                nswap.guard(lambda: nswap.make().start())

        echain.append([e0, e1, e2])
    net.items.append(nswap)

    def run(chain, i):
        chain[i]()

    todo = {
        0: [(cho, 0), (chi, 0), (chp, 0), (vchain, 0)],
        1: [(vchain, 1)],
        2: [(vchain, 2)],
        3: [],
        4: [(cho, 1), (vchain, 3)],
        5: [],
        6: [(chi, 1), (chp, 1)],
        7: [(cho, 2)],
        8: [],
        9: [(chi, 2), (chp, 2)],
    }
    point = 0
    npoints = T * (T + 1) // 2
    done = []

    def actions(i):
        scaled = i if npoints == 10 else None
        if scaled is not None:
            for chain, k in todo[i]:
                run(chain, k)
                done.append((id(chain), k))

    for s_ in range(T):
        b = order_b[s_]
        btile(b, b, True)
        actions(point)
        point += 1
        for u in range(1, T - s_):
            far = b - u + g * (2 * u)
            btile(jnp.maximum(b, far), jnp.minimum(b, far), False)
            actions(point)
            point += 1
        qsum = qsum + complete(b)
        run(echain[s_], 0)
        if s_ >= 1:
            run(echain[s_ - 1], 1)
        if s_ >= 2:
            run(echain[s_ - 2], 2)

    dwqb[...] = dwq[...].astype(BF)
    hq = D // 2
    qstart = now(lambda: dwqb.at[pl.ds(al((1 - c) * hq, hq), hq)], lambda: r0q.at[c], mate).start()

    def qadd0():
        s0q[c] = dwqb[pl.ds(al(c * hq, hq), hq), :]
        s0q[1 - c] = r0q[1 - c]

    chq = wgrad_chain(s0q, r0q, r1q, r2q, r3q, rxq, gq, None, qadd0, 2)

    def q_first():
        pltpu.make_async_remote_copy(
            src_ref=dwqb.at[pl.ds(0, hq)], dst_ref=r0q.at[1 - c], send_sem=net.sem(qstart.ss),
            recv_sem=net.sem(qstart.rs), device_id=mate, device_id_type=MESH,
        ).wait_recv()

    qb[c] = jnp.broadcast_to(qsum, (8, 3 * WP))
    qmate = now(lambda: qb.at[c], lambda: qb.at[c], mate).start(hold=False)
    qsums, qchain2 = sum_chain(qb, qr, plane)
    qover = now(lambda: qb.at[1], lambda: qr.at[len(plane), 0], (co.dp, co.other))

    run(echain[T - 1], 1)
    run(echain[T - 2], 2)
    qmate.got()
    qmate.wait_sent()
    qsums.start(hold=False)
    q_first()
    qadd0()
    chq[7].start()
    run(echain[T - 1], 2)

    def left(chain, k):
        return (id(chain), k) not in done

    nlocal.guard(nlocal.wait_sent)
    pl.when(co.swapped)(nswap.got)
    igrad[...] = nat[...]
    half = R // 2
    q1, q2 = half // 2, half // 4
    p0[...] = nat[...].astype(F32)
    pw0 = now(lambda: p0.at[pl.ds(al((1 - c) * half, half), half)], lambda: pr0, mate).start()
    for i in range(len(vchain)):
        if left(vchain, i):
            run(vchain, i)
    qchain2[0]()
    run(chq, 1)
    pw0.got()
    pr0[...] += p0[pl.ds(al(c * half, half), half), :]
    pw1 = now(lambda: pr0.at[pl.ds(al((1 - co.bf) * q1, q1), q1)], lambda: pr1, step1).start()
    for chain in (cho, chi, chp):
        for i in range(4):
            if left(chain, i):
                run(chain, i)
    for i in range(1, len(qchain2)):
        qchain2[i]()
    qover.start(hold=False)
    run(chq, 2)
    pw1.got()
    pr1[...] += pr0[pl.ds(al(co.bf * q1, q1), q1), :]
    pw2 = now(lambda: pr1.at[pl.ds(al((1 - co.bs) * q2, q2), q2)], lambda: pr2, step2).start()
    for chain in (cho, chi, chp):
        run(chain, 4)
    run(chq, 3)
    pw2.got()
    pr2[...] += pr1[pl.ds(al(co.bs * q2, q2), q2), :]
    psrc, size = pr2, q2
    for n_, bit in enumerate(range(2, G.nbits)):
        bb = (co.col // (1 << bit)) % 2
        size = size // 2
        dst = p1 if n_ % 2 == 0 else p2
        cp = now(
            lambda psrc=psrc, bb=bb, size=size: psrc.at[pl.ds(al((1 - bb) * size, 8), size)],
            lambda dst=dst, size=size: dst.at[pl.ds(0, size)], (co.extra(G, bit), z),
        ).start()
        cp.got()
        dst[0:size, :] += psrc[pl.ds(al(bb * size, 8), size), :]
        psrc = dst
    pw3 = net.remote(lambda: psrc.at[pl.ds(0, size)], lambda: pr3, (pdp, pz), away).start()
    qover.got()
    qover.wait_sent()
    qb[0] += qr[len(plane), 0]
    qvg[0:1, :] = qb[0, 0:1, :WP]
    qvg[1:2, :] = qb[0, 0:1, 2 * WP :]
    for chain in (cho, chi, chp):
        run(chain, 5)
    run(chq, 4)
    for chain, gx, dst in ((cho, go, ug), (chi, gi, ig), (chp, gpp, og)):
        run(chain, 6)
        dst[...] = gx[...]
    run(chq, 5)
    run(chq, 6)
    qg[...] = gq[...]
    pl.when(away)(pw3.got)

    @pl.when(jnp.logical_not(away))
    def _():
        pr3[...] = psrc[0 : G.PR, :]

    pgrad[...] = pr3[...]
    pl.when(co.swapped)(oswap.got)
    net.drain()

def on_device(G, *args):
    (inputs, teacher, lengths, positions, qkv_weight, query_value_bias, output_weight, output_bias,
     first_gain, first_shift, inner_weight, inner_bias, outer_weight, outer_bias, second_gain,
     second_shift) = args
    T, R, D, L, W, WP, NH, F, H = G.T, G.R, G.D, G.L, G.W, G.WP, G.NH, G.F, G.H
    dma = lambda n: pltpu.SemaphoreType.DMA((n,))
    vm = pltpu.VMEM
    wq = jnp.pad(qkv_weight, ((0, 0), (0, 0), (0, WP - W))).reshape(D, 3 * WP)
    wp = jnp.pad(output_weight, ((0, WP - W), (0, 0)))
    lane_pad = lambda v: jnp.pad(v, ((0, 0), (0, D - v.shape[1])))
    small = jnp.concatenate(
        [lane_pad(query_value_bias), lane_pad(inner_bias[None]), jnp.zeros((5, D), BF)]
    ).astype(F32)
    vecs = jnp.stack(
        [output_bias, first_gain, first_shift, outer_bias, second_gain, second_shift]
    ).astype(F32)
    sizes = [(D, F, T), (F, D, T), (WP, D, T), (D, 3 * WP, 2)]
    nplane = G.nbits
    V = 8 + (T + 7) // 8 * 8
    scratch = [
        vm((L, D), BF), vm((L, D), BF), vm((L, D), BF),
        vm((NH, L, WP), BF), vm((NH, L, WP), BF), vm((NH, L, WP), BF), vm((NH, L, WP), BF),
        vm((WP, L), BF), vm((2, L, WP), F32), vm((NH, L, WP), F32), vm((L, WP), BF),
        vm((T, R, WP), BF),
        vm((D, 3 * WP), BF), vm((D, 3 * WP), BF), vm((T, D, F), BF), vm((T, F, D), BF),
        vm((T, WP, D), BF), vm((T, 8, D), F32), vm((R, D), BF),
        vm((R, D), BF), vm((T, R, F), BF), vm((T, R, F), BF), vm((R, D), BF), vm((R, D), BF),
        vm((R, D), F32), vm((R, D), BF), vm((T, R, WP), BF), vm((L, WP), BF), vm((8, D), F32),
        vm((T, 1, F), F32),
        vm((T, D, F), BF), vm((T, F, D), BF), vm((T, WP, D), BF), vm((WP, L), F32),
        vm((L, 3 * WP), BF),
        vm((D, 3 * WP), F32), vm((D, 3 * WP), BF),
    ]
    for shift in (1, 1, 2, 3):
        scratch += [vm((n, r >> shift, w), BF) for r, w, n in sizes]
    scratch += [vm((T - 1, r >> 3, w), BF) for r, w, n in sizes[:3]] + [vm((1, D >> 3, 3 * WP), BF)]
    more = G.nbits - 2
    scratch += [vm((more, n, r >> 3, w) if more else (1, 1, 16, 128), BF) for r, w, n in sizes]
    scratch += [vm((r, w), BF) for r, w, n in sizes]
    scratch += [
        vm((T, R, D), BF), vm((T, R, D), BF), vm((max(H - 1, 1), R, D), BF), vm((R, D), F32),
        vm((R, D), BF), vm((R, D), BF), vm((R, D), F32), vm((max(R // 8, 8), D), F32),
        vm((max(R // 8, 8), D), F32), vm((R // 2, D), F32), vm((R // 4, D), F32),
        vm((R // 8, D), F32), vm((G.PR, D), F32), vm((V, D), F32), vm((1 + nplane + T - 1, V, D), F32),
        vm((2, 8, 3 * WP), F32), vm((nplane + 1, 2, 8, 3 * WP), F32), dma(NSEM),
    ]
    outs = [
        ((R, D), BF), ((R, D), BF), ((G.PR, D), F32), ((D, 3 * WP), BF), ((2, WP), F32),
        ((WP, D), BF), ((D, F), BF), ((F, D), BF), ((8, D), F32), ((1, D), F32),
    ]
    anyspec = pl.BlockSpec(memory_space=pl.ANY)
    out, igrad, pgrad, qg, qvg, og, ig, ug, vout, ibout = pl.pallas_call(
        functools.partial(layer_kernel, G),
        out_shape=tuple(jax.ShapeDtypeStruct(s, d) for s, d in outs),
        in_specs=[SM] + [anyspec] * 8 + [VM],
        out_specs=tuple([VM] * len(outs)),
        scratch_shapes=scratch,
        compiler_params=pltpu.CompilerParams(
            vmem_limit_bytes=63 << 20, collective_id=0, has_side_effects=True
        ),
        name="layer",
    )(lengths, inputs, teacher, wq, inner_weight, outer_weight, wp, small, positions, vecs)
    qg = qg.reshape(D, 3, WP)[:, :, :W].astype(F32)
    og, ig, ug = og.astype(F32), ig.astype(F32), ug.astype(F32)
    return (
        out, igrad, pgrad, qg, qvg[:, :W], og[:W], vout[0], vout[1], vout[2],
        ig, ibout[0, :F], ug, vout[3], vout[4], vout[5],
    )


def solution(mesh):
    rows = P(("dp", "tensor"), None)
    specs = (
        rows, rows, P(), P(), P(None, None, "tensor"), P(None, "tensor"), P("tensor", None), P(),
        P(), P(), P(None, "tensor"), P("tensor"), P("tensor", None), P(), P(), P(),
    )
    outs = (
        rows, rows, rows, P(None, None, "tensor"), P(None, "tensor"), P("tensor", None), P(), P(),
        P(), P(None, "tensor"), P("tensor"), P("tensor", None), P(), P(), P(),
    )

    def step(*args):
        G = Geo(mesh, args[2].shape[0], args[3].shape[0], args[0].shape[1], args[11].shape[0])
        body = jax.shard_map(
            functools.partial(on_device, G), mesh=mesh, in_specs=specs, out_specs=outs,
            check_vma=False,
        )
        return body(*args)

    return step
```

```python
import functools
import math

import jax
import jax.numpy as jnp
from jax import lax
from jax.experimental import pallas as pl
from jax.experimental.pallas import tpu as pltpu
from jax.sharding import PartitionSpec as P

HD = 64
EPS = 1e-05
NSEM = 480
NEG = -1e30
BF = jnp.bfloat16
F32 = jnp.float32
MESH = pl.DeviceIdType.MESH
VM = pl.BlockSpec(memory_space=pltpu.VMEM)
SM = pl.BlockSpec(memory_space=pltpu.SMEM)


class Geo:
    def __init__(self, mesh, slots, seq, width, hidden):
        self.T = mesh.shape["tensor"]
        self.DP = mesh.shape["dp"]
        self.H = self.T // 2
        self.NC = self.DP // 2
        self.nbits = self.NC.bit_length() - 1
        self.slots = slots
        self.L = seq
        self.D = width
        self.FF = hidden
        self.R = seq // self.T
        self.W = width // self.T
        self.WP = max(self.W, 128)
        self.NH = self.W // HD
        self.F = hidden // self.T
        self.PR = seq // (self.DP * self.T)


class Co:
    def __init__(self, G):
        self.dp = lax.axis_index("dp")
        self.z = lax.axis_index("tensor")
        self.c = self.dp % 2
        self.col = self.dp // 2
        self.g = self.z // G.H
        self.zz = self.z - self.g * G.H
        self.other = (self.z + G.H) % G.T
        self.native = self.c == self.g
        self.swapped = self.c != self.g
        self.hb = (self.z + self.c * G.H) % G.T
        self.ob = self.own_block(G, self.z, self.c)
        self.slot = 2 * self.col + self.g
        self.mate = self.dp + 1 - 2 * self.c
        b0 = self.col % 2
        b1 = (self.col // 2) % 2
        self.bf = b0 + self.c * (b1 - b0)
        self.bs = b1 + self.c * (b0 - b1)
        wf = 1 + self.c
        ws = 2 - self.c
        self.dpf = self.dp + 2 * wf * (1 - 2 * self.bf)
        self.dps = self.dp + 2 * ws * (1 - 2 * self.bs)

    @staticmethod
    def own_block(G, z, c):
        d = c - z // G.H
        return (z + d * d * G.H) % G.T

    def extra(self, G, bit):
        b = (self.col // (1 << bit)) % 2
        return self.dp + (2 << bit) * (1 - 2 * b)

    def piece(self):
        return self.c * 4 + self.bs * 2 + self.bf


def owner(G, co, b):
    out = (b // G.H - co.g) * (b // G.H - co.g)
    return co.g + out * (1 - 2 * co.g), (b + out * G.H) % G.T


class Net:
    def __init__(self, ref):
        self.ref = ref
        self.n = 0
        self.items = []

    def take(self, n=1):
        base = self.n
        self.n += n
        return base

    def sem(self, i):
        return self.ref.at[i]

    def remote(self, src, dst, dev, cond=None, ss=None, rs=None):
        ss = self.take() if ss is None else ss
        rs = self.take() if rs is None else rs
        return Copy(self, src, dst, dev, ss, rs, cond)

    def local(self, src, dst, cond=None):
        return Copy(self, src, dst, None, self.take(), None, cond)

    def drain(self):
        for copy in self.items:
            copy.guard(copy.wait_sent)
        self.items = []


class Copy:
    def __init__(self, net, src, dst, dev, ss, rs, cond):
        self.net, self.src, self.dst, self.dev = net, src, dst, dev
        self.ss, self.rs, self.cond = ss, rs, cond

    def make(self):
        net = self.net
        if self.dev is None:
            return pltpu.make_async_copy(self.src(), self.dst(), net.sem(self.ss))
        return pltpu.make_async_remote_copy(
            src_ref=self.src(), dst_ref=self.dst(), send_sem=net.sem(self.ss),
            recv_sem=net.sem(self.rs), device_id=self.dev, device_id_type=MESH,
        )

    def guard(self, fn):
        if self.cond is None:
            fn()
        else:
            pl.when(self.cond)(fn)

    def start(self, hold=True):
        self.guard(lambda: self.make().start())
        if hold:
            self.net.items.append(self)
        return self

    def wait_sent(self):
        if self.dev is None:
            self.make().wait()
        else:
            self.make().wait_send()

    def got(self):
        self.make().wait_recv()


def column_partners(G, co):
    out = [(co.mate, co.z), (co.dpf, co.z), (co.dps, co.z), (co.mate, co.other)]
    out += [(co.dp, (co.z + k) % G.T) for k in range(1, G.T)]
    out += [(co.mate, (co.z + k) % G.T) for k in range(1, G.T) if k != G.H]
    out += [(co.extra(G, b), co.z) for b in range(2, G.nbits)]
    return out


def lanes(shape):
    return lax.broadcasted_iota(jnp.int32, shape, len(shape) - 1)


def aug_base(h):
    return HD if h == 0 else 0


def dot(a, b):
    return lax.dot_general(a, b, (((1,), (0,)), ((), ())), preferred_element_type=F32)


def dot_nt(a, b):
    return lax.dot_general(a, b, (((1,), (1,)), ((), ())), preferred_element_type=F32)


def dot_tn(a, b):
    return lax.dot_general(a, b, (((0,), (0,)), ((), ())), preferred_element_type=F32)


def parts3(v):
    hi = v.astype(BF).astype(F32)
    mid = (v - hi).astype(BF).astype(F32)
    return hi, mid, v - hi - mid


def place3(base, lane, first, v):
    hi, mid, lo = parts3(v)
    base = jnp.where(lane == first, hi, base)
    base = jnp.where(lane == first + 1, mid, base)
    return jnp.where(lane == first + 2, lo, base)


def norm(v):
    centre = jnp.mean(v, axis=-1, keepdims=True)
    v = v - centre
    inv = lax.rsqrt(jnp.mean(v * v, axis=-1, keepdims=True) + EPS)
    return v * inv, inv


def norm_back(e, normal, inv):
    a = jnp.mean(e, axis=-1, keepdims=True)
    b = jnp.mean(e * normal, axis=-1, keepdims=True)
    return inv * (e - a - normal * b)


def colsum(v):
    return jnp.sum(v, axis=0, keepdims=True)


def al(v, n):
    return pl.multiple_of(v, n)


def layer_kernel(
    G, lengths, x, te, wq, wi, wo, wp, pos_in, qvbias, ibias, *rest,
):
    vectors = [v[...].astype(F32).reshape(1, G.D) for v in rest[:6]]
    layer_body(G, vectors, lengths, x, te, wq, wi, wo, wp, pos_in, qvbias, ibias, *rest[6:])


def layer_body(
    G, vectors, lengths, x, te, wq, wi, wo, wp, pos_in, qvbias, ibias,
    out, igrad, pgrad, qg, og, ig, ug, vout,
    xall, pos, emb, qa, ka, va, da, kt, acc, top, mixed, mixr,
    sm, wqm, wqo, wqh, wif, wof, wpf, smalls, teach,
    flow, hid, gpre, gfeed, gbr, gmid, osrc, gm, gmall, vsum, ibsum,
    dwi, dwo, dwp, dq, gp, dwq, dwqb, qsum,
    s0i, s0o, s0p, s0q, r0i, r0o, r0p, r0q, r1i, r1o, r1p, r1q, r2i, r2o, r2p, r2q,
    r3i, r3o, r3p, r3q, rxi, rxo, rxp, rxq, gi, go, gpp, gq,
    ec, hsum, hp, eo, eh, hsend, nat, ps1, ps2, px, py, pf, pr3, vb, vr, qb, qr,
    sem,
):
    co = Co(G)
    net = Net(sem)
    T, H, R, L, WP, NH, D, F = G.T, G.H, G.R, G.L, G.WP, G.NH, G.D, G.F
    z, c, g = co.z, co.c, co.g
    mate, step1, step2 = (co.mate, z), (co.dpf, z), (co.dps, z)
    length = lengths[co.slot]
    ge, dk, dv = xall, acc.at[0], acc.at[1]

    def rows(b, n=R):
        return pl.ds(al(b * R, R), n)

    pp = c * (G.DP // 2) + co.bf * (G.DP // 4) + co.bs * (G.DP // 8)
    for bit in range(2, G.nbits):
        pp = pp + ((co.col // (1 << bit)) % 2) * (G.DP // (4 << bit))
    dests = []
    for b in range(T):
        flat = b * G.DP + pp
        dests.append((flat // T, flat % T))
    mine = co.dp * T + z
    fp = mine % G.DP
    fc = fp // (G.DP // 2)
    f1 = (fp // (G.DP // 4)) % 2
    f2 = (fp // (G.DP // 8)) % 2
    fcol = (f1 + fc * (f2 - f1)) + 2 * (f2 + fc * (f1 - f2))
    for bit in range(2, G.nbits):
        fcol = fcol + ((fp // (G.DP // (4 << bit))) % 2) * (1 << bit)
    own_piece = 2 * fcol + fc == co.dp
    poscopy = net.local(lambda: pos_in, lambda: pos).start()
    bar = pltpu.get_barrier_semaphore()
    partners = column_partners(G, co)
    for dev in partners:
        pl.semaphore_signal(bar, inc=1, device_id=dev, device_id_type=MESH)

    for k in range(1, T):
        dev = (2 * fcol + fc, (z + k) % T)
        pl.semaphore_signal(bar, inc=1, device_id=dev, device_id_type=MESH)

    @pl.when(jnp.logical_not(own_piece))
    def _():
        pl.semaphore_signal(bar, inc=1, device_id=(2 * fcol + fc, z), device_id_type=MESH)

    pl.semaphore_wait(bar, len(partners) + T - own_piece.astype(jnp.int32))

    bs, br = net.take(T), net.take(T)
    sm[...] = jnp.zeros(sm.shape, F32)
    sm[0:2, : G.W] = qvbias[...].astype(F32)
    sm[2:3, :F] = ibias[...].astype(F32).reshape(1, F)
    small_own = net.local(lambda: sm, lambda: smalls.at[z]).start(hold=False)
    small = [
        net.remote(lambda: sm, lambda: smalls.at[z], (co.dp, (z + k) % T)).start()
        for k in range(1, T)
    ]
    p = co.piece()

    def weight_chain(src, dst, slab, k):
        size = src.shape[-2] // 8

        def view(ref, s, first, count):
            where = pl.ds(al(first * size, size), count * size)
            if s is None:
                return ref.at[:, where] if slab is None else ref.at[where]
            return ref.at[s, where]

        to = None if slab is None else z
        cps = [net.remote(lambda: view(src, None, p, 1), lambda: view(dst, to, p, 1), (co.dp, (z + k) % T))]
        for first, count, dev in ((p, 1, step1), (p // 2 * 2, 2, step2), (c * 4, 4, mate)):
            ref = lambda first=first, count=count: view(dst, slab, first, count)
            cps.append(net.remote(ref, ref, dev))
        return cps

    qchain = weight_chain(wq, wqo, None, H)
    qchain[0].start()
    q_own = net.local(lambda: wq, lambda: wqm).start(hold=False)
    wchains = []
    for src, dst in ((wp, wpf), (wi, wif), (wo, wof)):
        net.local(lambda src=src: src, lambda dst=dst: dst.at[z]).start()
        for k in range(1, T):
            wchains.append(weight_chain(src, dst, (z - k) % T, k))

    chunks = 2
    n = R // chunks
    xr = net.take(T * chunks)

    def order(r):
        if r == 0:
            return z
        if r < H:
            return g * H + (co.zz + r) % H
        k = r - H
        return (H - 1 - k) + (1 - g) * (2 * k + 1)

    blocks = [order(r) for r in range(T)]

    def block_at(r):
        out = blocks[0]
        for k in range(1, T):
            out = jnp.where(r == k, blocks[k], out)
        return out
    zb = H - 1 + c
    edge = jnp.logical_and(co.native, z == H - 1 + g)

    def xrow(b, ch):
        return lambda: xall.at[pl.ds(al(b * R + ch * n, n), n)]

    def xmine(ch):
        return lambda: x.at[pl.ds(ch * n, n)]

    def xsend(src, b, ch, dev, cond, ss=None):
        return net.remote(src, xrow(b, ch), dev, cond, rs=xr + b * chunks + ch, ss=ss)

    def swapped_sends(k):
        cond = jnp.logical_and(co.swapped, (z - zb) * (1 - 2 * c) == k + 1)
        return [xsend(xmine(ch), z, ch, (co.dp, zb), cond) for ch in range(chunks)]

    own_x = []
    for ch in range(chunks):
        for j in range(1, H):
            xsend(xmine(ch), z, ch, (co.dp, g * H + (co.zz + j) % H), co.native).start()
        xsend(xmine(ch), z, ch, mate, co.native).start()
        own_x.append(net.local(xmine(ch), xrow(z, ch), co.native).start(hold=False))
    for cp in swapped_sends(0):
        cp.start()

    tlocal = net.local(lambda: te, lambda: teach, co.native)
    tswap = net.remote(lambda: te, lambda: teach, (co.mate, co.other), co.swapped)

    for s in range(3):
        qchain[s].got()
        qchain[s + 1].start()
    qchain[3].got()

    q_own.wait_sent()
    for j in range(3):
        wqh[:, j * WP : (j + 1) * WP] = jnp.where(c == 0, wqm[j], wqo[j])
    small_own.wait_sent()
    for cp in small:
        cp.got()

    def project(b):
        CH = min(256, R)
        qb_, vb_ = smalls[co.hb, 0:1, :WP], smalls[co.hb, 1:2, :WP]

        def step(i, carry):
            first = b * R + i * CH
            rr = pl.ds(al(first, CH), CH)
            low = (xall[rr, :].astype(F32) + pos[rr, :].astype(F32)).astype(BF)
            emb[rr, :] = low
            pr = dot(low, wqh[...])
            q = (pr[:, :WP] + qb_).astype(BF).astype(F32) * (1.0 / math.sqrt(HD))
            k = pr[:, WP : 2 * WP].astype(BF).astype(F32)
            v = (pr[:, 2 * WP :] + vb_).astype(BF).astype(F32)
            lane = lanes((CH, WP))
            place = lax.broadcasted_iota(jnp.int32, (CH, WP), 0) + first
            limit = jnp.where(place < length, 0.0, NEG)
            for h in range(NH):
                a0 = aug_base(h)
                data = lane // HD == h
                ones = jnp.where((lane >= a0) & (lane < a0 + 4), 1.0, 0.0)
                qa[h, rr, :] = jnp.where(data, q, jnp.where(lane == a0, 1.0, 0.0)).astype(BF)
                ka[h, rr, :] = jnp.where(data, k, jnp.where(lane == a0, limit, ones)).astype(BF)
                va[h, rr, :] = jnp.where(data, v, ones).astype(BF)
                acc[h, rr, :] = jnp.zeros((CH, WP), F32)
                top[h, rr, :] = jnp.full((CH, WP), NEG, F32)
            return carry

        lax.fori_loop(0, R // CH, step, 0)

    def ftile(i, j, masked):
        qr, kr = rows(i), rows(j)
        for h in range(NH):
            s = dot_nt(qa[h, qr, :], ka[h, kr, :])
            if masked:
                below = lax.broadcasted_iota(jnp.int32, (R, R), 0) >= lanes((R, R))
                s = jnp.where(below, s, NEG)
            old = top[h, qr, :1]
            new = jnp.maximum(old, jnp.max(s, axis=-1, keepdims=True))
            e = jnp.exp(s - new).astype(BF)
            acc[h, qr, :] = acc[h, qr, :] * jnp.exp(old - new) + dot(e, va[h, kr, :])
            top[h, qr, :] = jnp.broadcast_to(new, (R, WP))

    def finalize(b):
        rr = rows(b)
        lane = lanes((R, WP))
        o = jnp.zeros((R, WP), F32)
        for h in range(NH):
            a0 = aug_base(h)
            total = acc[h, rr, a0 : a0 + 1]
            o = jnp.where(lane // HD == h, acc[h, rr, :] / total, o)
            lse = top[h, rr, :1] + jnp.log(total)
            q = qa[h, rr, :].astype(F32)
            qa[h, rr, :] = place3(q, lane, a0 + 1, -lse).astype(BF)
        mixed[rr, :] = o.astype(BF)

    def arrival(r, cond, pass_on):
        b = blocks[r]
        steps = []
        for ch in range(chunks):
            sends = []
            if pass_on:
                for j in range(1, H):
                    sends.append(xsend(xrow(b, ch), b, ch, (co.dp, g * H + (co.zz + j) % H), cond))
            sends.append(xsend(xrow(b, ch), b, ch, mate, cond))
            steps.append((xsend(xrow(b, ch), b, ch, mate, None, xr), sends))

        def act():
            for got, sends in steps:
                pl.when(cond)(got.got)
                for cp in sends:
                    cp.start()

        return act

    inner = jnp.logical_and(co.native, jnp.logical_not(edge))
    arrivals = {r: arrival(r, co.native if r < H else inner, False) for r in range(1, T)}
    early = {r: arrival(r, edge, True) for r in range(H, T)}
    from_mate = [
        [xsend(xrow(blocks[r], ch), blocks[r], ch, mate, None, xr) for ch in range(chunks)]
        for r in range(T)
    ]
    far = {k: swapped_sends(k) for k in range(1, H)}

    def mate_arrive(r):
        @pl.when(co.swapped)
        def _():
            for cp in from_mate[r]:
                cp.got()

    mr = net.take(T)
    mixed_out = []
    for r in range(T):
        oc, oz = owner(G, co, blocks[r])
        me = jnp.logical_and(oc == c, oz == z)
        src = lambda r=r: mixed.at[rows(blocks[r])]
        dst = lambda: mixr.at[co.hb]
        dev = (2 * co.col + oc, oz)
        mixed_out.append(net.remote(src, dst, dev, jnp.logical_not(me), rs=mr + co.hb))
        mixed_out.append(net.local(src, dst, me))

    poscopy.wait_sent()
    net.items.remove(poscopy)
    for cp in own_x:
        cp.guard(cp.wait_sent)

    def begin(r):
        if r == 0:
            mate_arrive(0)
            return
        arrivals[r]()
        mate_arrive(r)
        for cp in far.get(r, ()):
            cp.start()
        if r + 1 in early:
            early[r + 1]()
        if r == T - 2:
            for ch in wchains:
                ch[0].start()
        if r == T - 1:
            tlocal.start()
            tswap.start()

    def triangle(t):
        r = 0
        for k in range(1, T):
            r = r + (t >= k * (k + 1) // 2).astype(jnp.int32)
        return r, t - r * (r + 1) // 2

    ntiles = T * (T + 1) // 2

    def ftiles(t, carry):
        r, q = triangle(t)

        @pl.when(q == 0)
        def _():
            for k in range(T):
                pl.when(r == k)(functools.partial(begin, k))
            project(block_at(r))

        a, b = block_at(r), block_at(q)

        @pl.when(q < r)
        def _():
            ftile(jnp.maximum(a, b), jnp.minimum(a, b), False)

        @pl.when(q == r)
        def _():
            ftile(a, a, True)

        @pl.when(r == T - 1)
        def _():
            finalize(b)
            for k in range(T):

                @pl.when(q == k)
                def _():
                    mixed_out[2 * k].start()
                    mixed_out[2 * k + 1].start()

        for i, acts in polls.items():

            @pl.when(t == i)
            def _(acts=acts):
                for hop, n_ in acts:
                    hop_on(hop, n_)

        return carry

    def hop_on(hop, n_):
        wchains[n_][hop].got()
        wchains[n_][hop + 1].start()

    polls = {}
    hops = [(h_, n_) for h_ in range(3) for n_ in range(len(wchains))]
    if ntiles == 10:
        for i in range(4):
            polls[6 + i] = [
                (h_, n_) for h_ in range(3) for n_ in range(9) if n_ // 3 + h_ == i
            ]
    polled = [a for acts in polls.values() for a in acts]

    lax.fori_loop(0, ntiles, ftiles, 0)

    for a in sorted(hops, key=lambda a: a[0] + a[1] // 3):
        if a not in polled:
            hop_on(*a)
    for ch in wchains:
        ch[3].got()
    pl.when(co.swapped)(tswap.got)
    tlocal.guard(tlocal.wait_sent)
    net.items.remove(tlocal)
    for cp in net.items:
        if cp.dev is None:
            cp.guard(cp.wait_sent)
    net.items = [cp for cp in net.items if cp.dev is not None]
    for k in range(1, T):
        hb = (co.hb + k) % T
        net.remote(lambda: mixed.at[rows(0)], lambda hb=hb: mixr.at[hb], mate, rs=mr + hb, ss=mr).got()

    count = lengths[0]
    for i in range(1, G.slots):
        count = count + lengths[i]
    scale = (G.slots * L) / jnp.full((1, 1), count, jnp.int32).astype(F32)
    vsum[...] = jnp.zeros(vsum.shape, F32)
    ibsum[...] = jnp.zeros(ibsum.shape, F32)
    output_bias, g1, s1, outer_bias, g2, s2 = vectors
    CR = min(256, R)

    def ffn(off):
        rr = pl.ds(off, CR)
        base = co.ob * R + off
        grows = pl.ds(al(base, CR), CR)
        branch = lax.fori_loop(
            0, T, lambda t, a: a + dot(mixr[t, rr, :], wpf[t]), jnp.zeros((CR, D), F32)
        )
        e = xall[grows, :].astype(F32) + pos[grows, :].astype(F32)
        n1, inv1 = norm(e + branch + output_bias)
        first = n1 * g1 + s1
        low = first.astype(BF)
        flow[rr, :] = low

        def up(t, a):
            pre = dot(low, wif[t]) + smalls[t, 2:3, :F]
            h = jnp.maximum(pre, 0.0).astype(BF)
            hid[t, rr, :] = h
            return a + dot(h, wof[t])

        feed = lax.fori_loop(0, T, up, jnp.zeros((CR, D), F32))
        n2, inv2 = norm(first + feed + outer_bias)
        result = n2 * g2 + s2
        osrc[rr, :] = result.astype(BF)
        place = lax.broadcasted_iota(jnp.int32, (CR, 1), 0) + base
        valid = jnp.where(place < length, scale, 0.0)
        gr = valid * (result - teach[rr, :].astype(F32))
        gs = norm_back(gr * g2, n2, inv2)
        gf = gs.astype(BF)
        gfeed[rr, :] = gf

        def down(t, a):
            gh = dot_nt(gf, wof[t])
            gpt = jnp.where(hid[t, rr, :].astype(F32) > 0, gh, 0.0).astype(BF)
            gpre[t, rr, :] = gpt
            ibsum[t] += colsum(gpt.astype(F32))
            return a + dot_nt(gpt, wif[t])

        g_first = lax.fori_loop(0, T, down, gs)
        gv = norm_back(g_first * g1, n1, inv1)
        gmid[rr, :] = gv
        gb = gv.astype(BF)
        gbr[rr, :] = gb

        def mix(t, a):
            gm[t, rr, :] = dot_nt(gb, wpf[t]).astype(BF)
            return a

        lax.fori_loop(0, T, mix, 0)
        vsum[0:1] += colsum(gv)
        vsum[1:2] += colsum(g_first * n1)
        vsum[2:3] += colsum(g_first)
        vsum[3:4] += colsum(gs)
        vsum[4:5] += colsum(gr * n2)
        vsum[5:6] += colsum(gr)

    gmr = net.take(T * (R // CR))
    gm_in = []
    gm_own = []
    for i in range(R // CR):
        ffn(i * CR)
        if i == 0:
            net.drain()
        for k in range(T):
            m = (co.zz * 2 + c + k) % T
            c2, z2 = m % 2, g * H + m // 2
            hb2 = (z2 + c2 * H) % T
            src = lambda hb2=hb2, i=i: gm.at[hb2, pl.ds(i * CR, CR)]
            dst = lambda i=i: gmall.at[pl.ds(al(co.ob * R + i * CR, CR), CR)]
            if k == 0:
                gm_own.append(net.local(src, dst).start(hold=False))
                continue
            net.remote(src, dst, (2 * co.col + c2, z2), rs=gmr + k * (R // CR) + i).start()
            gm_in.append((k, i))

    olocal = net.local(lambda: osrc, lambda: out, co.native).start()
    oswap = net.remote(lambda: osrc, lambda: out, (co.mate, co.other), co.swapped).start()

    def now(src, dst, dev, ss=None):
        return net.remote(src, dst, dev, ss=ss)

    class Slabs:
        def __init__(self, X, k0, n, s0, r0, r1, r2, r3, rx, r3slot, stay):
            hr, q1, q2 = r0.shape[1], r1.shape[1], r2.shape[1]
            self.n, self.k0 = n, k0
            slabs = pl.ds(k0, n)
            self.start = now(
                lambda: X.at[slabs, pl.ds(al((1 - c) * hr, hr), hr)], lambda: r0.at[slabs], mate
            )
            self.s1 = now(
                lambda: s0.at[slabs, pl.ds(al((1 - co.bf) * q1, q1), q1)],
                lambda: r1.at[slabs], step1,
            )
            self.s2 = now(
                lambda: r1.at[slabs, pl.ds(al((1 - co.bs) * q2, q2), q2)],
                lambda: r2.at[slabs], step2,
            )
            self.over = [
                now(lambda k=k: r2.at[k], lambda k=k: r3.at[r3slot(k)], (co.dp, (z + k_z) % T))
                for k, k_z in stay
                if k0 <= k < k0 + n
            ]
            self.extra = [
                now(lambda: r2.at[slabs], lambda b=b: rx.at[b - 2, slabs], (co.extra(G, b), z))
                for b in range(2, G.nbits)
            ]
            self.refs = X, s0, r0, r1, r2, rx, hr, q1, q2

        def a0(self):
            X, s0, r0, r1, r2, rx, hr, q1, q2 = self.refs
            self.start.got()
            for k in range(self.k0, self.k0 + self.n):
                kept = X[k, pl.ds(al(c * hr, hr), hr), :]
                s0[k] = (kept.astype(F32) + r0[k].astype(F32)).astype(BF)
            self.s1.start()

        def a1(self):
            X, s0, r0, r1, r2, rx, hr, q1, q2 = self.refs
            self.s1.got()
            for k in range(self.k0, self.k0 + self.n):
                kept = s0[k, pl.ds(al(co.bf * q1, q1), q1), :]
                r1[k] = (kept.astype(F32) + r1[k].astype(F32)).astype(BF)
            self.s2.start()

        def a2(self):
            X, s0, r0, r1, r2, rx, hr, q1, q2 = self.refs
            self.s2.got()
            for k in range(self.k0, self.k0 + self.n):
                kept = r1[k, pl.ds(al(co.bs * q2, q2), q2), :]
                r2[k] = (kept.astype(F32) + r2[k].astype(F32)).astype(BF)
            for m, cp in enumerate(self.extra):
                cp.start(hold=False)
                cp.got()
                cp.wait_sent()
                for k in range(self.k0, self.k0 + self.n):
                    r2[k] = (r2[k].astype(F32) + rx[m, k].astype(F32)).astype(BF)
            for cp in self.over:
                cp.start()

    class Back:
        def __init__(self, chains, r2, r3, gx, dst):
            q2 = r2.shape[1]
            self.chains, self.r2, self.r3 = chains, r2, r3

            def place(width, first):
                return lambda: gx.at[pl.ds(al(first * q2, q2), width * q2)]

            own = c * 4 + co.bf * 2 + co.bs
            self.own = place(1, own)
            self.back = []
            for width, first, dev in ((1, own, step2), (2, own // 2 * 2, step1), (4, c * 4, mate)):
                self.back.append(now(place(width, first), place(width, first), dev))
            self.end = net.local(lambda: gx, lambda: dst)

        def a3(self):
            tot = self.r2[0].astype(F32)
            for k, cp in enumerate(cp for ch in self.chains for cp in ch.over):
                cp.got()
                tot = tot + self.r3[k].astype(F32)
            self.own()[...] = tot.astype(BF)
            self.back[0].start()

        def a4(self):
            self.back[0].got()
            self.back[1].start()

        def a5(self):
            self.back[1].got()
            self.back[2].start()

        def a6(self):
            self.back[2].got()
            self.end.start()

    to_z = [(k, k) for k in range(1, T)]
    minus = lambda k: k - 1
    ks = list(range(1, T)) + [0]
    co_ = [Slabs(dwo, k, 1, s0o, r0o, r1o, r2o, r3o, rxo, minus, to_z) for k in ks]
    ci_ = [Slabs(dwi, k, 1, s0i, r0i, r1i, r2i, r3i, rxi, minus, to_z) for k in ks]
    cp_ = Slabs(dwp, 0, T, s0p, r0p, r1p, r2p, r3p, rxp, minus, to_z)
    slabs = [ch for pair in zip(co_[:-1], ci_[:-1]) for ch in pair] + [co_[-1], ci_[-1], cp_]
    back_o = Back(co_, r2o, r3o, go, ug)
    back_i = Back(ci_, r2i, r3i, gi, ig)
    back_p = Back([cp_], r2p, r3p, gpp, og)

    def grads(i, carry):
        k = jnp.where(i == T - 1, 0, i + 1)
        t = (z + k) % T
        dwo[k] = dot_tn(hid[t], gfeed[...]).astype(BF)
        dwi[k] = dot_tn(flow[...], gpre[t]).astype(BF)
        dwp[k] = dot_tn(mixr[t], gbr[...]).astype(BF)
        for n_ in range(T):

            @pl.when(i == n_)
            def _():
                co_[n_].start.start()
                ci_[n_].start.start()

        return carry

    lax.fori_loop(0, T, grads, 0)
    cp_.start.start()

    vb[...] = jnp.zeros(vb.shape, F32)
    vb[0:6, :] = vsum[0:6, :]
    for t in range(T):
        vb[8 + t : 9 + t, :F] = ibsum[t]

    def sum_chain(v, r, devs):
        cps = [now(lambda: v, lambda i=i: r.at[i], dev) for i, dev in enumerate(devs)]

        def step(i):
            def act():
                cps[i].got()
                cps[i].wait_sent()
                v[...] += r[i]
                if i + 1 < len(cps):
                    cps[i + 1].start(hold=False)

            return act

        return cps[0], [step(i) for i in range(len(cps))]

    plane = [step1, step2] + [(co.extra(G, b), z) for b in range(2, G.nbits)]
    vstart, vchain = sum_chain(vb, vr, [mate] + plane)
    vstart.start(hold=False)
    nv = len(vchain)
    vover = [
        now(lambda: vb, lambda k=k: vr.at[nv + k - 1], (co.dp, (z + k) % T))
        for k in range(1, T)
    ]

    def vz():
        for cp in vover:
            cp.start(hold=False)

    def vdone():
        for cp in vover:
            cp.got()
            cp.wait_sent()
        for k in range(1, T):
            vb[...] += vr[nv + k - 1]
        vout[0:8, :] = vb[0:8, :]
        vrow = lax.broadcasted_iota(jnp.int32, vb.shape, 0)
        vout[8:9, :] = colsum(jnp.where(vrow == 8 + z, vb[...], 0.0))

    vchain = vchain + [vz, vdone]

    for ch in slabs:
        ch.a0()
    for k, i in gm_in:
        net.remote(
            lambda: gm.at[0, pl.ds(0, CR)], lambda: gmall.at[pl.ds(0, CR)], mate,
            rs=gmr + k * (R // CR) + i, ss=gmr,
        ).got()
    for cp in gm_own:
        cp.wait_sent()


    def prepare(i, carry):
        CH = min(256, R)
        rr = pl.ds(al(i * CH, CH), CH)
        gg = gmall[rr, :].astype(F32)
        prod = gg * mixed[rr, :].astype(F32)
        lane = lanes((CH, WP))
        k = jnp.zeros((CH, WP), F32)
        for h in range(NH):
            a0 = aug_base(h)
            data = lane // HD == h
            delta = jnp.sum(jnp.where(data, prod, 0.0), axis=-1, keepdims=True)
            base = place3(jnp.zeros((CH, WP), F32), lane, a0 + 1, -delta)
            da[h, rr, :] = jnp.where(data, gg, base).astype(BF)
            k = jnp.where(data, ka[h, rr, :].astype(F32), k)
        kt[:, rr] = k.T.astype(BF)
        zero = jnp.zeros((CH, WP), F32)
        dk[rr, :] = zero
        dv[rr, :] = zero
        dq[:, rr] = zero.T
        return carry

    lax.fori_loop(0, L // min(256, R), prepare, 0)

    def btile(i, j, masked):
        qr, kr = rows(i), rows(j)
        lane = lanes((R, WP))
        sub = lax.broadcasted_iota(jnp.int32, (WP, R), 0)
        dks, dvs, dqs = [], [], []
        for h in range(NH):
            q, d = qa[h, qr, :], da[h, qr, :]
            pm = jnp.exp(dot_nt(ka[h, kr, :], q))
            if masked:
                above = lax.broadcasted_iota(jnp.int32, (R, R), 0) <= lanes((R, R))
                pm = jnp.where(above, pm, 0.0)
            ds = (pm * dot_nt(va[h, kr, :], d)).astype(BF)
            dvs.append(dot(pm.astype(BF), d))
            dks.append(dot(ds, q))
            dqs.append(dot(kt[:, kr], ds))
        if NH == 1:
            dk[kr, :] += dks[0]
            dv[kr, :] += dvs[0]
            dq[:, qr] += dqs[0]
        else:
            dk[kr, :] += jnp.where(lane < HD, dks[0], dks[1])
            dv[kr, :] += jnp.where(lane < HD, dvs[0], dvs[1])
            dq[:, qr] += jnp.where(sub < HD, dqs[0], dqs[1])

    dwq[...] = jnp.zeros(dwq.shape, F32)
    qsum[...] = jnp.zeros(qsum.shape, F32)

    def complete(b):
        rr = rows(b)
        keep = lanes((R, WP)) < G.W
        q = dq[:, rr].T * (1.0 / math.sqrt(HD))
        sums = []
        for n_, part in enumerate((q, dk[rr, :], dv[rr, :])):
            part = jnp.where(keep, part, 0.0).astype(BF)
            gp[rr, n_ * WP : (n_ + 1) * WP] = part
            sums.append(colsum(part.astype(F32)))
        gg = gp[rr, :]
        back = dot_nt(gg, wqh[...])
        ge[rr, :] = back.astype(BF)
        oc, oz = owner(G, co, b)

        @pl.when(jnp.logical_and(oc == c, oz == z))
        def _():
            ge[rr, :] = (back + gmid[...]).astype(BF)

        dwq[...] += dot_tn(emb[rr, :], gg)
        qsum[0:1, :] += jnp.concatenate(sums, axis=1)

    order_b = [(T - 1 - s_) + g * (2 * s_ - T + 1) for s_ in range(T)]
    ends = [sum(T - i for i in range(s_ + 1)) - 1 for s_ in range(T)]
    half = R // 2
    edge_z = H - 1 + g
    eh_sem = net.take(2 * H)
    nat_sem = net.take(2)
    pf_sem = net.take(T)
    at_edge = z == edge_z

    class Rows:
        def __init__(self, s_):
            b = order_b[s_]
            self.s, self.b, self.inside = s_, b, s_ >= H
            self.core = net.remote(
                lambda: ge.at[pl.ds(al(b * R + (1 - c) * half, half), half)],
                lambda: ec.at[s_], mate,
            )
            h = lambda: hsum.at[s_]
            if self.inside:
                home = jnp.logical_and(c == g, z == b)
                self.over = [
                    net.remote(
                        h, lambda: eh.at[co.zz * 2 + c], (2 * co.col + g, b),
                        jnp.logical_not(home), rs=eh_sem + co.zz * 2 + c,
                    )
                ]
            else:
                slot = (co.zz - (edge_z - g * H) + H - 1) % H
                base = net.take(max(H - 1, 1))
                self.base = base
                self.over = [
                    net.remote(
                        h, lambda: eo.at[s_, slot], (co.dp, edge_z), jnp.logical_not(at_edge),
                        rs=base + slot,
                    )
                ]
                self.home = net.remote(
                    lambda: hsend.at[s_], lambda: nat.at[pl.ds(al(c * half, half), half)],
                    (2 * co.col + g, b), at_edge, rs=nat_sem + c,
                )
            q1, q2 = half // 2, half // 4
            self.p1 = net.remote(
                lambda: hp.at[s_, pl.ds(al((1 - co.bf) * q1, q1), q1)], lambda: ps1.at[s_], step1
            )
            self.p2 = net.remote(
                lambda: ps1.at[s_, pl.ds(al((1 - co.bs) * q2, q2), q2)], lambda: ps2.at[s_], step2
            )
            dp2, z2 = dests[0]
            for k in range(1, T):
                dp2 = jnp.where(b == k, dests[k][0], dp2)
                z2 = jnp.where(b == k, dests[k][1], z2)
            here = jnp.logical_and(dp2 == co.dp, z2 == z)
            self.more = []
            size = q2
            for n_, bit in enumerate(range(2, G.nbits)):
                size = size // 2
                bb = (co.col // (1 << bit)) % 2
                src = (ps2, px)[n_ % 2] if n_ else ps2
                dst = px if n_ % 2 == 0 else py
                src = ps2 if n_ == 0 else (px if n_ % 2 == 1 else py)
                cp = net.remote(
                    lambda src=src, bb=bb, size=size: src.at[s_, pl.ds(al((1 - bb) * size, 8), size)],
                    lambda dst=dst, size=size: dst.at[s_, pl.ds(0, size)],
                    (co.extra(G, bit), z),
                )
                self.more.append((cp, src, dst, bb, size))
            self.last = self.more[-1][2] if self.more else ps2
            piece = lambda: self.last.at[s_, pl.ds(0, G.PR)]
            self.fin = net.remote(
                piece, lambda: pf.at[z], (dp2, z2), jnp.logical_not(here), rs=pf_sem + z
            )
            self.fin_here = net.local(piece, lambda: pf.at[z], here)

        def k0(self):
            self.core.start()

        def k1(self):
            s_ = self.s
            self.core.got()
            own = ge[pl.ds(al(self.b * R + c * half, half), half), :].astype(F32)
            total = own + ec[s_].astype(F32)
            hsum[s_] = total.astype(BF)
            hp[s_] = total.astype(hp.dtype)
            for cp in self.over:
                cp.start()
            self.p1.start()

        def k2(self):
            s_, q1 = self.s, half // 2
            self.p1.got()
            kept = hp[s_, pl.ds(al(co.bf * q1, q1), q1), :].astype(F32)
            ps1[s_] = (kept + ps1[s_].astype(F32)).astype(ps1.dtype)
            self.p2.start()

        def k3(self):
            s_, q2 = self.s, half // 4
            self.p2.got()
            kept = ps1[s_, pl.ds(al(co.bs * q2, q2), q2), :].astype(F32)
            ps2[s_] = (kept + ps2[s_].astype(F32)).astype(ps2.dtype)
            for cp, src, dst, bb, size in self.more:
                cp.start()
                cp.got()
                kept = src[s_, pl.ds(al(bb * size, 8), size), :].astype(F32)
                dst[s_, 0:size, :] = (kept + dst[s_, 0:size, :].astype(F32)).astype(dst.dtype)
            self.fin.start()
            self.fin_here.start()

        def kx(self):
            s_ = self.s

            @pl.when(at_edge)
            def _():
                total = hsum[s_].astype(F32)
                for j in range(H - 1):
                    net.remote(
                        lambda: hsum.at[s_], lambda j=j: eo.at[s_, j], mate, rs=self.base + j,
                        ss=self.base,
                    ).got()
                    total = total + eo[s_, j].astype(F32)
                hsend[s_] = total.astype(BF)

            self.home.start()

    parts_ = [Rows(s_) for s_ in range(T)]

    def run(chain, i):
        chain[i]()

    jobs = {("v", i): act for i, act in enumerate(vchain)}
    for i, ch in enumerate(slabs):
        jobs["1", i] = ch.a1
        jobs["2", i] = ch.a2
    for name, bk in (("o", back_o), ("i", back_i), ("p", back_p)):
        for n_, act in enumerate((bk.a3, bk.a4, bk.a5, bk.a6)):
            jobs[name, n_] = act
    for rw in parts_:
        for name in ("k0", "k1", "k2", "k3", "kx"):
            if name != "kx" or not rw.inside:
                jobs[name, rw.s] = getattr(rw, name)
    plan = {
        0: [("1", 0), ("1", 1), ("v", 0)],
        1: [("1", 2), ("1", 3), ("v", 1)],
        2: [("2", 0), ("2", 1), ("1", 4), ("v", 2)],
        3: [("k0", 0), ("2", 2), ("2", 3), ("1", 5), ("1", 6), ("v", 3)],
        4: [("k1", 0), ("2", 4), ("1", 7), ("1", 8)],
        5: [("k2", 0), ("2", 5), ("2", 6), ("v", 4)],
        6: [("k0", 1), ("k3", 0), ("2", 7), ("2", 8)],
        7: [("k1", 1), ("kx", 0), ("o", 0)],
        8: [("k0", 2), ("k2", 1), ("i", 0), ("o", 1), ("p", 0)],
        9: [("k0", 3), ("k1", 2), ("k3", 1), ("kx", 1), ("i", 1), ("o", 2), ("p", 1)],
    }
    if ntiles != 10:
        plan = {e: [("k0", s_)] for s_, e in enumerate(ends)}
    left = [key for key in jobs if not any(key in acts for acts in plan.values())]
    def btiles(t, carry):
        s_, u = 0, t
        for k in range(1, T):
            past = (t > ends[k - 1]).astype(jnp.int32)
            s_ = s_ + past
            u = u - past * (T - k + 1)
        b = (T - 1 - s_) + g * (2 * s_ - T + 1)
        far = b - u + g * (2 * u)

        @pl.when(u == 0)
        def _():
            btile(b, b, True)

        @pl.when(u > 0)
        def _():
            btile(jnp.maximum(b, far), jnp.minimum(b, far), False)

        @pl.when(u == T - 1 - s_)
        def _():
            complete(b)

        for i in range(ntiles):
            acts = [jobs[key] for key in plan.get(i, ())]
            if acts:

                @pl.when(t == i)
                def _(acts=acts):
                    for act in acts:
                        act()

        return carry

    lax.fori_loop(0, ntiles, btiles, 0)

    dwqb[c] = dwq[...].astype(BF)
    chq = Slabs(dwqb, 0, 2, s0q, r0q, r1q, r2q, r3q, rxq, lambda k: 0, [(1, H)])
    hq = D // 2
    qstart = now(
        lambda: dwqb.at[c, pl.ds(al((1 - c) * hq, hq), hq)], lambda: r0q.at[c], mate
    ).start()
    back_q = Back([chq], r2q, r3q, gq, qg)

    qb[c] = qsum[...]
    qmate = now(lambda: qb.at[c], lambda: qb.at[c], mate).start(hold=False)
    qsums, qchain2 = sum_chain(qb, qr, plane)
    qover = now(lambda: qb.at[1], lambda: qr.at[len(plane), 0], (co.dp, co.other))

    def rest(*names):
        for key in left:
            if key[0] in names:
                jobs[key]()

    rest("k1")
    qmate.got()
    qmate.wait_sent()
    qsums.start(hold=False)
    pltpu.make_async_remote_copy(
        src_ref=dwqb.at[c, pl.ds(0, hq)], dst_ref=r0q.at[1 - c], send_sem=net.sem(qstart.ss),
        recv_sem=net.sem(qstart.rs), device_id=mate, device_id_type=MESH,
    ).wait_recv()
    s0q[c] = dwqb[c, pl.ds(al(c * hq, hq), hq), :]
    s0q[1 - c] = r0q[1 - c]
    chq.s1.start()
    rest("k2", "1", "2", "v")
    qchain2[0]()
    chq.a1()
    rest("k3")
    for n_ in range(2):
        for key in left:
            if key[0] in "oip" and key[1] == n_:
                jobs[key]()
    for i in range(1, len(qchain2)):
        qchain2[i]()
    qover.start(hold=False)
    chq.a2()
    rest("kx")
    for n_ in (2, 3):
        for key in left:
            if key[0] in "oip" and key[1] == n_:
                jobs[key]()
    back_q.a3()
    qover.got()
    qover.wait_sent()
    qb[0] += qr[len(plane), 0]
    vout[9:10, :WP] = qb[0, 0:1, :WP]
    vout[10:11, :WP] = qb[0, 0:1, 2 * WP :]
    back_q.a4()

    for i in range(2):

        @pl.when(co.swapped)
        def _():
            net.remote(
                lambda: hsend.at[0], lambda: nat.at[pl.ds(0, half)], mate, rs=nat_sem + i, ss=nat_sem
            ).got()

    @pl.when(co.native)
    def _():
        for i in range(2 * H):

            @pl.when(i != co.zz * 2 + c)
            def _():
                net.remote(
                    lambda: hsum.at[0], lambda: eh.at[i], mate, rs=eh_sem + i, ss=eh_sem
                ).got()

        mine_h = jnp.zeros((half, D), BF)
        for s_ in range(H, T):
            mine_h = jnp.where(order_b[s_] == z, hsum[s_], mine_h)
        for j in range(2):
            total = jnp.where(c == j, mine_h.astype(F32), 0.0)
            for k in range(H):
                one = eh[2 * k + j].astype(F32)
                total = total + jnp.where(k * 2 + j == co.zz * 2 + c, 0.0, one)
            nat[pl.ds(j * half, half), :] = total.astype(BF)

    net.local(lambda: nat, lambda: igrad).start()
    back_q.a5()
    for k in range(T):

        @pl.when(jnp.logical_not(jnp.logical_and(own_piece, z == k)))
        def _():
            net.remote(lambda: pf.at[k], lambda: pf.at[k], mate, rs=pf_sem + k, ss=pf_sem).got()

    for rw in parts_:
        rw.fin_here.guard(rw.fin_here.wait_sent)
    net.items = [cp for cp in net.items if all(cp is not rw.fin_here for rw in parts_)]
    total = pf[0].astype(F32)
    for k in range(1, T):
        total = total + pf[k].astype(F32)
    pr3[...] = total
    net.local(lambda: pr3, lambda: pgrad).start()
    back_q.a6()
    pl.when(co.swapped)(oswap.got)
    net.drain()

def emit_kernel(
    G, out_in, igrad_in, pgrad_in, qg_in, og_in, ig_in, ug_in, vin,
    out, igrad, pgrad, qg, qvg, og, ig, ug, ibg, v0, v1, v2, v3, v4, v5,
):
    out[...] = out_in[...]
    igrad[...] = igrad_in[...]
    pgrad[...] = pgrad_in[...]
    for j in range(3):
        qg[j] = qg_in[:, j * G.WP : j * G.WP + G.W].astype(F32)
    qvg[...] = vin[9:11, : G.W]
    og[...] = og_in[: G.W, :].astype(F32)
    ig[...] = ig_in[...].astype(F32)
    ug[...] = ug_in[...].astype(F32)
    ibg[...] = vin[8:9, : G.F].reshape(G.F)
    for i, v in enumerate((v0, v1, v2, v3, v4, v5)):
        v[...] = vin[i : i + 1, :].reshape(G.D)


def on_device(G, *args):
    (inputs, teacher, lengths, positions, qkv_weight, query_value_bias, output_weight, output_bias,
     first_gain, first_shift, inner_weight, inner_bias, outer_weight, outer_bias, second_gain,
     second_shift) = args
    T, R, D, L, W, WP, NH, F, H = G.T, G.R, G.D, G.L, G.W, G.WP, G.NH, G.F, G.H
    dma = lambda n: pltpu.SemaphoreType.DMA((n,))
    vm = pltpu.VMEM
    wq = jnp.pad(jnp.transpose(qkv_weight, (1, 0, 2)), ((0, 0), (0, 0), (0, WP - W)))
    wp = jnp.pad(output_weight, ((0, WP - W), (0, 0)))
    sizes = [(D, F, T), (F, D, T), (WP, D, T), (D, 3 * WP, 2)]
    nplane = G.nbits
    V = 8 + (T + 7) // 8 * 8
    scratch = [
        vm((L, D), BF), vm((L, D), BF), vm((L, D), BF),
        vm((NH, L, WP), BF), vm((NH, L, WP), BF), vm((NH, L, WP), BF), vm((NH, L, WP), BF),
        vm((WP, L), BF), vm((2, L, WP), F32), vm((NH, L, WP), F32), vm((L, WP), BF),
        vm((T, R, WP), BF),
        vm((8, D), F32), vm((3, D, WP), BF), vm((3, D, WP), BF), vm((D, 3 * WP), BF),
        vm((T, D, F), BF), vm((T, F, D), BF),
        vm((T, WP, D), BF), vm((T, 8, D), F32), vm((R, D), BF),
        vm((R, D), BF), vm((T, R, F), BF), vm((T, R, F), BF), vm((R, D), BF), vm((R, D), BF),
        vm((R, D), F32), vm((R, D), BF), vm((T, R, WP), BF), vm((L, WP), BF), vm((8, D), F32),
        vm((T, 1, F), F32),
        vm((T, D, F), BF), vm((T, F, D), BF), vm((T, WP, D), BF), vm((WP, L), F32),
        vm((L, 3 * WP), BF),
        vm((D, 3 * WP), F32), vm((2, D, 3 * WP), BF), vm((8, 3 * WP), F32),
    ]
    for shift in (1, 1, 2, 3):
        scratch += [vm((n, r >> shift, w), BF) for r, w, n in sizes]
    scratch += [vm((T - 1, r >> 3, w), BF) for r, w, n in sizes[:3]] + [vm((1, D >> 3, 3 * WP), BF)]
    more = G.nbits - 2
    PD = BF if G.PR % 16 == 0 else F32
    scratch += [vm((more, n, r >> 3, w) if more else (1, 1, 16, 128), BF) for r, w, n in sizes]
    scratch += [vm((r, w), BF) for r, w, n in sizes]
    scratch += [
        vm((T, R // 2, D), BF), vm((T, R // 2, D), BF), vm((T, R // 2, D), PD),
        vm((H, max(H - 1, 1), R // 2, D), BF), vm((2 * H, R // 2, D), BF), vm((H, R // 2, D), BF),
        vm((R, D), BF), vm((T, R // 4, D), PD), vm((T, R // 8, D), PD),
        vm((T, max(R // 16, 8), D) if more else (1, 8, 128), PD),
        vm((T, max(R // 32, 8), D) if more else (1, 8, 128), PD), vm((T, G.PR, D), PD),
        vm((G.PR, D), F32), vm((V, D), F32), vm((1 + nplane + T - 1, V, D), F32),
        vm((2, 8, 3 * WP), F32), vm((nplane + 1, 2, 8, 3 * WP), F32), dma(NSEM),
    ]
    outs = [
        ((R, D), BF), ((R, D), BF), ((G.PR, D), F32), ((D, 3 * WP), BF),
        ((WP, D), BF), ((D, F), BF), ((F, D), BF), ((16, D), F32),
    ]
    anyspec = pl.BlockSpec(memory_space=pl.ANY)
    results = pl.pallas_call(
        functools.partial(layer_kernel, G),
        out_shape=tuple(jax.ShapeDtypeStruct(s, d) for s, d in outs),
        in_specs=[SM] + [anyspec] * 7 + [VM] * 8,
        out_specs=tuple([anyspec] * 7 + [VM]),
        scratch_shapes=scratch,
        compiler_params=pltpu.CompilerParams(
            vmem_limit_bytes=63 << 20, collective_id=0, has_side_effects=True
        ),
        name="layer",
    )(lengths, inputs, teacher, wq, inner_weight, outer_weight, wp, positions, query_value_bias,
      inner_bias, output_bias, first_gain, first_shift, outer_bias, second_gain, second_shift)
    finals = [
        ((R, D), BF), ((R, D), BF), ((G.PR, D), F32), ((3, D, W), F32), ((2, W), F32),
        ((W, D), F32), ((D, F), F32), ((F, D), F32), ((F,), F32),
    ] + [((D,), F32)] * 6
    (out, igrad, pgrad, qg, qvg, og, ig, ug, ibg, *vs) = pl.pallas_call(
        functools.partial(emit_kernel, G),
        out_shape=tuple(jax.ShapeDtypeStruct(s, d) for s, d in finals),
        in_specs=[VM] * 8,
        out_specs=tuple([VM] * 15),
        compiler_params=pltpu.CompilerParams(vmem_limit_bytes=63 << 20),
        name="emit",
    )(*results)
    return (
        out, igrad, pgrad, jnp.transpose(qg, (1, 0, 2)), qvg, og, vs[0], vs[1], vs[2],
        ig, ibg, ug, vs[3], vs[4], vs[5],
    )


def solution(mesh):
    rows = P(("dp", "tensor"), None)
    specs = (
        rows, rows, P(), P(), P(None, None, "tensor"), P(None, "tensor"), P("tensor", None), P(),
        P(), P(), P(None, "tensor"), P("tensor"), P("tensor", None), P(), P(), P(),
    )
    outs = (
        rows, rows, rows, P(None, None, "tensor"), P(None, "tensor"), P("tensor", None), P(), P(),
        P(), P(None, "tensor"), P("tensor"), P("tensor", None), P(), P(), P(),
    )

    def step(*args):
        G = Geo(mesh, args[2].shape[0], args[3].shape[0], args[0].shape[1], args[11].shape[0])
        body = jax.shard_map(
            functools.partial(on_device, G), mesh=mesh, in_specs=specs, out_specs=outs,
            check_vma=False,
        )
        return body(*args)

    return step
```

```python
import functools
import math

import jax
import jax.numpy as jnp
from jax import lax
from jax.experimental import pallas as pl
from jax.experimental.pallas import tpu as pltpu
from jax.sharding import PartitionSpec as P

HD = 64
EPS = 1e-05
NSEM = 480
NEG = -1e30
BF = jnp.bfloat16
F32 = jnp.float32
MESH = pl.DeviceIdType.MESH
VM = pl.BlockSpec(memory_space=pltpu.VMEM)
SM = pl.BlockSpec(memory_space=pltpu.SMEM)


class Geo:
    def __init__(self, mesh, slots, seq, width, hidden):
        self.T = mesh.shape["tensor"]
        self.DP = mesh.shape["dp"]
        self.H = self.T // 2
        self.NC = self.DP // 2
        self.nbits = self.NC.bit_length() - 1
        self.slots = slots
        self.L = seq
        self.D = width
        self.FF = hidden
        self.R = seq // self.T
        self.W = width // self.T
        self.WP = max(self.W, 128)
        self.NH = self.W // HD
        self.F = hidden // self.T
        self.PR = seq // (self.DP * self.T)


class Co:
    def __init__(self, G):
        self.dp = lax.axis_index("dp")
        self.z = lax.axis_index("tensor")
        self.c = self.dp % 2
        self.col = self.dp // 2
        self.g = self.z // G.H
        self.zz = self.z - self.g * G.H
        self.other = (self.z + G.H) % G.T
        self.native = self.c == self.g
        self.swapped = self.c != self.g
        self.hb = (self.z + self.c * G.H) % G.T
        self.ob = self.own_block(G, self.z, self.c)
        self.slot = 2 * self.col + self.g
        self.mate = self.dp + 1 - 2 * self.c
        b0 = self.col % 2
        b1 = (self.col // 2) % 2
        self.bf = b0 + self.c * (b1 - b0)
        self.bs = b1 + self.c * (b0 - b1)
        wf = 1 + self.c
        ws = 2 - self.c
        self.dpf = self.dp + 2 * wf * (1 - 2 * self.bf)
        self.dps = self.dp + 2 * ws * (1 - 2 * self.bs)
        self.dpd = self.dpf + self.dps - self.dp

    @staticmethod
    def own_block(G, z, c):
        d = c - z // G.H
        return (z + d * d * G.H) % G.T

    def extra(self, G, bit):
        b = (self.col // (1 << bit)) % 2
        return self.dp + (2 << bit) * (1 - 2 * b)

    def piece(self):
        return self.c * 4 + self.bs * 2 + self.bf


def owner(G, co, b):
    out = (b // G.H - co.g) * (b // G.H - co.g)
    return co.g + out * (1 - 2 * co.g), (b + out * G.H) % G.T


class Net:
    def __init__(self, ref):
        self.ref = ref
        self.n = 0
        self.items = []

    def take(self, n=1):
        base = self.n
        self.n += n
        return base

    def sem(self, i):
        return self.ref.at[i]

    def remote(self, src, dst, dev, cond=None, ss=None, rs=None):
        ss = self.take() if ss is None else ss
        rs = self.take() if rs is None else rs
        return Copy(self, src, dst, dev, ss, rs, cond)

    def local(self, src, dst, cond=None):
        return Copy(self, src, dst, None, self.take(), None, cond)

    def drain(self):
        for copy in self.items:
            copy.guard(copy.wait_sent)
        self.items = []


class Copy:
    def __init__(self, net, src, dst, dev, ss, rs, cond):
        self.net, self.src, self.dst, self.dev = net, src, dst, dev
        self.ss, self.rs, self.cond = ss, rs, cond

    def make(self):
        net = self.net
        if self.dev is None:
            return pltpu.make_async_copy(self.src(), self.dst(), net.sem(self.ss))
        return pltpu.make_async_remote_copy(
            src_ref=self.src(), dst_ref=self.dst(), send_sem=net.sem(self.ss),
            recv_sem=net.sem(self.rs), device_id=self.dev, device_id_type=MESH,
        )

    def guard(self, fn):
        if self.cond is None:
            fn()
        else:
            pl.when(self.cond)(fn)

    def start(self, hold=True):
        self.guard(lambda: self.make().start())
        if hold:
            self.net.items.append(self)
        return self

    def wait_sent(self):
        if self.dev is None:
            self.make().wait()
        else:
            self.make().wait_send()

    def got(self):
        self.make().wait_recv()


def column_partners(G, co):
    out = [(co.mate, co.z), (co.dpf, co.z), (co.dps, co.z), (co.dpd, co.z), (co.mate, co.other)]
    out += [(co.dp, (co.z + k) % G.T) for k in range(1, G.T)]
    out += [(co.mate, (co.z + k) % G.T) for k in range(1, G.T) if k != G.H]
    out += [(co.extra(G, b), co.z) for b in range(2, G.nbits)]
    return out


def lanes(shape):
    return lax.broadcasted_iota(jnp.int32, shape, len(shape) - 1)


def aug_base(h):
    return HD if h == 0 else 0


def dot(a, b):
    return lax.dot_general(a, b, (((1,), (0,)), ((), ())), preferred_element_type=F32)


def dot_nt(a, b):
    return lax.dot_general(a, b, (((1,), (1,)), ((), ())), preferred_element_type=F32)


def dot_tn(a, b):
    return lax.dot_general(a, b, (((0,), (0,)), ((), ())), preferred_element_type=F32)


def parts3(v):
    hi = v.astype(BF).astype(F32)
    mid = (v - hi).astype(BF).astype(F32)
    return hi, mid, v - hi - mid


def place3(base, lane, first, v):
    hi, mid, lo = parts3(v)
    base = jnp.where(lane == first, hi, base)
    base = jnp.where(lane == first + 1, mid, base)
    return jnp.where(lane == first + 2, lo, base)


def norm(v):
    centre = jnp.mean(v, axis=-1, keepdims=True)
    v = v - centre
    inv = lax.rsqrt(jnp.mean(v * v, axis=-1, keepdims=True) + EPS)
    return v * inv, inv


def norm_back(e, normal, inv):
    a = jnp.mean(e, axis=-1, keepdims=True)
    b = jnp.mean(e * normal, axis=-1, keepdims=True)
    return inv * (e - a - normal * b)


def colsum(v):
    return jnp.sum(v, axis=0, keepdims=True)


def al(v, n):
    return pl.multiple_of(v, n)


def layer_kernel(
    G, lengths, x, te, wq, wi, wo, wp, pos_in, qvbias, ibias, *rest,
):
    vectors = [v[...].astype(F32).reshape(1, G.D) for v in rest[:6]]
    layer_body(G, vectors, lengths, x, te, wq, wi, wo, wp, pos_in, qvbias, ibias, *rest[6:])


def layer_body(
    G, vectors, lengths, x, te, wq, wi, wo, wp, pos_in, qvbias, ibias,
    out, igrad, pgrad, qg, og, ig, ug, vout,
    xall, pos, emb, qa, ka, va, da, kt, acc, top, mixed, mixr,
    sm, wqm, wqo, wqh, wif, wof, wpf, smalls, teach,
    flow, hid, gpre, gfeed, gbr, gmid, osrc, gm, gmall, vsum, ibsum,
    dwi, dwo, dwp, dq, gp, dwq, dwqb, qsum,
    s0i, s0o, s0p, s0q, r0i, r0o, r0p, r0q, r1i, r1o, r1p, r1q, r2i, r2o, r2p, r2q,
    r3i, r3o, r3p, r3q, rxi, rxo, rxp, rxq, gi, go, gpp, gq,
    ec, hsum, hp, eo, eh, hsend, nat, ps1, ps2, px, py, pf, pr3, vb, vr, qb, qr,
    sem,
):
    co = Co(G)
    net = Net(sem)
    T, H, R, L, WP, NH, D, F = G.T, G.H, G.R, G.L, G.WP, G.NH, G.D, G.F
    z, c, g = co.z, co.c, co.g
    mate, step1, step2 = (co.mate, z), (co.dpf, z), (co.dps, z)
    length = lengths[co.slot]
    ge, dk, dv = xall, acc.at[0], acc.at[1]

    def rows(b, n=R):
        return pl.ds(al(b * R, R), n)

    pp = c * (G.DP // 2) + co.bf * (G.DP // 4) + co.bs * (G.DP // 8)
    for bit in range(2, G.nbits):
        pp = pp + ((co.col // (1 << bit)) % 2) * (G.DP // (4 << bit))
    dests = []
    for b in range(T):
        flat = b * G.DP + pp
        dests.append((flat // T, flat % T))
    mine = co.dp * T + z
    fp = mine % G.DP
    fc = fp // (G.DP // 2)
    f1 = (fp // (G.DP // 4)) % 2
    f2 = (fp // (G.DP // 8)) % 2
    fcol = (f1 + fc * (f2 - f1)) + 2 * (f2 + fc * (f1 - f2))
    for bit in range(2, G.nbits):
        fcol = fcol + ((fp // (G.DP // (4 << bit))) % 2) * (1 << bit)
    own_piece = 2 * fcol + fc == co.dp
    poscopy = net.local(lambda: pos_in, lambda: pos).start()
    bar = pltpu.get_barrier_semaphore()
    partners = column_partners(G, co)
    for dev in partners:
        pl.semaphore_signal(bar, inc=1, device_id=dev, device_id_type=MESH)

    for k in range(1, T):
        dev = (2 * fcol + fc, (z + k) % T)
        pl.semaphore_signal(bar, inc=1, device_id=dev, device_id_type=MESH)

    @pl.when(jnp.logical_not(own_piece))
    def _():
        pl.semaphore_signal(bar, inc=1, device_id=(2 * fcol + fc, z), device_id_type=MESH)

    pl.semaphore_wait(bar, len(partners) + T - own_piece.astype(jnp.int32))

    bs, br = net.take(T), net.take(T)
    sm[...] = jnp.zeros(sm.shape, F32)
    sm[0:2, : G.W] = qvbias[...].astype(F32)
    sm[2:3, :F] = ibias[...].astype(F32).reshape(1, F)
    small_own = net.local(lambda: sm, lambda: smalls.at[z]).start(hold=False)
    small = [
        net.remote(lambda: sm, lambda: smalls.at[z], (co.dp, (z + k) % T)).start()
        for k in range(1, T)
    ]
    p = co.piece()

    def weight_chain(src, dst, slab, k):
        size = src.shape[-2] // 8

        def view(ref, s, first, count):
            where = pl.ds(al(first * size, size), count * size)
            if s is None:
                return ref.at[:, where] if slab is None else ref.at[where]
            return ref.at[s, where]

        to = None if slab is None else z
        cps = [net.remote(lambda: view(src, None, p, 1), lambda: view(dst, to, p, 1), (co.dp, (z + k) % T))]
        for first, count, dev in ((p, 1, step1), (p // 2 * 2, 2, step2), (c * 4, 4, mate)):
            ref = lambda first=first, count=count: view(dst, slab, first, count)
            cps.append(net.remote(ref, ref, dev))
        return cps

    qchain = weight_chain(wq, wqo, None, H)
    qchain[0].start()
    q_own = net.local(lambda: wq, lambda: wqm).start(hold=False)
    wchains = []
    whole = ((wp, wpf), (wi, wif), (wo, wof))
    for src, dst in whole:
        net.local(lambda src=src: src, lambda dst=dst: dst.at[z]).start()
    for k in range(1, T):
        for src, dst in whole:
            wchains.append(weight_chain(src, dst, (z - k) % T, k))

    chunks = 2
    n = R // chunks
    xr = net.take(T * chunks)

    def order(r):
        if r == 0:
            return z
        if r < H:
            return g * H + (co.zz + r) % H
        k = r - H
        return (H - 1 - k) + (1 - g) * (2 * k + 1)

    blocks = [order(r) for r in range(T)]

    def block_at(r):
        out = blocks[0]
        for k in range(1, T):
            out = jnp.where(r == k, blocks[k], out)
        return out
    zb = H - 1 + c
    edge = jnp.logical_and(co.native, z == H - 1 + g)

    def xrow(b, ch):
        return lambda: xall.at[pl.ds(al(b * R + ch * n, n), n)]

    def xmine(ch):
        return lambda: x.at[pl.ds(ch * n, n)]

    def xsend(src, b, ch, dev, cond, ss=None):
        return net.remote(src, xrow(b, ch), dev, cond, rs=xr + b * chunks + ch, ss=ss)

    def swapped_sends(k):
        cond = jnp.logical_and(co.swapped, (z - zb) * (1 - 2 * c) == k + 1)
        return [xsend(xmine(ch), z, ch, (co.dp, zb), cond) for ch in range(chunks)]

    own_x = []
    for ch in range(chunks):
        for j in range(1, H):
            xsend(xmine(ch), z, ch, (co.dp, g * H + (co.zz + j) % H), co.native).start()
        xsend(xmine(ch), z, ch, mate, co.native).start()
        own_x.append(net.local(xmine(ch), xrow(z, ch), co.native).start(hold=False))
    for cp in swapped_sends(0):
        cp.start()

    tlocal = net.local(lambda: te, lambda: teach, co.native)
    tswap = net.remote(lambda: te, lambda: teach, (co.mate, co.other), co.swapped)

    def project(b):
        CH = min(256, R)
        qb_, vb_ = smalls[co.hb, 0:1, :WP], smalls[co.hb, 1:2, :WP]

        def step(i, carry):
            first = b * R + i * CH
            rr = pl.ds(al(first, CH), CH)
            low = (xall[rr, :].astype(F32) + pos[rr, :].astype(F32)).astype(BF)
            emb[rr, :] = low
            pr = dot(low, wqh[...])
            q = (pr[:, :WP] + qb_).astype(BF).astype(F32) * (1.0 / math.sqrt(HD))
            k = pr[:, WP : 2 * WP].astype(BF).astype(F32)
            v = (pr[:, 2 * WP :] + vb_).astype(BF).astype(F32)
            lane = lanes((CH, WP))
            place = lax.broadcasted_iota(jnp.int32, (CH, WP), 0) + first
            limit = jnp.where(place < length, 0.0, NEG)
            for h in range(NH):
                a0 = aug_base(h)
                data = lane // HD == h
                ones = jnp.where((lane >= a0) & (lane < a0 + 4), 1.0, 0.0)
                qa[h, rr, :] = jnp.where(data, q, jnp.where(lane == a0, 1.0, 0.0)).astype(BF)
                ka[h, rr, :] = jnp.where(data, k, jnp.where(lane == a0, limit, ones)).astype(BF)
                va[h, rr, :] = jnp.where(data, v, ones).astype(BF)
                acc[h, rr, :] = jnp.zeros((CH, WP), F32)
                top[h, rr, :] = jnp.full((CH, WP), NEG, F32)
            return carry

        lax.fori_loop(0, R // CH, step, 0)

    def ftile(i, j, masked):
        qr, kr = rows(i), rows(j)
        for h in range(NH):
            s = dot_nt(qa[h, qr, :], ka[h, kr, :])
            if masked:
                below = lax.broadcasted_iota(jnp.int32, (R, R), 0) >= lanes((R, R))
                s = jnp.where(below, s, NEG)
            old = top[h, qr, :1]
            new = jnp.maximum(old, jnp.max(s, axis=-1, keepdims=True))
            e = jnp.exp(s - new).astype(BF)
            acc[h, qr, :] = acc[h, qr, :] * jnp.exp(old - new) + dot(e, va[h, kr, :])
            top[h, qr, :] = jnp.broadcast_to(new, (R, WP))

    def finalize(b):
        rr = rows(b)
        lane = lanes((R, WP))
        o = jnp.zeros((R, WP), F32)
        for h in range(NH):
            a0 = aug_base(h)
            total = acc[h, rr, a0 : a0 + 1]
            o = jnp.where(lane // HD == h, acc[h, rr, :] / total, o)
            lse = top[h, rr, :1] + jnp.log(total)
            q = qa[h, rr, :].astype(F32)
            qa[h, rr, :] = place3(q, lane, a0 + 1, -lse).astype(BF)
        mixed[rr, :] = o.astype(BF)

    def arrival(r, cond, pass_on):
        b = blocks[r]
        steps = []
        for ch in range(chunks):
            sends = []
            if pass_on:
                for j in range(1, H):
                    sends.append(xsend(xrow(b, ch), b, ch, (co.dp, g * H + (co.zz + j) % H), cond))
            sends.append(xsend(xrow(b, ch), b, ch, mate, cond))
            steps.append((xsend(xrow(b, ch), b, ch, mate, None, xr), sends))

        def act():
            for got, sends in steps:
                pl.when(cond)(got.got)
                for cp in sends:
                    cp.start()

        return act

    inner = jnp.logical_and(co.native, jnp.logical_not(edge))
    arrivals = {r: arrival(r, co.native if r < H else inner, False) for r in range(1, T)}
    early = {r: arrival(r, edge, True) for r in range(H, T)}
    from_mate = [
        [xsend(xrow(blocks[r], ch), blocks[r], ch, mate, None, xr) for ch in range(chunks)]
        for r in range(T)
    ]
    far = {k: swapped_sends(k) for k in range(1, H)}

    def mate_arrive(r):
        @pl.when(co.swapped)
        def _():
            for cp in from_mate[r]:
                cp.got()

    mr = net.take(T)
    mixed_out = []
    for r in range(T):
        oc, oz = owner(G, co, blocks[r])
        me = jnp.logical_and(oc == c, oz == z)
        src = lambda r=r: mixed.at[rows(blocks[r])]
        dst = lambda: mixr.at[co.hb]
        dev = (2 * co.col + oc, oz)
        mixed_out.append(net.remote(src, dst, dev, jnp.logical_not(me), rs=mr + co.hb))
        mixed_out.append(net.local(src, dst, me))

    poscopy.wait_sent()
    net.items.remove(poscopy)
    for cp in own_x:
        cp.guard(cp.wait_sent)

    qchain[0].got()
    qchain[1].start()
    for k in far:
        for cp in far[k]:
            cp.start()
    qchain[1].got()
    qchain[2].start()
    early[H]()
    for ch in wchains:
        ch[0].start()
    qchain[2].got()
    qchain[3].start()
    qchain[3].got()

    q_own.wait_sent()
    for j in range(3):
        wqh[:, j * WP : (j + 1) * WP] = jnp.where(c == 0, wqm[j], wqo[j])
    small_own.wait_sent()
    for cp in small:
        cp.got()


    def begin(r):
        if r == 0:
            mate_arrive(0)
            return
        arrivals[r]()
        mate_arrive(r)
        if r + 1 in early and r + 1 > H:
            early[r + 1]()

    def triangle(t):
        r = 0
        for k in range(1, T):
            r = r + (t >= k * (k + 1) // 2).astype(jnp.int32)
        return r, t - r * (r + 1) // 2

    ntiles = T * (T + 1) // 2

    def ftiles(t, carry):
        r, q = triangle(t)

        @pl.when(q == 0)
        def _():
            for k in range(T):
                pl.when(r == k)(functools.partial(begin, k))
            project(block_at(r))

        a, b = block_at(r), block_at(q)

        @pl.when(q < r)
        def _():
            ftile(jnp.maximum(a, b), jnp.minimum(a, b), False)

        @pl.when(q == r)
        def _():
            ftile(a, a, True)

        @pl.when(r == T - 1)
        def _():
            finalize(b)
            for k in range(T):

                @pl.when(q == k)
                def _():
                    mixed_out[2 * k].start()
                    mixed_out[2 * k + 1].start()

        for i, acts in polls.items():

            @pl.when(t == i)
            def _(acts=acts):
                for hop, n_ in acts:
                    hop_on(hop, n_)

        return carry

    def hop_on(hop, n_):
        wchains[n_][hop].got()
        wchains[n_][hop + 1].start()

    polls = {}
    hops = [(h_, n_) for h_ in range(3) for n_ in range(len(wchains))]
    if ntiles == 10:
        when = {1: [(0, 0)], 2: [(0, 1), (1, 0)], 5: [(0, 2), (1, 1), (2, 0)], 7: [(1, 2)], 8: [(2, 1)]}
        for i, acts in when.items():
            polls[i] = [(h_, 3 * n_ + m) for h_, n_ in acts for m in range(3)]
    polled = [a for acts in polls.values() for a in acts]

    lax.fori_loop(0, ntiles, ftiles, 0)
    tlocal.start()
    tswap.start()

    for a in sorted(hops, key=lambda a: a[0] + a[1] // 3):
        if a not in polled:
            hop_on(*a)
    for ch in wchains:
        ch[3].got()
    net.items.remove(tlocal)
    for cp in net.items:
        if cp.dev is None:
            cp.guard(cp.wait_sent)
    net.items = [cp for cp in net.items if cp.dev is not None]
    for k in range(1, T):
        hb = (co.hb + k) % T
        net.remote(lambda: mixed.at[rows(0)], lambda hb=hb: mixr.at[hb], mate, rs=mr + hb, ss=mr).got()

    count = lengths[0]
    for i in range(1, G.slots):
        count = count + lengths[i]
    scale = (G.slots * L) / jnp.full((1, 1), count, jnp.int32).astype(F32)
    vsum[...] = jnp.zeros(vsum.shape, F32)
    ibsum[...] = jnp.zeros(ibsum.shape, F32)
    output_bias, g1, s1, outer_bias, g2, s2 = vectors
    CR = min(256, R)

    def ffn(off):
        rr = pl.ds(off, CR)
        base = co.ob * R + off
        grows = pl.ds(al(base, CR), CR)
        branch = lax.fori_loop(
            0, T, lambda t, a: a + dot(mixr[t, rr, :], wpf[t]), jnp.zeros((CR, D), F32)
        )
        e = xall[grows, :].astype(F32) + pos[grows, :].astype(F32)
        n1, inv1 = norm(e + branch + output_bias)
        first = n1 * g1 + s1
        low = first.astype(BF)
        flow[rr, :] = low

        def up(t, a):
            pre = dot(low, wif[t]) + smalls[t, 2:3, :F]
            h = jnp.maximum(pre, 0.0).astype(BF)
            hid[t, rr, :] = h
            return a + dot(h, wof[t])

        feed = lax.fori_loop(0, T, up, jnp.zeros((CR, D), F32))
        n2, inv2 = norm(first + feed + outer_bias)
        result = n2 * g2 + s2
        osrc[rr, :] = result.astype(BF)
        if off == 0:
            pl.when(co.swapped)(tswap.got)
            tlocal.guard(tlocal.wait_sent)
        place = lax.broadcasted_iota(jnp.int32, (CR, 1), 0) + base
        valid = jnp.where(place < length, scale, 0.0)
        gr = valid * (result - teach[rr, :].astype(F32))
        gs = norm_back(gr * g2, n2, inv2)
        gf = gs.astype(BF)
        gfeed[rr, :] = gf

        def down(t, a):
            gh = dot_nt(gf, wof[t])
            gpt = jnp.where(hid[t, rr, :].astype(F32) > 0, gh, 0.0).astype(BF)
            gpre[t, rr, :] = gpt
            ibsum[t] += colsum(gpt.astype(F32))
            return a + dot_nt(gpt, wif[t])

        g_first = lax.fori_loop(0, T, down, gs)
        gv = norm_back(g_first * g1, n1, inv1)
        gmid[rr, :] = gv
        gb = gv.astype(BF)
        gbr[rr, :] = gb

        def mix(t, a):
            gm[t, rr, :] = dot_nt(gb, wpf[t]).astype(BF)
            return a

        lax.fori_loop(0, T, mix, 0)
        vsum[0:1] += colsum(gv)
        vsum[1:2] += colsum(g_first * n1)
        vsum[2:3] += colsum(g_first)
        vsum[3:4] += colsum(gs)
        vsum[4:5] += colsum(gr * n2)
        vsum[5:6] += colsum(gr)

    gmr = net.take(T * (R // CR))
    gm_in = []
    gm_own = []
    for i in range(R // CR):
        ffn(i * CR)
        if i == 0:
            net.drain()
        for k in range(T):
            m = (co.zz * 2 + c + k) % T
            c2, z2 = m % 2, g * H + m // 2
            hb2 = (z2 + c2 * H) % T
            src = lambda hb2=hb2, i=i: gm.at[hb2, pl.ds(i * CR, CR)]
            dst = lambda i=i: gmall.at[pl.ds(al(co.ob * R + i * CR, CR), CR)]
            if k == 0:
                gm_own.append(net.local(src, dst).start(hold=False))
                continue
            net.remote(src, dst, (2 * co.col + c2, z2), rs=gmr + k * (R // CR) + i).start()
            gm_in.append((k, i))

    olocal = net.local(lambda: osrc, lambda: out, co.native).start()
    oswap = net.remote(lambda: osrc, lambda: out, (co.mate, co.other), co.swapped).start()

    def now(src, dst, dev, ss=None):
        return net.remote(src, dst, dev, ss=ss)

    quarter = co.bf * 2 + co.bs
    plane3 = (
        ((co.dpf, z), (1 - co.bf) * 2 + co.bs),
        ((co.dps, z), co.bf * 2 + 1 - co.bs),
        ((co.dpd, z), (1 - co.bf) * 2 + 1 - co.bs),
    )

    def scatter3(src, land):
        return [
            now(lambda piece=piece: src(piece), lambda j=j: land(j), dev)
            for j, (dev, piece) in enumerate(plane3)
        ]

    class Slabs:
        def __init__(self, X, k0, n, s0, r0, r1, r2, r3, rx, r3slot, stay):
            hr, q1, q2 = r0.shape[1], r1.shape[1], r2.shape[1]
            self.n, self.k0 = n, k0
            slabs = pl.ds(k0, n)
            self.start = now(
                lambda: X.at[slabs, pl.ds(al((1 - c) * hr, hr), hr)], lambda: r0.at[slabs], mate
            )
            self.s1 = now(
                lambda: s0.at[slabs, pl.ds(al((1 - co.bf) * q1, q1), q1)],
                lambda: r1.at[slabs], step1,
            )
            self.s2 = now(
                lambda: r1.at[slabs, pl.ds(al((1 - co.bs) * q2, q2), q2)],
                lambda: r2.at[slabs], step2,
            )
            self.over = [
                now(lambda k=k: r2.at[k], lambda k=k: r3.at[r3slot(k)], (co.dp, (z + k_z) % T))
                for k, k_z in stay
                if k0 <= k < k0 + n
            ]
            self.extra = [
                now(lambda: r2.at[slabs], lambda b=b: rx.at[b - 2, slabs], (co.extra(G, b), z))
                for b in range(2, G.nbits)
            ]
            self.refs = X, s0, r0, r1, r2, rx, hr, q1, q2

        def a0(self):
            X, s0, r0, r1, r2, rx, hr, q1, q2 = self.refs
            self.start.got()
            for k in range(self.k0, self.k0 + self.n):
                kept = X[k, pl.ds(al(c * hr, hr), hr), :]
                s0[k] = (kept.astype(F32) + r0[k].astype(F32)).astype(BF)

        def go(self):
            self.s1.start()

        def a1(self):
            X, s0, r0, r1, r2, rx, hr, q1, q2 = self.refs
            self.s1.got()
            for k in range(self.k0, self.k0 + self.n):
                kept = s0[k, pl.ds(al(co.bf * q1, q1), q1), :]
                r1[k] = (kept.astype(F32) + r1[k].astype(F32)).astype(BF)
            self.s2.start()

        def a2(self):
            X, s0, r0, r1, r2, rx, hr, q1, q2 = self.refs
            self.s2.got()
            for k in range(self.k0, self.k0 + self.n):
                kept = r1[k, pl.ds(al(co.bs * q2, q2), q2), :]
                r2[k] = (kept.astype(F32) + r2[k].astype(F32)).astype(BF)
            for m, cp in enumerate(self.extra):
                cp.start(hold=False)
                cp.got()
                cp.wait_sent()
                for k in range(self.k0, self.k0 + self.n):
                    r2[k] = (r2[k].astype(F32) + rx[m, k].astype(F32)).astype(BF)
            for cp in self.over:
                cp.start()

    class Back:
        def __init__(self, chains, r2, r3, gx, dst):
            q2 = r2.shape[1]
            self.chains, self.r2, self.r3 = chains, r2, r3

            def place(width, first):
                return lambda: gx.at[pl.ds(al(first * q2, q2), width * q2)]

            own = c * 4 + co.bf * 2 + co.bs
            self.own = place(1, own)
            self.back = []
            for width, first, dev in ((1, own, step2), (2, own // 2 * 2, step1), (4, c * 4, mate)):
                self.back.append(now(place(width, first), place(width, first), dev))
            self.end = net.local(lambda: gx, lambda: dst)

        def a3(self):
            tot = self.r2[0].astype(F32)
            for k, cp in enumerate(cp for ch in self.chains for cp in ch.over):
                cp.got()
                tot = tot + self.r3[k].astype(F32)
            self.own()[...] = tot.astype(BF)
            self.back[0].start()

        def a4(self):
            self.back[0].got()
            self.back[1].start()

        def a5(self):
            self.back[1].got()
            self.back[2].start()

        def a6(self):
            self.back[2].got()
            self.end.start()

    to_z = [(k, k) for k in range(1, T)]
    minus = lambda k: k - 1
    ks = list(range(1, T)) + [0]
    co_ = [Slabs(dwo, k, 1, s0o, r0o, r1o, r2o, r3o, rxo, minus, to_z) for k in ks]
    ci_ = [Slabs(dwi, k, 1, s0i, r0i, r1i, r2i, r3i, rxi, minus, to_z) for k in ks]
    cp_ = Slabs(dwp, 0, T, s0p, r0p, r1p, r2p, r3p, rxp, minus, to_z)
    slabs = [ch for pair in zip(co_[:-1], ci_[:-1]) for ch in pair] + [co_[-1], ci_[-1], cp_]
    back_o = Back(co_, r2o, r3o, go, ug)
    back_i = Back(ci_, r2i, r3i, gi, ig)
    back_p = Back([cp_], r2p, r3p, gpp, og)

    def grads(i, carry):
        k = jnp.where(i == T - 1, 0, i + 1)
        t = (z + k) % T
        dwo[k] = dot_tn(hid[t], gfeed[...]).astype(BF)
        dwi[k] = dot_tn(flow[...], gpre[t]).astype(BF)
        dwp[k] = dot_tn(mixr[t], gbr[...]).astype(BF)
        for n_ in range(T):

            @pl.when(i == n_)
            def _():
                co_[n_].start.start()
                ci_[n_].start.start()

        return carry

    lax.fori_loop(0, T, grads, 0)
    cp_.start.start()

    vb[...] = jnp.zeros(vb.shape, F32)
    vb[0:6, :] = vsum[0:6, :]
    for t in range(T):
        vb[8 + t : 9 + t, :F] = ibsum[t]

    def sum_chain(v, r, devs):
        cps = [now(lambda: v, lambda i=i: r.at[i], dev) for i, dev in enumerate(devs)]

        def step(i):
            def act():
                cps[i].got()
                cps[i].wait_sent()
                v[...] += r[i]
                if i + 1 < len(cps):
                    cps[i + 1].start(hold=False)

            return act

        return cps[0], [step(i) for i in range(len(cps))]

    plane = [step1, step2] + [(co.extra(G, b), z) for b in range(2, G.nbits)]
    vstart, vchain = sum_chain(vb, vr, [mate] + plane)
    vstart.start(hold=False)
    nv = len(vchain)
    vover = [
        now(lambda: vb, lambda k=k: vr.at[nv + k - 1], (co.dp, (z + k) % T))
        for k in range(1, T)
    ]

    def vz():
        for cp in vover:
            cp.start(hold=False)

    def vdone():
        for cp in vover:
            cp.got()
            cp.wait_sent()
        for k in range(1, T):
            vb[...] += vr[nv + k - 1]
        vout[0:8, :] = vb[0:8, :]
        vrow = lax.broadcasted_iota(jnp.int32, vb.shape, 0)
        vout[8:9, :] = colsum(jnp.where(vrow == 8 + z, vb[...], 0.0))

    vchain = vchain + [vz, vdone]

    for i, ch in enumerate(slabs):
        ch.a0()
        if i < 2:
            ch.go()
    for k, i in gm_in:
        net.remote(
            lambda: gm.at[0, pl.ds(0, CR)], lambda: gmall.at[pl.ds(0, CR)], mate,
            rs=gmr + k * (R // CR) + i, ss=gmr,
        ).got()
    for cp in gm_own:
        cp.wait_sent()


    def prepare(i, carry):
        CH = min(256, R)
        rr = pl.ds(al(i * CH, CH), CH)
        gg = gmall[rr, :].astype(F32)
        prod = gg * mixed[rr, :].astype(F32)
        lane = lanes((CH, WP))
        k = jnp.zeros((CH, WP), F32)
        for h in range(NH):
            a0 = aug_base(h)
            data = lane // HD == h
            delta = jnp.sum(jnp.where(data, prod, 0.0), axis=-1, keepdims=True)
            base = place3(jnp.zeros((CH, WP), F32), lane, a0 + 1, -delta)
            da[h, rr, :] = jnp.where(data, gg, base).astype(BF)
            k = jnp.where(data, ka[h, rr, :].astype(F32), k)
        kt[:, rr] = k.T.astype(BF)
        zero = jnp.zeros((CH, WP), F32)
        dk[rr, :] = zero
        dv[rr, :] = zero
        dq[:, rr] = zero.T
        return carry

    lax.fori_loop(0, L // min(256, R), prepare, 0)

    def btile(i, j, masked):
        qr, kr = rows(i), rows(j)
        lane = lanes((R, WP))
        sub = lax.broadcasted_iota(jnp.int32, (WP, R), 0)
        dks, dvs, dqs = [], [], []
        for h in range(NH):
            q, d = qa[h, qr, :], da[h, qr, :]
            pm = jnp.exp(dot_nt(ka[h, kr, :], q))
            if masked:
                above = lax.broadcasted_iota(jnp.int32, (R, R), 0) <= lanes((R, R))
                pm = jnp.where(above, pm, 0.0)
            ds = (pm * dot_nt(va[h, kr, :], d)).astype(BF)
            dvs.append(dot(pm.astype(BF), d))
            dks.append(dot(ds, q))
            dqs.append(dot(kt[:, kr], ds))
        if NH == 1:
            dk[kr, :] += dks[0]
            dv[kr, :] += dvs[0]
            dq[:, qr] += dqs[0]
        else:
            dk[kr, :] += jnp.where(lane < HD, dks[0], dks[1])
            dv[kr, :] += jnp.where(lane < HD, dvs[0], dvs[1])
            dq[:, qr] += jnp.where(sub < HD, dqs[0], dqs[1])

    dwq[...] = jnp.zeros(dwq.shape, F32)
    qsum[...] = jnp.zeros(qsum.shape, F32)

    def complete(b):
        rr = rows(b)
        keep = lanes((R, WP)) < G.W
        q = dq[:, rr].T * (1.0 / math.sqrt(HD))
        sums = []
        for n_, part in enumerate((q, dk[rr, :], dv[rr, :])):
            part = jnp.where(keep, part, 0.0).astype(BF)
            gp[rr, n_ * WP : (n_ + 1) * WP] = part
            sums.append(colsum(part.astype(F32)))
        gg = gp[rr, :]
        back = dot_nt(gg, wqh[...])
        ge[rr, :] = back.astype(BF)
        oc, oz = owner(G, co, b)

        @pl.when(jnp.logical_and(oc == c, oz == z))
        def _():
            ge[rr, :] = (back + gmid[...]).astype(BF)

        dwq[...] += dot_tn(emb[rr, :], gg)
        qsum[0:1, :] += jnp.concatenate(sums, axis=1)

    order_b = [(T - 1 - s_) + g * (2 * s_ - T + 1) for s_ in range(T)]
    ends = [sum(T - i for i in range(s_ + 1)) - 1 for s_ in range(T)]
    half = R // 2
    edge_z = H - 1 + g
    eh_sem = net.take(2 * H)
    nat_sem = net.take(2)
    pf_sem = net.take(T)
    at_edge = z == edge_z

    class Rows:
        def __init__(self, s_):
            b = order_b[s_]
            self.s, self.b, self.inside = s_, b, s_ >= H
            self.core = net.remote(
                lambda: ge.at[pl.ds(al(b * R + (1 - c) * half, half), half)],
                lambda: ec.at[s_], mate,
            )
            h = lambda: hsum.at[s_]
            if self.inside:
                home = jnp.logical_and(c == g, z == b)
                self.over = [
                    net.remote(
                        h, lambda: eh.at[co.zz * 2 + c], (2 * co.col + g, b),
                        jnp.logical_not(home), rs=eh_sem + co.zz * 2 + c,
                    )
                ]
            else:
                slot = (co.zz - (edge_z - g * H) + H - 1) % H
                base = net.take(max(H - 1, 1))
                self.base = base
                self.over = [
                    net.remote(
                        h, lambda: eo.at[s_, slot], (co.dp, edge_z), jnp.logical_not(at_edge),
                        rs=base + slot,
                    )
                ]
                self.home = net.remote(
                    lambda: hsend.at[s_], lambda: nat.at[pl.ds(al(c * half, half), half)],
                    (2 * co.col + g, b), at_edge, rs=nat_sem + c,
                )
            q2 = half // 4
            self.p1 = scatter3(
                lambda piece: hp.at[s_, pl.ds(al(piece * q2, q2), q2)], lambda j: ps1.at[s_, j]
            )
            dp2, z2 = dests[0]
            for k in range(1, T):
                dp2 = jnp.where(b == k, dests[k][0], dp2)
                z2 = jnp.where(b == k, dests[k][1], z2)
            here = jnp.logical_and(dp2 == co.dp, z2 == z)
            self.more = []
            size = q2
            for n_, bit in enumerate(range(2, G.nbits)):
                size = size // 2
                bb = (co.col // (1 << bit)) % 2
                src = (ps2, px)[n_ % 2] if n_ else ps2
                dst = px if n_ % 2 == 0 else py
                src = ps2 if n_ == 0 else (px if n_ % 2 == 1 else py)
                cp = net.remote(
                    lambda src=src, bb=bb, size=size: src.at[s_, pl.ds(al((1 - bb) * size, 8), size)],
                    lambda dst=dst, size=size: dst.at[s_, pl.ds(0, size)],
                    (co.extra(G, bit), z),
                )
                self.more.append((cp, src, dst, bb, size))
            self.last = self.more[-1][2] if self.more else ps2
            piece = lambda: self.last.at[s_, pl.ds(0, G.PR)]
            self.fin = net.remote(
                piece, lambda: pf.at[z], (dp2, z2), jnp.logical_not(here), rs=pf_sem + z
            )
            self.fin_here = net.local(piece, lambda: pf.at[z], here)

        def k0(self):
            self.core.start()

        def k1(self):
            s_ = self.s
            self.core.got()
            own = ge[pl.ds(al(self.b * R + c * half, half), half), :].astype(F32)
            total = own + ec[s_].astype(F32)
            hsum[s_] = total.astype(BF)
            hp[s_] = total.astype(hp.dtype)
            for cp in self.over:
                cp.start()
            for cp in self.p1:
                cp.start()

        def k2(self):
            s_, q2 = self.s, half // 4
            total = hp[s_, pl.ds(al(quarter * q2, q2), q2), :].astype(F32)
            for j, cp in enumerate(self.p1):
                cp.got()
                total = total + ps1[s_, j].astype(F32)
            ps2[s_] = total.astype(ps2.dtype)
            for cp, src, dst, bb, size in self.more:
                cp.start()
                cp.got()
                kept = src[s_, pl.ds(al(bb * size, 8), size), :].astype(F32)
                dst[s_, 0:size, :] = (kept + dst[s_, 0:size, :].astype(F32)).astype(dst.dtype)
            self.fin.start()
            self.fin_here.start()

        def kx(self):
            s_ = self.s

            @pl.when(at_edge)
            def _():
                total = hsum[s_].astype(F32)
                for j in range(H - 1):
                    net.remote(
                        lambda: hsum.at[s_], lambda j=j: eo.at[s_, j], mate, rs=self.base + j,
                        ss=self.base,
                    ).got()
                    total = total + eo[s_, j].astype(F32)
                hsend[s_] = total.astype(BF)

            self.home.start()

    parts_ = [Rows(s_) for s_ in range(T)]

    def run(chain, i):
        chain[i]()

    jobs = {("v", i): act for i, act in enumerate(vchain)}
    for i, ch in enumerate(slabs):
        if i >= 2:
            jobs["s", i] = ch.go
        jobs["1", i] = ch.a1
        jobs["2", i] = ch.a2
    for name, bk in (("o", back_o), ("i", back_i), ("p", back_p)):
        for n_, act in enumerate((bk.a3, bk.a4, bk.a5, bk.a6)):
            jobs[name, n_] = act
    for rw in parts_:
        for name in ("k0", "k1", "k2", "kx"):
            if name != "kx" or not rw.inside:
                jobs[name, rw.s] = getattr(rw, name)
    plan = {
        0: [],
        1: [("v", 0)],
        2: [],
        3: [("k0", 0), ("v", 1)],
        4: [("k1", 0)],
        5: [("v", 2), ("v", 3)],
        6: [("k0", 1), ("k2", 0)],
        7: [("k1", 1), ("kx", 0)],
        8: [("k0", 2), ("v", 4)],
        9: [("k0", 3), ("k1", 2), ("k2", 1)],
    }
    for i in range(10):
        plan[i] += [("1", i), ("2", i - 2), ("s", i + 2)]
    plan = {i: [key for key in acts if key in jobs] for i, acts in plan.items()}
    if ntiles != 10:
        plan = {e: [("k0", s_)] for s_, e in enumerate(ends)}
    left = [key for key in jobs if not any(key in acts for acts in plan.values())]
    def btiles(t, carry):
        s_, u = 0, t
        for k in range(1, T):
            past = (t > ends[k - 1]).astype(jnp.int32)
            s_ = s_ + past
            u = u - past * (T - k + 1)
        b = (T - 1 - s_) + g * (2 * s_ - T + 1)
        far = b - u + g * (2 * u)

        @pl.when(u == 0)
        def _():
            btile(b, b, True)

        @pl.when(u > 0)
        def _():
            btile(jnp.maximum(b, far), jnp.minimum(b, far), False)

        @pl.when(u == T - 1 - s_)
        def _():
            complete(b)

        for i in range(ntiles):
            acts = [jobs[key] for key in plan.get(i, ())]
            if acts:

                @pl.when(t == i)
                def _(acts=acts):
                    for act in acts:
                        act()

        return carry

    lax.fori_loop(0, ntiles, btiles, 0)

    dwqb[c] = dwq[...].astype(BF)
    hq = D // 2
    e8 = D // 8
    qstart = now(
        lambda: dwqb.at[c, pl.ds(al((1 - c) * hq, hq), hq)], lambda: r0q.at[c], mate
    ).start()
    q_rs = scatter3(lambda piece: s0q.at[:, pl.ds(al(piece * e8, e8), e8)], lambda j: r1q.at[j])
    q_extra = [
        now(lambda: r2q, lambda b=b: rxq.at[b - 2], (co.extra(G, b), z)) for b in range(2, G.nbits)
    ]
    q_over = now(lambda: r2q.at[1], lambda: r3q.at[0], (co.dp, co.other))
    q_own = lambda: gq.at[pl.ds(al((c * 4 + quarter) * e8, e8), e8)]
    q_ag = [now(q_own, q_own, dev) for dev, _ in plane3]
    q_half = lambda: gq.at[pl.ds(al(c * hq, hq), hq)]
    q_core = now(q_half, q_half, mate)
    q_out = net.local(lambda: gq, lambda: qg)

    def q_sum():
        total = s0q[:, pl.ds(al(quarter * e8, e8), e8), :].astype(F32)
        for j, cp in enumerate(q_rs):
            cp.got()
            total = total + r1q[j].astype(F32)
        r2q[...] = total.astype(BF)
        for m, cp in enumerate(q_extra):
            cp.start(hold=False)
            cp.got()
            cp.wait_sent()
            r2q[...] = (r2q[...].astype(F32) + rxq[m].astype(F32)).astype(BF)
        q_over.start()

    def q_back():
        q_over.got()
        q_own()[...] = (r2q[0].astype(F32) + r3q[0].astype(F32)).astype(BF)
        for cp in q_ag:
            cp.start()

    def q_join():
        for cp in q_ag:
            cp.got()
        q_core.start()

    def q_end():
        q_core.got()
        q_out.start()

    qb[c] = qsum[...]
    qmate = now(lambda: qb.at[c], lambda: qb.at[c], mate).start(hold=False)
    qsums, qchain2 = sum_chain(qb, qr, plane)
    qover = now(lambda: qb.at[1], lambda: qr.at[len(plane), 0], (co.dp, co.other))

    def rest(*names):
        for key in left:
            if key[0] in names:
                jobs[key]()

    def backs(n_):
        for key in left:
            if key[0] in "oip" and key[1] == n_:
                jobs[key]()

    rest("k1")
    pltpu.make_async_remote_copy(
        src_ref=dwqb.at[c, pl.ds(0, hq)], dst_ref=r0q.at[1 - c], send_sem=net.sem(qstart.ss),
        recv_sem=net.sem(qstart.rs), device_id=mate, device_id_type=MESH,
    ).wait_recv()
    s0q[c] = dwqb[c, pl.ds(al(c * hq, hq), hq), :]
    s0q[1 - c] = r0q[1 - c]
    for cp in q_rs:
        cp.start()
    qmate.got()
    qmate.wait_sent()
    qsums.start(hold=False)
    rest("s", "1", "v")
    rest("2")
    rest("k2")
    backs(0)
    qchain2[0]()
    q_sum()
    for i in range(1, len(qchain2)):
        qchain2[i]()
    qover.start(hold=False)
    rest("kx")
    backs(1)
    q_back()
    qover.got()
    qover.wait_sent()
    qb[0] += qr[len(plane), 0]
    vout[9:10, :WP] = qb[0, 0:1, :WP]
    vout[10:11, :WP] = qb[0, 0:1, 2 * WP :]
    backs(2)

    for i in range(2):

        @pl.when(co.swapped)
        def _():
            net.remote(
                lambda: hsend.at[0], lambda: nat.at[pl.ds(0, half)], mate, rs=nat_sem + i, ss=nat_sem
            ).got()

    @pl.when(co.native)
    def _():
        for i in range(2 * H):

            @pl.when(i != co.zz * 2 + c)
            def _():
                net.remote(
                    lambda: hsum.at[0], lambda: eh.at[i], mate, rs=eh_sem + i, ss=eh_sem
                ).got()

        mine_h = jnp.zeros((half, D), BF)
        for s_ in range(H, T):
            mine_h = jnp.where(order_b[s_] == z, hsum[s_], mine_h)
        for j in range(2):
            total = jnp.where(c == j, mine_h.astype(F32), 0.0)
            for k in range(H):
                one = eh[2 * k + j].astype(F32)
                total = total + jnp.where(k * 2 + j == co.zz * 2 + c, 0.0, one)
            nat[pl.ds(j * half, half), :] = total.astype(BF)

    net.local(lambda: nat, lambda: igrad).start()
    q_join()
    backs(3)
    for k in range(T):

        @pl.when(jnp.logical_not(jnp.logical_and(own_piece, z == k)))
        def _():
            net.remote(lambda: pf.at[k], lambda: pf.at[k], mate, rs=pf_sem + k, ss=pf_sem).got()

    for rw in parts_:
        rw.fin_here.guard(rw.fin_here.wait_sent)
    net.items = [cp for cp in net.items if all(cp is not rw.fin_here for rw in parts_)]
    total = pf[0].astype(F32)
    for k in range(1, T):
        total = total + pf[k].astype(F32)
    pr3[...] = total
    net.local(lambda: pr3, lambda: pgrad).start()
    q_end()
    pl.when(co.swapped)(oswap.got)
    net.drain()

def emit_kernel(
    G, out_in, igrad_in, pgrad_in, qg_in, og_in, ig_in, ug_in, vin,
    out, igrad, pgrad, qg, qvg, og, ig, ug, ibg, v0, v1, v2, v3, v4, v5,
):
    out[...] = out_in[...]
    igrad[...] = igrad_in[...]
    pgrad[...] = pgrad_in[...]
    for j in range(3):
        qg[j] = qg_in[:, j * G.WP : j * G.WP + G.W].astype(F32)
    qvg[...] = vin[9:11, : G.W]
    og[...] = og_in[: G.W, :].astype(F32)
    ig[...] = ig_in[...].astype(F32)
    ug[...] = ug_in[...].astype(F32)
    ibg[...] = vin[8:9, : G.F].reshape(G.F)
    for i, v in enumerate((v0, v1, v2, v3, v4, v5)):
        v[...] = vin[i : i + 1, :].reshape(G.D)


def on_device(G, *args):
    (inputs, teacher, lengths, positions, qkv_weight, query_value_bias, output_weight, output_bias,
     first_gain, first_shift, inner_weight, inner_bias, outer_weight, outer_bias, second_gain,
     second_shift) = args
    T, R, D, L, W, WP, NH, F, H = G.T, G.R, G.D, G.L, G.W, G.WP, G.NH, G.F, G.H
    dma = lambda n: pltpu.SemaphoreType.DMA((n,))
    vm = pltpu.VMEM
    wq = jnp.pad(jnp.transpose(qkv_weight, (1, 0, 2)), ((0, 0), (0, 0), (0, WP - W)))
    wp = jnp.pad(output_weight, ((0, WP - W), (0, 0)))
    sizes = [(D, F, T), (F, D, T), (WP, D, T), (D, 3 * WP, 2)]
    nplane = G.nbits
    V = 8 + (T + 7) // 8 * 8
    scratch = [
        vm((L, D), BF), vm((L, D), BF), vm((L, D), BF),
        vm((NH, L, WP), BF), vm((NH, L, WP), BF), vm((NH, L, WP), BF), vm((NH, L, WP), BF),
        vm((WP, L), BF), vm((2, L, WP), F32), vm((NH, L, WP), F32), vm((L, WP), BF),
        vm((T, R, WP), BF),
        vm((8, D), F32), vm((3, D, WP), BF), vm((3, D, WP), BF), vm((D, 3 * WP), BF),
        vm((T, D, F), BF), vm((T, F, D), BF),
        vm((T, WP, D), BF), vm((T, 8, D), F32), vm((R, D), BF),
        vm((R, D), BF), vm((T, R, F), BF), vm((T, R, F), BF), vm((R, D), BF), vm((R, D), BF),
        vm((R, D), F32), vm((R, D), BF), vm((T, R, WP), BF), vm((L, WP), BF), vm((8, D), F32),
        vm((T, 1, F), F32),
        vm((T, D, F), BF), vm((T, F, D), BF), vm((T, WP, D), BF), vm((WP, L), F32),
        vm((L, 3 * WP), BF),
        vm((D, 3 * WP), F32), vm((2, D, 3 * WP), BF), vm((8, 3 * WP), F32),
    ]
    for shift in (1, 1, 2, 3):
        scratch += [vm((n, r >> shift, w), BF) for r, w, n in sizes]
        if shift == 2:
            scratch[-1] = vm((3, 2, D >> 3, 3 * WP), BF)
    scratch += [vm((T - 1, r >> 3, w), BF) for r, w, n in sizes[:3]] + [vm((1, D >> 3, 3 * WP), BF)]
    more = G.nbits - 2
    PD = BF if G.PR % 16 == 0 else F32
    scratch += [vm((more, n, r >> 3, w) if more else (1, 1, 16, 128), BF) for r, w, n in sizes]
    scratch += [vm((r, w), BF) for r, w, n in sizes]
    scratch += [
        vm((T, R // 2, D), BF), vm((T, R // 2, D), BF), vm((T, R // 2, D), PD),
        vm((H, max(H - 1, 1), R // 2, D), BF), vm((2 * H, R // 2, D), BF), vm((H, R // 2, D), BF),
        vm((R, D), BF), vm((T, 3, R // 8, D), PD), vm((T, R // 8, D), PD),
        vm((T, max(R // 16, 8), D) if more else (1, 8, 128), PD),
        vm((T, max(R // 32, 8), D) if more else (1, 8, 128), PD), vm((T, G.PR, D), PD),
        vm((G.PR, D), F32), vm((V, D), F32), vm((1 + nplane + T - 1, V, D), F32),
        vm((2, 8, 3 * WP), F32), vm((nplane + 1, 2, 8, 3 * WP), F32), dma(NSEM),
    ]
    outs = [
        ((R, D), BF), ((R, D), BF), ((G.PR, D), F32), ((D, 3 * WP), BF),
        ((WP, D), BF), ((D, F), BF), ((F, D), BF), ((16, D), F32),
    ]
    anyspec = pl.BlockSpec(memory_space=pl.ANY)
    results = pl.pallas_call(
        functools.partial(layer_kernel, G),
        out_shape=tuple(jax.ShapeDtypeStruct(s, d) for s, d in outs),
        in_specs=[SM] + [anyspec] * 7 + [VM] * 8,
        out_specs=tuple([anyspec] * 7 + [VM]),
        scratch_shapes=scratch,
        compiler_params=pltpu.CompilerParams(
            vmem_limit_bytes=63 << 20, collective_id=0, has_side_effects=True
        ),
        name="layer",
    )(lengths, inputs, teacher, wq, inner_weight, outer_weight, wp, positions, query_value_bias,
      inner_bias, output_bias, first_gain, first_shift, outer_bias, second_gain, second_shift)
    finals = [
        ((R, D), BF), ((R, D), BF), ((G.PR, D), F32), ((3, D, W), F32), ((2, W), F32),
        ((W, D), F32), ((D, F), F32), ((F, D), F32), ((F,), F32),
    ] + [((D,), F32)] * 6
    (out, igrad, pgrad, qg, qvg, og, ig, ug, ibg, *vs) = pl.pallas_call(
        functools.partial(emit_kernel, G),
        out_shape=tuple(jax.ShapeDtypeStruct(s, d) for s, d in finals),
        in_specs=[VM] * 8,
        out_specs=tuple([VM] * 15),
        compiler_params=pltpu.CompilerParams(vmem_limit_bytes=63 << 20),
        name="emit",
    )(*results)
    return (
        out, igrad, pgrad, jnp.transpose(qg, (1, 0, 2)), qvg, og, vs[0], vs[1], vs[2],
        ig, ibg, ug, vs[3], vs[4], vs[5],
    )


def solution(mesh):
    rows = P(("dp", "tensor"), None)
    specs = (
        rows, rows, P(), P(), P(None, None, "tensor"), P(None, "tensor"), P("tensor", None), P(),
        P(), P(), P(None, "tensor"), P("tensor"), P("tensor", None), P(), P(), P(),
    )
    outs = (
        rows, rows, rows, P(None, None, "tensor"), P(None, "tensor"), P("tensor", None), P(), P(),
        P(), P(None, "tensor"), P("tensor"), P("tensor", None), P(), P(), P(),
    )

    def step(*args):
        G = Geo(mesh, args[2].shape[0], args[3].shape[0], args[0].shape[1], args[11].shape[0])
        body = jax.shard_map(
            functools.partial(on_device, G), mesh=mesh, in_specs=specs, out_specs=outs,
            check_vma=False,
        )
        return body(*args)

    return step
```

```python
import functools
import math

import jax
import jax.numpy as jnp
from jax import lax
from jax.experimental import pallas as pl
from jax.experimental.pallas import tpu as pltpu
from jax.sharding import PartitionSpec as P

HD = 64
EPS = 1e-05
NSEM = 480
NEG = -1e30
BF = jnp.bfloat16
F32 = jnp.float32
MESH = pl.DeviceIdType.MESH
VM = pl.BlockSpec(memory_space=pltpu.VMEM)
SM = pl.BlockSpec(memory_space=pltpu.SMEM)


class Geo:
    def __init__(self, mesh, slots, seq, width, hidden):
        self.T = mesh.shape["tensor"]
        self.DP = mesh.shape["dp"]
        self.H = self.T // 2
        self.NC = self.DP // 2
        self.nbits = self.NC.bit_length() - 1
        self.slots = slots
        self.L = seq
        self.D = width
        self.FF = hidden
        self.R = seq // self.T
        self.W = width // self.T
        self.WP = max(self.W, 128)
        self.NH = self.W // HD
        self.F = hidden // self.T
        self.PR = seq // (self.DP * self.T)


class Co:
    def __init__(self, G):
        self.dp = lax.axis_index("dp")
        self.z = lax.axis_index("tensor")
        self.c = self.dp % 2
        self.col = self.dp // 2
        self.g = self.z // G.H
        self.zz = self.z - self.g * G.H
        self.other = (self.z + G.H) % G.T
        self.native = self.c == self.g
        self.swapped = self.c != self.g
        self.hb = (self.z + self.c * G.H) % G.T
        self.ob = self.own_block(G, self.z, self.c)
        self.slot = 2 * self.col + self.g
        self.mate = self.dp + 1 - 2 * self.c
        b0 = self.col % 2
        b1 = (self.col // 2) % 2
        self.bf = b0 + self.c * (b1 - b0)
        self.bs = b1 + self.c * (b0 - b1)
        wf = 1 + self.c
        ws = 2 - self.c
        self.dpf = self.dp + 2 * wf * (1 - 2 * self.bf)
        self.dps = self.dp + 2 * ws * (1 - 2 * self.bs)
        self.dpd = self.dpf + self.dps - self.dp

    @staticmethod
    def own_block(G, z, c):
        d = c - z // G.H
        return (z + d * d * G.H) % G.T

    def extra(self, G, bit):
        b = (self.col // (1 << bit)) % 2
        return self.dp + (2 << bit) * (1 - 2 * b)

    def piece(self):
        return self.c * 4 + self.bs * 2 + self.bf


def owner(G, co, b):
    out = (b // G.H - co.g) * (b // G.H - co.g)
    return co.g + out * (1 - 2 * co.g), (b + out * G.H) % G.T


class Net:
    def __init__(self, ref):
        self.ref = ref
        self.n = 0
        self.items = []

    def take(self, n=1):
        base = self.n
        self.n += n
        return base

    def sem(self, i):
        return self.ref.at[i]

    def remote(self, src, dst, dev, cond=None, ss=None, rs=None):
        ss = self.take() if ss is None else ss
        rs = self.take() if rs is None else rs
        return Copy(self, src, dst, dev, ss, rs, cond)

    def local(self, src, dst, cond=None):
        return Copy(self, src, dst, None, self.take(), None, cond)

    def drain(self):
        for copy in self.items:
            copy.guard(copy.wait_sent)
        self.items = []


class Copy:
    def __init__(self, net, src, dst, dev, ss, rs, cond):
        self.net, self.src, self.dst, self.dev = net, src, dst, dev
        self.ss, self.rs, self.cond = ss, rs, cond

    def make(self):
        net = self.net
        if self.dev is None:
            return pltpu.make_async_copy(self.src(), self.dst(), net.sem(self.ss))
        return pltpu.make_async_remote_copy(
            src_ref=self.src(), dst_ref=self.dst(), send_sem=net.sem(self.ss),
            recv_sem=net.sem(self.rs), device_id=self.dev, device_id_type=MESH,
        )

    def guard(self, fn):
        if self.cond is None:
            fn()
        else:
            pl.when(self.cond)(fn)

    def start(self, hold=True):
        self.guard(lambda: self.make().start())
        if hold:
            self.net.items.append(self)
        return self

    def wait_sent(self):
        if self.dev is None:
            self.make().wait()
        else:
            self.make().wait_send()

    def got(self):
        self.make().wait_recv()


def column_partners(G, co):
    out = [(co.mate, co.z), (co.dpf, co.z), (co.dps, co.z), (co.dpd, co.z), (co.mate, co.other)]
    out += [(co.dp, (co.z + k) % G.T) for k in range(1, G.T)]
    out += [(co.mate, (co.z + k) % G.T) for k in range(1, G.T) if k != G.H]
    out += [(co.extra(G, b), co.z) for b in range(2, G.nbits)]
    return out


def lanes(shape):
    return lax.broadcasted_iota(jnp.int32, shape, len(shape) - 1)


def aug_base(h):
    return HD if h == 0 else 0


def dot(a, b):
    return lax.dot_general(a, b, (((1,), (0,)), ((), ())), preferred_element_type=F32)


def dot_nt(a, b):
    return lax.dot_general(a, b, (((1,), (1,)), ((), ())), preferred_element_type=F32)


def dot_tn(a, b):
    return lax.dot_general(a, b, (((0,), (0,)), ((), ())), preferred_element_type=F32)


def parts3(v):
    hi = v.astype(BF).astype(F32)
    mid = (v - hi).astype(BF).astype(F32)
    return hi, mid, v - hi - mid


def place3(base, lane, first, v):
    hi, mid, lo = parts3(v)
    base = jnp.where(lane == first, hi, base)
    base = jnp.where(lane == first + 1, mid, base)
    return jnp.where(lane == first + 2, lo, base)


def norm(v):
    centre = jnp.mean(v, axis=-1, keepdims=True)
    v = v - centre
    inv = lax.rsqrt(jnp.mean(v * v, axis=-1, keepdims=True) + EPS)
    return v * inv, inv


def norm_back(e, normal, inv):
    a = jnp.mean(e, axis=-1, keepdims=True)
    b = jnp.mean(e * normal, axis=-1, keepdims=True)
    return inv * (e - a - normal * b)


def colsum(v):
    return jnp.sum(v, axis=0, keepdims=True)


def al(v, n):
    return pl.multiple_of(v, n)


def layer_kernel(
    G, lengths, x, te, wq, wi, wo, wp, pos_in, qvbias, ibias, *rest,
):
    vectors = [v[...].astype(F32).reshape(1, G.D) for v in rest[:6]]
    layer_body(G, vectors, lengths, x, te, wq, wi, wo, wp, pos_in, qvbias, ibias, *rest[6:])


def layer_body(
    G, vectors, lengths, x, te, wq, wi, wo, wp, pos_in, qvbias, ibias,
    out, igrad, pgrad, qg, og, ig, ug, vout,
    xall, pos, emb, qa, ka, va, da, kt, acc, top, mixed, mixr,
    sm, wqm, wqo, wqh, wif, wof, wpf, smalls, teach,
    flow, hid, gpre, gfeed, gbr, gmid, osrc, gm, gmall, vsum, ibsum,
    dwi, dwo, dwp, dq, gp, dwq, dwqb, qsum,
    s0i, s0o, s0p, s0q, r0i, r0o, r0p, r0q, r1i, r1o, r1p, r1q, r2i, r2o, r2p, r2q,
    r3i, r3o, r3p, r3q, rxi, rxo, rxp, rxq, gi, go, gpp, gq,
    ec, hsum, hp, eo, eh, hsend, native_half, foreign, give, nat,
    ps1, ps2, px, py, pf, pr3, vb, vr, qb, qr,
    sem,
):
    co = Co(G)
    net = Net(sem)
    T, H, R, L, WP, NH, D, F = G.T, G.H, G.R, G.L, G.WP, G.NH, G.D, G.F
    z, c, g = co.z, co.c, co.g
    mate, step1, step2 = (co.mate, z), (co.dpf, z), (co.dps, z)
    length = lengths[co.slot]
    ge, dk, dv = xall, acc.at[0], acc.at[1]

    def rows(b, n=R):
        return pl.ds(al(b * R, R), n)

    pp = c * (G.DP // 2) + co.bf * (G.DP // 4) + co.bs * (G.DP // 8)
    for bit in range(2, G.nbits):
        pp = pp + ((co.col // (1 << bit)) % 2) * (G.DP // (4 << bit))
    flat = z * G.DP + pp
    pdp, pz = flat // T, flat % T
    away = jnp.logical_or(pdp != co.dp, pz != z)
    mine = co.dp * T + z
    fz, fp = mine // G.DP, mine % G.DP
    fc = fp // (G.DP // 2)
    f1 = (fp // (G.DP // 4)) % 2
    f2 = (fp // (G.DP // 8)) % 2
    fcol = (f1 + fc * (f2 - f1)) + 2 * (f2 + fc * (f1 - f2))
    for bit in range(2, G.nbits):
        fcol = fcol + ((fp // (G.DP // (4 << bit))) % 2) * (1 << bit)
    poscopy = net.local(lambda: pos_in, lambda: pos).start()
    bar = pltpu.get_barrier_semaphore()
    partners = column_partners(G, co)
    for dev in partners:
        pl.semaphore_signal(bar, inc=1, device_id=dev, device_id_type=MESH)

    @pl.when(away)
    def _():
        pl.semaphore_signal(bar, inc=1, device_id=(2 * fcol + fc, fz), device_id_type=MESH)

    pl.semaphore_wait(bar, len(partners) + away.astype(jnp.int32))

    bs, br = net.take(T), net.take(T)
    sm[...] = jnp.zeros(sm.shape, F32)
    sm[0:2, : G.W] = qvbias[...].astype(F32)
    sm[2:3, :F] = ibias[...].astype(F32).reshape(1, F)
    small_own = net.local(lambda: sm, lambda: smalls.at[z]).start(hold=False)
    small = [
        net.remote(lambda: sm, lambda: smalls.at[z], (co.dp, (z + k) % T)).start()
        for k in range(1, T)
    ]
    p = co.piece()

    def weight_chain(src, dst, slab, k):
        size = src.shape[-2] // 8

        def view(ref, s, first, count):
            where = pl.ds(al(first * size, size), count * size)
            if s is None:
                return ref.at[:, where] if slab is None else ref.at[where]
            return ref.at[s, where]

        to = None if slab is None else z
        cps = [net.remote(lambda: view(src, None, p, 1), lambda: view(dst, to, p, 1), (co.dp, (z + k) % T))]
        for first, count, dev in ((p, 1, step1), (p // 2 * 2, 2, step2), (c * 4, 4, mate)):
            ref = lambda first=first, count=count: view(dst, slab, first, count)
            cps.append(net.remote(ref, ref, dev))
        return cps

    qchain = weight_chain(wq, wqo, None, H)
    qchain[0].start()
    q_own = net.local(lambda: wq, lambda: wqm).start(hold=False)
    wchains = []
    whole = ((wp, wpf), (wi, wif), (wo, wof))
    for src, dst in whole:
        net.local(lambda src=src: src, lambda dst=dst: dst.at[z]).start()
    for k in range(1, T):
        for src, dst in whole:
            wchains.append(weight_chain(src, dst, (z - k) % T, k))

    chunks = 2
    n = R // chunks
    xr = net.take(T * chunks)

    def order(r):
        if r == 0:
            return z
        if r < H:
            return g * H + (co.zz + r) % H
        k = r - H
        return (H - 1 - k) + (1 - g) * (2 * k + 1)

    blocks = [order(r) for r in range(T)]

    def block_at(r):
        out = blocks[0]
        for k in range(1, T):
            out = jnp.where(r == k, blocks[k], out)
        return out
    zb = H - 1 + c
    edge = jnp.logical_and(co.native, z == H - 1 + g)

    def xrow(b, ch):
        return lambda: xall.at[pl.ds(al(b * R + ch * n, n), n)]

    def xmine(ch):
        return lambda: x.at[pl.ds(ch * n, n)]

    def xsend(src, b, ch, dev, cond, ss=None):
        return net.remote(src, xrow(b, ch), dev, cond, rs=xr + b * chunks + ch, ss=ss)

    def swapped_sends(k):
        cond = jnp.logical_and(co.swapped, (z - zb) * (1 - 2 * c) == k + 1)
        return [xsend(xmine(ch), z, ch, (co.dp, zb), cond) for ch in range(chunks)]

    own_x = []
    for ch in range(chunks):
        for j in range(1, H):
            xsend(xmine(ch), z, ch, (co.dp, g * H + (co.zz + j) % H), co.native).start()
        xsend(xmine(ch), z, ch, mate, co.native).start()
        own_x.append(net.local(xmine(ch), xrow(z, ch), co.native).start(hold=False))
    for cp in swapped_sends(0):
        cp.start()

    tlocal = net.local(lambda: te, lambda: teach, co.native)
    CR = min(256, R)
    tswap = {}
    for off in range(0, R, CR):
        part = lambda ref, off=off: ref.at[pl.ds(off, CR)]
        tswap[off] = net.remote(
            lambda part=part: part(te), lambda part=part: part(teach), (co.mate, co.other),
            co.swapped,
        )

    def project(b):
        CH = min(256, R)
        qb_, vb_ = smalls[co.hb, 0:1, :WP], smalls[co.hb, 1:2, :WP]

        def step(i, carry):
            first = b * R + i * CH
            rr = pl.ds(al(first, CH), CH)
            low = (xall[rr, :].astype(F32) + pos[rr, :].astype(F32)).astype(BF)
            emb[rr, :] = low
            pr = dot(low, wqh[...])
            q = (pr[:, :WP] + qb_).astype(BF).astype(F32) * (1.0 / math.sqrt(HD))
            k = pr[:, WP : 2 * WP].astype(BF).astype(F32)
            v = (pr[:, 2 * WP :] + vb_).astype(BF).astype(F32)
            lane = lanes((CH, WP))
            place = lax.broadcasted_iota(jnp.int32, (CH, WP), 0) + first
            limit = jnp.where(place < length, 0.0, NEG)
            for h in range(NH):
                a0 = aug_base(h)
                data = lane // HD == h
                ones = jnp.where((lane >= a0) & (lane < a0 + 4), 1.0, 0.0)
                qa[h, rr, :] = jnp.where(data, q, jnp.where(lane == a0, 1.0, 0.0)).astype(BF)
                ka[h, rr, :] = jnp.where(data, k, jnp.where(lane == a0, limit, ones)).astype(BF)
                va[h, rr, :] = jnp.where(data, v, ones).astype(BF)
                acc[h, rr, :] = jnp.zeros((CH, WP), F32)
                top[h, rr, :] = jnp.full((CH, WP), NEG, F32)
            return carry

        lax.fori_loop(0, R // CH, step, 0)

    def ftile(i, j, masked):
        qr, kr = rows(i), rows(j)
        for h in range(NH):
            s = dot_nt(qa[h, qr, :], ka[h, kr, :])
            if masked:
                below = lax.broadcasted_iota(jnp.int32, (R, R), 0) >= lanes((R, R))
                s = jnp.where(below, s, NEG)
            old = top[h, qr, :1]
            new = jnp.maximum(old, jnp.max(s, axis=-1, keepdims=True))
            e = jnp.exp(s - new).astype(BF)
            acc[h, qr, :] = acc[h, qr, :] * jnp.exp(old - new) + dot(e, va[h, kr, :])
            top[h, qr, :] = jnp.broadcast_to(new, (R, WP))

    def finalize(b):
        rr = rows(b)
        lane = lanes((R, WP))
        o = jnp.zeros((R, WP), F32)
        for h in range(NH):
            a0 = aug_base(h)
            total = acc[h, rr, a0 : a0 + 1]
            o = jnp.where(lane // HD == h, acc[h, rr, :] / total, o)
            lse = top[h, rr, :1] + jnp.log(total)
            q = qa[h, rr, :].astype(F32)
            qa[h, rr, :] = place3(q, lane, a0 + 1, -lse).astype(BF)
        mixed[rr, :] = o.astype(BF)

    def arrival(r, cond, pass_on):
        b = blocks[r]
        steps = []
        for ch in range(chunks):
            sends = []
            if pass_on:
                for j in range(1, H):
                    sends.append(xsend(xrow(b, ch), b, ch, (co.dp, g * H + (co.zz + j) % H), cond))
            sends.append(xsend(xrow(b, ch), b, ch, mate, cond))
            steps.append((xsend(xrow(b, ch), b, ch, mate, None, xr), sends))

        def act():
            for got, sends in steps:
                pl.when(cond)(got.got)
                for cp in sends:
                    cp.start()

        return act

    inner = jnp.logical_and(co.native, jnp.logical_not(edge))
    arrivals = {r: arrival(r, co.native if r < H else inner, False) for r in range(1, T)}
    early = {r: arrival(r, edge, True) for r in range(H, T)}
    from_mate = [
        [xsend(xrow(blocks[r], ch), blocks[r], ch, mate, None, xr) for ch in range(chunks)]
        for r in range(T)
    ]
    far = {k: swapped_sends(k) for k in range(1, H)}

    def mate_arrive(r):
        @pl.when(co.swapped)
        def _():
            for cp in from_mate[r]:
                cp.got()

    mr = net.take(T)
    mixed_out = []
    for r in range(T):
        oc, oz = owner(G, co, blocks[r])
        me = jnp.logical_and(oc == c, oz == z)
        src = lambda r=r: mixed.at[rows(blocks[r])]
        dst = lambda: mixr.at[co.hb]
        dev = (2 * co.col + oc, oz)
        mixed_out.append(net.remote(src, dst, dev, jnp.logical_not(me), rs=mr + co.hb))
        mixed_out.append(net.local(src, dst, me))

    poscopy.wait_sent()
    net.items.remove(poscopy)
    for cp in own_x:
        cp.guard(cp.wait_sent)

    qchain[0].got()
    qchain[1].start()
    for k in far:
        for cp in far[k]:
            cp.start()
    qchain[1].got()
    qchain[2].start()
    early[H]()
    for ch in wchains:
        ch[0].start()
    qchain[2].got()
    qchain[3].start()
    qchain[3].got()

    q_own.wait_sent()
    for j in range(3):
        wqh[:, j * WP : (j + 1) * WP] = jnp.where(c == 0, wqm[j], wqo[j])
    small_own.wait_sent()
    for cp in small:
        cp.got()


    def begin(r):
        if r == 0:
            mate_arrive(0)
            return
        arrivals[r]()
        mate_arrive(r)
        if r + 1 in early and r + 1 > H:
            early[r + 1]()

    def triangle(t):
        r = 0
        for k in range(1, T):
            r = r + (t >= k * (k + 1) // 2).astype(jnp.int32)
        return r, t - r * (r + 1) // 2

    ntiles = T * (T + 1) // 2

    def ftiles(t, carry):
        r, q = triangle(t)

        @pl.when(q == 0)
        def _():
            for k in range(T):
                pl.when(r == k)(functools.partial(begin, k))
            project(block_at(r))

        a, b = block_at(r), block_at(q)

        @pl.when(q < r)
        def _():
            ftile(jnp.maximum(a, b), jnp.minimum(a, b), False)

        @pl.when(q == r)
        def _():
            ftile(a, a, True)

        @pl.when(r == T - 1)
        def _():
            finalize(b)
            for k in range(T):

                @pl.when(q == k)
                def _():
                    mixed_out[2 * k].start()
                    mixed_out[2 * k + 1].start()

        for i, acts in polls.items():

            @pl.when(t == i)
            def _(acts=acts):
                for hop, n_ in acts:
                    hop_on(hop, n_)

        return carry

    def hop_on(hop, n_):
        wchains[n_][hop].got()
        wchains[n_][hop + 1].start()

    polls = {}
    hops = [(h_, n_) for h_ in range(3) for n_ in range(len(wchains))]
    if ntiles == 10:
        when = {1: [(0, 0)], 2: [(0, 1), (1, 0)], 5: [(0, 2), (1, 1), (2, 0)], 7: [(1, 2)], 8: [(2, 1)]}
        for i, acts in when.items():
            polls[i] = [(h_, 3 * n_ + m) for h_, n_ in acts for m in range(3)]
    polled = [a for acts in polls.values() for a in acts]

    lax.fori_loop(0, ntiles, ftiles, 0)
    tlocal.start()
    for cp in tswap.values():
        cp.start()

    for a in sorted(hops, key=lambda a: a[0] + a[1] // 3):
        if a not in polled:
            hop_on(*a)
    for ch in wchains:
        ch[3].got()
    net.items.remove(tlocal)
    for cp in net.items:
        if cp.dev is None:
            cp.guard(cp.wait_sent)
    net.items = [cp for cp in net.items if cp.dev is not None]
    for k in range(1, T):
        hb = (co.hb + k) % T
        net.remote(lambda: mixed.at[rows(0)], lambda hb=hb: mixr.at[hb], mate, rs=mr + hb, ss=mr).got()

    count = lengths[0]
    for i in range(1, G.slots):
        count = count + lengths[i]
    scale = (G.slots * L) / jnp.full((1, 1), count, jnp.int32).astype(F32)
    vsum[...] = jnp.zeros(vsum.shape, F32)
    ibsum[...] = jnp.zeros(ibsum.shape, F32)
    output_bias, g1, s1, outer_bias, g2, s2 = vectors
    CR = min(256, R)

    o_out = {}
    for off in range(0, R, CR):
        part = lambda ref, off=off: ref.at[pl.ds(off, CR)]
        o_out[off] = (
            net.local(lambda part=part: part(osrc), lambda part=part: part(out), co.native),
            net.remote(
                lambda part=part: part(osrc), lambda part=part: part(out), (co.mate, co.other),
                co.swapped,
            ),
        )

    def ffn(off):
        rr = pl.ds(off, CR)
        base = co.ob * R + off
        grows = pl.ds(al(base, CR), CR)
        branch = lax.fori_loop(
            0, T, lambda t, a: a + dot(mixr[t, rr, :], wpf[t]), jnp.zeros((CR, D), F32)
        )
        e = xall[grows, :].astype(F32) + pos[grows, :].astype(F32)
        n1, inv1 = norm(e + branch + output_bias)
        first = n1 * g1 + s1
        low = first.astype(BF)
        flow[rr, :] = low

        def up(t, a):
            pre = dot(low, wif[t]) + smalls[t, 2:3, :F]
            h = jnp.maximum(pre, 0.0).astype(BF)
            hid[t, rr, :] = h
            return a + dot(h, wof[t])

        feed = lax.fori_loop(0, T, up, jnp.zeros((CR, D), F32))
        n2, inv2 = norm(first + feed + outer_bias)
        result = n2 * g2 + s2
        osrc[rr, :] = result.astype(BF)
        for cp in o_out[off]:
            cp.start()
        pl.when(co.swapped)(tswap[off].got)
        if off == 0:
            tlocal.guard(tlocal.wait_sent)
        place = lax.broadcasted_iota(jnp.int32, (CR, 1), 0) + base
        valid = jnp.where(place < length, scale, 0.0)
        gr = valid * (result - teach[rr, :].astype(F32))
        gs = norm_back(gr * g2, n2, inv2)
        gf = gs.astype(BF)
        gfeed[rr, :] = gf

        def down(t, a):
            gh = dot_nt(gf, wof[t])
            gpt = jnp.where(hid[t, rr, :].astype(F32) > 0, gh, 0.0).astype(BF)
            gpre[t, rr, :] = gpt
            ibsum[t] += colsum(gpt.astype(F32))
            return a + dot_nt(gpt, wif[t])

        g_first = lax.fori_loop(0, T, down, gs)
        gv = norm_back(g_first * g1, n1, inv1)
        gmid[rr, :] = gv
        gb = gv.astype(BF)
        gbr[rr, :] = gb

        def mix(t, a):
            gm[t, rr, :] = dot_nt(gb, wpf[t]).astype(BF)
            return a

        lax.fori_loop(0, T, mix, 0)
        vsum[0:1] += colsum(gv)
        vsum[1:2] += colsum(g_first * n1)
        vsum[2:3] += colsum(g_first)
        vsum[3:4] += colsum(gs)
        vsum[4:5] += colsum(gr * n2)
        vsum[5:6] += colsum(gr)

    used = [cp for cp in net.items if all(cp is not own for own in tswap.values())]
    net.items = list(tswap.values())
    gmr = net.take(T * (R // CR))
    gm_in = []
    gm_own = []
    for i in range(R // CR):
        ffn(i * CR)
        if i == 0:
            for cp in used:
                cp.guard(cp.wait_sent)
        for k in range(T):
            m = (co.zz * 2 + c + k) % T
            c2, z2 = m % 2, g * H + m // 2
            hb2 = (z2 + c2 * H) % T
            src = lambda hb2=hb2, i=i: gm.at[hb2, pl.ds(i * CR, CR)]
            dst = lambda i=i: gmall.at[pl.ds(al(co.ob * R + i * CR, CR), CR)]
            if k == 0:
                gm_own.append(net.local(src, dst).start(hold=False))
                continue
            net.remote(src, dst, (2 * co.col + c2, z2), rs=gmr + k * (R // CR) + i).start()
            gm_in.append((k, i))


    def now(src, dst, dev, ss=None):
        return net.remote(src, dst, dev, ss=ss)

    quarter = co.bf * 2 + co.bs
    plane3 = (
        ((co.dpf, z), (1 - co.bf) * 2 + co.bs),
        ((co.dps, z), co.bf * 2 + 1 - co.bs),
        ((co.dpd, z), (1 - co.bf) * 2 + 1 - co.bs),
    )

    def scatter3(src, land):
        return [
            now(lambda piece=piece: src(piece), lambda j=j: land(j), dev)
            for j, (dev, piece) in enumerate(plane3)
        ]

    class Slabs:
        def __init__(self, X, k0, n, s0, r0, r1, r2, r3, rx, r3slot, stay):
            hr, q1, q2 = r0.shape[1], r1.shape[1], r2.shape[1]
            self.n, self.k0 = n, k0
            slabs = pl.ds(k0, n)
            self.start = now(
                lambda: X.at[slabs, pl.ds(al((1 - c) * hr, hr), hr)], lambda: r0.at[slabs], mate
            )
            self.s1 = now(
                lambda: s0.at[slabs, pl.ds(al((1 - co.bf) * q1, q1), q1)],
                lambda: r1.at[slabs], step1,
            )
            self.s2 = now(
                lambda: r1.at[slabs, pl.ds(al((1 - co.bs) * q2, q2), q2)],
                lambda: r2.at[slabs], step2,
            )
            self.over = [
                now(lambda k=k: r2.at[k], lambda k=k: r3.at[r3slot(k)], (co.dp, (z + k_z) % T))
                for k, k_z in stay
                if k0 <= k < k0 + n
            ]
            self.extra = [
                now(lambda: r2.at[slabs], lambda b=b: rx.at[b - 2, slabs], (co.extra(G, b), z))
                for b in range(2, G.nbits)
            ]
            self.refs = X, s0, r0, r1, r2, rx, hr, q1, q2

        def a0(self):
            X, s0, r0, r1, r2, rx, hr, q1, q2 = self.refs
            self.start.got()
            for k in range(self.k0, self.k0 + self.n):
                kept = X[k, pl.ds(al(c * hr, hr), hr), :]
                s0[k] = (kept.astype(F32) + r0[k].astype(F32)).astype(BF)

        def go(self):
            self.s1.start()

        def a1(self):
            X, s0, r0, r1, r2, rx, hr, q1, q2 = self.refs
            self.s1.got()
            for k in range(self.k0, self.k0 + self.n):
                kept = s0[k, pl.ds(al(co.bf * q1, q1), q1), :]
                r1[k] = (kept.astype(F32) + r1[k].astype(F32)).astype(BF)
            self.s2.start()

        def a2(self):
            X, s0, r0, r1, r2, rx, hr, q1, q2 = self.refs
            self.s2.got()
            for k in range(self.k0, self.k0 + self.n):
                kept = r1[k, pl.ds(al(co.bs * q2, q2), q2), :]
                r2[k] = (kept.astype(F32) + r2[k].astype(F32)).astype(BF)
            for m, cp in enumerate(self.extra):
                cp.start(hold=False)
                cp.got()
                cp.wait_sent()
                for k in range(self.k0, self.k0 + self.n):
                    r2[k] = (r2[k].astype(F32) + rx[m, k].astype(F32)).astype(BF)
            for cp in self.over:
                cp.start()

    class Back:
        def __init__(self, chains, r2, r3, gx, dst):
            q2 = r2.shape[1]
            self.chains, self.r2, self.r3 = chains, r2, r3

            def place(width, first):
                return lambda: gx.at[pl.ds(al(first * q2, q2), width * q2)]

            own = c * 4 + co.bf * 2 + co.bs
            self.own = place(1, own)
            self.back = []
            for width, first, dev in ((1, own, step2), (2, own // 2 * 2, step1), (4, c * 4, mate)):
                self.back.append(now(place(width, first), place(width, first), dev))
            self.end = net.local(lambda: gx, lambda: dst)

        def a3(self):
            tot = self.r2[0].astype(F32)
            for k, cp in enumerate(cp for ch in self.chains for cp in ch.over):
                cp.got()
                tot = tot + self.r3[k].astype(F32)
            self.own()[...] = tot.astype(BF)
            self.back[0].start()

        def a4(self):
            self.back[0].got()
            self.back[1].start()

        def a5(self):
            self.back[1].got()
            self.back[2].start()

        def a6(self):
            self.back[2].got()
            self.end.start()

    to_z = [(k, k) for k in range(1, T)]
    minus = lambda k: k - 1
    ks = list(range(1, T)) + [0]
    co_ = [Slabs(dwo, k, 1, s0o, r0o, r1o, r2o, r3o, rxo, minus, to_z) for k in ks]
    ci_ = [Slabs(dwi, k, 1, s0i, r0i, r1i, r2i, r3i, rxi, minus, to_z) for k in ks]
    cp_ = Slabs(dwp, 0, T, s0p, r0p, r1p, r2p, r3p, rxp, minus, to_z)
    slabs = [ch for pair in zip(co_[:-1], ci_[:-1]) for ch in pair] + [co_[-1], ci_[-1], cp_]
    back_o = Back(co_, r2o, r3o, go, ug)
    back_i = Back(ci_, r2i, r3i, gi, ig)
    back_p = Back([cp_], r2p, r3p, gpp, og)

    def grads(i, carry):
        k = jnp.where(i == T - 1, 0, i + 1)
        t = (z + k) % T
        dwo[k] = dot_tn(hid[t], gfeed[...]).astype(BF)
        dwi[k] = dot_tn(flow[...], gpre[t]).astype(BF)
        dwp[k] = dot_tn(mixr[t], gbr[...]).astype(BF)
        for n_ in range(T):

            @pl.when(i == n_)
            def _():
                co_[n_].start.start()
                ci_[n_].start.start()

        return carry

    lax.fori_loop(0, T, grads, 0)
    cp_.start.start()

    vb[...] = jnp.zeros(vb.shape, F32)
    vb[0:6, :] = vsum[0:6, :]
    for t in range(T):
        vb[8 + t : 9 + t, :F] = ibsum[t]

    def sum_chain(v, r, devs):
        cps = [now(lambda: v, lambda i=i: r.at[i], dev) for i, dev in enumerate(devs)]

        def step(i):
            def act():
                cps[i].got()
                cps[i].wait_sent()
                v[...] += r[i]
                if i + 1 < len(cps):
                    cps[i + 1].start(hold=False)

            return act

        return cps[0], [step(i) for i in range(len(cps))]

    plane = [step1, step2] + [(co.extra(G, b), z) for b in range(2, G.nbits)]
    vstart, vchain = sum_chain(vb, vr, [mate] + plane)
    vstart.start(hold=False)
    nv = len(vchain)
    vover = [
        now(lambda: vb, lambda k=k: vr.at[nv + k - 1], (co.dp, (z + k) % T))
        for k in range(1, T)
    ]

    def vz():
        for cp in vover:
            cp.start(hold=False)

    def vdone():
        for cp in vover:
            cp.got()
            cp.wait_sent()
        for k in range(1, T):
            vb[...] += vr[nv + k - 1]
        vout[0:8, :] = vb[0:8, :]
        vrow = lax.broadcasted_iota(jnp.int32, vb.shape, 0)
        vout[8:9, :] = colsum(jnp.where(vrow == 8 + z, vb[...], 0.0))

    vchain = vchain + [vz, vdone]

    for i, ch in enumerate(slabs):
        ch.a0()
        if i < 2:
            ch.go()
    for k, i in gm_in:
        net.remote(
            lambda: gm.at[0, pl.ds(0, CR)], lambda: gmall.at[pl.ds(0, CR)], mate,
            rs=gmr + k * (R // CR) + i, ss=gmr,
        ).got()
    for cp in gm_own:
        cp.wait_sent()


    def prepare(i, carry):
        CH = min(256, R)
        rr = pl.ds(al(i * CH, CH), CH)
        gg = gmall[rr, :].astype(F32)
        prod = gg * mixed[rr, :].astype(F32)
        lane = lanes((CH, WP))
        k = jnp.zeros((CH, WP), F32)
        for h in range(NH):
            a0 = aug_base(h)
            data = lane // HD == h
            delta = jnp.sum(jnp.where(data, prod, 0.0), axis=-1, keepdims=True)
            base = place3(jnp.zeros((CH, WP), F32), lane, a0 + 1, -delta)
            da[h, rr, :] = jnp.where(data, gg, base).astype(BF)
            k = jnp.where(data, ka[h, rr, :].astype(F32), k)
        kt[:, rr] = k.T.astype(BF)
        zero = jnp.zeros((CH, WP), F32)
        dk[rr, :] = zero
        dv[rr, :] = zero
        dq[:, rr] = zero.T
        return carry

    lax.fori_loop(0, L // min(256, R), prepare, 0)

    def btile(i, j, masked):
        qr, kr = rows(i), rows(j)
        lane = lanes((R, WP))
        sub = lax.broadcasted_iota(jnp.int32, (WP, R), 0)
        dks, dvs, dqs = [], [], []
        for h in range(NH):
            q, d = qa[h, qr, :], da[h, qr, :]
            pm = jnp.exp(dot_nt(ka[h, kr, :], q))
            if masked:
                above = lax.broadcasted_iota(jnp.int32, (R, R), 0) <= lanes((R, R))
                pm = jnp.where(above, pm, 0.0)
            ds = (pm * dot_nt(va[h, kr, :], d)).astype(BF)
            dvs.append(dot(pm.astype(BF), d))
            dks.append(dot(ds, q))
            dqs.append(dot(kt[:, kr], ds))
        if NH == 1:
            dk[kr, :] += dks[0]
            dv[kr, :] += dvs[0]
            dq[:, qr] += dqs[0]
        else:
            dk[kr, :] += jnp.where(lane < HD, dks[0], dks[1])
            dv[kr, :] += jnp.where(lane < HD, dvs[0], dvs[1])
            dq[:, qr] += jnp.where(sub < HD, dqs[0], dqs[1])

    dwq[...] = jnp.zeros(dwq.shape, F32)
    qsum[...] = jnp.zeros(qsum.shape, F32)

    def complete(b):
        rr = rows(b)
        keep = lanes((R, WP)) < G.W
        q = dq[:, rr].T * (1.0 / math.sqrt(HD))
        sums = []
        for n_, part in enumerate((q, dk[rr, :], dv[rr, :])):
            part = jnp.where(keep, part, 0.0).astype(BF)
            gp[rr, n_ * WP : (n_ + 1) * WP] = part
            sums.append(colsum(part.astype(F32)))
        gg = gp[rr, :]
        back = dot_nt(gg, wqh[...])
        ge[rr, :] = back.astype(BF)
        oc, oz = owner(G, co, b)

        @pl.when(jnp.logical_and(oc == c, oz == z))
        def _():
            ge[rr, :] = (back + gmid[...]).astype(BF)

        dwq[...] += dot_tn(emb[rr, :], gg)
        qsum[0:1, :] += jnp.concatenate(sums, axis=1)

    order_b = [(T - 1 - s_) + g * (2 * s_ - T + 1) for s_ in range(T)]
    ends = [sum(T - i for i in range(s_ + 1)) - 1 for s_ in range(T)]
    half = R // 2
    edge_z = H - 1 + g
    at_edge = z == edge_z
    eh_sem = net.take(max(H - 1, 1))

    def slot_of(z_to):
        return (co.zz - (z_to - g * H) + H - 1) % H

    class Rows:
        def __init__(self, s_):
            b = order_b[s_]
            self.s, self.b, self.inside = s_, b, s_ >= H
            self.core = net.remote(
                lambda: ge.at[pl.ds(al(b * R + (1 - c) * half, half), half)],
                lambda: ec.at[s_], mate,
            )
            h = lambda: hsum.at[s_]
            if self.inside:
                slot, self.base = slot_of(b), eh_sem
                self.home_chip = z == b
                self.over = net.remote(
                    h, lambda: eh.at[slot], (co.dp, b), jnp.logical_not(self.home_chip),
                    rs=self.base + slot,
                )
            else:
                slot, self.base = slot_of(edge_z), net.take(max(H - 1, 1))
                self.over = net.remote(
                    h, lambda: eo.at[s_, slot], (co.dp, edge_z), jnp.logical_not(at_edge),
                    rs=self.base + slot,
                )
                self.home = net.remote(
                    lambda: hsend.at[s_], lambda: foreign, (co.dp, b), at_edge, rs=f_sem
                )

        def k0(self):
            self.core.start()

        def k1(self):
            s_ = self.s
            self.core.got()
            own = ge[pl.ds(al(self.b * R + c * half, half), half), :].astype(F32)
            hsum[s_] = (own + ec[s_].astype(F32)).astype(BF)
            self.over.start()

        def collect(self, land):
            total = hsum[self.s].astype(F32)
            for j in range(H - 1):
                net.remote(
                    lambda: hsum.at[0], lambda: land(j), mate, rs=self.base + j, ss=self.base
                ).got()
                total = total + land(j)[...].astype(F32)
            return total.astype(BF)

        def kx(self):
            @pl.when(at_edge)
            def _():
                hsend[self.s] = self.collect(lambda j: eo.at[self.s, j])

            self.home.start()

        def ky(self):
            @pl.when(self.home_chip)
            def _():
                native_half[...] = self.collect(lambda j: eh.at[j])

    f_sem = net.take()
    parts_ = [Rows(s_) for s_ in range(T)]
    foreign_in = net.remote(lambda: hsend.at[0], lambda: foreign, mate, rs=f_sem, ss=f_sem)
    to_mate = net.remote(
        lambda: give, lambda: nat.at[pl.ds(al(c * half, half), half)], mate
    )
    from_mate_half = net.remote(
        lambda: give, lambda: nat.at[pl.ds(al((1 - c) * half, half), half)], mate,
        ss=to_mate.ss, rs=to_mate.rs,
    )
    q2p = half // 4
    p_rs = scatter3(lambda piece: hp.at[pl.ds(al(piece * q2p, q2p), q2p)], lambda j: ps1.at[j])
    p_more = []
    size = q2p
    for n_, bit in enumerate(range(2, G.nbits)):
        size = size // 2
        bb = (co.col // (1 << bit)) % 2
        src = ps2 if n_ == 0 else (px if n_ % 2 == 1 else py)
        dst = px if n_ % 2 == 0 else py
        cp = net.remote(
            lambda src=src, bb=bb, size=size: src.at[pl.ds(al((1 - bb) * size, 8), size)],
            lambda dst=dst, size=size: dst.at[pl.ds(0, size)], (co.extra(G, bit), z),
        )
        p_more.append((cp, src, dst, bb, size))
    p_last = p_more[-1][2] if p_more else ps2
    p_fin = net.remote(lambda: p_last.at[pl.ds(0, G.PR)], lambda: pf, (pdp, pz), away)

    def p_first():
        foreign_in.got()
        own, other_ = native_half[...], foreign[...]
        give[...] = jnp.where(co.native, other_, own)
        to_mate.start()
        nat[pl.ds(al(c * half, half), half), :] = jnp.where(co.native, own, other_)
        hp[...] = (own.astype(F32) + other_.astype(F32)).astype(hp.dtype)
        for cp in p_rs:
            cp.start()

    def p_second():
        total = hp[pl.ds(al(quarter * q2p, q2p), q2p), :].astype(F32)
        for j, cp in enumerate(p_rs):
            cp.got()
            total = total + ps1[j].astype(F32)
        ps2[...] = total.astype(ps2.dtype)
        for cp, src, dst, bb, size in p_more:
            cp.start()
            cp.got()
            kept = src[pl.ds(al(bb * size, 8), size), :].astype(F32)
            dst[0:size, :] = (kept + dst[0:size, :].astype(F32)).astype(dst.dtype)
        p_fin.start()

    def p_third():
        pl.when(away)(p_fin.got)

        @pl.when(jnp.logical_not(away))
        def _():
            pf[...] = p_last[0 : G.PR, :]

        pr3[...] = pf[...].astype(F32)
        net.local(lambda: pr3, lambda: pgrad).start()

    def igrad_out():
        from_mate_half.got()
        net.local(lambda: nat, lambda: igrad).start()

    def run(chain, i):
        chain[i]()

    jobs = {("v", i): act for i, act in enumerate(vchain)}
    for i, ch in enumerate(slabs):
        if i >= 2:
            jobs["s", i] = ch.go
        jobs["1", i] = ch.a1
        jobs["2", i] = ch.a2
    for name, bk in (("o", back_o), ("i", back_i), ("p", back_p)):
        for n_, act in enumerate((bk.a3, bk.a4, bk.a5, bk.a6)):
            jobs[name, n_] = act
    for rw in parts_:
        for name in ("k0", "k1", "ky" if rw.inside else "kx"):
            jobs[name, rw.s] = getattr(rw, name)
    plan = {
        0: [],
        1: [("v", 0)],
        2: [],
        3: [("k0", 0), ("v", 1)],
        4: [("k1", 0)],
        5: [("v", 2), ("v", 3)],
        6: [("k0", 1)],
        7: [("k1", 1), ("kx", 0)],
        8: [("k0", 2), ("v", 4)],
        9: [("k0", 3), ("k1", 2), ("kx", 1)],
    }
    for i in range(10):
        plan[i] += [("1", i), ("2", i - 2), ("s", i + 2)]
    plan = {i: [key for key in acts if key in jobs] for i, acts in plan.items()}
    if ntiles != 10:
        plan = {e: [("k0", s_)] for s_, e in enumerate(ends)}
    left = [key for key in jobs if not any(key in acts for acts in plan.values())]
    def btiles(t, carry):
        s_, u = 0, t
        for k in range(1, T):
            past = (t > ends[k - 1]).astype(jnp.int32)
            s_ = s_ + past
            u = u - past * (T - k + 1)
        b = (T - 1 - s_) + g * (2 * s_ - T + 1)
        far = b - u + g * (2 * u)

        @pl.when(u == 0)
        def _():
            btile(b, b, True)

        @pl.when(u > 0)
        def _():
            btile(jnp.maximum(b, far), jnp.minimum(b, far), False)

        @pl.when(u == T - 1 - s_)
        def _():
            complete(b)

        for i in range(ntiles):
            acts = [jobs[key] for key in plan.get(i, ())]
            if acts:

                @pl.when(t == i)
                def _(acts=acts):
                    for act in acts:
                        act()

        return carry

    lax.fori_loop(0, ntiles, btiles, 0)

    dwqb[c] = dwq[...].astype(BF)
    hq = D // 2
    e8 = D // 8
    qstart = now(
        lambda: dwqb.at[c, pl.ds(al((1 - c) * hq, hq), hq)], lambda: r0q.at[c], mate
    ).start()
    q_rs = scatter3(lambda piece: s0q.at[:, pl.ds(al(piece * e8, e8), e8)], lambda j: r1q.at[j])
    q_extra = [
        now(lambda: r2q, lambda b=b: rxq.at[b - 2], (co.extra(G, b), z)) for b in range(2, G.nbits)
    ]
    q_over = now(lambda: r2q.at[1], lambda: r3q.at[0], (co.dp, co.other))
    q_own = lambda: gq.at[pl.ds(al((c * 4 + quarter) * e8, e8), e8)]
    q_ag = [now(q_own, q_own, dev) for dev, _ in plane3]
    q_half = lambda: gq.at[pl.ds(al(c * hq, hq), hq)]
    q_core = now(q_half, q_half, mate)
    q_out = net.local(lambda: gq, lambda: qg)

    def q_sum():
        total = s0q[:, pl.ds(al(quarter * e8, e8), e8), :].astype(F32)
        for j, cp in enumerate(q_rs):
            cp.got()
            total = total + r1q[j].astype(F32)
        r2q[...] = total.astype(BF)
        for m, cp in enumerate(q_extra):
            cp.start(hold=False)
            cp.got()
            cp.wait_sent()
            r2q[...] = (r2q[...].astype(F32) + rxq[m].astype(F32)).astype(BF)
        q_over.start()

    def q_back():
        q_over.got()
        q_own()[...] = (r2q[0].astype(F32) + r3q[0].astype(F32)).astype(BF)
        for cp in q_ag:
            cp.start()

    def q_join():
        for cp in q_ag:
            cp.got()
        q_core.start()

    def q_end():
        q_core.got()
        q_out.start()

    qb[c] = qsum[...]
    qmate = now(lambda: qb.at[c], lambda: qb.at[c], mate).start(hold=False)
    qsums, qchain2 = sum_chain(qb, qr, plane)
    qover = now(lambda: qb.at[1], lambda: qr.at[len(plane), 0], (co.dp, co.other))

    def rest(*names):
        for key in left:
            if key[0] in names:
                jobs[key]()

    def backs(n_):
        for key in left:
            if key[0] in "oip" and key[1] == n_:
                jobs[key]()

    rest("k1")
    pltpu.make_async_remote_copy(
        src_ref=dwqb.at[c, pl.ds(0, hq)], dst_ref=r0q.at[1 - c], send_sem=net.sem(qstart.ss),
        recv_sem=net.sem(qstart.rs), device_id=mate, device_id_type=MESH,
    ).wait_recv()
    s0q[c] = dwqb[c, pl.ds(al(c * hq, hq), hq), :]
    s0q[1 - c] = r0q[1 - c]
    for cp in q_rs:
        cp.start()
    qmate.got()
    qmate.wait_sent()
    qsums.start(hold=False)
    rest("s", "1", "v")
    rest("2")
    rest("kx")
    backs(0)
    qchain2[0]()
    rest("ky")
    p_first()
    q_sum()
    for i in range(1, len(qchain2)):
        qchain2[i]()
    qover.start(hold=False)
    backs(1)
    igrad_out()
    p_second()
    q_back()
    qover.got()
    qover.wait_sent()
    qb[0] += qr[len(plane), 0]
    vout[9:10, :WP] = qb[0, 0:1, :WP]
    vout[10:11, :WP] = qb[0, 0:1, 2 * WP :]
    backs(2)
    q_join()
    backs(3)
    p_third()
    q_end()
    for off in o_out:
        pl.when(co.swapped)(o_out[off][1].got)
    net.drain()

def emit_kernel(
    G, out_in, igrad_in, pgrad_in, qg_in, og_in, ig_in, ug_in, vin,
    out, igrad, pgrad, qg, qvg, og, ig, ug, ibg, v0, v1, v2, v3, v4, v5,
):
    out[...] = out_in[...]
    igrad[...] = igrad_in[...]
    pgrad[...] = pgrad_in[...]
    for j in range(3):
        qg[j] = qg_in[:, j * G.WP : j * G.WP + G.W].astype(F32)
    qvg[...] = vin[9:11, : G.W]
    og[...] = og_in[: G.W, :].astype(F32)
    ig[...] = ig_in[...].astype(F32)
    ug[...] = ug_in[...].astype(F32)
    ibg[...] = vin[8:9, : G.F].reshape(G.F)
    for i, v in enumerate((v0, v1, v2, v3, v4, v5)):
        v[...] = vin[i : i + 1, :].reshape(G.D)


def on_device(G, *args):
    (inputs, teacher, lengths, positions, qkv_weight, query_value_bias, output_weight, output_bias,
     first_gain, first_shift, inner_weight, inner_bias, outer_weight, outer_bias, second_gain,
     second_shift) = args
    T, R, D, L, W, WP, NH, F, H = G.T, G.R, G.D, G.L, G.W, G.WP, G.NH, G.F, G.H
    dma = lambda n: pltpu.SemaphoreType.DMA((n,))
    vm = pltpu.VMEM
    wq = jnp.pad(jnp.transpose(qkv_weight, (1, 0, 2)), ((0, 0), (0, 0), (0, WP - W)))
    wp = jnp.pad(output_weight, ((0, WP - W), (0, 0)))
    sizes = [(D, F, T), (F, D, T), (WP, D, T), (D, 3 * WP, 2)]
    nplane = G.nbits
    V = 8 + (T + 7) // 8 * 8
    scratch = [
        vm((L, D), BF), vm((L, D), BF), vm((L, D), BF),
        vm((NH, L, WP), BF), vm((NH, L, WP), BF), vm((NH, L, WP), BF), vm((NH, L, WP), BF),
        vm((WP, L), BF), vm((2, L, WP), F32), vm((NH, L, WP), F32), vm((L, WP), BF),
        vm((T, R, WP), BF),
        vm((8, D), F32), vm((3, D, WP), BF), vm((3, D, WP), BF), vm((D, 3 * WP), BF),
        vm((T, D, F), BF), vm((T, F, D), BF),
        vm((T, WP, D), BF), vm((T, 8, D), F32), vm((R, D), BF),
        vm((R, D), BF), vm((T, R, F), BF), vm((T, R, F), BF), vm((R, D), BF), vm((R, D), BF),
        vm((R, D), F32), vm((R, D), BF), vm((T, R, WP), BF), vm((L, WP), BF), vm((8, D), F32),
        vm((T, 1, F), F32),
        vm((T, D, F), BF), vm((T, F, D), BF), vm((T, WP, D), BF), vm((WP, L), F32),
        vm((L, 3 * WP), BF),
        vm((D, 3 * WP), F32), vm((2, D, 3 * WP), BF), vm((8, 3 * WP), F32),
    ]
    for shift in (1, 1, 2, 3):
        scratch += [vm((n, r >> shift, w), BF) for r, w, n in sizes]
        if shift == 2:
            scratch[-1] = vm((3, 2, D >> 3, 3 * WP), BF)
    scratch += [vm((T - 1, r >> 3, w), BF) for r, w, n in sizes[:3]] + [vm((1, D >> 3, 3 * WP), BF)]
    more = G.nbits - 2
    PD = BF if G.PR % 16 == 0 else F32
    scratch += [vm((more, n, r >> 3, w) if more else (1, 1, 16, 128), BF) for r, w, n in sizes]
    scratch += [vm((r, w), BF) for r, w, n in sizes]
    scratch += [
        vm((T, R // 2, D), BF), vm((T, R // 2, D), BF), vm((R // 2, D), PD),
        vm((H, max(H - 1, 1), R // 2, D), BF), vm((max(H - 1, 1), R // 2, D), BF),
        vm((H, R // 2, D), BF), vm((R // 2, D), BF), vm((R // 2, D), BF), vm((R // 2, D), BF),
        vm((R, D), BF), vm((3, R // 8, D), PD), vm((R // 8, D), PD),
        vm((max(R // 16, 8), D) if more else (8, 128), PD),
        vm((max(R // 32, 8), D) if more else (8, 128), PD), vm((G.PR, D), PD),
        vm((G.PR, D), F32), vm((V, D), F32), vm((1 + nplane + T - 1, V, D), F32),
        vm((2, 8, 3 * WP), F32), vm((nplane + 1, 2, 8, 3 * WP), F32), dma(NSEM),
    ]
    outs = [
        ((R, D), BF), ((R, D), BF), ((G.PR, D), F32), ((D, 3 * WP), BF),
        ((WP, D), BF), ((D, F), BF), ((F, D), BF), ((16, D), F32),
    ]
    anyspec = pl.BlockSpec(memory_space=pl.ANY)
    results = pl.pallas_call(
        functools.partial(layer_kernel, G),
        out_shape=tuple(jax.ShapeDtypeStruct(s, d) for s, d in outs),
        in_specs=[SM] + [anyspec] * 7 + [VM] * 8,
        out_specs=tuple([anyspec] * 7 + [VM]),
        scratch_shapes=scratch,
        compiler_params=pltpu.CompilerParams(
            vmem_limit_bytes=63 << 20, collective_id=0, has_side_effects=True
        ),
        name="layer",
    )(lengths, inputs, teacher, wq, inner_weight, outer_weight, wp, positions, query_value_bias,
      inner_bias, output_bias, first_gain, first_shift, outer_bias, second_gain, second_shift)
    finals = [
        ((R, D), BF), ((R, D), BF), ((G.PR, D), F32), ((3, D, W), F32), ((2, W), F32),
        ((W, D), F32), ((D, F), F32), ((F, D), F32), ((F,), F32),
    ] + [((D,), F32)] * 6
    (out, igrad, pgrad, qg, qvg, og, ig, ug, ibg, *vs) = pl.pallas_call(
        functools.partial(emit_kernel, G),
        out_shape=tuple(jax.ShapeDtypeStruct(s, d) for s, d in finals),
        in_specs=[VM] * 8,
        out_specs=tuple([VM] * 15),
        compiler_params=pltpu.CompilerParams(vmem_limit_bytes=63 << 20),
        name="emit",
    )(*results)
    return (
        out, igrad, pgrad, jnp.transpose(qg, (1, 0, 2)), qvg, og, vs[0], vs[1], vs[2],
        ig, ibg, ug, vs[3], vs[4], vs[5],
    )


def solution(mesh):
    rows = P(("dp", "tensor"), None)
    specs = (
        rows, rows, P(), P(), P(None, None, "tensor"), P(None, "tensor"), P("tensor", None), P(),
        P(), P(), P(None, "tensor"), P("tensor"), P("tensor", None), P(), P(), P(),
    )
    outs = (
        rows, rows, rows, P(None, None, "tensor"), P(None, "tensor"), P("tensor", None), P(), P(),
        P(), P(None, "tensor"), P("tensor"), P("tensor", None), P(), P(), P(),
    )

    def step(*args):
        G = Geo(mesh, args[2].shape[0], args[3].shape[0], args[0].shape[1], args[11].shape[0])
        body = jax.shard_map(
            functools.partial(on_device, G), mesh=mesh, in_specs=specs, out_specs=outs,
            check_vma=False,
        )
        return body(*args)

    return step
```

```python
import functools
import math

import jax
import jax.numpy as jnp
from jax import lax
from jax.experimental import pallas as pl
from jax.experimental.pallas import tpu as pltpu
from jax.sharding import PartitionSpec as P

HD = 64
EPS = 1e-05
NEG = -1e30
BF = jnp.bfloat16
F32 = jnp.float32
MESH = pl.DeviceIdType.MESH
VM = pl.BlockSpec(memory_space=pltpu.VMEM)
SM = pl.BlockSpec(memory_space=pltpu.SMEM)


class Geo:
    def __init__(self, mesh, slots, seq, width, hidden):
        self.T = mesh.shape["tensor"]
        self.DP = mesh.shape["dp"]
        self.H = self.T // 2
        self.NC = self.DP // 2
        self.nbits = self.NC.bit_length() - 1
        self.slots = slots
        self.L = seq
        self.D = width
        self.FF = hidden
        self.R = seq // self.T
        self.W = width // self.T
        self.WP = max(self.W, 128)
        self.NH = self.W // HD
        self.F = hidden // self.T
        self.PR = seq // (self.DP * self.T)


class Co:
    def __init__(self, G):
        self.dp = lax.axis_index("dp")
        self.z = lax.axis_index("tensor")
        self.c = self.dp % 2
        self.col = self.dp // 2
        self.g = self.z // G.H
        self.zz = self.z - self.g * G.H
        self.other = (self.z + G.H) % G.T
        self.native = self.c == self.g
        self.swapped = self.c != self.g
        self.hb = (self.z + self.c * G.H) % G.T
        self.ob = self.own_block(G, self.z, self.c)
        self.slot = 2 * self.col + self.g
        self.mate = self.dp + 1 - 2 * self.c
        b0 = self.col % 2
        b1 = (self.col // 2) % 2
        self.bf = b0 + self.c * (b1 - b0)
        self.bs = b1 + self.c * (b0 - b1)
        wf = 1 + self.c
        ws = 2 - self.c
        self.dpf = self.dp + 2 * wf * (1 - 2 * self.bf)
        self.dps = self.dp + 2 * ws * (1 - 2 * self.bs)
        self.dpd = self.dpf + self.dps - self.dp

    @staticmethod
    def own_block(G, z, c):
        d = c - z // G.H
        return (z + d * d * G.H) % G.T

    def extra(self, G, bit):
        b = (self.col // (1 << bit)) % 2
        return self.dp + (2 << bit) * (1 - 2 * b)

    def piece(self):
        return self.c * 4 + self.bs * 2 + self.bf


def owner(G, co, b):
    out = (b // G.H - co.g) * (b // G.H - co.g)
    return co.g + out * (1 - 2 * co.g), (b + out * G.H) % G.T


class Net:
    def __init__(self, ref):
        self.ref = ref
        self.n = 0
        self.items = []

    def take(self, n=1):
        base = self.n
        self.n += n
        return base

    def sem(self, i):
        return self.ref.at[i]

    def remote(self, src, dst, dev, cond=None, ss=None, rs=None):
        ss = self.take() if ss is None else ss
        rs = self.take() if rs is None else rs
        return Copy(self, src, dst, dev, ss, rs, cond)

    def local(self, src, dst, cond=None):
        return Copy(self, src, dst, None, self.take(), None, cond)

    def drain(self):
        for copy in self.items:
            copy.guard(copy.wait_sent)
        self.items = []


class Copy:
    def __init__(self, net, src, dst, dev, ss, rs, cond):
        self.net, self.src, self.dst, self.dev = net, src, dst, dev
        self.ss, self.rs, self.cond = ss, rs, cond

    def make(self):
        net = self.net
        if self.dev is None:
            return pltpu.make_async_copy(self.src(), self.dst(), net.sem(self.ss))
        return pltpu.make_async_remote_copy(
            src_ref=self.src(), dst_ref=self.dst(), send_sem=net.sem(self.ss),
            recv_sem=net.sem(self.rs), device_id=self.dev, device_id_type=MESH,
        )

    def guard(self, fn):
        if self.cond is None:
            fn()
        else:
            pl.when(self.cond)(fn)

    def start(self, hold=True):
        self.guard(lambda: self.make().start())
        if hold:
            self.net.items.append(self)
        return self

    def wait_sent(self):
        if self.dev is None:
            self.make().wait()
        else:
            self.make().wait_send()

    def got(self):
        self.make().wait_recv()


def column_partners(G, co):
    out = [(co.mate, co.z), (co.dpf, co.z), (co.dps, co.z), (co.dpd, co.z), (co.mate, co.other)]
    out += [(co.dp, (co.z + k) % G.T) for k in range(1, G.T)]
    out += [(co.mate, (co.z + k) % G.T) for k in range(1, G.T) if k != G.H]
    out += [(co.extra(G, b), co.z) for b in range(2, G.nbits)]
    return out


def lanes(shape):
    return lax.broadcasted_iota(jnp.int32, shape, len(shape) - 1)


def aug_base(h):
    return HD if h == 0 else 0


def dot(a, b):
    return lax.dot_general(a, b, (((1,), (0,)), ((), ())), preferred_element_type=F32)


def dot_nt(a, b):
    return lax.dot_general(a, b, (((1,), (1,)), ((), ())), preferred_element_type=F32)


def dot_tn(a, b):
    return lax.dot_general(a, b, (((0,), (0,)), ((), ())), preferred_element_type=F32)


def parts3(v):
    hi = v.astype(BF).astype(F32)
    mid = (v - hi).astype(BF).astype(F32)
    return hi, mid, v - hi - mid


def place3(base, lane, first, v):
    hi, mid, lo = parts3(v)
    base = jnp.where(lane == first, hi, base)
    base = jnp.where(lane == first + 1, mid, base)
    return jnp.where(lane == first + 2, lo, base)


def norm(v):
    centre = jnp.mean(v, axis=-1, keepdims=True)
    v = v - centre
    inv = lax.rsqrt(jnp.mean(v * v, axis=-1, keepdims=True) + EPS)
    return v * inv, inv


def norm_back(e, normal, inv):
    a = jnp.mean(e, axis=-1, keepdims=True)
    b = jnp.mean(e * normal, axis=-1, keepdims=True)
    return inv * (e - a - normal * b)


def colsum(v):
    return jnp.sum(v, axis=0, keepdims=True)


def al(v, n):
    return pl.multiple_of(v, n)


def layer_kernel(
    G, lengths, x, te, wq, wi, wo, wp, pos_in, qvbias, ibias, *rest,
):
    vectors = [v[...].astype(F32).reshape(1, G.D) for v in rest[:6]]
    layer_body(G, vectors, lengths, x, te, wq, wi, wo, wp, pos_in, qvbias, ibias, *rest[6:])


def layer_body(
    G, vectors, lengths, x, te, wq, wi, wo, wp, pos_in, qvbias, ibias,
    out, igrad, pgrad, qg, og, ig, ug, vout,
    xall, pos, emb, qa, ka, va, da, kt, acc, top, mixed, mixr,
    sm, wqm, wqo, wqh, wif, wof, wpf, smalls, teach,
    flow, hid, gpre, gfeed, gbr, gmid, osrc, gm, gmall, vsum, ibsum,
    dwi, dwo, dwp, dq, gp, dwq, dwqb, qsum,
    s0i, s0o, s0p, s0q, r0i, r0o, r0p, r0q, r1i, r1o, r1p, r1q, r2i, r2o, r2p, r2q,
    r3i, r3o, r3p, r3q, rxi, rxo, rxp, rxq, gi, go, gpp, gq,
    ec, hsum, hp, eo, eh, hsend, native_half, foreign, give, nat,
    ps1, ps2, px, py, pf, pr3, vb, vr, qb, qr,
    sem,
):
    co = Co(G)
    net = Net(sem)
    T, H, R, L, WP, NH, D, F = G.T, G.H, G.R, G.L, G.WP, G.NH, G.D, G.F
    z, c, g = co.z, co.c, co.g
    mate, step1, step2 = (co.mate, z), (co.dpf, z), (co.dps, z)
    length = lengths[co.slot]
    ge, dk, dv = xall, acc.at[0], acc.at[1]

    def rows(b, n=R):
        return pl.ds(al(b * R, R), n)

    pp = c * (G.DP // 2) + co.bf * (G.DP // 4) + co.bs * (G.DP // 8)
    for bit in range(2, G.nbits):
        pp = pp + ((co.col // (1 << bit)) % 2) * (G.DP // (4 << bit))
    flat = z * G.DP + pp
    pdp, pz = flat // T, flat % T
    away = jnp.logical_or(pdp != co.dp, pz != z)
    mine = co.dp * T + z
    fz, fp = mine // G.DP, mine % G.DP
    fc = fp // (G.DP // 2)
    f1 = (fp // (G.DP // 4)) % 2
    f2 = (fp // (G.DP // 8)) % 2
    fcol = (f1 + fc * (f2 - f1)) + 2 * (f2 + fc * (f1 - f2))
    for bit in range(2, G.nbits):
        fcol = fcol + ((fp // (G.DP // (4 << bit))) % 2) * (1 << bit)
    poscopy = net.local(lambda: pos_in, lambda: pos).start()
    bar = pltpu.get_barrier_semaphore()
    partners = column_partners(G, co)
    for dev in partners:
        pl.semaphore_signal(bar, inc=1, device_id=dev, device_id_type=MESH)

    @pl.when(away)
    def _():
        pl.semaphore_signal(bar, inc=1, device_id=(2 * fcol + fc, fz), device_id_type=MESH)

    pl.semaphore_wait(bar, len(partners) + away.astype(jnp.int32))

    bs, br = net.take(T), net.take(T)
    sm[...] = jnp.zeros(sm.shape, F32)
    sm[0:2, : G.W] = qvbias[...].astype(F32)
    sm[2:3, :F] = ibias[...].astype(F32).reshape(1, F)
    small_own = net.local(lambda: sm, lambda: smalls.at[z]).start(hold=False)
    small = [
        net.remote(lambda: sm, lambda: smalls.at[z], (co.dp, (z + k) % T)).start()
        for k in range(1, T)
    ]
    p = co.piece()

    def weight_chain(src, dst, slab, k):
        size = src.shape[-2] // 8

        def view(ref, s, first, count):
            where = pl.ds(al(first * size, size), count * size)
            if s is None:
                return ref.at[:, where] if slab is None else ref.at[where]
            return ref.at[s, where]

        to = None if slab is None else z
        cps = [net.remote(lambda: view(src, None, p, 1), lambda: view(dst, to, p, 1), (co.dp, (z + k) % T))]
        for first, count, dev in ((p, 1, step1), (p // 2 * 2, 2, step2), (c * 4, 4, mate)):
            ref = lambda first=first, count=count: view(dst, slab, first, count)
            cps.append(net.remote(ref, ref, dev))
        return cps

    qchain = weight_chain(wq, wqo, None, H)
    qchain[0].start()
    q_own = net.local(lambda: wq, lambda: wqm).start(hold=False)
    wchains = []
    whole = ((wp, wpf), (wi, wif), (wo, wof))
    for src, dst in whole:
        net.local(lambda src=src: src, lambda dst=dst: dst.at[z]).start()
    for k in range(1, T):
        for src, dst in whole:
            wchains.append(weight_chain(src, dst, (z - k) % T, k))

    chunks = 2
    n = R // chunks
    xr = net.take(T * chunks)

    def order(r):
        if r == 0:
            return z
        if r < H:
            return g * H + (co.zz + r) % H
        k = r - H
        return (H - 1 - k) + (1 - g) * (2 * k + 1)

    blocks = [order(r) for r in range(T)]

    def block_at(r):
        out = blocks[0]
        for k in range(1, T):
            out = jnp.where(r == k, blocks[k], out)
        return out
    zb = H - 1 + c
    edge = jnp.logical_and(co.native, z == H - 1 + g)

    def xrow(b, ch):
        return lambda: xall.at[pl.ds(al(b * R + ch * n, n), n)]

    def xmine(ch):
        return lambda: x.at[pl.ds(ch * n, n)]

    def xsend(src, b, ch, dev, cond, ss=None):
        return net.remote(src, xrow(b, ch), dev, cond, rs=xr + b * chunks + ch, ss=ss)

    def swapped_sends(k):
        cond = jnp.logical_and(co.swapped, (z - zb) * (1 - 2 * c) == k + 1)
        return [xsend(xmine(ch), z, ch, (co.dp, zb), cond) for ch in range(chunks)]

    own_x = []
    for ch in range(chunks):
        for j in range(1, H):
            xsend(xmine(ch), z, ch, (co.dp, g * H + (co.zz + j) % H), co.native).start()
        xsend(xmine(ch), z, ch, mate, co.native).start()
        own_x.append(net.local(xmine(ch), xrow(z, ch), co.native).start(hold=False))
    for cp in swapped_sends(0):
        cp.start()

    tlocal = net.local(lambda: te, lambda: teach, co.native)
    CR = min(256, R)
    tswap = {}
    for off in range(0, R, CR):
        part = lambda ref, off=off: ref.at[pl.ds(off, CR)]
        tswap[off] = net.remote(
            lambda part=part: part(te), lambda part=part: part(teach), (co.mate, co.other),
            co.swapped,
        )

    def project(b):
        CH = min(256, R)
        qb_, vb_ = smalls[co.hb, 0:1, :WP], smalls[co.hb, 1:2, :WP]

        def step(i, carry):
            first = b * R + i * CH
            rr = pl.ds(al(first, CH), CH)
            low = (xall[rr, :].astype(F32) + pos[rr, :].astype(F32)).astype(BF)
            emb[rr, :] = low
            pr = dot(low, wqh[...])
            q = (pr[:, :WP] + qb_).astype(BF).astype(F32) * (1.0 / math.sqrt(HD))
            k = pr[:, WP : 2 * WP].astype(BF).astype(F32)
            v = (pr[:, 2 * WP :] + vb_).astype(BF).astype(F32)
            lane = lanes((CH, WP))
            place = lax.broadcasted_iota(jnp.int32, (CH, WP), 0) + first
            limit = jnp.where(place < length, 0.0, NEG)
            for h in range(NH):
                a0 = aug_base(h)
                data = lane // HD == h
                ones = jnp.where((lane >= a0) & (lane < a0 + 4), 1.0, 0.0)
                qa[h, rr, :] = jnp.where(data, q, jnp.where(lane == a0, 1.0, 0.0)).astype(BF)
                ka[h, rr, :] = jnp.where(data, k, jnp.where(lane == a0, limit, ones)).astype(BF)
                va[h, rr, :] = jnp.where(data, v, ones).astype(BF)
                acc[h, rr, :] = jnp.zeros((CH, WP), F32)
                top[h, rr, :] = jnp.full((CH, WP), NEG, F32)
            return carry

        lax.fori_loop(0, R // CH, step, 0)

    def ftile(i, j, masked):
        qr, kr = rows(i), rows(j)
        heads = range(NH)
        s = [dot_nt(qa[h, qr, :], ka[h, kr, :]) for h in heads]
        if masked:
            below = lax.broadcasted_iota(jnp.int32, (R, R), 0) >= lanes((R, R))
            s = [jnp.where(below, v, NEG) for v in s]
        old = [top[h, qr, :] for h in heads]
        new = [jnp.maximum(old[h], jnp.max(s[h], axis=-1, keepdims=True)) for h in heads]
        wide = [jnp.concatenate([new[h]] * (R // WP), axis=1) for h in heads]
        e = [jnp.exp(s[h] - wide[h]).astype(BF) for h in heads]
        more = [dot(e[h], va[h, kr, :]) for h in heads]
        for h in heads:
            acc[h, qr, :] = acc[h, qr, :] * jnp.exp(old[h] - new[h]) + more[h]
            top[h, qr, :] = new[h]

    def finalize(b):
        rr = rows(b)
        lane = lanes((R, WP))
        o = jnp.zeros((R, WP), F32)
        for h in range(NH):
            a0 = aug_base(h)
            total = acc[h, rr, a0 : a0 + 1]
            o = jnp.where(lane // HD == h, acc[h, rr, :] / total, o)
            lse = top[h, rr, :1] + jnp.log(total)
            q = qa[h, rr, :].astype(F32)
            qa[h, rr, :] = place3(q, lane, a0 + 1, -lse).astype(BF)
        mixed[rr, :] = o.astype(BF)

    def arrival(r, cond, pass_on):
        b = blocks[r]
        steps = []
        for ch in range(chunks):
            sends = []
            if pass_on:
                for j in range(1, H):
                    sends.append(xsend(xrow(b, ch), b, ch, (co.dp, g * H + (co.zz + j) % H), cond))
            sends.append(xsend(xrow(b, ch), b, ch, mate, cond))
            steps.append((xsend(xrow(b, ch), b, ch, mate, None, xr), sends))

        def act():
            for got, sends in steps:
                pl.when(cond)(got.got)
                for cp in sends:
                    cp.start()

        return act

    inner = jnp.logical_and(co.native, jnp.logical_not(edge))
    arrivals = {r: arrival(r, co.native if r < H else inner, False) for r in range(1, T)}
    early = {r: arrival(r, edge, True) for r in range(H, T)}
    from_mate = [
        [xsend(xrow(blocks[r], ch), blocks[r], ch, mate, None, xr) for ch in range(chunks)]
        for r in range(T)
    ]
    far = {k: swapped_sends(k) for k in range(1, H)}

    def mate_arrive(r):
        @pl.when(co.swapped)
        def _():
            for cp in from_mate[r]:
                cp.got()

    mr = net.take(T)
    mixed_out = []
    for r in range(T):
        oc, oz = owner(G, co, blocks[r])
        me = jnp.logical_and(oc == c, oz == z)
        src = lambda r=r: mixed.at[rows(blocks[r])]
        dst = lambda: mixr.at[co.hb]
        dev = (2 * co.col + oc, oz)
        mixed_out.append(net.remote(src, dst, dev, jnp.logical_not(me), rs=mr + co.hb))
        mixed_out.append(net.local(src, dst, me))

    poscopy.wait_sent()
    net.items.remove(poscopy)
    for cp in own_x:
        cp.guard(cp.wait_sent)

    qchain[0].got()
    qchain[1].start()
    for k in far:
        for cp in far[k]:
            cp.start()
    qchain[1].got()
    qchain[2].start()
    early[H]()
    for ch in wchains:
        ch[0].start()
    qchain[2].got()
    qchain[3].start()
    qchain[3].got()

    q_own.wait_sent()
    for j in range(3):
        wqh[:, j * WP : (j + 1) * WP] = jnp.where(c == 0, wqm[j], wqo[j])
    small_own.wait_sent()
    for cp in small:
        cp.got()


    def begin(r):
        if r == 0:
            mate_arrive(0)
            return
        arrivals[r]()
        mate_arrive(r)
        if r + 1 in early and r + 1 > H:
            early[r + 1]()

    def triangle(t):
        r = 0
        for k in range(1, T):
            r = r + (t >= k * (k + 1) // 2).astype(jnp.int32)
        return r, t - r * (r + 1) // 2

    ntiles = T * (T + 1) // 2

    def ftiles(t, carry):
        r, q = triangle(t)

        @pl.when(q == 0)
        def _():
            for k in range(T):
                pl.when(r == k)(functools.partial(begin, k))
            project(block_at(r))

        a, b = block_at(r), block_at(q)

        @pl.when(q < r)
        def _():
            ftile(jnp.maximum(a, b), jnp.minimum(a, b), False)

        @pl.when(q == r)
        def _():
            ftile(a, a, True)

        @pl.when(r == T - 1)
        def _():
            finalize(b)
            for k in range(T):

                @pl.when(q == k)
                def _():
                    mixed_out[2 * k].start()
                    mixed_out[2 * k + 1].start()

        for i, acts in polls.items():

            @pl.when(t == i)
            def _(acts=acts):
                for hop, n_ in acts:
                    hop_on(hop, n_)

        return carry

    def hop_on(hop, n_):
        wchains[n_][hop].got()
        wchains[n_][hop + 1].start()

    polls = {}
    hops = [(h_, n_) for h_ in range(3) for n_ in range(len(wchains))]
    if ntiles == 10:
        when = {1: [(0, 0)], 2: [(0, 1), (1, 0)], 5: [(0, 2), (1, 1), (2, 0)], 7: [(1, 2)], 8: [(2, 1)]}
        for i, acts in when.items():
            polls[i] = [(h_, 3 * n_ + m) for h_, n_ in acts for m in range(3)]
    polled = [a for acts in polls.values() for a in acts]

    lax.fori_loop(0, ntiles, ftiles, 0)
    tlocal.start()
    for cp in tswap.values():
        cp.start()

    for a in sorted(hops, key=lambda a: a[0] + a[1] // 3):
        if a not in polled:
            hop_on(*a)
    for ch in wchains:
        ch[3].got()
    net.items.remove(tlocal)
    for cp in net.items:
        if cp.dev is None:
            cp.guard(cp.wait_sent)
    net.items = [cp for cp in net.items if cp.dev is not None]
    for k in range(1, T):
        hb = (co.hb + k) % T
        net.remote(lambda: mixed.at[rows(0)], lambda hb=hb: mixr.at[hb], mate, rs=mr + hb, ss=mr).got()

    count = lengths[0]
    for i in range(1, G.slots):
        count = count + lengths[i]
    scale = (G.slots * L) / jnp.full((1, 1), count, jnp.int32).astype(F32)
    vsum[...] = jnp.zeros(vsum.shape, F32)
    ibsum[...] = jnp.zeros(ibsum.shape, F32)
    output_bias, g1, s1, outer_bias, g2, s2 = vectors
    CR = min(256, R)

    o_out = {}
    for off in range(0, R, CR):
        part = lambda ref, off=off: ref.at[pl.ds(off, CR)]
        o_out[off] = (
            net.local(lambda part=part: part(osrc), lambda part=part: part(out), co.native),
            net.remote(
                lambda part=part: part(osrc), lambda part=part: part(out), (co.mate, co.other),
                co.swapped,
            ),
        )

    def ffn(off):
        rr = pl.ds(off, CR)
        base = co.ob * R + off
        grows = pl.ds(al(base, CR), CR)
        branch = lax.fori_loop(
            0, T, lambda t, a: a + dot(mixr[t, rr, :], wpf[t]), jnp.zeros((CR, D), F32), unroll=True
        )
        e = xall[grows, :].astype(F32) + pos[grows, :].astype(F32)
        n1, inv1 = norm(e + branch + output_bias)
        first = n1 * g1 + s1
        low = first.astype(BF)
        flow[rr, :] = low

        def up(t, a):
            pre = dot(low, wif[t]) + smalls[t, 2:3, :F]
            h = jnp.maximum(pre, 0.0).astype(BF)
            hid[t, rr, :] = h
            return a + dot(h, wof[t])

        feed = lax.fori_loop(0, T, up, jnp.zeros((CR, D), F32), unroll=True)
        n2, inv2 = norm(first + feed + outer_bias)
        result = n2 * g2 + s2
        osrc[rr, :] = result.astype(BF)
        for cp in o_out[off]:
            cp.start()
        pl.when(co.swapped)(tswap[off].got)
        if off == 0:
            tlocal.guard(tlocal.wait_sent)
        place = lax.broadcasted_iota(jnp.int32, (CR, 1), 0) + base
        valid = jnp.where(place < length, scale, 0.0)
        gr = valid * (result - teach[rr, :].astype(F32))
        gs = norm_back(gr * g2, n2, inv2)
        gf = gs.astype(BF)
        gfeed[rr, :] = gf

        def down(t, a):
            gh = dot_nt(gf, wof[t])
            gpt = jnp.where(hid[t, rr, :].astype(F32) > 0, gh, 0.0).astype(BF)
            gpre[t, rr, :] = gpt
            ibsum[t] += colsum(gpt.astype(F32))
            return a + dot_nt(gpt, wif[t])

        g_first = lax.fori_loop(0, T, down, gs, unroll=True)
        gv = norm_back(g_first * g1, n1, inv1)
        gmid[rr, :] = gv
        gb = gv.astype(BF)
        gbr[rr, :] = gb

        def mix(t, a):
            gm[t, rr, :] = dot_nt(gb, wpf[t]).astype(BF)
            return a

        lax.fori_loop(0, T, mix, 0, unroll=True)
        vsum[0:1] += colsum(gv)
        vsum[1:2] += colsum(g_first * n1)
        vsum[2:3] += colsum(g_first)
        vsum[3:4] += colsum(gs)
        vsum[4:5] += colsum(gr * n2)
        vsum[5:6] += colsum(gr)

    used = [cp for cp in net.items if all(cp is not own for own in tswap.values())]
    net.items = list(tswap.values())
    gmr = net.take(T * (R // CR))
    gm_in = []
    gm_own = []
    for i in range(R // CR):
        ffn(i * CR)
        if i == 0:
            for cp in used:
                cp.guard(cp.wait_sent)
        for k in range(T):
            m = (co.zz * 2 + c + k) % T
            c2, z2 = m % 2, g * H + m // 2
            hb2 = (z2 + c2 * H) % T
            src = lambda hb2=hb2, i=i: gm.at[hb2, pl.ds(i * CR, CR)]
            dst = lambda i=i: gmall.at[pl.ds(al(co.ob * R + i * CR, CR), CR)]
            if k == 0:
                gm_own.append(net.local(src, dst).start(hold=False))
                continue
            net.remote(src, dst, (2 * co.col + c2, z2), rs=gmr + k * (R // CR) + i).start()
            gm_in.append((k, i))


    def now(src, dst, dev, ss=None):
        return net.remote(src, dst, dev, ss=ss)

    quarter = co.bf * 2 + co.bs
    plane3 = (
        ((co.dpf, z), (1 - co.bf) * 2 + co.bs),
        ((co.dps, z), co.bf * 2 + 1 - co.bs),
        ((co.dpd, z), (1 - co.bf) * 2 + 1 - co.bs),
    )

    def scatter3(src, land):
        return [
            now(lambda piece=piece: src(piece), lambda j=j: land(j), dev)
            for j, (dev, piece) in enumerate(plane3)
        ]

    class Slabs:
        def __init__(self, X, k0, n, s0, r0, r1, r2, r3, rx, r3slot, stay):
            hr, q1, q2 = r0.shape[1], r1.shape[1], r2.shape[1]
            self.n, self.k0 = n, k0
            slabs = pl.ds(k0, n)
            self.start = now(
                lambda: X.at[slabs, pl.ds(al((1 - c) * hr, hr), hr)], lambda: r0.at[slabs], mate
            )
            self.s1 = now(
                lambda: s0.at[slabs, pl.ds(al((1 - co.bf) * q1, q1), q1)],
                lambda: r1.at[slabs], step1,
            )
            self.s2 = now(
                lambda: r1.at[slabs, pl.ds(al((1 - co.bs) * q2, q2), q2)],
                lambda: r2.at[slabs], step2,
            )
            self.over = [
                now(lambda k=k: r2.at[k], lambda k=k: r3.at[r3slot(k)], (co.dp, (z + k_z) % T))
                for k, k_z in stay
                if k0 <= k < k0 + n
            ]
            self.extra = [
                now(lambda: r2.at[slabs], lambda b=b: rx.at[b - 2, slabs], (co.extra(G, b), z))
                for b in range(2, G.nbits)
            ]
            self.refs = X, s0, r0, r1, r2, rx, hr, q1, q2

        def a0(self):
            X, s0, r0, r1, r2, rx, hr, q1, q2 = self.refs
            self.start.got()
            for k in range(self.k0, self.k0 + self.n):
                kept = X[k, pl.ds(al(c * hr, hr), hr), :]
                s0[k] = (kept.astype(F32) + r0[k].astype(F32)).astype(BF)

        def go(self):
            self.s1.start()

        def a1(self):
            X, s0, r0, r1, r2, rx, hr, q1, q2 = self.refs
            self.s1.got()
            for k in range(self.k0, self.k0 + self.n):
                kept = s0[k, pl.ds(al(co.bf * q1, q1), q1), :]
                r1[k] = (kept.astype(F32) + r1[k].astype(F32)).astype(BF)
            self.s2.start()

        def a2(self):
            X, s0, r0, r1, r2, rx, hr, q1, q2 = self.refs
            self.s2.got()
            for k in range(self.k0, self.k0 + self.n):
                kept = r1[k, pl.ds(al(co.bs * q2, q2), q2), :]
                r2[k] = (kept.astype(F32) + r2[k].astype(F32)).astype(BF)
            for m, cp in enumerate(self.extra):
                cp.start(hold=False)
                cp.got()
                cp.wait_sent()
                for k in range(self.k0, self.k0 + self.n):
                    r2[k] = (r2[k].astype(F32) + rx[m, k].astype(F32)).astype(BF)
            for cp in self.over:
                cp.start()

    class Back:
        def __init__(self, chains, r2, r3, gx, dst):
            q2 = r2.shape[1]
            self.chains, self.r2, self.r3 = chains, r2, r3

            def place(width, first):
                return lambda: gx.at[pl.ds(al(first * q2, q2), width * q2)]

            own = c * 4 + co.bf * 2 + co.bs
            self.own = place(1, own)
            self.back = []
            for width, first, dev in ((1, own, step2), (2, own // 2 * 2, step1), (4, c * 4, mate)):
                self.back.append(now(place(width, first), place(width, first), dev))
            self.end = net.local(lambda: gx, lambda: dst)

        def a3(self):
            tot = self.r2[0].astype(F32)
            for k, cp in enumerate(cp for ch in self.chains for cp in ch.over):
                cp.got()
                tot = tot + self.r3[k].astype(F32)
            self.own()[...] = tot.astype(BF)
            self.back[0].start()

        def a4(self):
            self.back[0].got()
            self.back[1].start()

        def a5(self):
            self.back[1].got()
            self.back[2].start()

        def a6(self):
            self.back[2].got()
            self.end.start()

    to_z = [(k, k) for k in range(1, T)]
    minus = lambda k: k - 1
    ks = list(range(1, T)) + [0]
    co_ = [Slabs(dwo, k, 1, s0o, r0o, r1o, r2o, r3o, rxo, minus, to_z) for k in ks]
    ci_ = [Slabs(dwi, k, 1, s0i, r0i, r1i, r2i, r3i, rxi, minus, to_z) for k in ks]
    cp_ = Slabs(dwp, 0, T, s0p, r0p, r1p, r2p, r3p, rxp, minus, to_z)
    slabs = [ch for pair in zip(co_[:-1], ci_[:-1]) for ch in pair] + [co_[-1], ci_[-1], cp_]
    back_o = Back(co_, r2o, r3o, go, ug)
    back_i = Back(ci_, r2i, r3i, gi, ig)
    back_p = Back([cp_], r2p, r3p, gpp, og)

    def grads(i, carry):
        k = jnp.where(i == T - 1, 0, i + 1)
        t = (z + k) % T
        dwo[k] = dot_tn(hid[t], gfeed[...]).astype(BF)
        dwi[k] = dot_tn(flow[...], gpre[t]).astype(BF)
        dwp[k] = dot_tn(mixr[t], gbr[...]).astype(BF)
        for n_ in range(T):

            @pl.when(i == n_)
            def _():
                co_[n_].start.start()
                ci_[n_].start.start()

        return carry

    lax.fori_loop(0, T, grads, 0)
    cp_.start.start()

    vb[...] = jnp.zeros(vb.shape, F32)
    vb[0:6, :] = vsum[0:6, :]
    for t in range(T):
        vb[8 + t : 9 + t, :F] = ibsum[t]

    def sum_chain(v, r, devs):
        cps = [now(lambda: v, lambda i=i: r.at[i], dev) for i, dev in enumerate(devs)]

        def step(i):
            def act():
                cps[i].got()
                cps[i].wait_sent()
                v[...] += r[i]
                if i + 1 < len(cps):
                    cps[i + 1].start(hold=False)

            return act

        return cps[0], [step(i) for i in range(len(cps))]

    plane = [step1, step2] + [(co.extra(G, b), z) for b in range(2, G.nbits)]
    vstart, vchain = sum_chain(vb, vr, [mate] + plane)
    vstart.start(hold=False)
    nv = len(vchain)
    vover = [
        now(lambda: vb, lambda k=k: vr.at[nv + k - 1], (co.dp, (z + k) % T))
        for k in range(1, T)
    ]

    def vz():
        for cp in vover:
            cp.start(hold=False)

    def vdone():
        for cp in vover:
            cp.got()
            cp.wait_sent()
        for k in range(1, T):
            vb[...] += vr[nv + k - 1]
        vout[0:8, :] = vb[0:8, :]
        vrow = lax.broadcasted_iota(jnp.int32, vb.shape, 0)
        vout[8:9, :] = colsum(jnp.where(vrow == 8 + z, vb[...], 0.0))

    vchain = vchain + [vz, vdone]

    for i, ch in enumerate(slabs):
        ch.a0()
        if i < 2:
            ch.go()
    for k, i in gm_in:
        net.remote(
            lambda: gm.at[0, pl.ds(0, CR)], lambda: gmall.at[pl.ds(0, CR)], mate,
            rs=gmr + k * (R // CR) + i, ss=gmr,
        ).got()
    for cp in gm_own:
        cp.wait_sent()


    def prepare(i, carry):
        CH = min(256, R)
        rr = pl.ds(al(i * CH, CH), CH)
        gg = gmall[rr, :].astype(F32)
        prod = gg * mixed[rr, :].astype(F32)
        lane = lanes((CH, WP))
        k = jnp.zeros((CH, WP), F32)
        for h in range(NH):
            a0 = aug_base(h)
            data = lane // HD == h
            delta = jnp.sum(jnp.where(data, prod, 0.0), axis=-1, keepdims=True)
            base = place3(jnp.zeros((CH, WP), F32), lane, a0 + 1, -delta)
            da[h, rr, :] = jnp.where(data, gg, base).astype(BF)
            k = jnp.where(data, ka[h, rr, :].astype(F32), k)
        kt[:, rr] = k.T.astype(BF)
        zero = jnp.zeros((CH, WP), F32)
        dk[rr, :] = zero
        dv[rr, :] = zero
        dq[:, rr] = zero.T
        return carry

    lax.fori_loop(0, L // min(256, R), prepare, 0)

    def btile(i, j, masked):
        qr, kr = rows(i), rows(j)
        lane = lanes((R, WP))
        sub = lax.broadcasted_iota(jnp.int32, (WP, R), 0)
        dks, dvs, dqs = [], [], []
        for h in range(NH):
            q, d = qa[h, qr, :], da[h, qr, :]
            pm = jnp.exp(dot_nt(ka[h, kr, :], q))
            if masked:
                above = lax.broadcasted_iota(jnp.int32, (R, R), 0) <= lanes((R, R))
                pm = jnp.where(above, pm, 0.0)
            ds = (pm * dot_nt(va[h, kr, :], d)).astype(BF)
            dvs.append(dot(pm.astype(BF), d))
            dks.append(dot(ds, q))
            dqs.append(dot(kt[:, kr], ds))
        if NH == 1:
            dk[kr, :] += dks[0]
            dv[kr, :] += dvs[0]
            dq[:, qr] += dqs[0]
        else:
            dk[kr, :] += jnp.where(lane < HD, dks[0], dks[1])
            dv[kr, :] += jnp.where(lane < HD, dvs[0], dvs[1])
            dq[:, qr] += jnp.where(sub < HD, dqs[0], dqs[1])

    dwq[...] = jnp.zeros(dwq.shape, F32)
    qsum[...] = jnp.zeros(qsum.shape, F32)

    def complete(b):
        rr = rows(b)
        keep = lanes((R, WP)) < G.W
        q = dq[:, rr].T * (1.0 / math.sqrt(HD))
        sums = []
        for n_, part in enumerate((q, dk[rr, :], dv[rr, :])):
            part = jnp.where(keep, part, 0.0).astype(BF)
            gp[rr, n_ * WP : (n_ + 1) * WP] = part
            sums.append(colsum(part.astype(F32)))
        gg = gp[rr, :]
        back = dot_nt(gg, wqh[...])
        ge[rr, :] = back.astype(BF)
        oc, oz = owner(G, co, b)

        @pl.when(jnp.logical_and(oc == c, oz == z))
        def _():
            ge[rr, :] = (back + gmid[...]).astype(BF)

        dwq[...] += dot_tn(emb[rr, :], gg)
        qsum[0:1, :] += jnp.concatenate(sums, axis=1)

    order_b = [(T - 1 - s_) + g * (2 * s_ - T + 1) for s_ in range(T)]
    ends = [sum(T - i for i in range(s_ + 1)) - 1 for s_ in range(T)]
    half = R // 2
    edge_z = H - 1 + g
    at_edge = z == edge_z
    eh_sem = net.take(max(H - 1, 1))

    def slot_of(z_to):
        return (co.zz - (z_to - g * H) + H - 1) % H

    class Rows:
        def __init__(self, s_):
            b = order_b[s_]
            self.s, self.b, self.inside = s_, b, s_ >= H
            self.core = net.remote(
                lambda: ge.at[pl.ds(al(b * R + (1 - c) * half, half), half)],
                lambda: ec.at[s_], mate,
            )
            h = lambda: hsum.at[s_]
            if self.inside:
                slot, self.base = slot_of(b), eh_sem
                self.home_chip = z == b
                self.over = net.remote(
                    h, lambda: eh.at[slot], (co.dp, b), jnp.logical_not(self.home_chip),
                    rs=self.base + slot,
                )
            else:
                slot, self.base = slot_of(edge_z), net.take(max(H - 1, 1))
                self.over = net.remote(
                    h, lambda: eo.at[s_, slot], (co.dp, edge_z), jnp.logical_not(at_edge),
                    rs=self.base + slot,
                )
                self.home = net.remote(
                    lambda: hsend.at[s_], lambda: foreign, (co.dp, b), at_edge, rs=f_sem
                )

        def k0(self):
            self.core.start()

        def k1(self):
            s_ = self.s
            self.core.got()
            own = ge[pl.ds(al(self.b * R + c * half, half), half), :].astype(F32)
            hsum[s_] = (own + ec[s_].astype(F32)).astype(BF)
            self.over.start()

        def collect(self, land):
            total = hsum[self.s].astype(F32)
            for j in range(H - 1):
                net.remote(
                    lambda: hsum.at[0], lambda: land(j), mate, rs=self.base + j, ss=self.base
                ).got()
                total = total + land(j)[...].astype(F32)
            return total.astype(BF)

        def kx(self):
            @pl.when(at_edge)
            def _():
                hsend[self.s] = self.collect(lambda j: eo.at[self.s, j])

            self.home.start()

        def ky(self):
            @pl.when(self.home_chip)
            def _():
                native_half[...] = self.collect(lambda j: eh.at[j])

    f_sem = net.take()
    parts_ = [Rows(s_) for s_ in range(T)]
    foreign_in = net.remote(lambda: hsend.at[0], lambda: foreign, mate, rs=f_sem, ss=f_sem)
    to_mate = net.remote(
        lambda: give, lambda: nat.at[pl.ds(al(c * half, half), half)], mate
    )
    from_mate_half = net.remote(
        lambda: give, lambda: nat.at[pl.ds(al((1 - c) * half, half), half)], mate,
        ss=to_mate.ss, rs=to_mate.rs,
    )
    q2p = half // 4
    p_rs = scatter3(lambda piece: hp.at[pl.ds(al(piece * q2p, q2p), q2p)], lambda j: ps1.at[j])
    p_more = []
    size = q2p
    for n_, bit in enumerate(range(2, G.nbits)):
        size = size // 2
        bb = (co.col // (1 << bit)) % 2
        src = ps2 if n_ == 0 else (px if n_ % 2 == 1 else py)
        dst = px if n_ % 2 == 0 else py
        cp = net.remote(
            lambda src=src, bb=bb, size=size: src.at[pl.ds(al((1 - bb) * size, 8), size)],
            lambda dst=dst, size=size: dst.at[pl.ds(0, size)], (co.extra(G, bit), z),
        )
        p_more.append((cp, src, dst, bb, size))
    p_last = p_more[-1][2] if p_more else ps2
    p_fin = net.remote(lambda: p_last.at[pl.ds(0, G.PR)], lambda: pf, (pdp, pz), away)

    def p_first():
        foreign_in.got()
        own, other_ = native_half[...], foreign[...]
        give[...] = jnp.where(co.native, other_, own)
        to_mate.start()
        nat[pl.ds(al(c * half, half), half), :] = jnp.where(co.native, own, other_)
        hp[...] = (own.astype(F32) + other_.astype(F32)).astype(hp.dtype)
        for cp in p_rs:
            cp.start()

    def p_second():
        total = hp[pl.ds(al(quarter * q2p, q2p), q2p), :].astype(F32)
        for j, cp in enumerate(p_rs):
            cp.got()
            total = total + ps1[j].astype(F32)
        ps2[...] = total.astype(ps2.dtype)
        for cp, src, dst, bb, size in p_more:
            cp.start()
            cp.got()
            kept = src[pl.ds(al(bb * size, 8), size), :].astype(F32)
            dst[0:size, :] = (kept + dst[0:size, :].astype(F32)).astype(dst.dtype)
        p_fin.start()

    def p_third():
        pl.when(away)(p_fin.got)

        @pl.when(jnp.logical_not(away))
        def _():
            pf[...] = p_last[0 : G.PR, :]

        pr3[...] = pf[...].astype(F32)
        net.local(lambda: pr3, lambda: pgrad).start()

    def igrad_out():
        from_mate_half.got()
        net.local(lambda: nat, lambda: igrad).start()

    def run(chain, i):
        chain[i]()

    jobs = {("v", i): act for i, act in enumerate(vchain)}
    for i, ch in enumerate(slabs):
        if i >= 2:
            jobs["s", i] = ch.go
        jobs["1", i] = ch.a1
        jobs["2", i] = ch.a2
    for name, bk in (("o", back_o), ("i", back_i), ("p", back_p)):
        for n_, act in enumerate((bk.a3, bk.a4, bk.a5, bk.a6)):
            jobs[name, n_] = act
    for rw in parts_:
        for name in ("k0", "k1", "ky" if rw.inside else "kx"):
            jobs[name, rw.s] = getattr(rw, name)
    plan = {
        0: [],
        1: [("v", 0)],
        2: [],
        3: [("k0", 0), ("v", 1)],
        4: [("k1", 0)],
        5: [("v", 2), ("v", 3)],
        6: [("k0", 1)],
        7: [("k1", 1), ("kx", 0)],
        8: [("k0", 2), ("v", 4)],
        9: [("k0", 3), ("k1", 2), ("kx", 1)],
    }
    for i in range(10):
        plan[i] += [("1", i), ("2", i - 2), ("s", i + 2)]
    plan = {i: [key for key in acts if key in jobs] for i, acts in plan.items()}
    if ntiles != 10:
        plan = {e: [("k0", s_)] for s_, e in enumerate(ends)}
    left = [key for key in jobs if not any(key in acts for acts in plan.values())]
    def btiles(t, carry):
        s_, u = 0, t
        for k in range(1, T):
            past = (t > ends[k - 1]).astype(jnp.int32)
            s_ = s_ + past
            u = u - past * (T - k + 1)
        b = (T - 1 - s_) + g * (2 * s_ - T + 1)
        far = b - u + g * (2 * u)

        @pl.when(u == 0)
        def _():
            btile(b, b, True)

        @pl.when(u > 0)
        def _():
            btile(jnp.maximum(b, far), jnp.minimum(b, far), False)

        @pl.when(u == T - 1 - s_)
        def _():
            complete(b)

        for i in range(ntiles):
            acts = [jobs[key] for key in plan.get(i, ())]
            if acts:

                @pl.when(t == i)
                def _(acts=acts):
                    for act in acts:
                        act()

        return carry

    lax.fori_loop(0, ntiles, btiles, 0)

    dwqb[c] = dwq[...].astype(BF)
    hq = D // 2
    e8 = D // 8
    qstart = now(
        lambda: dwqb.at[c, pl.ds(al((1 - c) * hq, hq), hq)], lambda: r0q.at[c], mate
    ).start()
    q_rs = scatter3(lambda piece: s0q.at[:, pl.ds(al(piece * e8, e8), e8)], lambda j: r1q.at[j])
    q_extra = [
        now(lambda: r2q, lambda b=b: rxq.at[b - 2], (co.extra(G, b), z)) for b in range(2, G.nbits)
    ]
    q_over = now(lambda: r2q.at[1], lambda: r3q.at[0], (co.dp, co.other))
    q_own = lambda: gq.at[pl.ds(al((c * 4 + quarter) * e8, e8), e8)]
    q_ag = [now(q_own, q_own, dev) for dev, _ in plane3]
    q_half = lambda: gq.at[pl.ds(al(c * hq, hq), hq)]
    q_core = now(q_half, q_half, mate)
    q_out = net.local(lambda: gq, lambda: qg)

    def q_sum():
        total = s0q[:, pl.ds(al(quarter * e8, e8), e8), :].astype(F32)
        for j, cp in enumerate(q_rs):
            cp.got()
            total = total + r1q[j].astype(F32)
        r2q[...] = total.astype(BF)
        for m, cp in enumerate(q_extra):
            cp.start(hold=False)
            cp.got()
            cp.wait_sent()
            r2q[...] = (r2q[...].astype(F32) + rxq[m].astype(F32)).astype(BF)
        q_over.start()

    def q_back():
        q_over.got()
        q_own()[...] = (r2q[0].astype(F32) + r3q[0].astype(F32)).astype(BF)
        for cp in q_ag:
            cp.start()

    def q_join():
        for cp in q_ag:
            cp.got()
        q_core.start()

    def q_end():
        q_core.got()
        q_out.start()

    qb[c] = qsum[...]
    qmate = now(lambda: qb.at[c], lambda: qb.at[c], mate).start(hold=False)
    qsums, qchain2 = sum_chain(qb, qr, plane)
    qover = now(lambda: qb.at[1], lambda: qr.at[len(plane), 0], (co.dp, co.other))

    def rest(*names):
        for key in left:
            if key[0] in names:
                jobs[key]()

    def backs(n_):
        for key in left:
            if key[0] in "oip" and key[1] == n_:
                jobs[key]()

    rest("k1")
    pltpu.make_async_remote_copy(
        src_ref=dwqb.at[c, pl.ds(0, hq)], dst_ref=r0q.at[1 - c], send_sem=net.sem(qstart.ss),
        recv_sem=net.sem(qstart.rs), device_id=mate, device_id_type=MESH,
    ).wait_recv()
    s0q[c] = dwqb[c, pl.ds(al(c * hq, hq), hq), :]
    s0q[1 - c] = r0q[1 - c]
    for cp in q_rs:
        cp.start()
    qmate.got()
    qmate.wait_sent()
    qsums.start(hold=False)
    rest("s", "1", "v")
    rest("2")
    rest("kx")
    backs(0)
    qchain2[0]()
    rest("ky")
    p_first()
    q_sum()
    for i in range(1, len(qchain2)):
        qchain2[i]()
    qover.start(hold=False)
    backs(1)
    igrad_out()
    p_second()
    q_back()
    qover.got()
    qover.wait_sent()
    qb[0] += qr[len(plane), 0]
    vout[9:10, :WP] = qb[0, 0:1, :WP]
    vout[10:11, :WP] = qb[0, 0:1, 2 * WP :]
    backs(2)
    q_join()
    backs(3)
    p_third()
    q_end()
    for off in o_out:
        pl.when(co.swapped)(o_out[off][1].got)
    net.drain()
    assert net.n <= sem.shape[0], net.n


def emit_kernel(
    G, out_in, igrad_in, pgrad_in, qg_in, og_in, ig_in, ug_in, vin,
    out, igrad, pgrad, qg, qvg, og, ig, ug, ibg, v0, v1, v2, v3, v4, v5,
):
    out[...] = out_in[...]
    igrad[...] = igrad_in[...]
    pgrad[...] = pgrad_in[...]
    for j in range(3):
        qg[j] = qg_in[:, j * G.WP : j * G.WP + G.W].astype(F32)
    qvg[...] = vin[9:11, : G.W]
    og[...] = og_in[: G.W, :].astype(F32)
    ig[...] = ig_in[...].astype(F32)
    ug[...] = ug_in[...].astype(F32)
    ibg[...] = vin[8:9, : G.F].reshape(G.F)
    for i, v in enumerate((v0, v1, v2, v3, v4, v5)):
        v[...] = vin[i : i + 1, :].reshape(G.D)


def on_device(G, *args):
    (inputs, teacher, lengths, positions, qkv_weight, query_value_bias, output_weight, output_bias,
     first_gain, first_shift, inner_weight, inner_bias, outer_weight, outer_bias, second_gain,
     second_shift) = args
    T, R, D, L, W, WP, NH, F, H = G.T, G.R, G.D, G.L, G.W, G.WP, G.NH, G.F, G.H
    dma = lambda n: pltpu.SemaphoreType.DMA((n,))
    vm = pltpu.VMEM
    wq = jnp.pad(jnp.transpose(qkv_weight, (1, 0, 2)), ((0, 0), (0, 0), (0, WP - W)))
    wp = jnp.pad(output_weight, ((0, WP - W), (0, 0)))
    sizes = [(D, F, T), (F, D, T), (WP, D, T), (D, 3 * WP, 2)]
    nplane = G.nbits
    V = 8 + (T + 7) // 8 * 8
    scratch = [
        vm((L, D), BF), vm((L, D), BF), vm((L, D), BF),
        vm((NH, L, WP), BF), vm((NH, L, WP), BF), vm((NH, L, WP), BF), vm((NH, L, WP), BF),
        vm((WP, L), BF), vm((2, L, WP), F32), vm((NH, L, WP), F32), vm((L, WP), BF),
        vm((T, R, WP), BF),
        vm((8, D), F32), vm((3, D, WP), BF), vm((3, D, WP), BF), vm((D, 3 * WP), BF),
        vm((T, D, F), BF), vm((T, F, D), BF),
        vm((T, WP, D), BF), vm((T, 8, D), F32), vm((R, D), BF),
        vm((R, D), BF), vm((T, R, F), BF), vm((T, R, F), BF), vm((R, D), BF), vm((R, D), BF),
        vm((R, D), F32), vm((R, D), BF), vm((T, R, WP), BF), vm((L, WP), BF), vm((8, D), F32),
        vm((T, 1, F), F32),
        vm((T, D, F), BF), vm((T, F, D), BF), vm((T, WP, D), BF), vm((WP, L), F32),
        vm((L, 3 * WP), BF),
        vm((D, 3 * WP), F32), vm((2, D, 3 * WP), BF), vm((8, 3 * WP), F32),
    ]
    for shift in (1, 1, 2, 3):
        scratch += [vm((n, r >> shift, w), BF) for r, w, n in sizes]
        if shift == 2:
            scratch[-1] = vm((3, 2, D >> 3, 3 * WP), BF)
    scratch += [vm((T - 1, r >> 3, w), BF) for r, w, n in sizes[:3]] + [vm((1, D >> 3, 3 * WP), BF)]
    more = G.nbits - 2
    PD = BF if G.PR % 16 == 0 else F32
    scratch += [vm((more, n, r >> 3, w) if more else (1, 1, 16, 128), BF) for r, w, n in sizes]
    scratch += [vm((r, w), BF) for r, w, n in sizes]
    scratch += [
        vm((T, R // 2, D), BF), vm((T, R // 2, D), BF), vm((R // 2, D), PD),
        vm((H, max(H - 1, 1), R // 2, D), BF), vm((max(H - 1, 1), R // 2, D), BF),
        vm((H, R // 2, D), BF), vm((R // 2, D), BF), vm((R // 2, D), BF), vm((R // 2, D), BF),
        vm((R, D), BF), vm((3, R // 8, D), PD), vm((R // 8, D), PD),
        vm((max(R // 16, 8), D) if more else (8, 128), PD),
        vm((max(R // 32, 8), D) if more else (8, 128), PD), vm((G.PR, D), PD),
        vm((G.PR, D), F32), vm((V, D), F32), vm((1 + nplane + T - 1, V, D), F32),
        vm((2, 8, 3 * WP), F32), vm((nplane + 1, 2, 8, 3 * WP), F32), dma(21 * T * T),
    ]
    outs = [
        ((R, D), BF), ((R, D), BF), ((G.PR, D), F32), ((D, 3 * WP), BF),
        ((WP, D), BF), ((D, F), BF), ((F, D), BF), ((16, D), F32),
    ]
    anyspec = pl.BlockSpec(memory_space=pl.ANY)
    results = pl.pallas_call(
        functools.partial(layer_kernel, G),
        out_shape=tuple(jax.ShapeDtypeStruct(s, d) for s, d in outs),
        in_specs=[SM] + [anyspec] * 7 + [VM] * 8,
        out_specs=tuple([anyspec] * 7 + [VM]),
        scratch_shapes=scratch,
        compiler_params=pltpu.CompilerParams(
            vmem_limit_bytes=63 << 20, collective_id=0, has_side_effects=True
        ),
        name="layer",
    )(lengths, inputs, teacher, wq, inner_weight, outer_weight, wp, positions, query_value_bias,
      inner_bias, output_bias, first_gain, first_shift, outer_bias, second_gain, second_shift)
    finals = [
        ((R, D), BF), ((R, D), BF), ((G.PR, D), F32), ((3, D, W), F32), ((2, W), F32),
        ((W, D), F32), ((D, F), F32), ((F, D), F32), ((F,), F32),
    ] + [((D,), F32)] * 6
    (out, igrad, pgrad, qg, qvg, og, ig, ug, ibg, *vs) = pl.pallas_call(
        functools.partial(emit_kernel, G),
        out_shape=tuple(jax.ShapeDtypeStruct(s, d) for s, d in finals),
        in_specs=[VM] * 8,
        out_specs=tuple([VM] * 15),
        compiler_params=pltpu.CompilerParams(vmem_limit_bytes=63 << 20),
        name="emit",
    )(*results)
    return (
        out, igrad, pgrad, jnp.transpose(qg, (1, 0, 2)), qvg, og, vs[0], vs[1], vs[2],
        ig, ibg, ug, vs[3], vs[4], vs[5],
    )


def solution(mesh):
    rows = P(("dp", "tensor"), None)
    specs = (
        rows, rows, P(), P(), P(None, None, "tensor"), P(None, "tensor"), P("tensor", None), P(),
        P(), P(), P(None, "tensor"), P("tensor"), P("tensor", None), P(), P(), P(),
    )
    outs = (
        rows, rows, rows, P(None, None, "tensor"), P(None, "tensor"), P("tensor", None), P(), P(),
        P(), P(None, "tensor"), P("tensor"), P("tensor", None), P(), P(), P(),
    )

    def step(*args):
        G = Geo(mesh, args[2].shape[0], args[3].shape[0], args[0].shape[1], args[11].shape[0])
        body = jax.shard_map(
            functools.partial(on_device, G), mesh=mesh, in_specs=specs, out_specs=outs,
            check_vma=False,
        )
        return body(*args)

    return step
```

```python
import functools
import math

import jax
import jax.numpy as jnp
from jax import lax
from jax.experimental import pallas as pl
from jax.experimental.pallas import tpu as pltpu
from jax.sharding import PartitionSpec as P

HD = 64
EPS = 1e-05
NEG = -1e30
BF = jnp.bfloat16
F32 = jnp.float32
MESH = pl.DeviceIdType.MESH
VM = pl.BlockSpec(memory_space=pltpu.VMEM)
SM = pl.BlockSpec(memory_space=pltpu.SMEM)


class Geo:
    def __init__(self, mesh, slots, seq, width, hidden):
        self.T = mesh.shape["tensor"]
        self.DP = mesh.shape["dp"]
        self.H = self.T // 2
        self.NC = self.DP // 2
        self.nbits = self.NC.bit_length() - 1
        self.slots = slots
        self.L = seq
        self.D = width
        self.FF = hidden
        self.R = seq // self.T
        self.W = width // self.T
        self.WP = max(self.W, 128)
        self.NH = self.W // HD
        self.F = hidden // self.T
        self.PR = seq // (self.DP * self.T)


class Co:
    def __init__(self, G):
        self.dp = lax.axis_index("dp")
        self.z = lax.axis_index("tensor")
        self.c = self.dp % 2
        self.col = self.dp // 2
        self.g = self.z // G.H
        self.zz = self.z - self.g * G.H
        self.other = (self.z + G.H) % G.T
        self.native = self.c == self.g
        self.swapped = self.c != self.g
        self.hb = (self.z + self.c * G.H) % G.T
        self.ob = self.own_block(G, self.z, self.c)
        self.slot = 2 * self.col + self.g
        self.mate = self.dp + 1 - 2 * self.c
        b0 = self.col % 2
        b1 = (self.col // 2) % 2
        self.bf = b0 + self.c * (b1 - b0)
        self.bs = b1 + self.c * (b0 - b1)
        wf = 1 + self.c
        ws = 2 - self.c
        self.dpf = self.dp + 2 * wf * (1 - 2 * self.bf)
        self.dps = self.dp + 2 * ws * (1 - 2 * self.bs)
        self.dpd = self.dpf + self.dps - self.dp

    @staticmethod
    def own_block(G, z, c):
        d = c - z // G.H
        return (z + d * d * G.H) % G.T

    def extra(self, G, bit):
        b = (self.col // (1 << bit)) % 2
        return self.dp + (2 << bit) * (1 - 2 * b)

    def piece(self):
        return self.c * 4 + self.bs * 2 + self.bf


def owner(G, co, b):
    out = (b // G.H - co.g) * (b // G.H - co.g)
    return co.g + out * (1 - 2 * co.g), (b + out * G.H) % G.T


class Net:
    def __init__(self, ref):
        self.ref = ref
        self.n = 0
        self.items = []

    def take(self, n=1):
        base = self.n
        self.n += n
        return base

    def sem(self, i):
        return self.ref.at[i]

    def remote(self, src, dst, dev, cond=None, ss=None, rs=None):
        ss = self.take() if ss is None else ss
        rs = self.take() if rs is None else rs
        return Copy(self, src, dst, dev, ss, rs, cond)

    def local(self, src, dst, cond=None):
        return Copy(self, src, dst, None, self.take(), None, cond)

    def drain(self):
        for copy in self.items:
            copy.guard(copy.wait_sent)
        self.items = []


class Copy:
    def __init__(self, net, src, dst, dev, ss, rs, cond):
        self.net, self.src, self.dst, self.dev = net, src, dst, dev
        self.ss, self.rs, self.cond = ss, rs, cond

    def make(self):
        net = self.net
        if self.dev is None:
            return pltpu.make_async_copy(self.src(), self.dst(), net.sem(self.ss))
        return pltpu.make_async_remote_copy(
            src_ref=self.src(), dst_ref=self.dst(), send_sem=net.sem(self.ss),
            recv_sem=net.sem(self.rs), device_id=self.dev, device_id_type=MESH,
        )

    def guard(self, fn):
        if self.cond is None:
            fn()
        else:
            pl.when(self.cond)(fn)

    def start(self, hold=True):
        self.guard(lambda: self.make().start())
        if hold:
            self.net.items.append(self)
        return self

    def wait_sent(self):
        if self.dev is None:
            self.make().wait()
        else:
            self.make().wait_send()

    def got(self):
        self.make().wait_recv()


def column_partners(G, co):
    out = [(co.mate, co.z), (co.dpf, co.z), (co.dps, co.z), (co.dpd, co.z), (co.mate, co.other)]
    out += [(co.dp, (co.z + k) % G.T) for k in range(1, G.T)]
    out += [(co.mate, (co.z + k) % G.T) for k in range(1, G.T) if k != G.H]
    out += [(co.extra(G, b), co.z) for b in range(2, G.nbits)]
    return out


def lanes(shape):
    return lax.broadcasted_iota(jnp.int32, shape, len(shape) - 1)


def aug_base(h):
    return HD if h == 0 else 0


def dot(a, b):
    return lax.dot_general(a, b, (((1,), (0,)), ((), ())), preferred_element_type=F32)


def dot_nt(a, b):
    return lax.dot_general(a, b, (((1,), (1,)), ((), ())), preferred_element_type=F32)


def dot_tn(a, b):
    return lax.dot_general(a, b, (((0,), (0,)), ((), ())), preferred_element_type=F32)


def parts3(v):
    hi = v.astype(BF).astype(F32)
    mid = (v - hi).astype(BF).astype(F32)
    return hi, mid, v - hi - mid


def place3(base, lane, first, v):
    hi, mid, lo = parts3(v)
    base = jnp.where(lane == first, hi, base)
    base = jnp.where(lane == first + 1, mid, base)
    return jnp.where(lane == first + 2, lo, base)


def norm(v):
    centre = jnp.mean(v, axis=-1, keepdims=True)
    v = v - centre
    inv = lax.rsqrt(jnp.mean(v * v, axis=-1, keepdims=True) + EPS)
    return v * inv, inv


def norm_back(e, normal, inv):
    a = jnp.mean(e, axis=-1, keepdims=True)
    b = jnp.mean(e * normal, axis=-1, keepdims=True)
    return inv * (e - a - normal * b)


def colsum(v):
    return jnp.sum(v, axis=0, keepdims=True)


def al(v, n):
    return pl.multiple_of(v, n)


def layer_kernel(
    G, lengths, x, te, wq, wi, wo, wp, pos_in, qvbias, ibias, *rest,
):
    vectors = [v[...].astype(F32).reshape(1, G.D) for v in rest[:6]]
    layer_body(G, vectors, lengths, x, te, wq, wi, wo, wp, pos_in, qvbias, ibias, *rest[6:])


def layer_body(
    G, vectors, lengths, x, te, wq, wi, wo, wp, pos_in, qvbias, ibias,
    out, igrad, pgrad, qg, og, ig, ug, vout,
    xall, pos, emb, qa, ka, va, da, kt, acc, top, mixed, mixr,
    sm, wqm, wqo, wqh, wif, wof, wpf, smalls, teach,
    flow, hid, gpre, gfeed, gbr, gmid, osrc, gm, gmall, vsum, ibsum,
    dwi, dwo, dwp, dq, gp, dwq, dwqb, qsum,
    s0i, s0o, s0p, s0q, r0i, r0o, r0p, r0q, r1i, r1o, r1p, r1q, r2i, r2o, r2p, r2q,
    r3i, r3o, r3p, r3q, rxi, rxo, rxp, rxq, gi, go, gpp, gq,
    ec, hsum, hp, eo, eh, hsend, native_half, foreign, give, nat,
    ps1, ps2, px, py, pf, pr3, vb, vr, qb, qr,
    sem,
):
    co = Co(G)
    net = Net(sem)
    T, H, R, L, WP, NH, D, F = G.T, G.H, G.R, G.L, G.WP, G.NH, G.D, G.F
    z, c, g = co.z, co.c, co.g
    mate, step1, step2 = (co.mate, z), (co.dpf, z), (co.dps, z)
    length = lengths[co.slot]
    ge, dk, dv = xall, acc.at[0], acc.at[1]

    def rows(b, n=R):
        return pl.ds(al(b * R, R), n)

    pp = c * (G.DP // 2) + co.bf * (G.DP // 4) + co.bs * (G.DP // 8)
    for bit in range(2, G.nbits):
        pp = pp + ((co.col // (1 << bit)) % 2) * (G.DP // (4 << bit))
    flat = z * G.DP + pp
    pdp, pz = flat // T, flat % T
    away = jnp.logical_or(pdp != co.dp, pz != z)
    mine = co.dp * T + z
    fz, fp = mine // G.DP, mine % G.DP
    fc = fp // (G.DP // 2)
    f1 = (fp // (G.DP // 4)) % 2
    f2 = (fp // (G.DP // 8)) % 2
    fcol = (f1 + fc * (f2 - f1)) + 2 * (f2 + fc * (f1 - f2))
    for bit in range(2, G.nbits):
        fcol = fcol + ((fp // (G.DP // (4 << bit))) % 2) * (1 << bit)
    poscopy = net.local(lambda: pos_in, lambda: pos).start()
    bar = pltpu.get_barrier_semaphore()
    partners = column_partners(G, co)
    for dev in partners:
        pl.semaphore_signal(bar, inc=1, device_id=dev, device_id_type=MESH)

    @pl.when(away)
    def _():
        pl.semaphore_signal(bar, inc=1, device_id=(2 * fcol + fc, fz), device_id_type=MESH)

    pl.semaphore_wait(bar, len(partners) + away.astype(jnp.int32))

    bs, br = net.take(T), net.take(T)
    sm[...] = jnp.zeros(sm.shape, F32)
    sm[0:2, : G.W] = qvbias[...].astype(F32)
    sm[2:3, :F] = ibias[...].astype(F32).reshape(1, F)
    small_own = net.local(lambda: sm, lambda: smalls.at[z]).start(hold=False)
    small = [
        net.remote(lambda: sm, lambda: smalls.at[z], (co.dp, (z + k) % T)).start()
        for k in range(1, T)
    ]
    p = co.piece()

    def weight_chain(src, dst, slab, k):
        size = src.shape[-2] // 8

        def view(ref, s, first, count):
            where = pl.ds(al(first * size, size), count * size)
            if s is None:
                return ref.at[:, where] if slab is None else ref.at[where]
            return ref.at[s, where]

        to = None if slab is None else z
        cps = [net.remote(lambda: view(src, None, p, 1), lambda: view(dst, to, p, 1), (co.dp, (z + k) % T))]
        for first, count, dev in ((p, 1, step1), (p // 2 * 2, 2, step2), (c * 4, 4, mate)):
            ref = lambda first=first, count=count: view(dst, slab, first, count)
            cps.append(net.remote(ref, ref, dev))
        return cps

    qchain = weight_chain(wq, wqo, None, H)
    qchain[0].start()
    q_own = net.local(lambda: wq, lambda: wqm).start(hold=False)
    wchains = []
    whole = ((wp, wpf), (wi, wif), (wo, wof))
    for src, dst in whole:
        net.local(lambda src=src: src, lambda dst=dst: dst.at[z]).start()
    for k in range(1, T):
        for src, dst in whole:
            wchains.append(weight_chain(src, dst, (z - k) % T, k))

    chunks = 1
    n = R // chunks
    xr = net.take(T * chunks)

    def order(r):
        if r == 0:
            return z
        if r < H:
            return g * H + (co.zz + r) % H
        k = r - H
        return (H - 1 - k) + (1 - g) * (2 * k + 1)

    blocks = [order(r) for r in range(T)]

    def block_at(r):
        out = blocks[0]
        for k in range(1, T):
            out = jnp.where(r == k, blocks[k], out)
        return out
    zb = H - 1 + c
    edge = jnp.logical_and(co.native, z == H - 1 + g)

    def xrow(b, ch):
        return lambda: xall.at[pl.ds(al(b * R + ch * n, n), n)]

    def xmine(ch):
        return lambda: x.at[pl.ds(ch * n, n)]

    def xsend(src, b, ch, dev, cond, ss=None):
        return net.remote(src, xrow(b, ch), dev, cond, rs=xr + b * chunks + ch, ss=ss)

    def swapped_sends(k):
        cond = jnp.logical_and(co.swapped, (z - zb) * (1 - 2 * c) == k + 1)
        return [xsend(xmine(ch), z, ch, (co.dp, zb), cond) for ch in range(chunks)]

    own_x = []
    for ch in range(chunks):
        for j in range(1, H):
            xsend(xmine(ch), z, ch, (co.dp, g * H + (co.zz + j) % H), co.native).start()
        xsend(xmine(ch), z, ch, mate, co.native).start()
        own_x.append(net.local(xmine(ch), xrow(z, ch), co.native).start(hold=False))
    for cp in swapped_sends(0):
        cp.start()

    tlocal = net.local(lambda: te, lambda: teach, co.native)
    CR = min(256, R)
    tswap = {}
    for off in range(0, R, CR):
        part = lambda ref, off=off: ref.at[pl.ds(off, CR)]
        tswap[off] = net.remote(
            lambda part=part: part(te), lambda part=part: part(teach), (co.mate, co.other),
            co.swapped,
        )

    def project(b):
        CH = min(256, R)
        qb_, vb_ = smalls[co.hb, 0:1, :WP], smalls[co.hb, 1:2, :WP]

        def step(i, carry):
            first = b * R + i * CH
            rr = pl.ds(al(first, CH), CH)
            low = (xall[rr, :].astype(F32) + pos[rr, :].astype(F32)).astype(BF)
            emb[rr, :] = low
            pr = dot(low, wqh[...])
            q = (pr[:, :WP] + qb_).astype(BF).astype(F32) * (1.0 / math.sqrt(HD))
            k = pr[:, WP : 2 * WP].astype(BF).astype(F32)
            v = (pr[:, 2 * WP :] + vb_).astype(BF).astype(F32)
            lane = lanes((CH, WP))
            place = lax.broadcasted_iota(jnp.int32, (CH, WP), 0) + first
            limit = jnp.where(place < length, 0.0, NEG)
            for h in range(NH):
                a0 = aug_base(h)
                data = lane // HD == h
                ones = jnp.where((lane >= a0) & (lane < a0 + 4), 1.0, 0.0)
                qa[h, rr, :] = jnp.where(data, q, jnp.where(lane == a0, 1.0, 0.0)).astype(BF)
                ka[h, rr, :] = jnp.where(data, k, jnp.where(lane == a0, limit, ones)).astype(BF)
                va[h, rr, :] = jnp.where(data, v, ones).astype(BF)
                acc[h, rr, :] = jnp.zeros((CH, WP), F32)
                top[h, rr, :] = jnp.full((CH, WP), NEG, F32)
            return carry

        lax.fori_loop(0, R // CH, step, 0)

    def ftile(i, j, masked):
        qr, kr = rows(i), rows(j)
        heads = range(NH)
        s = [dot_nt(qa[h, qr, :], ka[h, kr, :]) for h in heads]
        if masked:
            below = lax.broadcasted_iota(jnp.int32, (R, R), 0) >= lanes((R, R))
            s = [jnp.where(below, v, NEG) for v in s]
        old = [top[h, qr, :] for h in heads]
        new = [jnp.maximum(old[h], jnp.max(s[h], axis=-1, keepdims=True)) for h in heads]
        wide = [jnp.concatenate([new[h]] * (R // WP), axis=1) for h in heads]
        e = [jnp.exp(s[h] - wide[h]).astype(BF) for h in heads]
        more = [dot(e[h], va[h, kr, :]) for h in heads]
        for h in heads:
            acc[h, qr, :] = acc[h, qr, :] * jnp.exp(old[h] - new[h]) + more[h]
            top[h, qr, :] = new[h]

    def finalize(b):
        rr = rows(b)
        lane = lanes((R, WP))
        o = jnp.zeros((R, WP), F32)
        for h in range(NH):
            a0 = aug_base(h)
            total = acc[h, rr, a0 : a0 + 1]
            o = jnp.where(lane // HD == h, acc[h, rr, :] / total, o)
            lse = top[h, rr, :1] + jnp.log(total)
            q = qa[h, rr, :].astype(F32)
            qa[h, rr, :] = place3(q, lane, a0 + 1, -lse).astype(BF)
        mixed[rr, :] = o.astype(BF)

    def arrival(r, cond, pass_on):
        b = blocks[r]
        steps = []
        for ch in range(chunks):
            sends = []
            if pass_on:
                for j in range(1, H):
                    sends.append(xsend(xrow(b, ch), b, ch, (co.dp, g * H + (co.zz + j) % H), cond))
            sends.append(xsend(xrow(b, ch), b, ch, mate, cond))
            steps.append((xsend(xrow(b, ch), b, ch, mate, None, xr), sends))

        def act():
            for got, sends in steps:
                pl.when(cond)(got.got)
                for cp in sends:
                    cp.start()

        return act

    inner = jnp.logical_and(co.native, jnp.logical_not(edge))
    arrivals = {r: arrival(r, co.native if r < H else inner, False) for r in range(1, T)}
    early = {r: arrival(r, edge, True) for r in range(H, T)}
    from_mate = [
        [xsend(xrow(blocks[r], ch), blocks[r], ch, mate, None, xr) for ch in range(chunks)]
        for r in range(T)
    ]
    far = {k: swapped_sends(k) for k in range(1, H)}

    def mate_arrive(r):
        @pl.when(co.swapped)
        def _():
            for cp in from_mate[r]:
                cp.got()

    mr = net.take(T)
    mixed_out = []
    for r in range(T):
        oc, oz = owner(G, co, blocks[r])
        me = jnp.logical_and(oc == c, oz == z)
        src = lambda r=r: mixed.at[rows(blocks[r])]
        dst = lambda: mixr.at[co.hb]
        dev = (2 * co.col + oc, oz)
        mixed_out.append(net.remote(src, dst, dev, jnp.logical_not(me), rs=mr + co.hb))
        mixed_out.append(net.local(src, dst, me))

    poscopy.wait_sent()
    net.items.remove(poscopy)
    for cp in own_x:
        cp.guard(cp.wait_sent)

    qchain[0].got()
    qchain[1].start()
    for k in far:
        for cp in far[k]:
            cp.start()
    qchain[1].got()
    qchain[2].start()
    early[H]()
    for ch in wchains:
        ch[0].start()
    qchain[2].got()
    qchain[3].start()
    qchain[3].got()

    q_own.wait_sent()
    for j in range(3):
        wqh[:, j * WP : (j + 1) * WP] = jnp.where(c == 0, wqm[j], wqo[j])
    small_own.wait_sent()
    for cp in small:
        cp.got()


    def begin(r):
        if r == 0:
            mate_arrive(0)
            return
        arrivals[r]()
        mate_arrive(r)
        if r + 1 in early and r + 1 > H:
            early[r + 1]()

    def triangle(t):
        r = 0
        for k in range(1, T):
            r = r + (t >= k * (k + 1) // 2).astype(jnp.int32)
        return r, t - r * (r + 1) // 2

    ntiles = T * (T + 1) // 2

    def ftiles(t, carry):
        r, q = triangle(t)

        @pl.when(q == 0)
        def _():
            for k in range(T):
                pl.when(r == k)(functools.partial(begin, k))
            project(block_at(r))

        a, b = block_at(r), block_at(q)

        @pl.when(q < r)
        def _():
            ftile(jnp.maximum(a, b), jnp.minimum(a, b), False)

        @pl.when(q == r)
        def _():
            ftile(a, a, True)

        @pl.when(r == T - 1)
        def _():
            finalize(b)
            for k in range(T):

                @pl.when(q == k)
                def _():
                    mixed_out[2 * k].start()
                    mixed_out[2 * k + 1].start()

        for i, acts in polls.items():

            @pl.when(t == i)
            def _(acts=acts):
                for hop, n_ in acts:
                    hop_on(hop, n_)

        return carry

    def hop_on(hop, n_):
        wchains[n_][hop].got()
        wchains[n_][hop + 1].start()

    polls = {}
    hops = [(h_, n_) for h_ in range(3) for n_ in range(len(wchains))]
    if ntiles == 10:
        when = {1: [(0, 0)], 2: [(0, 1), (1, 0)], 5: [(0, 2), (1, 1), (2, 0)], 7: [(1, 2)], 8: [(2, 1)]}
        for i, acts in when.items():
            polls[i] = [(h_, 3 * n_ + m) for h_, n_ in acts for m in range(3)]
    polled = [a for acts in polls.values() for a in acts]

    lax.fori_loop(0, ntiles, ftiles, 0)
    tlocal.start()
    for cp in tswap.values():
        cp.start()

    for a in sorted(hops, key=lambda a: a[0] + a[1] // 3):
        if a not in polled:
            hop_on(*a)
    for ch in wchains:
        ch[3].got()
    net.items.remove(tlocal)
    for cp in net.items:
        if cp.dev is None:
            cp.guard(cp.wait_sent)
    net.items = [cp for cp in net.items if cp.dev is not None]
    for k in range(1, T):
        hb = (co.hb + k) % T
        net.remote(lambda: mixed.at[rows(0)], lambda hb=hb: mixr.at[hb], mate, rs=mr + hb, ss=mr).got()

    count = lengths[0]
    for i in range(1, G.slots):
        count = count + lengths[i]
    scale = (G.slots * L) / jnp.full((1, 1), count, jnp.int32).astype(F32)
    vsum[...] = jnp.zeros(vsum.shape, F32)
    ibsum[...] = jnp.zeros(ibsum.shape, F32)
    output_bias, g1, s1, outer_bias, g2, s2 = vectors
    CR = min(256, R)

    o_out = {}
    for off in range(0, R, CR):
        part = lambda ref, off=off: ref.at[pl.ds(off, CR)]
        o_out[off] = (
            net.local(lambda part=part: part(osrc), lambda part=part: part(out), co.native),
            net.remote(
                lambda part=part: part(osrc), lambda part=part: part(out), (co.mate, co.other),
                co.swapped,
            ),
        )

    def ffn(off):
        rr = pl.ds(off, CR)
        base = co.ob * R + off
        grows = pl.ds(al(base, CR), CR)
        branch = lax.fori_loop(
            0, T, lambda t, a: a + dot(mixr[t, rr, :], wpf[t]), jnp.zeros((CR, D), F32), unroll=True
        )
        e = xall[grows, :].astype(F32) + pos[grows, :].astype(F32)
        n1, inv1 = norm(e + branch + output_bias)
        first = n1 * g1 + s1
        low = first.astype(BF)
        flow[rr, :] = low

        def up(t, a):
            pre = dot(low, wif[t]) + smalls[t, 2:3, :F]
            h = jnp.maximum(pre, 0.0).astype(BF)
            hid[t, rr, :] = h
            return a + dot(h, wof[t])

        feed = lax.fori_loop(0, T, up, jnp.zeros((CR, D), F32), unroll=True)
        n2, inv2 = norm(first + feed + outer_bias)
        result = n2 * g2 + s2
        osrc[rr, :] = result.astype(BF)
        for cp in o_out[off]:
            cp.start()
        pl.when(co.swapped)(tswap[off].got)
        if off == 0:
            tlocal.guard(tlocal.wait_sent)
        place = lax.broadcasted_iota(jnp.int32, (CR, 1), 0) + base
        valid = jnp.where(place < length, scale, 0.0)
        gr = valid * (result - teach[rr, :].astype(F32))
        gs = norm_back(gr * g2, n2, inv2)
        gf = gs.astype(BF)
        gfeed[rr, :] = gf

        def down(t, a):
            gh = dot_nt(gf, wof[t])
            gpt = jnp.where(hid[t, rr, :].astype(F32) > 0, gh, 0.0).astype(BF)
            gpre[t, rr, :] = gpt
            ibsum[t] += colsum(gpt.astype(F32))
            return a + dot_nt(gpt, wif[t])

        g_first = lax.fori_loop(0, T, down, gs, unroll=True)
        gv = norm_back(g_first * g1, n1, inv1)
        gmid[rr, :] = gv
        gb = gv.astype(BF)
        gbr[rr, :] = gb

        def mix(t, a):
            gm[t, rr, :] = dot_nt(gb, wpf[t]).astype(BF)
            return a

        lax.fori_loop(0, T, mix, 0, unroll=True)
        vsum[0:1] += colsum(gv)
        vsum[1:2] += colsum(g_first * n1)
        vsum[2:3] += colsum(g_first)
        vsum[3:4] += colsum(gs)
        vsum[4:5] += colsum(gr * n2)
        vsum[5:6] += colsum(gr)

    used = [cp for cp in net.items if all(cp is not own for own in tswap.values())]
    net.items = list(tswap.values())
    gmr = net.take(T * (R // CR))
    gm_in = []
    gm_own = []
    for i in range(R // CR):
        ffn(i * CR)
        if i == 0:
            for cp in used:
                cp.guard(cp.wait_sent)
        for k in range(T):
            m = (co.zz * 2 + c + k) % T
            c2, z2 = m % 2, g * H + m // 2
            hb2 = (z2 + c2 * H) % T
            src = lambda hb2=hb2, i=i: gm.at[hb2, pl.ds(i * CR, CR)]
            dst = lambda i=i: gmall.at[pl.ds(al(co.ob * R + i * CR, CR), CR)]
            if k == 0:
                gm_own.append(net.local(src, dst).start(hold=False))
                continue
            net.remote(src, dst, (2 * co.col + c2, z2), rs=gmr + k * (R // CR) + i).start()
            gm_in.append((k, i))


    def now(src, dst, dev, ss=None):
        return net.remote(src, dst, dev, ss=ss)

    quarter = co.bf * 2 + co.bs
    plane3 = (
        ((co.dpf, z), (1 - co.bf) * 2 + co.bs),
        ((co.dps, z), co.bf * 2 + 1 - co.bs),
        ((co.dpd, z), (1 - co.bf) * 2 + 1 - co.bs),
    )

    def scatter3(src, land):
        return [
            now(lambda piece=piece: src(piece), lambda j=j: land(j), dev)
            for j, (dev, piece) in enumerate(plane3)
        ]

    class Slabs:
        def __init__(self, X, k0, n, s0, r0, r1, r2, r3, rx, r3slot, stay):
            hr, q1, q2 = r0.shape[1], r1.shape[1], r2.shape[1]
            self.n, self.k0 = n, k0
            slabs = pl.ds(k0, n)
            self.start = now(
                lambda: X.at[slabs, pl.ds(al((1 - c) * hr, hr), hr)], lambda: r0.at[slabs], mate
            )
            self.s1 = now(
                lambda: s0.at[slabs, pl.ds(al((1 - co.bf) * q1, q1), q1)],
                lambda: r1.at[slabs], step1,
            )
            self.s2 = now(
                lambda: r1.at[slabs, pl.ds(al((1 - co.bs) * q2, q2), q2)],
                lambda: r2.at[slabs], step2,
            )
            self.over = [
                now(lambda k=k: r2.at[k], lambda k=k: r3.at[r3slot(k)], (co.dp, (z + k_z) % T))
                for k, k_z in stay
                if k0 <= k < k0 + n
            ]
            self.extra = [
                now(lambda: r2.at[slabs], lambda b=b: rx.at[b - 2, slabs], (co.extra(G, b), z))
                for b in range(2, G.nbits)
            ]
            self.refs = X, s0, r0, r1, r2, rx, hr, q1, q2

        def a0(self):
            X, s0, r0, r1, r2, rx, hr, q1, q2 = self.refs
            self.start.got()
            for k in range(self.k0, self.k0 + self.n):
                kept = X[k, pl.ds(al(c * hr, hr), hr), :]
                s0[k] = (kept.astype(F32) + r0[k].astype(F32)).astype(BF)

        def go(self):
            self.s1.start()

        def a1(self):
            X, s0, r0, r1, r2, rx, hr, q1, q2 = self.refs
            self.s1.got()
            for k in range(self.k0, self.k0 + self.n):
                kept = s0[k, pl.ds(al(co.bf * q1, q1), q1), :]
                r1[k] = (kept.astype(F32) + r1[k].astype(F32)).astype(BF)
            self.s2.start()

        def a2(self):
            X, s0, r0, r1, r2, rx, hr, q1, q2 = self.refs
            self.s2.got()
            for k in range(self.k0, self.k0 + self.n):
                kept = r1[k, pl.ds(al(co.bs * q2, q2), q2), :]
                r2[k] = (kept.astype(F32) + r2[k].astype(F32)).astype(BF)
            for m, cp in enumerate(self.extra):
                cp.start(hold=False)
                cp.got()
                cp.wait_sent()
                for k in range(self.k0, self.k0 + self.n):
                    r2[k] = (r2[k].astype(F32) + rx[m, k].astype(F32)).astype(BF)
            for cp in self.over:
                cp.start()

    class Back:
        def __init__(self, chains, r2, r3, gx, dst):
            q2 = r2.shape[1]
            self.chains, self.r2, self.r3 = chains, r2, r3

            def place(width, first):
                return lambda: gx.at[pl.ds(al(first * q2, q2), width * q2)]

            own = c * 4 + co.bf * 2 + co.bs
            self.own = place(1, own)
            self.back = []
            for width, first, dev in ((1, own, step2), (2, own // 2 * 2, step1), (4, c * 4, mate)):
                self.back.append(now(place(width, first), place(width, first), dev))
            self.end = net.local(lambda: gx, lambda: dst)

        def a3(self):
            tot = self.r2[0].astype(F32)
            for k, cp in enumerate(cp for ch in self.chains for cp in ch.over):
                cp.got()
                tot = tot + self.r3[k].astype(F32)
            self.own()[...] = tot.astype(BF)
            self.back[0].start()

        def a4(self):
            self.back[0].got()
            self.back[1].start()

        def a5(self):
            self.back[1].got()
            self.back[2].start()

        def a6(self):
            self.back[2].got()
            self.end.start()

    to_z = [(k, k) for k in range(1, T)]
    minus = lambda k: k - 1
    ks = list(range(1, T)) + [0]
    co_ = [Slabs(dwo, k, 1, s0o, r0o, r1o, r2o, r3o, rxo, minus, to_z) for k in ks]
    ci_ = [Slabs(dwi, k, 1, s0i, r0i, r1i, r2i, r3i, rxi, minus, to_z) for k in ks]
    cp_ = Slabs(dwp, 0, T, s0p, r0p, r1p, r2p, r3p, rxp, minus, to_z)
    slabs = [ch for pair in zip(co_[:-1], ci_[:-1]) for ch in pair] + [co_[-1], ci_[-1], cp_]
    back_o = Back(co_, r2o, r3o, go, ug)
    back_i = Back(ci_, r2i, r3i, gi, ig)
    back_p = Back([cp_], r2p, r3p, gpp, og)

    def grads(i, carry):
        k = jnp.where(i == T - 1, 0, i + 1)
        t = (z + k) % T
        dwo[k] = dot_tn(hid[t], gfeed[...]).astype(BF)
        dwi[k] = dot_tn(flow[...], gpre[t]).astype(BF)
        dwp[k] = dot_tn(mixr[t], gbr[...]).astype(BF)
        for n_ in range(T):

            @pl.when(i == n_)
            def _():
                co_[n_].start.start()
                ci_[n_].start.start()

        return carry

    lax.fori_loop(0, T, grads, 0)
    cp_.start.start()

    vb[...] = jnp.zeros(vb.shape, F32)
    vb[0:6, :] = vsum[0:6, :]
    for t in range(T):
        vb[8 + t : 9 + t, :F] = ibsum[t]

    def sum_chain(v, r, devs):
        cps = [now(lambda: v, lambda i=i: r.at[i], dev) for i, dev in enumerate(devs)]

        def step(i):
            def act():
                cps[i].got()
                cps[i].wait_sent()
                v[...] += r[i]
                if i + 1 < len(cps):
                    cps[i + 1].start(hold=False)

            return act

        return cps[0], [step(i) for i in range(len(cps))]

    plane = [step1, step2] + [(co.extra(G, b), z) for b in range(2, G.nbits)]
    vstart, vchain = sum_chain(vb, vr, [mate] + plane)
    vstart.start(hold=False)
    nv = len(vchain)
    vover = [
        now(lambda: vb, lambda k=k: vr.at[nv + k - 1], (co.dp, (z + k) % T))
        for k in range(1, T)
    ]

    def vz():
        for cp in vover:
            cp.start(hold=False)

    def vdone():
        for cp in vover:
            cp.got()
            cp.wait_sent()
        for k in range(1, T):
            vb[...] += vr[nv + k - 1]
        vout[0:8, :] = vb[0:8, :]
        vrow = lax.broadcasted_iota(jnp.int32, vb.shape, 0)
        vout[8:9, :] = colsum(jnp.where(vrow == 8 + z, vb[...], 0.0))

    vchain = vchain + [vz, vdone]

    for i, ch in enumerate(slabs):
        ch.a0()
        if i < 2:
            ch.go()
    for k, i in gm_in:
        net.remote(
            lambda: gm.at[0, pl.ds(0, CR)], lambda: gmall.at[pl.ds(0, CR)], mate,
            rs=gmr + k * (R // CR) + i, ss=gmr,
        ).got()
    for cp in gm_own:
        cp.wait_sent()


    def prepare(i, carry):
        CH = min(256, R)
        rr = pl.ds(al(i * CH, CH), CH)
        gg = gmall[rr, :].astype(F32)
        prod = gg * mixed[rr, :].astype(F32)
        lane = lanes((CH, WP))
        k = jnp.zeros((CH, WP), F32)
        for h in range(NH):
            a0 = aug_base(h)
            data = lane // HD == h
            delta = jnp.sum(jnp.where(data, prod, 0.0), axis=-1, keepdims=True)
            base = place3(jnp.zeros((CH, WP), F32), lane, a0 + 1, -delta)
            da[h, rr, :] = jnp.where(data, gg, base).astype(BF)
            k = jnp.where(data, ka[h, rr, :].astype(F32), k)
        kt[:, rr] = k.T.astype(BF)
        zero = jnp.zeros((CH, WP), F32)
        dk[rr, :] = zero
        dv[rr, :] = zero
        dq[:, rr] = zero.T
        return carry

    lax.fori_loop(0, L // min(256, R), prepare, 0)

    def btile(i, j, masked):
        qr, kr = rows(i), rows(j)
        lane = lanes((R, WP))
        sub = lax.broadcasted_iota(jnp.int32, (WP, R), 0)
        dks, dvs, dqs = [], [], []
        for h in range(NH):
            q, d = qa[h, qr, :], da[h, qr, :]
            pm = jnp.exp(dot_nt(ka[h, kr, :], q))
            if masked:
                above = lax.broadcasted_iota(jnp.int32, (R, R), 0) <= lanes((R, R))
                pm = jnp.where(above, pm, 0.0)
            ds = (pm * dot_nt(va[h, kr, :], d)).astype(BF)
            dvs.append(dot(pm.astype(BF), d))
            dks.append(dot(ds, q))
            dqs.append(dot(kt[:, kr], ds))
        if NH == 1:
            dk[kr, :] += dks[0]
            dv[kr, :] += dvs[0]
            dq[:, qr] += dqs[0]
        else:
            dk[kr, :] += jnp.where(lane < HD, dks[0], dks[1])
            dv[kr, :] += jnp.where(lane < HD, dvs[0], dvs[1])
            dq[:, qr] += jnp.where(sub < HD, dqs[0], dqs[1])

    dwq[...] = jnp.zeros(dwq.shape, F32)
    qsum[...] = jnp.zeros(qsum.shape, F32)

    def complete(b):
        rr = rows(b)
        keep = lanes((R, WP)) < G.W
        q = dq[:, rr].T * (1.0 / math.sqrt(HD))
        sums = []
        for n_, part in enumerate((q, dk[rr, :], dv[rr, :])):
            part = jnp.where(keep, part, 0.0).astype(BF)
            gp[rr, n_ * WP : (n_ + 1) * WP] = part
            sums.append(colsum(part.astype(F32)))
        gg = gp[rr, :]
        back = dot_nt(gg, wqh[...])
        ge[rr, :] = back.astype(BF)
        oc, oz = owner(G, co, b)

        @pl.when(jnp.logical_and(oc == c, oz == z))
        def _():
            ge[rr, :] = (back + gmid[...]).astype(BF)

        dwq[...] += dot_tn(emb[rr, :], gg)
        qsum[0:1, :] += jnp.concatenate(sums, axis=1)

    order_b = [(T - 1 - s_) + g * (2 * s_ - T + 1) for s_ in range(T)]
    ends = [sum(T - i for i in range(s_ + 1)) - 1 for s_ in range(T)]
    half = R // 2
    edge_z = H - 1 + g
    at_edge = z == edge_z
    eh_sem = net.take(max(H - 1, 1))

    def slot_of(z_to):
        return (co.zz - (z_to - g * H) + H - 1) % H

    class Rows:
        def __init__(self, s_):
            b = order_b[s_]
            self.s, self.b, self.inside = s_, b, s_ >= H
            self.core = net.remote(
                lambda: ge.at[pl.ds(al(b * R + (1 - c) * half, half), half)],
                lambda: ec.at[s_], mate,
            )
            h = lambda: hsum.at[s_]
            if self.inside:
                slot, self.base = slot_of(b), eh_sem
                self.home_chip = z == b
                self.over = net.remote(
                    h, lambda: eh.at[slot], (co.dp, b), jnp.logical_not(self.home_chip),
                    rs=self.base + slot,
                )
            else:
                slot, self.base = slot_of(edge_z), net.take(max(H - 1, 1))
                self.over = net.remote(
                    h, lambda: eo.at[s_, slot], (co.dp, edge_z), jnp.logical_not(at_edge),
                    rs=self.base + slot,
                )
                self.home = net.remote(
                    lambda: hsend.at[s_], lambda: foreign, (co.dp, b), at_edge, rs=f_sem
                )

        def k0(self):
            self.core.start()

        def k1(self):
            s_ = self.s
            self.core.got()
            own = ge[pl.ds(al(self.b * R + c * half, half), half), :].astype(F32)
            hsum[s_] = (own + ec[s_].astype(F32)).astype(BF)
            self.over.start()

        def collect(self, land):
            total = hsum[self.s].astype(F32)
            for j in range(H - 1):
                net.remote(
                    lambda: hsum.at[0], lambda: land(j), mate, rs=self.base + j, ss=self.base
                ).got()
                total = total + land(j)[...].astype(F32)
            return total.astype(BF)

        def kx(self):
            @pl.when(at_edge)
            def _():
                hsend[self.s] = self.collect(lambda j: eo.at[self.s, j])

            self.home.start()

        def ky(self):
            @pl.when(self.home_chip)
            def _():
                native_half[...] = self.collect(lambda j: eh.at[j])

    f_sem = net.take()
    parts_ = [Rows(s_) for s_ in range(T)]
    foreign_in = net.remote(lambda: hsend.at[0], lambda: foreign, mate, rs=f_sem, ss=f_sem)
    to_mate = net.remote(
        lambda: give, lambda: nat.at[pl.ds(al(c * half, half), half)], mate
    )
    from_mate_half = net.remote(
        lambda: give, lambda: nat.at[pl.ds(al((1 - c) * half, half), half)], mate,
        ss=to_mate.ss, rs=to_mate.rs,
    )
    q2p = half // 4
    p_rs = scatter3(lambda piece: hp.at[pl.ds(al(piece * q2p, q2p), q2p)], lambda j: ps1.at[j])
    p_more = []
    size = q2p
    for n_, bit in enumerate(range(2, G.nbits)):
        size = size // 2
        bb = (co.col // (1 << bit)) % 2
        src = ps2 if n_ == 0 else (px if n_ % 2 == 1 else py)
        dst = px if n_ % 2 == 0 else py
        cp = net.remote(
            lambda src=src, bb=bb, size=size: src.at[pl.ds(al((1 - bb) * size, 8), size)],
            lambda dst=dst, size=size: dst.at[pl.ds(0, size)], (co.extra(G, bit), z),
        )
        p_more.append((cp, src, dst, bb, size))
    p_last = p_more[-1][2] if p_more else ps2
    p_fin = net.remote(lambda: p_last.at[pl.ds(0, G.PR)], lambda: pf, (pdp, pz), away)

    def p_first():
        foreign_in.got()
        own, other_ = native_half[...], foreign[...]
        give[...] = jnp.where(co.native, other_, own)
        to_mate.start()
        nat[pl.ds(al(c * half, half), half), :] = jnp.where(co.native, own, other_)
        hp[...] = (own.astype(F32) + other_.astype(F32)).astype(hp.dtype)
        for cp in p_rs:
            cp.start()

    def p_second():
        total = hp[pl.ds(al(quarter * q2p, q2p), q2p), :].astype(F32)
        for j, cp in enumerate(p_rs):
            cp.got()
            total = total + ps1[j].astype(F32)
        ps2[...] = total.astype(ps2.dtype)
        for cp, src, dst, bb, size in p_more:
            cp.start()
            cp.got()
            kept = src[pl.ds(al(bb * size, 8), size), :].astype(F32)
            dst[0:size, :] = (kept + dst[0:size, :].astype(F32)).astype(dst.dtype)
        p_fin.start()

    def p_third():
        pl.when(away)(p_fin.got)

        @pl.when(jnp.logical_not(away))
        def _():
            pf[...] = p_last[0 : G.PR, :]

        pr3[...] = pf[...].astype(F32)
        net.local(lambda: pr3, lambda: pgrad).start()

    def igrad_out():
        from_mate_half.got()
        net.local(lambda: nat, lambda: igrad).start()

    def run(chain, i):
        chain[i]()

    jobs = {("v", i): act for i, act in enumerate(vchain)}
    for i, ch in enumerate(slabs):
        if i >= 2:
            jobs["s", i] = ch.go
        jobs["1", i] = ch.a1
        jobs["2", i] = ch.a2
    for name, bk in (("o", back_o), ("i", back_i), ("p", back_p)):
        for n_, act in enumerate((bk.a3, bk.a4, bk.a5, bk.a6)):
            jobs[name, n_] = act
    for rw in parts_:
        for name in ("k0", "k1", "ky" if rw.inside else "kx"):
            jobs[name, rw.s] = getattr(rw, name)
    plan = {
        0: [],
        1: [("v", 0)],
        2: [],
        3: [("k0", 0), ("v", 1)],
        4: [("k1", 0)],
        5: [("v", 2), ("v", 3)],
        6: [("k0", 1)],
        7: [("k1", 1), ("kx", 0)],
        8: [("k0", 2), ("v", 4)],
        9: [("k0", 3), ("k1", 2), ("kx", 1)],
    }
    for i in range(10):
        plan[i] += [("1", i), ("2", i - 2), ("s", i + 2)]
    plan = {i: [key for key in acts if key in jobs] for i, acts in plan.items()}
    if ntiles != 10:
        plan = {e: [("k0", s_)] for s_, e in enumerate(ends)}
    left = [key for key in jobs if not any(key in acts for acts in plan.values())]
    def btiles(t, carry):
        s_, u = 0, t
        for k in range(1, T):
            past = (t > ends[k - 1]).astype(jnp.int32)
            s_ = s_ + past
            u = u - past * (T - k + 1)
        b = (T - 1 - s_) + g * (2 * s_ - T + 1)
        far = b - u + g * (2 * u)

        @pl.when(u == 0)
        def _():
            btile(b, b, True)

        @pl.when(u > 0)
        def _():
            btile(jnp.maximum(b, far), jnp.minimum(b, far), False)

        @pl.when(u == T - 1 - s_)
        def _():
            complete(b)

        for i in range(ntiles):
            acts = [jobs[key] for key in plan.get(i, ())]
            if acts:

                @pl.when(t == i)
                def _(acts=acts):
                    for act in acts:
                        act()

        return carry

    lax.fori_loop(0, ntiles, btiles, 0)

    dwqb[c] = dwq[...].astype(BF)
    hq = D // 2
    e8 = D // 8
    qstart = now(
        lambda: dwqb.at[c, pl.ds(al((1 - c) * hq, hq), hq)], lambda: r0q.at[c], mate
    ).start()
    q_rs = scatter3(lambda piece: s0q.at[:, pl.ds(al(piece * e8, e8), e8)], lambda j: r1q.at[j])
    q_extra = [
        now(lambda: r2q, lambda b=b: rxq.at[b - 2], (co.extra(G, b), z)) for b in range(2, G.nbits)
    ]
    q_over = now(lambda: r2q.at[1], lambda: r3q.at[0], (co.dp, co.other))
    q_own = lambda: gq.at[pl.ds(al((c * 4 + quarter) * e8, e8), e8)]
    q_ag = [now(q_own, q_own, dev) for dev, _ in plane3]
    q_half = lambda: gq.at[pl.ds(al(c * hq, hq), hq)]
    q_core = now(q_half, q_half, mate)
    q_out = net.local(lambda: gq, lambda: qg)

    def q_sum():
        total = s0q[:, pl.ds(al(quarter * e8, e8), e8), :].astype(F32)
        for j, cp in enumerate(q_rs):
            cp.got()
            total = total + r1q[j].astype(F32)
        r2q[...] = total.astype(BF)
        for m, cp in enumerate(q_extra):
            cp.start(hold=False)
            cp.got()
            cp.wait_sent()
            r2q[...] = (r2q[...].astype(F32) + rxq[m].astype(F32)).astype(BF)
        q_over.start()

    def q_back():
        q_over.got()
        q_own()[...] = (r2q[0].astype(F32) + r3q[0].astype(F32)).astype(BF)
        for cp in q_ag:
            cp.start()

    def q_join():
        for cp in q_ag:
            cp.got()
        q_core.start()

    def q_end():
        q_core.got()
        q_out.start()

    qb[c] = qsum[...]
    qmate = now(lambda: qb.at[c], lambda: qb.at[c], mate).start(hold=False)
    qsums, qchain2 = sum_chain(qb, qr, plane)
    qover = now(lambda: qb.at[1], lambda: qr.at[len(plane), 0], (co.dp, co.other))

    def rest(*names):
        for key in left:
            if key[0] in names:
                jobs[key]()

    def backs(n_):
        for key in left:
            if key[0] in "oip" and key[1] == n_:
                jobs[key]()

    rest("k1")
    pltpu.make_async_remote_copy(
        src_ref=dwqb.at[c, pl.ds(0, hq)], dst_ref=r0q.at[1 - c], send_sem=net.sem(qstart.ss),
        recv_sem=net.sem(qstart.rs), device_id=mate, device_id_type=MESH,
    ).wait_recv()
    s0q[c] = dwqb[c, pl.ds(al(c * hq, hq), hq), :]
    s0q[1 - c] = r0q[1 - c]
    for cp in q_rs:
        cp.start()
    qmate.got()
    qmate.wait_sent()
    qsums.start(hold=False)
    rest("s", "1", "v")
    rest("2")
    rest("kx")
    backs(0)
    qchain2[0]()
    rest("ky")
    p_first()
    q_sum()
    for i in range(1, len(qchain2)):
        qchain2[i]()
    qover.start(hold=False)
    backs(1)
    igrad_out()
    p_second()
    q_back()
    qover.got()
    qover.wait_sent()
    qb[0] += qr[len(plane), 0]
    vout[9:10, :WP] = qb[0, 0:1, :WP]
    vout[10:11, :WP] = qb[0, 0:1, 2 * WP :]
    backs(2)
    q_join()
    backs(3)
    p_third()
    q_end()
    for off in o_out:
        pl.when(co.swapped)(o_out[off][1].got)
    net.drain()
    assert net.n <= sem.shape[0], net.n


def emit_kernel(
    G, out_in, igrad_in, pgrad_in, qg_in, og_in, ig_in, ug_in, vin,
    out, igrad, pgrad, qg, qvg, og, ig, ug, ibg, v0, v1, v2, v3, v4, v5,
):
    out[...] = out_in[...]
    igrad[...] = igrad_in[...]
    pgrad[...] = pgrad_in[...]
    for j in range(3):
        qg[j] = qg_in[:, j * G.WP : j * G.WP + G.W].astype(F32)
    qvg[...] = vin[9:11, : G.W]
    og[...] = og_in[: G.W, :].astype(F32)
    ig[...] = ig_in[...].astype(F32)
    ug[...] = ug_in[...].astype(F32)
    ibg[...] = vin[8:9, : G.F].reshape(G.F)
    for i, v in enumerate((v0, v1, v2, v3, v4, v5)):
        v[...] = vin[i : i + 1, :].reshape(G.D)


def on_device(G, *args):
    (inputs, teacher, lengths, positions, qkv_weight, query_value_bias, output_weight, output_bias,
     first_gain, first_shift, inner_weight, inner_bias, outer_weight, outer_bias, second_gain,
     second_shift) = args
    T, R, D, L, W, WP, NH, F, H = G.T, G.R, G.D, G.L, G.W, G.WP, G.NH, G.F, G.H
    dma = lambda n: pltpu.SemaphoreType.DMA((n,))
    vm = pltpu.VMEM
    wq = jnp.pad(jnp.transpose(qkv_weight, (1, 0, 2)), ((0, 0), (0, 0), (0, WP - W)))
    wp = jnp.pad(output_weight, ((0, WP - W), (0, 0)))
    sizes = [(D, F, T), (F, D, T), (WP, D, T), (D, 3 * WP, 2)]
    nplane = G.nbits
    V = 8 + (T + 7) // 8 * 8
    scratch = [
        vm((L, D), BF), vm((L, D), BF), vm((L, D), BF),
        vm((NH, L, WP), BF), vm((NH, L, WP), BF), vm((NH, L, WP), BF), vm((NH, L, WP), BF),
        vm((WP, L), BF), vm((2, L, WP), F32), vm((NH, L, WP), F32), vm((L, WP), BF),
        vm((T, R, WP), BF),
        vm((8, D), F32), vm((3, D, WP), BF), vm((3, D, WP), BF), vm((D, 3 * WP), BF),
        vm((T, D, F), BF), vm((T, F, D), BF),
        vm((T, WP, D), BF), vm((T, 8, D), F32), vm((R, D), BF),
        vm((R, D), BF), vm((T, R, F), BF), vm((T, R, F), BF), vm((R, D), BF), vm((R, D), BF),
        vm((R, D), F32), vm((R, D), BF), vm((T, R, WP), BF), vm((L, WP), BF), vm((8, D), F32),
        vm((T, 1, F), F32),
        vm((T, D, F), BF), vm((T, F, D), BF), vm((T, WP, D), BF), vm((WP, L), F32),
        vm((L, 3 * WP), BF),
        vm((D, 3 * WP), F32), vm((2, D, 3 * WP), BF), vm((8, 3 * WP), F32),
    ]
    for shift in (1, 1, 2, 3):
        scratch += [vm((n, r >> shift, w), BF) for r, w, n in sizes]
        if shift == 2:
            scratch[-1] = vm((3, 2, D >> 3, 3 * WP), BF)
    scratch += [vm((T - 1, r >> 3, w), BF) for r, w, n in sizes[:3]] + [vm((1, D >> 3, 3 * WP), BF)]
    more = G.nbits - 2
    PD = BF if G.PR % 16 == 0 else F32
    scratch += [vm((more, n, r >> 3, w) if more else (1, 1, 16, 128), BF) for r, w, n in sizes]
    scratch += [vm((r, w), BF) for r, w, n in sizes]
    scratch += [
        vm((T, R // 2, D), BF), vm((T, R // 2, D), BF), vm((R // 2, D), PD),
        vm((H, max(H - 1, 1), R // 2, D), BF), vm((max(H - 1, 1), R // 2, D), BF),
        vm((H, R // 2, D), BF), vm((R // 2, D), BF), vm((R // 2, D), BF), vm((R // 2, D), BF),
        vm((R, D), BF), vm((3, R // 8, D), PD), vm((R // 8, D), PD),
        vm((max(R // 16, 8), D) if more else (8, 128), PD),
        vm((max(R // 32, 8), D) if more else (8, 128), PD), vm((G.PR, D), PD),
        vm((G.PR, D), F32), vm((V, D), F32), vm((1 + nplane + T - 1, V, D), F32),
        vm((2, 8, 3 * WP), F32), vm((nplane + 1, 2, 8, 3 * WP), F32), dma(21 * T * T),
    ]
    outs = [
        ((R, D), BF), ((R, D), BF), ((G.PR, D), F32), ((D, 3 * WP), BF),
        ((WP, D), BF), ((D, F), BF), ((F, D), BF), ((16, D), F32),
    ]
    anyspec = pl.BlockSpec(memory_space=pl.ANY)
    results = pl.pallas_call(
        functools.partial(layer_kernel, G),
        out_shape=tuple(jax.ShapeDtypeStruct(s, d) for s, d in outs),
        in_specs=[SM] + [anyspec] * 7 + [VM] * 8,
        out_specs=tuple([anyspec] * 7 + [VM]),
        scratch_shapes=scratch,
        compiler_params=pltpu.CompilerParams(
            vmem_limit_bytes=63 << 20, collective_id=0, has_side_effects=True
        ),
        name="layer",
    )(lengths, inputs, teacher, wq, inner_weight, outer_weight, wp, positions, query_value_bias,
      inner_bias, output_bias, first_gain, first_shift, outer_bias, second_gain, second_shift)
    finals = [
        ((R, D), BF), ((R, D), BF), ((G.PR, D), F32), ((3, D, W), F32), ((2, W), F32),
        ((W, D), F32), ((D, F), F32), ((F, D), F32), ((F,), F32),
    ] + [((D,), F32)] * 6
    (out, igrad, pgrad, qg, qvg, og, ig, ug, ibg, *vs) = pl.pallas_call(
        functools.partial(emit_kernel, G),
        out_shape=tuple(jax.ShapeDtypeStruct(s, d) for s, d in finals),
        in_specs=[VM] * 8,
        out_specs=tuple([VM] * 15),
        compiler_params=pltpu.CompilerParams(vmem_limit_bytes=63 << 20),
        name="emit",
    )(*results)
    return (
        out, igrad, pgrad, jnp.transpose(qg, (1, 0, 2)), qvg, og, vs[0], vs[1], vs[2],
        ig, ibg, ug, vs[3], vs[4], vs[5],
    )


def solution(mesh):
    rows = P(("dp", "tensor"), None)
    specs = (
        rows, rows, P(), P(), P(None, None, "tensor"), P(None, "tensor"), P("tensor", None), P(),
        P(), P(), P(None, "tensor"), P("tensor"), P("tensor", None), P(), P(), P(),
    )
    outs = (
        rows, rows, rows, P(None, None, "tensor"), P(None, "tensor"), P("tensor", None), P(), P(),
        P(), P(None, "tensor"), P("tensor"), P("tensor", None), P(), P(), P(),
    )

    def step(*args):
        G = Geo(mesh, args[2].shape[0], args[3].shape[0], args[0].shape[1], args[11].shape[0])
        body = jax.shard_map(
            functools.partial(on_device, G), mesh=mesh, in_specs=specs, out_specs=outs,
            check_vma=False,
        )
        return body(*args)

    return step
```

```python
import functools
import math

import jax
import jax.numpy as jnp
from jax import lax
from jax.experimental import pallas as pl
from jax.experimental.pallas import tpu as pltpu
from jax.sharding import PartitionSpec as P

HD = 64
EPS = 1e-05
NEG = -1e30
BF = jnp.bfloat16
F32 = jnp.float32
MESH = pl.DeviceIdType.MESH
VM = pl.BlockSpec(memory_space=pltpu.VMEM)
SM = pl.BlockSpec(memory_space=pltpu.SMEM)


class Geo:
    def __init__(self, mesh, slots, seq, width, hidden):
        self.T = mesh.shape["tensor"]
        self.DP = mesh.shape["dp"]
        self.H = self.T // 2
        self.NC = self.DP // 2
        self.nbits = self.NC.bit_length() - 1
        self.slots = slots
        self.L = seq
        self.D = width
        self.FF = hidden
        self.R = seq // self.T
        self.W = width // self.T
        self.WP = max(self.W, 128)
        self.NH = self.W // HD
        self.F = hidden // self.T
        self.PR = seq // (self.DP * self.T)


class Co:
    def __init__(self, G):
        self.dp = lax.axis_index("dp")
        self.z = lax.axis_index("tensor")
        self.c = self.dp % 2
        self.col = self.dp // 2
        self.g = self.z // G.H
        self.zz = self.z - self.g * G.H
        self.other = (self.z + G.H) % G.T
        self.native = self.c == self.g
        self.swapped = self.c != self.g
        self.hb = (self.z + self.c * G.H) % G.T
        self.ob = self.own_block(G, self.z, self.c)
        self.slot = 2 * self.col + self.g
        self.mate = self.dp + 1 - 2 * self.c
        b0 = self.col % 2
        b1 = (self.col // 2) % 2
        self.bf = b0 + self.c * (b1 - b0)
        self.bs = b1 + self.c * (b0 - b1)
        wf = 1 + self.c
        ws = 2 - self.c
        self.dpf = self.dp + 2 * wf * (1 - 2 * self.bf)
        self.dps = self.dp + 2 * ws * (1 - 2 * self.bs)
        self.dpd = self.dpf + self.dps - self.dp

    @staticmethod
    def own_block(G, z, c):
        d = c - z // G.H
        return (z + d * d * G.H) % G.T

    def extra(self, G, bit):
        b = (self.col // (1 << bit)) % 2
        return self.dp + (2 << bit) * (1 - 2 * b)

    def piece(self):
        return self.c * 4 + self.bs * 2 + self.bf


def owner(G, co, b):
    out = (b // G.H - co.g) * (b // G.H - co.g)
    return co.g + out * (1 - 2 * co.g), (b + out * G.H) % G.T


class Net:
    def __init__(self, ref):
        self.ref = ref
        self.n = 0
        self.items = []

    def take(self, n=1):
        base = self.n
        self.n += n
        return base

    def sem(self, i):
        return self.ref.at[i]

    def remote(self, src, dst, dev, cond=None, ss=None, rs=None):
        ss = self.take() if ss is None else ss
        rs = self.take() if rs is None else rs
        return Copy(self, src, dst, dev, ss, rs, cond)

    def local(self, src, dst, cond=None):
        return Copy(self, src, dst, None, self.take(), None, cond)

    def drain(self):
        for copy in self.items:
            copy.guard(copy.wait_sent)
        self.items = []


class Copy:
    def __init__(self, net, src, dst, dev, ss, rs, cond):
        self.net, self.src, self.dst, self.dev = net, src, dst, dev
        self.ss, self.rs, self.cond = ss, rs, cond

    def make(self):
        net = self.net
        if self.dev is None:
            return pltpu.make_async_copy(self.src(), self.dst(), net.sem(self.ss))
        return pltpu.make_async_remote_copy(
            src_ref=self.src(), dst_ref=self.dst(), send_sem=net.sem(self.ss),
            recv_sem=net.sem(self.rs), device_id=self.dev, device_id_type=MESH,
        )

    def guard(self, fn):
        if self.cond is None:
            fn()
        else:
            pl.when(self.cond)(fn)

    def start(self, hold=True):
        self.guard(lambda: self.make().start())
        if hold:
            self.net.items.append(self)
        return self

    def wait_sent(self):
        if self.dev is None:
            self.make().wait()
        else:
            self.make().wait_send()

    def got(self):
        self.make().wait_recv()


def column_partners(G, co):
    out = [(co.mate, co.z), (co.dpf, co.z), (co.dps, co.z), (co.dpd, co.z), (co.mate, co.other)]
    out += [(co.dp, (co.z + k) % G.T) for k in range(1, G.T)]
    out += [(co.mate, (co.z + k) % G.T) for k in range(1, G.T) if k != G.H]
    out += [(co.extra(G, b), co.z) for b in range(2, G.nbits)]
    return out


def lanes(shape):
    return lax.broadcasted_iota(jnp.int32, shape, len(shape) - 1)


def aug_base(h):
    return HD if h == 0 else 0


def dot(a, b):
    return lax.dot_general(a, b, (((1,), (0,)), ((), ())), preferred_element_type=F32)


def dot_nt(a, b):
    return lax.dot_general(a, b, (((1,), (1,)), ((), ())), preferred_element_type=F32)


def dot_tn(a, b):
    return lax.dot_general(a, b, (((0,), (0,)), ((), ())), preferred_element_type=F32)


def parts3(v):
    hi = v.astype(BF).astype(F32)
    mid = (v - hi).astype(BF).astype(F32)
    return hi, mid, v - hi - mid


def place3(base, lane, first, v):
    hi, mid, lo = parts3(v)
    base = jnp.where(lane == first, hi, base)
    base = jnp.where(lane == first + 1, mid, base)
    return jnp.where(lane == first + 2, lo, base)


def norm(v):
    centre = jnp.mean(v, axis=-1, keepdims=True)
    v = v - centre
    inv = lax.rsqrt(jnp.mean(v * v, axis=-1, keepdims=True) + EPS)
    return v * inv, inv


def norm_back(e, normal, inv):
    a = jnp.mean(e, axis=-1, keepdims=True)
    b = jnp.mean(e * normal, axis=-1, keepdims=True)
    return inv * (e - a - normal * b)


def colsum(v):
    return jnp.sum(v, axis=0, keepdims=True)


def al(v, n):
    return pl.multiple_of(v, n)


def layer_kernel(
    G, lengths, x, te, wq, wi, wo, wp, pos_in, qvbias, ibias, *rest,
):
    vectors = [v[...].astype(F32).reshape(1, G.D) for v in rest[:6]]
    layer_body(G, vectors, lengths, x, te, wq, wi, wo, wp, pos_in, qvbias, ibias, *rest[6:])


def layer_body(
    G, vectors, lengths, x, te, wq, wi, wo, wp, pos_in, qvbias, ibias,
    out, igrad, pgrad, qg, og, ig, ug, vout,
    xall, pos, emb, qa, ka, va, da, kt, acc, top, mixed, mixr,
    sm, wqm, wqo, wqh, wif, wof, wpf, smalls, teach,
    flow, hid, gpre, gfeed, gbr, gmid, osrc, gm, gmall, vsum, ibsum,
    dwi, dwo, dwp, dq, gp, dwq, dwqb, qsum,
    s0i, s0o, s0p, s0q, r0i, r0o, r0p, r0q, r1i, r1o, r1p, r1q, r2i, r2o, r2p, r2q,
    r3i, r3o, r3p, r3q, rxi, rxo, rxp, rxq, gi, go, gpp, gq,
    ec, hsum, hp, eo, eh, hsend, native_half, foreign, give, nat,
    ps1, ps2, px, py, pf, pr3, vb, vr, qb, qr,
    sem,
):
    co = Co(G)
    net = Net(sem)
    T, H, R, L, WP, NH, D, F = G.T, G.H, G.R, G.L, G.WP, G.NH, G.D, G.F
    z, c, g = co.z, co.c, co.g
    mate, step1, step2 = (co.mate, z), (co.dpf, z), (co.dps, z)
    length = lengths[co.slot]
    ge, dk, dv = xall, acc.at[0], acc.at[1]

    def rows(b, n=R):
        return pl.ds(al(b * R, R), n)

    pp = c * (G.DP // 2) + co.bf * (G.DP // 4) + co.bs * (G.DP // 8)
    for bit in range(2, G.nbits):
        pp = pp + ((co.col // (1 << bit)) % 2) * (G.DP // (4 << bit))
    flat = z * G.DP + pp
    pdp, pz = flat // T, flat % T
    away = jnp.logical_or(pdp != co.dp, pz != z)
    mine = co.dp * T + z
    fz, fp = mine // G.DP, mine % G.DP
    fc = fp // (G.DP // 2)
    f1 = (fp // (G.DP // 4)) % 2
    f2 = (fp // (G.DP // 8)) % 2
    fcol = (f1 + fc * (f2 - f1)) + 2 * (f2 + fc * (f1 - f2))
    for bit in range(2, G.nbits):
        fcol = fcol + ((fp // (G.DP // (4 << bit))) % 2) * (1 << bit)
    poscopy = net.local(lambda: pos_in, lambda: pos).start()
    bar = pltpu.get_barrier_semaphore()
    partners = column_partners(G, co)
    for dev in partners:
        pl.semaphore_signal(bar, inc=1, device_id=dev, device_id_type=MESH)

    @pl.when(away)
    def _():
        pl.semaphore_signal(bar, inc=1, device_id=(2 * fcol + fc, fz), device_id_type=MESH)

    pl.semaphore_wait(bar, len(partners) + away.astype(jnp.int32))

    bs, br = net.take(T), net.take(T)
    sm[...] = jnp.zeros(sm.shape, F32)
    sm[0:2, : G.W] = qvbias[...].astype(F32)
    sm[2:3, :F] = ibias[...].astype(F32).reshape(1, F)
    small_own = net.local(lambda: sm, lambda: smalls.at[z]).start(hold=False)
    small = [
        net.remote(lambda: sm, lambda: smalls.at[z], (co.dp, (z + k) % T)).start()
        for k in range(1, T)
    ]
    p = co.piece()

    def weight_chain(src, dst, slab, k):
        size = src.shape[-2] // 8

        def view(ref, s, first, count):
            where = pl.ds(al(first * size, size), count * size)
            if s is None:
                return ref.at[:, where] if slab is None else ref.at[where]
            return ref.at[s, where]

        to = None if slab is None else z
        cps = [net.remote(lambda: view(src, None, p, 1), lambda: view(dst, to, p, 1), (co.dp, (z + k) % T))]
        for first, count, dev in ((p, 1, step1), (p // 2 * 2, 2, step2), (c * 4, 4, mate)):
            ref = lambda first=first, count=count: view(dst, slab, first, count)
            cps.append(net.remote(ref, ref, dev))
        return cps

    qchain = weight_chain(wq, wqo, None, H)
    qchain[0].start()
    q_own = net.local(lambda: wq, lambda: wqm).start(hold=False)
    wchains = []
    whole = ((wp, wpf), (wi, wif), (wo, wof))
    for src, dst in whole:
        net.local(lambda src=src: src, lambda dst=dst: dst.at[z]).start()
    for k in range(1, T):
        for src, dst in whole:
            wchains.append(weight_chain(src, dst, (z - k) % T, k))

    chunks = 1
    n = R // chunks
    xr = net.take(T * chunks)

    def order(r):
        if r == 0:
            return z
        if r < H:
            return g * H + (co.zz + r) % H
        k = r - H
        return (H - 1 - k) + (1 - g) * (2 * k + 1)

    blocks = [order(r) for r in range(T)]

    def block_at(r):
        out = blocks[0]
        for k in range(1, T):
            out = jnp.where(r == k, blocks[k], out)
        return out
    zb = H - 1 + c
    edge = jnp.logical_and(co.native, z == H - 1 + g)

    def xrow(b, ch):
        return lambda: xall.at[pl.ds(al(b * R + ch * n, n), n)]

    def xmine(ch):
        return lambda: x.at[pl.ds(ch * n, n)]

    def xsend(src, b, ch, dev, cond, ss=None):
        return net.remote(src, xrow(b, ch), dev, cond, rs=xr + b * chunks + ch, ss=ss)

    def swapped_sends(k):
        cond = jnp.logical_and(co.swapped, (z - zb) * (1 - 2 * c) == k + 1)
        return [xsend(xmine(ch), z, ch, (co.dp, zb), cond) for ch in range(chunks)]

    own_x = []
    for ch in range(chunks):
        for j in range(1, H):
            xsend(xmine(ch), z, ch, (co.dp, g * H + (co.zz + j) % H), co.native).start()
        xsend(xmine(ch), z, ch, mate, co.native).start()
        own_x.append(net.local(xmine(ch), xrow(z, ch), co.native).start(hold=False))
    for cp in swapped_sends(0):
        cp.start()

    tlocal = net.local(lambda: te, lambda: teach, co.native)
    CR = min(256, R)
    tswap = {}
    for off in range(0, R, CR):
        part = lambda ref, off=off: ref.at[pl.ds(off, CR)]
        tswap[off] = net.remote(
            lambda part=part: part(te), lambda part=part: part(teach), (co.mate, co.other),
            co.swapped,
        )

    def project(b):
        CH = min(256, R)
        qb_, vb_ = smalls[co.hb, 0:1, :WP], smalls[co.hb, 1:2, :WP]

        def step(i, carry):
            first = b * R + i * CH
            rr = pl.ds(al(first, CH), CH)
            low = (xall[rr, :].astype(F32) + pos[rr, :].astype(F32)).astype(BF)
            emb[rr, :] = low
            pr = dot(low, wqh[...])
            q = (pr[:, :WP] + qb_).astype(BF).astype(F32) * (1.0 / math.sqrt(HD))
            k = pr[:, WP : 2 * WP].astype(BF).astype(F32)
            v = (pr[:, 2 * WP :] + vb_).astype(BF).astype(F32)
            lane = lanes((CH, WP))
            place = lax.broadcasted_iota(jnp.int32, (CH, WP), 0) + first
            limit = jnp.where(place < length, 0.0, NEG)
            for h in range(NH):
                a0 = aug_base(h)
                data = lane // HD == h
                ones = jnp.where((lane >= a0) & (lane < a0 + 4), 1.0, 0.0)
                qa[h, rr, :] = jnp.where(data, q, jnp.where(lane == a0, 1.0, 0.0)).astype(BF)
                ka[h, rr, :] = jnp.where(data, k, jnp.where(lane == a0, limit, ones)).astype(BF)
                va[h, rr, :] = jnp.where(data, v, ones).astype(BF)
                acc[h, rr, :] = jnp.zeros((CH, WP), F32)
                top[h, rr, :] = jnp.full((CH, WP), NEG, F32)
            return carry

        lax.fori_loop(0, R // CH, step, 0, unroll=True)

    def ftile(i, j, masked):
        qr, kr = rows(i), rows(j)
        heads = range(NH)
        s = [dot_nt(qa[h, qr, :], ka[h, kr, :]) for h in heads]
        if masked:
            below = lax.broadcasted_iota(jnp.int32, (R, R), 0) >= lanes((R, R))
            s = [jnp.where(below, v, NEG) for v in s]
        old = [top[h, qr, :] for h in heads]
        new = [jnp.maximum(old[h], jnp.max(s[h], axis=-1, keepdims=True)) for h in heads]
        wide = [jnp.concatenate([new[h]] * (R // WP), axis=1) for h in heads]
        e = [jnp.exp(s[h] - wide[h]).astype(BF) for h in heads]
        more = [dot(e[h], va[h, kr, :]) for h in heads]
        for h in heads:
            acc[h, qr, :] = acc[h, qr, :] * jnp.exp(old[h] - new[h]) + more[h]
            top[h, qr, :] = new[h]

    def finalize(b):
        rr = rows(b)
        lane = lanes((R, WP))
        o = jnp.zeros((R, WP), F32)
        for h in range(NH):
            a0 = aug_base(h)
            total = acc[h, rr, a0 : a0 + 1]
            o = jnp.where(lane // HD == h, acc[h, rr, :] / total, o)
            lse = top[h, rr, :1] + jnp.log(total)
            q = qa[h, rr, :].astype(F32)
            qa[h, rr, :] = place3(q, lane, a0 + 1, -lse).astype(BF)
        mixed[rr, :] = o.astype(BF)

    def arrival(r, cond, pass_on):
        b = blocks[r]
        steps = []
        for ch in range(chunks):
            sends = []
            if pass_on:
                for j in range(1, H):
                    sends.append(xsend(xrow(b, ch), b, ch, (co.dp, g * H + (co.zz + j) % H), cond))
            sends.append(xsend(xrow(b, ch), b, ch, mate, cond))
            steps.append((xsend(xrow(b, ch), b, ch, mate, None, xr), sends))

        def act():
            for got, sends in steps:
                pl.when(cond)(got.got)
                for cp in sends:
                    cp.start()

        return act

    inner = jnp.logical_and(co.native, jnp.logical_not(edge))
    arrivals = {r: arrival(r, co.native if r < H else inner, False) for r in range(1, T)}
    early = {r: arrival(r, edge, True) for r in range(H, T)}
    from_mate = [
        [xsend(xrow(blocks[r], ch), blocks[r], ch, mate, None, xr) for ch in range(chunks)]
        for r in range(T)
    ]
    far = {k: swapped_sends(k) for k in range(1, H)}

    def mate_arrive(r):
        @pl.when(co.swapped)
        def _():
            for cp in from_mate[r]:
                cp.got()

    mr = net.take(T)
    mixed_out = []
    for r in range(T):
        oc, oz = owner(G, co, blocks[r])
        me = jnp.logical_and(oc == c, oz == z)
        src = lambda r=r: mixed.at[rows(blocks[r])]
        dst = lambda: mixr.at[co.hb]
        dev = (2 * co.col + oc, oz)
        mixed_out.append(net.remote(src, dst, dev, jnp.logical_not(me), rs=mr + co.hb))
        mixed_out.append(net.local(src, dst, me))

    poscopy.wait_sent()
    net.items.remove(poscopy)
    for cp in own_x:
        cp.guard(cp.wait_sent)

    qchain[0].got()
    qchain[1].start()
    for k in far:
        for cp in far[k]:
            cp.start()
    qchain[1].got()
    qchain[2].start()
    early[H]()
    for ch in wchains:
        ch[0].start()
    qchain[2].got()
    qchain[3].start()
    qchain[3].got()

    q_own.wait_sent()
    for j in range(3):
        wqh[:, j * WP : (j + 1) * WP] = jnp.where(c == 0, wqm[j], wqo[j])
    small_own.wait_sent()
    for cp in small:
        cp.got()


    def begin(r):
        if r == 0:
            mate_arrive(0)
            return
        arrivals[r]()
        mate_arrive(r)
        if r + 1 in early and r + 1 > H:
            early[r + 1]()

    def triangle(t):
        r = 0
        for k in range(1, T):
            r = r + (t >= k * (k + 1) // 2).astype(jnp.int32)
        return r, t - r * (r + 1) // 2

    ntiles = T * (T + 1) // 2

    def ftiles(t, carry):
        r, q = triangle(t)

        @pl.when(q == 0)
        def _():
            for k in range(T):
                pl.when(r == k)(functools.partial(begin, k))
            project(block_at(r))

        a, b = block_at(r), block_at(q)

        @pl.when(q < r)
        def _():
            ftile(jnp.maximum(a, b), jnp.minimum(a, b), False)

        @pl.when(q == r)
        def _():
            ftile(a, a, True)

        @pl.when(r == T - 1)
        def _():
            finalize(b)
            for k in range(T):

                @pl.when(q == k)
                def _():
                    mixed_out[2 * k].start()
                    mixed_out[2 * k + 1].start()

        for i, acts in polls.items():

            @pl.when(t == i)
            def _(acts=acts):
                for hop, n_ in acts:
                    hop_on(hop, n_)

        return carry

    def hop_on(hop, n_):
        wchains[n_][hop].got()
        wchains[n_][hop + 1].start()

    polls = {}
    hops = [(h_, n_) for h_ in range(3) for n_ in range(len(wchains))]
    if ntiles == 10:
        when = {1: [(0, 0)], 2: [(0, 1), (1, 0)], 5: [(0, 2), (1, 1), (2, 0)], 7: [(1, 2)], 8: [(2, 1)]}
        for i, acts in when.items():
            polls[i] = [(h_, 3 * n_ + m) for h_, n_ in acts for m in range(3)]
    polled = [a for acts in polls.values() for a in acts]

    lax.fori_loop(0, ntiles, ftiles, 0)
    tlocal.start()
    for cp in tswap.values():
        cp.start()

    for a in sorted(hops, key=lambda a: a[0] + a[1] // 3):
        if a not in polled:
            hop_on(*a)
    for k in range(T - 1):
        wchains[3 * k][3].got()
    net.items.remove(tlocal)
    for cp in net.items:
        if cp.dev is None:
            cp.guard(cp.wait_sent)
    net.items = [cp for cp in net.items if cp.dev is not None]
    for k in range(1, T):
        hb = (co.hb + k) % T
        net.remote(lambda: mixed.at[rows(0)], lambda hb=hb: mixr.at[hb], mate, rs=mr + hb, ss=mr).got()

    count = lengths[0]
    for i in range(1, G.slots):
        count = count + lengths[i]
    scale = (G.slots * L) / jnp.full((1, 1), count, jnp.int32).astype(F32)
    vsum[...] = jnp.zeros(vsum.shape, F32)
    ibsum[...] = jnp.zeros(ibsum.shape, F32)
    output_bias, g1, s1, outer_bias, g2, s2 = vectors
    CR = min(256, R)

    o_out = {}
    for off in range(0, R, CR):
        part = lambda ref, off=off: ref.at[pl.ds(off, CR)]
        o_out[off] = (
            net.local(lambda part=part: part(osrc), lambda part=part: part(out), co.native),
            net.remote(
                lambda part=part: part(osrc), lambda part=part: part(out), (co.mate, co.other),
                co.swapped,
            ),
        )

    def ffn(off):
        rr = pl.ds(off, CR)
        base = co.ob * R + off
        grows = pl.ds(al(base, CR), CR)
        branch = lax.fori_loop(
            0, T, lambda t, a: a + dot(mixr[t, rr, :], wpf[t]), jnp.zeros((CR, D), F32), unroll=True
        )
        e = xall[grows, :].astype(F32) + pos[grows, :].astype(F32)
        n1, inv1 = norm(e + branch + output_bias)
        first = n1 * g1 + s1
        low = first.astype(BF)
        flow[rr, :] = low

        def up(t, a):
            pre = dot(low, wif[t]) + smalls[t, 2:3, :F]
            h = jnp.maximum(pre, 0.0).astype(BF)
            hid[t, rr, :] = h
            return a + dot(h, wof[t])

        feed = jnp.zeros((CR, D), F32)
        for k in range(T):
            if off == 0 and k > 0:
                wchains[3 * k - 2][3].got()
                wchains[3 * k - 1][3].got()
            feed = up((z - k) % T, feed)
        n2, inv2 = norm(first + feed + outer_bias)
        result = n2 * g2 + s2
        osrc[rr, :] = result.astype(BF)
        for cp in o_out[off]:
            cp.start()
        pl.when(co.swapped)(tswap[off].got)
        if off == 0:
            tlocal.guard(tlocal.wait_sent)
        place = lax.broadcasted_iota(jnp.int32, (CR, 1), 0) + base
        valid = jnp.where(place < length, scale, 0.0)
        gr = valid * (result - teach[rr, :].astype(F32))
        gs = norm_back(gr * g2, n2, inv2)
        gf = gs.astype(BF)
        gfeed[rr, :] = gf

        def down(t, a):
            gh = dot_nt(gf, wof[t])
            gpt = jnp.where(hid[t, rr, :].astype(F32) > 0, gh, 0.0).astype(BF)
            gpre[t, rr, :] = gpt
            ibsum[t] += colsum(gpt.astype(F32))
            return a + dot_nt(gpt, wif[t])

        g_first = lax.fori_loop(0, T, down, gs, unroll=True)
        gv = norm_back(g_first * g1, n1, inv1)
        gmid[rr, :] = gv
        gb = gv.astype(BF)
        gbr[rr, :] = gb

        def mix(t, a):
            gm[t, rr, :] = dot_nt(gb, wpf[t]).astype(BF)
            return a

        lax.fori_loop(0, T, mix, 0, unroll=True)
        vsum[0:1] += colsum(gv)
        vsum[1:2] += colsum(g_first * n1)
        vsum[2:3] += colsum(g_first)
        vsum[3:4] += colsum(gs)
        vsum[4:5] += colsum(gr * n2)
        vsum[5:6] += colsum(gr)

    used = [cp for cp in net.items if all(cp is not own for own in tswap.values())]
    net.items = list(tswap.values())
    gmr = net.take(T * (R // CR))
    gm_in = []
    gm_own = []
    for i in range(R // CR):
        ffn(i * CR)
        if i == 0:
            for cp in used:
                cp.guard(cp.wait_sent)
        for k in range(T):
            m = (co.zz * 2 + c + k) % T
            c2, z2 = m % 2, g * H + m // 2
            hb2 = (z2 + c2 * H) % T
            src = lambda hb2=hb2, i=i: gm.at[hb2, pl.ds(i * CR, CR)]
            dst = lambda i=i: gmall.at[pl.ds(al(co.ob * R + i * CR, CR), CR)]
            if k == 0:
                gm_own.append(net.local(src, dst).start(hold=False))
                continue
            net.remote(src, dst, (2 * co.col + c2, z2), rs=gmr + k * (R // CR) + i).start()
            gm_in.append((k, i))


    def now(src, dst, dev, ss=None):
        return net.remote(src, dst, dev, ss=ss)

    quarter = co.bf * 2 + co.bs
    plane3 = (
        ((co.dpf, z), (1 - co.bf) * 2 + co.bs),
        ((co.dps, z), co.bf * 2 + 1 - co.bs),
        ((co.dpd, z), (1 - co.bf) * 2 + 1 - co.bs),
    )

    def scatter3(src, land):
        return [
            now(lambda piece=piece: src(piece), lambda j=j: land(j), dev)
            for j, (dev, piece) in enumerate(plane3)
        ]

    class Slabs:
        def __init__(self, X, k0, n, s0, r0, r1, r2, r3, rx, r3slot, stay):
            hr, q1, q2 = r0.shape[1], r1.shape[1], r2.shape[1]
            self.n, self.k0 = n, k0
            slabs = pl.ds(k0, n)
            self.start = now(
                lambda: X.at[slabs, pl.ds(al((1 - c) * hr, hr), hr)], lambda: r0.at[slabs], mate
            )
            self.s1 = now(
                lambda: s0.at[slabs, pl.ds(al((1 - co.bf) * q1, q1), q1)],
                lambda: r1.at[slabs], step1,
            )
            self.s2 = now(
                lambda: r1.at[slabs, pl.ds(al((1 - co.bs) * q2, q2), q2)],
                lambda: r2.at[slabs], step2,
            )
            self.over = [
                now(lambda k=k: r2.at[k], lambda k=k: r3.at[r3slot(k)], (co.dp, (z + k_z) % T))
                for k, k_z in stay
                if k0 <= k < k0 + n
            ]
            self.extra = [
                now(lambda: r2.at[slabs], lambda b=b: rx.at[b - 2, slabs], (co.extra(G, b), z))
                for b in range(2, G.nbits)
            ]
            self.refs = X, s0, r0, r1, r2, rx, hr, q1, q2

        def a0(self):
            X, s0, r0, r1, r2, rx, hr, q1, q2 = self.refs
            self.start.got()
            for k in range(self.k0, self.k0 + self.n):
                kept = X[k, pl.ds(al(c * hr, hr), hr), :]
                s0[k] = (kept.astype(F32) + r0[k].astype(F32)).astype(BF)

        def go(self):
            self.s1.start()

        def a1(self):
            X, s0, r0, r1, r2, rx, hr, q1, q2 = self.refs
            self.s1.got()
            for k in range(self.k0, self.k0 + self.n):
                kept = s0[k, pl.ds(al(co.bf * q1, q1), q1), :]
                r1[k] = (kept.astype(F32) + r1[k].astype(F32)).astype(BF)
            self.s2.start()

        def a2(self):
            X, s0, r0, r1, r2, rx, hr, q1, q2 = self.refs
            self.s2.got()
            for k in range(self.k0, self.k0 + self.n):
                kept = r1[k, pl.ds(al(co.bs * q2, q2), q2), :]
                r2[k] = (kept.astype(F32) + r2[k].astype(F32)).astype(BF)
            for m, cp in enumerate(self.extra):
                cp.start(hold=False)
                cp.got()
                cp.wait_sent()
                for k in range(self.k0, self.k0 + self.n):
                    r2[k] = (r2[k].astype(F32) + rx[m, k].astype(F32)).astype(BF)
            for cp in self.over:
                cp.start()

    class Back:
        def __init__(self, chains, r2, r3, gx, dst):
            q2 = r2.shape[1]
            self.chains, self.r2, self.r3 = chains, r2, r3

            def place(width, first):
                return lambda: gx.at[pl.ds(al(first * q2, q2), width * q2)]

            own = c * 4 + co.bf * 2 + co.bs
            self.own = place(1, own)
            self.back = []
            for width, first, dev in ((1, own, step2), (2, own // 2 * 2, step1), (4, c * 4, mate)):
                self.back.append(now(place(width, first), place(width, first), dev))
            self.end = net.local(lambda: gx, lambda: dst)

        def a3(self):
            tot = self.r2[0].astype(F32)
            for k, cp in enumerate(cp for ch in self.chains for cp in ch.over):
                cp.got()
                tot = tot + self.r3[k].astype(F32)
            self.own()[...] = tot.astype(BF)
            self.back[0].start()

        def a4(self):
            self.back[0].got()
            self.back[1].start()

        def a5(self):
            self.back[1].got()
            self.back[2].start()

        def a6(self):
            self.back[2].got()
            self.end.start()

    to_z = [(k, k) for k in range(1, T)]
    minus = lambda k: k - 1
    ks = list(range(1, T)) + [0]
    co_ = [Slabs(dwo, k, 1, s0o, r0o, r1o, r2o, r3o, rxo, minus, to_z) for k in ks]
    ci_ = [Slabs(dwi, k, 1, s0i, r0i, r1i, r2i, r3i, rxi, minus, to_z) for k in ks]
    cp_ = Slabs(dwp, 0, T, s0p, r0p, r1p, r2p, r3p, rxp, minus, to_z)
    slabs = [ch for pair in zip(co_[:-1], ci_[:-1]) for ch in pair] + [co_[-1], ci_[-1], cp_]
    back_o = Back(co_, r2o, r3o, go, ug)
    back_i = Back(ci_, r2i, r3i, gi, ig)
    back_p = Back([cp_], r2p, r3p, gpp, og)

    def grads(i, carry):
        k = jnp.where(i == T - 1, 0, i + 1)
        t = (z + k) % T
        dwo[k] = dot_tn(hid[t], gfeed[...]).astype(BF)
        dwi[k] = dot_tn(flow[...], gpre[t]).astype(BF)
        dwp[k] = dot_tn(mixr[t], gbr[...]).astype(BF)
        for n_ in range(T):

            @pl.when(i == n_)
            def _():
                co_[n_].start.start()
                ci_[n_].start.start()

        return carry

    lax.fori_loop(0, T, grads, 0)
    cp_.start.start()

    vb[...] = jnp.zeros(vb.shape, F32)
    vb[0:6, :] = vsum[0:6, :]
    for t in range(T):
        vb[8 + t : 9 + t, :F] = ibsum[t]

    def sum_chain(v, r, devs):
        cps = [now(lambda: v, lambda i=i: r.at[i], dev) for i, dev in enumerate(devs)]

        def step(i):
            def act():
                cps[i].got()
                cps[i].wait_sent()
                v[...] += r[i]
                if i + 1 < len(cps):
                    cps[i + 1].start(hold=False)

            return act

        return cps[0], [step(i) for i in range(len(cps))]

    plane = [step1, step2] + [(co.extra(G, b), z) for b in range(2, G.nbits)]
    vstart, vchain = sum_chain(vb, vr, [mate] + plane)
    vstart.start(hold=False)
    nv = len(vchain)
    vover = [
        now(lambda: vb, lambda k=k: vr.at[nv + k - 1], (co.dp, (z + k) % T))
        for k in range(1, T)
    ]

    def vz():
        for cp in vover:
            cp.start(hold=False)

    def vdone():
        for cp in vover:
            cp.got()
            cp.wait_sent()
        for k in range(1, T):
            vb[...] += vr[nv + k - 1]
        vout[0:8, :] = vb[0:8, :]
        vrow = lax.broadcasted_iota(jnp.int32, vb.shape, 0)
        vout[8:9, :] = colsum(jnp.where(vrow == 8 + z, vb[...], 0.0))

    vchain = vchain + [vz, vdone]

    for i, ch in enumerate(slabs):
        ch.a0()
        if i < 2:
            ch.go()
    for k, i in gm_in:
        net.remote(
            lambda: gm.at[0, pl.ds(0, CR)], lambda: gmall.at[pl.ds(0, CR)], mate,
            rs=gmr + k * (R // CR) + i, ss=gmr,
        ).got()
    for cp in gm_own:
        cp.wait_sent()


    def prepare(i, carry):
        CH = min(256, R)
        rr = pl.ds(al(i * CH, CH), CH)
        gg = gmall[rr, :].astype(F32)
        prod = gg * mixed[rr, :].astype(F32)
        lane = lanes((CH, WP))
        k = jnp.zeros((CH, WP), F32)
        for h in range(NH):
            a0 = aug_base(h)
            data = lane // HD == h
            delta = jnp.sum(jnp.where(data, prod, 0.0), axis=-1, keepdims=True)
            base = place3(jnp.zeros((CH, WP), F32), lane, a0 + 1, -delta)
            da[h, rr, :] = jnp.where(data, gg, base).astype(BF)
            k = jnp.where(data, ka[h, rr, :].astype(F32), k)
        kt[:, rr] = k.T.astype(BF)
        zero = jnp.zeros((CH, WP), F32)
        dk[rr, :] = zero
        dv[rr, :] = zero
        dq[:, rr] = zero.T
        return carry

    lax.fori_loop(0, L // min(256, R), prepare, 0)

    def btile(i, j, masked):
        qr, kr = rows(i), rows(j)
        lane = lanes((R, WP))
        sub = lax.broadcasted_iota(jnp.int32, (WP, R), 0)
        dks, dvs, dqs = [], [], []
        for h in range(NH):
            q, d = qa[h, qr, :], da[h, qr, :]
            pm = jnp.exp(dot_nt(ka[h, kr, :], q))
            if masked:
                above = lax.broadcasted_iota(jnp.int32, (R, R), 0) <= lanes((R, R))
                pm = jnp.where(above, pm, 0.0)
            ds = (pm * dot_nt(va[h, kr, :], d)).astype(BF)
            dvs.append(dot(pm.astype(BF), d))
            dks.append(dot(ds, q))
            dqs.append(dot(kt[:, kr], ds))
        if NH == 1:
            dk[kr, :] += dks[0]
            dv[kr, :] += dvs[0]
            dq[:, qr] += dqs[0]
        else:
            dk[kr, :] += jnp.where(lane < HD, dks[0], dks[1])
            dv[kr, :] += jnp.where(lane < HD, dvs[0], dvs[1])
            dq[:, qr] += jnp.where(sub < HD, dqs[0], dqs[1])

    dwq[...] = jnp.zeros(dwq.shape, F32)
    qsum[...] = jnp.zeros(qsum.shape, F32)

    def complete(b):
        rr = rows(b)
        keep = lanes((R, WP)) < G.W
        q = dq[:, rr].T * (1.0 / math.sqrt(HD))
        sums = []
        for n_, part in enumerate((q, dk[rr, :], dv[rr, :])):
            part = jnp.where(keep, part, 0.0).astype(BF)
            gp[rr, n_ * WP : (n_ + 1) * WP] = part
            sums.append(colsum(part.astype(F32)))
        gg = gp[rr, :]
        back = dot_nt(gg, wqh[...])
        ge[rr, :] = back.astype(BF)
        oc, oz = owner(G, co, b)

        @pl.when(jnp.logical_and(oc == c, oz == z))
        def _():
            ge[rr, :] = (back + gmid[...]).astype(BF)

        dwq[...] += dot_tn(emb[rr, :], gg)
        qsum[0:1, :] += jnp.concatenate(sums, axis=1)

    order_b = [(T - 1 - s_) + g * (2 * s_ - T + 1) for s_ in range(T)]
    ends = [sum(T - i for i in range(s_ + 1)) - 1 for s_ in range(T)]
    half = R // 2
    edge_z = H - 1 + g
    at_edge = z == edge_z
    eh_sem = net.take(max(H - 1, 1))

    def slot_of(z_to):
        return (co.zz - (z_to - g * H) + H - 1) % H

    class Rows:
        def __init__(self, s_):
            b = order_b[s_]
            self.s, self.b, self.inside = s_, b, s_ >= H
            self.core = net.remote(
                lambda: ge.at[pl.ds(al(b * R + (1 - c) * half, half), half)],
                lambda: ec.at[s_], mate,
            )
            h = lambda: hsum.at[s_]
            if self.inside:
                slot, self.base = slot_of(b), eh_sem
                self.home_chip = z == b
                self.over = net.remote(
                    h, lambda: eh.at[slot], (co.dp, b), jnp.logical_not(self.home_chip),
                    rs=self.base + slot,
                )
            else:
                slot, self.base = slot_of(edge_z), net.take(max(H - 1, 1))
                self.over = net.remote(
                    h, lambda: eo.at[s_, slot], (co.dp, edge_z), jnp.logical_not(at_edge),
                    rs=self.base + slot,
                )
                self.home = net.remote(
                    lambda: hsend.at[s_], lambda: foreign, (co.dp, b), at_edge, rs=f_sem
                )

        def k0(self):
            self.core.start()

        def k1(self):
            s_ = self.s
            self.core.got()
            own = ge[pl.ds(al(self.b * R + c * half, half), half), :].astype(F32)
            hsum[s_] = (own + ec[s_].astype(F32)).astype(BF)
            self.over.start()

        def collect(self, land):
            total = hsum[self.s].astype(F32)
            for j in range(H - 1):
                net.remote(
                    lambda: hsum.at[0], lambda: land(j), mate, rs=self.base + j, ss=self.base
                ).got()
                total = total + land(j)[...].astype(F32)
            return total.astype(BF)

        def kx(self):
            @pl.when(at_edge)
            def _():
                hsend[self.s] = self.collect(lambda j: eo.at[self.s, j])

            self.home.start()

        def ky(self):
            @pl.when(self.home_chip)
            def _():
                native_half[...] = self.collect(lambda j: eh.at[j])

    f_sem = net.take()
    parts_ = [Rows(s_) for s_ in range(T)]
    foreign_in = net.remote(lambda: hsend.at[0], lambda: foreign, mate, rs=f_sem, ss=f_sem)
    to_mate = net.remote(
        lambda: give, lambda: nat.at[pl.ds(al(c * half, half), half)], mate
    )
    from_mate_half = net.remote(
        lambda: give, lambda: nat.at[pl.ds(al((1 - c) * half, half), half)], mate,
        ss=to_mate.ss, rs=to_mate.rs,
    )
    q2p = half // 4
    p_rs = scatter3(lambda piece: hp.at[pl.ds(al(piece * q2p, q2p), q2p)], lambda j: ps1.at[j])
    p_more = []
    size = q2p
    for n_, bit in enumerate(range(2, G.nbits)):
        size = size // 2
        bb = (co.col // (1 << bit)) % 2
        src = ps2 if n_ == 0 else (px if n_ % 2 == 1 else py)
        dst = px if n_ % 2 == 0 else py
        cp = net.remote(
            lambda src=src, bb=bb, size=size: src.at[pl.ds(al((1 - bb) * size, 8), size)],
            lambda dst=dst, size=size: dst.at[pl.ds(0, size)], (co.extra(G, bit), z),
        )
        p_more.append((cp, src, dst, bb, size))
    p_last = p_more[-1][2] if p_more else ps2
    p_fin = net.remote(lambda: p_last.at[pl.ds(0, G.PR)], lambda: pf, (pdp, pz), away)

    def p_first():
        foreign_in.got()
        own, other_ = native_half[...], foreign[...]
        give[...] = jnp.where(co.native, other_, own)
        to_mate.start()
        nat[pl.ds(al(c * half, half), half), :] = jnp.where(co.native, own, other_)
        hp[...] = (own.astype(F32) + other_.astype(F32)).astype(hp.dtype)
        for cp in p_rs:
            cp.start()

    def p_second():
        total = hp[pl.ds(al(quarter * q2p, q2p), q2p), :].astype(F32)
        for j, cp in enumerate(p_rs):
            cp.got()
            total = total + ps1[j].astype(F32)
        ps2[...] = total.astype(ps2.dtype)
        for cp, src, dst, bb, size in p_more:
            cp.start()
            cp.got()
            kept = src[pl.ds(al(bb * size, 8), size), :].astype(F32)
            dst[0:size, :] = (kept + dst[0:size, :].astype(F32)).astype(dst.dtype)
        p_fin.start()

    def p_third():
        pl.when(away)(p_fin.got)

        @pl.when(jnp.logical_not(away))
        def _():
            pf[...] = p_last[0 : G.PR, :]

        pr3[...] = pf[...].astype(F32)
        net.local(lambda: pr3, lambda: pgrad).start()

    def igrad_out():
        from_mate_half.got()
        net.local(lambda: nat, lambda: igrad).start()

    def run(chain, i):
        chain[i]()

    jobs = {("v", i): act for i, act in enumerate(vchain)}
    for i, ch in enumerate(slabs):
        if i >= 2:
            jobs["s", i] = ch.go
        jobs["1", i] = ch.a1
        jobs["2", i] = ch.a2
    for name, bk in (("o", back_o), ("i", back_i), ("p", back_p)):
        for n_, act in enumerate((bk.a3, bk.a4, bk.a5, bk.a6)):
            jobs[name, n_] = act
    for rw in parts_:
        for name in ("k0", "k1", "ky" if rw.inside else "kx"):
            jobs[name, rw.s] = getattr(rw, name)
    plan = {
        0: [],
        1: [("v", 0)],
        2: [],
        3: [("k0", 0), ("v", 1)],
        4: [("k1", 0)],
        5: [("v", 2), ("v", 3)],
        6: [("k0", 1)],
        7: [("k1", 1), ("kx", 0)],
        8: [("k0", 2), ("v", 4)],
        9: [("k0", 3), ("k1", 2), ("kx", 1)],
    }
    for i in range(10):
        plan[i] += [("1", i), ("2", i - 2), ("s", i + 2)]
    plan = {i: [key for key in acts if key in jobs] for i, acts in plan.items()}
    if ntiles != 10:
        plan = {e: [("k0", s_)] for s_, e in enumerate(ends)}
    left = [key for key in jobs if not any(key in acts for acts in plan.values())]
    def btiles(t, carry):
        s_, u = 0, t
        for k in range(1, T):
            past = (t > ends[k - 1]).astype(jnp.int32)
            s_ = s_ + past
            u = u - past * (T - k + 1)
        b = (T - 1 - s_) + g * (2 * s_ - T + 1)
        far = b - u + g * (2 * u)

        @pl.when(u == 0)
        def _():
            btile(b, b, True)

        @pl.when(u > 0)
        def _():
            btile(jnp.maximum(b, far), jnp.minimum(b, far), False)

        @pl.when(u == T - 1 - s_)
        def _():
            complete(b)

        for i in range(ntiles):
            acts = [jobs[key] for key in plan.get(i, ())]
            if acts:

                @pl.when(t == i)
                def _(acts=acts):
                    for act in acts:
                        act()

        return carry

    lax.fori_loop(0, ntiles, btiles, 0)

    dwqb[c] = dwq[...].astype(BF)
    hq = D // 2
    e8 = D // 8
    qstart = now(
        lambda: dwqb.at[c, pl.ds(al((1 - c) * hq, hq), hq)], lambda: r0q.at[c], mate
    ).start()
    q_rs = scatter3(lambda piece: s0q.at[:, pl.ds(al(piece * e8, e8), e8)], lambda j: r1q.at[j])
    q_extra = [
        now(lambda: r2q, lambda b=b: rxq.at[b - 2], (co.extra(G, b), z)) for b in range(2, G.nbits)
    ]
    q_over = now(lambda: r2q.at[1], lambda: r3q.at[0], (co.dp, co.other))
    q_own = lambda: gq.at[pl.ds(al((c * 4 + quarter) * e8, e8), e8)]
    q_ag = [now(q_own, q_own, dev) for dev, _ in plane3]
    q_half = lambda: gq.at[pl.ds(al(c * hq, hq), hq)]
    q_core = now(q_half, q_half, mate)
    q_out = net.local(lambda: gq, lambda: qg)

    def q_sum():
        total = s0q[:, pl.ds(al(quarter * e8, e8), e8), :].astype(F32)
        for j, cp in enumerate(q_rs):
            cp.got()
            total = total + r1q[j].astype(F32)
        r2q[...] = total.astype(BF)
        for m, cp in enumerate(q_extra):
            cp.start(hold=False)
            cp.got()
            cp.wait_sent()
            r2q[...] = (r2q[...].astype(F32) + rxq[m].astype(F32)).astype(BF)
        q_over.start()

    def q_back():
        q_over.got()
        q_own()[...] = (r2q[0].astype(F32) + r3q[0].astype(F32)).astype(BF)
        for cp in q_ag:
            cp.start()

    def q_join():
        for cp in q_ag:
            cp.got()
        q_core.start()

    def q_end():
        q_core.got()
        q_out.start()

    qb[c] = qsum[...]
    qmate = now(lambda: qb.at[c], lambda: qb.at[c], mate).start(hold=False)
    qsums, qchain2 = sum_chain(qb, qr, plane)
    qover = now(lambda: qb.at[1], lambda: qr.at[len(plane), 0], (co.dp, co.other))

    def rest(*names):
        for key in left:
            if key[0] in names:
                jobs[key]()

    def backs(n_):
        for key in left:
            if key[0] in "oip" and key[1] == n_:
                jobs[key]()

    rest("k1")
    pltpu.make_async_remote_copy(
        src_ref=dwqb.at[c, pl.ds(0, hq)], dst_ref=r0q.at[1 - c], send_sem=net.sem(qstart.ss),
        recv_sem=net.sem(qstart.rs), device_id=mate, device_id_type=MESH,
    ).wait_recv()
    s0q[c] = dwqb[c, pl.ds(al(c * hq, hq), hq), :]
    s0q[1 - c] = r0q[1 - c]
    for cp in q_rs:
        cp.start()
    qmate.got()
    qmate.wait_sent()
    qsums.start(hold=False)
    rest("s", "1", "v")
    rest("2")
    rest("kx")
    backs(0)
    qchain2[0]()
    rest("ky")
    p_first()
    q_sum()
    for i in range(1, len(qchain2)):
        qchain2[i]()
    qover.start(hold=False)
    backs(1)
    igrad_out()
    p_second()
    q_back()
    qover.got()
    qover.wait_sent()
    qb[0] += qr[len(plane), 0]
    vout[9:10, :WP] = qb[0, 0:1, :WP]
    vout[10:11, :WP] = qb[0, 0:1, 2 * WP :]
    backs(2)
    q_join()
    backs(3)
    p_third()
    q_end()
    for off in o_out:
        pl.when(co.swapped)(o_out[off][1].got)
    net.drain()
    assert net.n <= sem.shape[0], net.n


def emit_kernel(
    G, out_in, igrad_in, pgrad_in, qg_in, og_in, ig_in, ug_in, vin,
    out, igrad, pgrad, qg, qvg, og, ig, ug, ibg, v0, v1, v2, v3, v4, v5,
):
    out[...] = out_in[...]
    igrad[...] = igrad_in[...]
    pgrad[...] = pgrad_in[...]
    for j in range(3):
        qg[j] = qg_in[:, j * G.WP : j * G.WP + G.W].astype(F32)
    qvg[...] = vin[9:11, : G.W]
    og[...] = og_in[: G.W, :].astype(F32)
    ig[...] = ig_in[...].astype(F32)
    ug[...] = ug_in[...].astype(F32)
    ibg[...] = vin[8:9, : G.F].reshape(G.F)
    for i, v in enumerate((v0, v1, v2, v3, v4, v5)):
        v[...] = vin[i : i + 1, :].reshape(G.D)


def on_device(G, *args):
    (inputs, teacher, lengths, positions, qkv_weight, query_value_bias, output_weight, output_bias,
     first_gain, first_shift, inner_weight, inner_bias, outer_weight, outer_bias, second_gain,
     second_shift) = args
    T, R, D, L, W, WP, NH, F, H = G.T, G.R, G.D, G.L, G.W, G.WP, G.NH, G.F, G.H
    dma = lambda n: pltpu.SemaphoreType.DMA((n,))
    vm = pltpu.VMEM
    wq = jnp.pad(jnp.transpose(qkv_weight, (1, 0, 2)), ((0, 0), (0, 0), (0, WP - W)))
    wp = jnp.pad(output_weight, ((0, WP - W), (0, 0)))
    sizes = [(D, F, T), (F, D, T), (WP, D, T), (D, 3 * WP, 2)]
    nplane = G.nbits
    V = 8 + (T + 7) // 8 * 8
    scratch = [
        vm((L, D), BF), vm((L, D), BF), vm((L, D), BF),
        vm((NH, L, WP), BF), vm((NH, L, WP), BF), vm((NH, L, WP), BF), vm((NH, L, WP), BF),
        vm((WP, L), BF), vm((2, L, WP), F32), vm((NH, L, WP), F32), vm((L, WP), BF),
        vm((T, R, WP), BF),
        vm((8, D), F32), vm((3, D, WP), BF), vm((3, D, WP), BF), vm((D, 3 * WP), BF),
        vm((T, D, F), BF), vm((T, F, D), BF),
        vm((T, WP, D), BF), vm((T, 8, D), F32), vm((R, D), BF),
        vm((R, D), BF), vm((T, R, F), BF), vm((T, R, F), BF), vm((R, D), BF), vm((R, D), BF),
        vm((R, D), F32), vm((R, D), BF), vm((T, R, WP), BF), vm((L, WP), BF), vm((8, D), F32),
        vm((T, 1, F), F32),
        vm((T, D, F), BF), vm((T, F, D), BF), vm((T, WP, D), BF), vm((WP, L), F32),
        vm((L, 3 * WP), BF),
        vm((D, 3 * WP), F32), vm((2, D, 3 * WP), BF), vm((8, 3 * WP), F32),
    ]
    for shift in (1, 1, 2, 3):
        scratch += [vm((n, r >> shift, w), BF) for r, w, n in sizes]
        if shift == 2:
            scratch[-1] = vm((3, 2, D >> 3, 3 * WP), BF)
    scratch += [vm((T - 1, r >> 3, w), BF) for r, w, n in sizes[:3]] + [vm((1, D >> 3, 3 * WP), BF)]
    more = G.nbits - 2
    PD = BF if G.PR % 16 == 0 else F32
    scratch += [vm((more, n, r >> 3, w) if more else (1, 1, 16, 128), BF) for r, w, n in sizes]
    scratch += [vm((r, w), BF) for r, w, n in sizes]
    scratch += [
        vm((T, R // 2, D), BF), vm((T, R // 2, D), BF), vm((R // 2, D), PD),
        vm((H, max(H - 1, 1), R // 2, D), BF), vm((max(H - 1, 1), R // 2, D), BF),
        vm((H, R // 2, D), BF), vm((R // 2, D), BF), vm((R // 2, D), BF), vm((R // 2, D), BF),
        vm((R, D), BF), vm((3, R // 8, D), PD), vm((R // 8, D), PD),
        vm((max(R // 16, 8), D) if more else (8, 128), PD),
        vm((max(R // 32, 8), D) if more else (8, 128), PD), vm((G.PR, D), PD),
        vm((G.PR, D), F32), vm((V, D), F32), vm((1 + nplane + T - 1, V, D), F32),
        vm((2, 8, 3 * WP), F32), vm((nplane + 1, 2, 8, 3 * WP), F32), dma(21 * T * T),
    ]
    outs = [
        ((R, D), BF), ((R, D), BF), ((G.PR, D), F32), ((D, 3 * WP), BF),
        ((WP, D), BF), ((D, F), BF), ((F, D), BF), ((16, D), F32),
    ]
    anyspec = pl.BlockSpec(memory_space=pl.ANY)
    results = pl.pallas_call(
        functools.partial(layer_kernel, G),
        out_shape=tuple(jax.ShapeDtypeStruct(s, d) for s, d in outs),
        in_specs=[SM] + [anyspec] * 7 + [VM] * 8,
        out_specs=tuple([anyspec] * 7 + [VM]),
        scratch_shapes=scratch,
        compiler_params=pltpu.CompilerParams(
            vmem_limit_bytes=63 << 20, collective_id=0, has_side_effects=True
        ),
        name="layer",
    )(lengths, inputs, teacher, wq, inner_weight, outer_weight, wp, positions, query_value_bias,
      inner_bias, output_bias, first_gain, first_shift, outer_bias, second_gain, second_shift)
    finals = [
        ((R, D), BF), ((R, D), BF), ((G.PR, D), F32), ((3, D, W), F32), ((2, W), F32),
        ((W, D), F32), ((D, F), F32), ((F, D), F32), ((F,), F32),
    ] + [((D,), F32)] * 6
    (out, igrad, pgrad, qg, qvg, og, ig, ug, ibg, *vs) = pl.pallas_call(
        functools.partial(emit_kernel, G),
        out_shape=tuple(jax.ShapeDtypeStruct(s, d) for s, d in finals),
        in_specs=[VM] * 8,
        out_specs=tuple([VM] * 15),
        compiler_params=pltpu.CompilerParams(vmem_limit_bytes=63 << 20),
        name="emit",
    )(*results)
    return (
        out, igrad, pgrad, jnp.transpose(qg, (1, 0, 2)), qvg, og, vs[0], vs[1], vs[2],
        ig, ibg, ug, vs[3], vs[4], vs[5],
    )


def solution(mesh):
    rows = P(("dp", "tensor"), None)
    specs = (
        rows, rows, P(), P(), P(None, None, "tensor"), P(None, "tensor"), P("tensor", None), P(),
        P(), P(), P(None, "tensor"), P("tensor"), P("tensor", None), P(), P(), P(),
    )
    outs = (
        rows, rows, rows, P(None, None, "tensor"), P(None, "tensor"), P("tensor", None), P(), P(),
        P(), P(None, "tensor"), P("tensor"), P("tensor", None), P(), P(), P(),
    )

    def step(*args):
        G = Geo(mesh, args[2].shape[0], args[3].shape[0], args[0].shape[1], args[11].shape[0])
        body = jax.shard_map(
            functools.partial(on_device, G), mesh=mesh, in_specs=specs, out_specs=outs,
            check_vma=False,
        )
        return body(*args)

    return step
```
